32 devices in a mesh: replica: 4 (over y, x), fsdp: 8 (over z, core).
Axes of the slice: x: 2, y: 2, z: 4, core: 2. Of those that a mesh axis runs over, the one named last changes fastest.
Arguments:
- hidden_in: bfloat16 [8192, 1024], P(('replica', 'fsdp')), may hold values from -8 to 8
- seq_lengths: int32 [32, 4], P(('replica', 'fsdp')), may hold values from 0 to 256, as said below
- routes: int32 [8192, 8], P(('replica', 'fsdp')), may hold values from 0 to 15, all different within a row; in each aligned block of 256 rows (0 to 255, 256 to 511, ...) at most 144 rows name the same one
- norm1_gain: bfloat16 [1024], P('fsdp'), may hold values from 0.25 to 1.75
- w_query: bfloat16 [1024, 1024], P('fsdp'), may hold values from -1 to 1
- w_key: bfloat16 [1024, 512], P('fsdp'), may hold values from -1 to 1
- w_value: bfloat16 [1024, 512], P('fsdp'), may hold values from -0.1875 to 0.1875
- w_output: bfloat16 [1024, 1024], P('fsdp'), may hold values from -6 to 6
- norm2_gain: bfloat16 [1024], P('fsdp'), may hold values from 0.25 to 1.75
- w_router: bfloat16 [1024, 16], P('fsdp'), may hold values from -3 to 3
- expert_weights: bfloat16 [16, 1536, 1024], P('fsdp'), may hold values from -3 to 3
- out_cotangent: bfloat16 [8192, 1024], P(('replica', 'fsdp')), may hold values from -6 to 6
Outputs:
- layer_out: bfloat16 [8192, 1024], P(('replica', 'fsdp'))
- grad_in: float32 [8192, 1024], P(('replica', 'fsdp'))
- grad_norm1: float32 [1024], P('fsdp')
- grad_query: float32 [1024, 1024], P('fsdp')
- grad_key: float32 [1024, 512], P('fsdp')
- grad_value: float32 [1024, 512], P('fsdp')
- grad_output: float32 [1024, 1024], P('fsdp')
- grad_norm2: float32 [1024], P('fsdp')
- grad_router: float32 [1024, 16], P('fsdp')
- grad_experts: float32 [16, 1536, 1024], P('fsdp')
The draws below stay inside these ranges and needn't reach their ends.
Inputs may be any that keep to these rules, and one draw needn't show every extreme that they name: `seq_lengths`: each row sums to 256; a length may be 0; some row holds one sequence of 256. `routes`: A token's experts differ; among the rows of one device no expert is named more than 144 times, a bound that some block reaches.
All inputs are finite; a program needn't handle non-finite values.
Results may differ from the reference program's by a relative error of at most 0.015.
The reference program's roundings to bfloat16 on the way count: a program that leaves them out, or rounds other values in their place, can miss the bound.
Values may be sent and summed in bfloat16 or wider, within the bound.
A program may use at most 384 MiB of HBM per device.

```python
import math
import jax
import jax.numpy as jnp
import numpy as np
from jax import lax

D = 1024
H = 16
KVH = 8
HD = 64
FF = 512
TOPK = 8
E = 16
SEQ_SLOTS = 4
TOK_DEV = 256
CAP = 144
DEVS = 32
TOKENS = 8192


def draw_hidden_in(key, part):
    base = jax.random.normal(jax.random.fold_in(key, 1), (TOKENS, D), jnp.float32)
    return jnp.clip(base, -6.0, 6.0).astype(jnp.bfloat16)


def draw_w_query(key, part):
    base = jnp.clip(jax.random.normal(jax.random.fold_in(key, 4), (D, H * HD), jnp.float32), -6.0, 6.0) * D ** (-0.5)
    return base.astype(jnp.bfloat16)


def draw_w_key(key, part):
    base = jnp.clip(jax.random.normal(jax.random.fold_in(key, 5), (D, KVH * HD), jnp.float32), -6.0, 6.0) * D ** (-0.5)
    return base.astype(jnp.bfloat16)


def draw_w_router(key, part):
    base = jnp.clip(jax.random.normal(jax.random.fold_in(key, 6), (D, E), jnp.float32), -5.0, 5.0) * 0.25 * D ** (-0.5)
    return base.astype(jnp.bfloat16)


def draw_expert_weights(key, part):
    base = jnp.clip(jax.random.normal(jax.random.fold_in(key, 7), (E, 3 * FF, D), jnp.float32), -6.0, 6.0)
    return (base * (2.0 * D ** (-0.5))).astype(jnp.bfloat16)


def draw_seq_lengths(key, part):
    counts = jax.random.randint(jax.random.fold_in(key, 21), (DEVS,), 1, SEQ_SLOTS + 1)
    single = jax.random.randint(jax.random.fold_in(key, 22), (), 0, DEVS)
    counts = jnp.where(jnp.arange(DEVS) == single, 1, counts)
    cuts = jnp.sort(jax.random.randint(jax.random.fold_in(key, 23), (DEVS, SEQ_SLOTS - 1), 1, TOK_DEV), axis=1)
    used = jnp.arange(SEQ_SLOTS - 1)[None, :] < counts[:, None] - 1
    cuts = jnp.where(used, cuts, TOK_DEV)
    bounds = jnp.concatenate([jnp.zeros((DEVS, 1), jnp.int32), cuts.astype(jnp.int32), jnp.full((DEVS, 1), TOK_DEV, jnp.int32)], axis=1)
    return (bounds[:, 1:] - bounds[:, :-1]).astype(jnp.int32)


def shard_levels(rng, shape, shards, least, top_value):
    level, own = 1.0, jax.random.fold_in(rng, 6)
    for axis_at, shards_of in shards:
        heights = jnp.exp(jax.random.uniform(jax.random.fold_in(own, axis_at), (shards_of,), jnp.float32, least / len(shards), top_value / len(shards)))
        level = level * jnp.repeat(heights, shape[axis_at] // shards_of).reshape([-1 if axis == axis_at else 1 for axis in range(len(shape))])
    return level


def assign_block(rng, own, number, rows, count, top, limit, lean):
    sequence = jax.random.permutation(rng, count)
    crowded, usual = shares(count, rows * top, limit, lean, True), shares(count, rows * top, limit, lean, False)
    places = jnp.arange(count)

    def named(sizes, rotation):
        used = int((sizes > 0).sum())
        fixed = max(1, used // 4)
        shifted = fixed + (places - fixed + rotation * (used - fixed)) % max(1, count - fixed)
        return jnp.zeros((count,), jnp.int32).at[sequence[jnp.where(places < fixed, places, shifted)]].set(jnp.asarray(sizes, jnp.int32))

    sizes = jnp.where(number % 4 == 0, named(crowded, number // 4), named(usual, number - number // 4 - 1))
    mixed = jax.random.permutation(jax.random.fold_in(own, 3), count)
    giver, taker = mixed[0:count // 2 * 2:2], mixed[1:count // 2 * 2:2]
    room = jnp.minimum(sizes[giver] - 1, limit - sizes[taker]) // 2
    room = jnp.where((giver == sequence[0]) | (taker == sequence[0]) | (sizes[taker] == 0), 0, jnp.maximum(room, 0))
    shifted = jax.random.randint(jax.random.fold_in(own, 4), (count // 2,), 0, 1 << 20) % (room + 1)
    sizes = sizes.at[giver].add(-shifted).at[taker].add(shifted)
    items = jnp.searchsorted(jnp.cumsum(sizes), jnp.arange(rows * top), side="right").astype(jnp.int32)
    table = items.reshape(top, rows).T
    table = table[jax.random.permutation(jax.random.fold_in(own, 1), rows)]
    rotation = jax.random.randint(jax.random.fold_in(own, 2), (rows, 1), 0, top)
    return jnp.take_along_axis(table, (jnp.arange(top)[None, :] + rotation) % top, axis=1)


def shares(number_of, total, most, slope, full):
    loads = [(1 << 20) // math.isqrt(standing ** slope) + 1 for standing in range(1, number_of + 1)]
    largest = most if full else min(most, max(-(-total // number_of), total * loads[0] // sum(loads)))
    least = 1 if total - largest >= number_of - 1 else 0
    holding, rest = [largest] + [least] * (number_of - 1), total - largest - least * (number_of - 1)
    while rest > 0:
        candidates = [i for i in range(1, number_of) if holding[i] < largest] or [i for i in range(1, number_of) if holding[i] < most]
        whole, left = sum([loads[i] for i in candidates]), rest
        for i in candidates:
            addition = min(most - holding[i], max(1, left * loads[i] // whole), rest)
            holding[i] = holding[i] + addition
            rest = rest - addition
    return np.array(holding)


def gaussian(key, shape, deviation, limit, shards=(), held_as=jnp.bfloat16):
    factor_of = shard_levels(key, shape, shards, -0.22, 0.18) if shards else 1.0
    entries = jax.random.normal(key, shape, jnp.float32) * deviation * factor_of
    return jnp.minimum(jnp.maximum(entries, -limit), limit).astype(held_as)


def setup_inputs(seed: int = 0) -> dict:
    splits = jax.random.split(jax.random.key(seed), 13)
    hidden_in = draw_hidden_in(jax.random.fold_in(splits[12], 71), 0)
    seq_lengths = draw_seq_lengths(jax.random.fold_in(splits[12], 71), 0)
    routes_keys = jax.random.split(jax.random.fold_in(splits[2], 1), TOKENS // TOK_DEV)
    routes_turns = jax.random.permutation(jax.random.fold_in(splits[2], 3), TOKENS // TOK_DEV)
    routes = jax.vmap(lambda own, number: assign_block(jax.random.fold_in(splits[2], 2), own, number, TOK_DEV, E, TOPK, CAP, 1))(routes_keys, routes_turns).reshape((TOKENS, TOPK))
    norm1_gain = jnp.clip(1.0 + 0.15 * jax.random.normal(splits[3], (D,), jnp.float32), 0.25, 1.75).astype(jnp.bfloat16)
    w_query = draw_w_query(jax.random.fold_in(splits[12], 71), 0)
    w_key = draw_w_key(jax.random.fold_in(splits[12], 71), 0)
    w_value = gaussian(splits[6], (D, KVH * HD), D ** -0.5, 0.1875, ((0, 8),))
    w_output = gaussian(splits[7], (H * HD, D), 0.6, 6.0, ((0, 8),))
    norm2_gain = jnp.clip(1.0 + 0.15 * jax.random.normal(splits[8], (D,), jnp.float32), 0.25, 1.75).astype(jnp.bfloat16)
    w_router = draw_w_router(jax.random.fold_in(splits[12], 71), 0)
    expert_weights = draw_expert_weights(jax.random.fold_in(splits[12], 71), 0)
    out_cotangent = gaussian(splits[11], (TOKENS, D), 1.0, 6.0, ((0, 32),))
    return dict(hidden_in=hidden_in, seq_lengths=seq_lengths, routes=routes, norm1_gain=norm1_gain, w_query=w_query, w_key=w_key, w_value=w_value, w_output=w_output, norm2_gain=norm2_gain, w_router=w_router, expert_weights=expert_weights, out_cotangent=out_cotangent)


norm_eps = 1e-06
score_scale = 0.015625
residual_scale = 0.22
rope_base = 10000.0
masked_score = -1e+30

@jax.custom_vjp
def low(v):
    return lax.optimization_barrier(v.astype(jnp.bfloat16)).astype(jnp.float32)

@jax.custom_vjp
def low_back(v):
    return v

def low_keep(v):
    return (low(v), None)

def low_pass(kept, grad):
    return (grad,)

def back_keep(v):
    return (v, None)

def back_low(kept, grad):
    return (low(grad),)
low.defvjp(low_keep, low_pass)
low_back.defvjp(back_keep, back_low)

def matmul(left, right):
    return jnp.dot(left, right, precision=lax.Precision.HIGHEST, preferred_element_type=jnp.float32)

def product(form, left, right):
    return jnp.einsum(form, left, right, precision=lax.Precision.HIGHEST, preferred_element_type=jnp.float32)

def rms_scale(vector, gain_full):
    return vector * lax.rsqrt(lax.optimization_barrier(jnp.mean(vector * vector, axis=-1, keepdims=True)) + norm_eps) * gain_full

def rotate(vector, cosines, sine_table):
    half_size = vector.shape[-1] // 2
    turned = jnp.concatenate([-vector[..., half_size:], vector[..., :half_size]], axis=-1)
    return vector * cosines[:, None, :] + turned * sine_table[:, None, :]

def layer_block(weights_all, block_in):
    gain_one, query_w, key_w, value_w, output_w, gain_two, router_w, experts = weights_all
    hidden, lengths, route_rows = block_in
    tokens = hidden.shape[0]
    group = H // KVH
    token_index = jnp.arange(tokens, dtype=jnp.int32)
    seq_ends = jnp.cumsum(lengths).astype(jnp.int32)
    passed = token_index[:, None] >= seq_ends[None, :]
    segment = lax.optimization_barrier(jnp.sum(passed.astype(jnp.int32), axis=1)).astype(jnp.int32)
    position = (token_index - lax.optimization_barrier(jnp.max(jnp.where(passed, seq_ends[None, :], 0), axis=1))).astype(jnp.int32)
    frequency = rope_base ** (-jnp.arange(0, HD, 2).astype(jnp.float32) / HD)
    angles = position.astype(jnp.float32)[:, None] * frequency[None, :]
    angles = jnp.concatenate([angles, angles], axis=1)
    cosines = jnp.cos(angles)
    sine_table = jnp.sin(angles)
    normed = low(rms_scale(hidden, gain_one))
    query = low(rotate(low_back(matmul(normed, query_w)).reshape(tokens, H, HD), cosines, sine_table))
    query = query.reshape(tokens, KVH, group, HD)
    key_rot = low(rotate(low_back(matmul(normed, key_w)).reshape(tokens, KVH, HD), cosines, sine_table))
    value_rows = low(low_back(matmul(normed, value_w))).reshape(tokens, KVH, HD)
    scores = low_back(score_scale * product('qkgd,tkd->kgqt', query, key_rot))
    allowed = (segment[:, None] == segment[None, :]) & (token_index[None, :] <= token_index[:, None])
    scores = jnp.where(allowed[None, None], scores, masked_score)
    weights = low(jax.nn.softmax(scores, axis=-1))
    mixed = product('kgqt,tkd->qkgd', weights, value_rows)
    mixed = low_back(low(mixed.reshape(tokens, H * HD)))
    after = hidden + residual_scale * low_back(matmul(mixed, output_w))
    normed_two = low(rms_scale(after, gain_two))
    logits = low_back(matmul(normed_two, router_w))
    chosen = jnp.take_along_axis(logits, route_rows, axis=1)
    gate_probs = jax.nn.softmax(chosen, axis=-1)
    flat_routes = route_rows.reshape(-1).astype(jnp.int32)
    flat_hits = (flat_routes[:, None] == jnp.arange(E, dtype=jnp.int32)[None, :]).astype(jnp.int32)
    running = jnp.cumsum(flat_hits, axis=0).astype(jnp.int32) - flat_hits
    slot_rank = lax.optimization_barrier(jnp.sum(running * flat_hits, axis=1)).astype(jnp.int32)
    slot_ids = (flat_routes * CAP + slot_rank).astype(jnp.int32)
    numbered = jnp.arange(tokens * TOPK, dtype=jnp.int32) + 1
    slot_owner = jnp.zeros((E * CAP,), jnp.int32).at[slot_ids].set(numbered) - 1
    filled = slot_owner >= 0
    owner_rows = (jnp.maximum(slot_owner, 0) // TOPK).astype(jnp.int32)
    slot_inputs = low_back(jnp.where(filled[:, None], normed_two[owner_rows], 0.0)).reshape(E, CAP, D)
    gate_pre = low_back(product('ecd,efd->ecf', slot_inputs, experts[:, :FF]))
    up_pre = low_back(product('ecd,efd->ecf', slot_inputs, experts[:, FF:2 * FF]))
    hidden_act = low(jax.nn.silu(gate_pre) * up_pre)
    produced = low(low_back(product('ecf,efd->ecd', hidden_act, experts[:, 2 * FF:]))).reshape(E * CAP, D)
    picked = produced[slot_ids].reshape(tokens, TOPK, D)
    mixture = lax.optimization_barrier(jnp.sum(gate_probs[:, :, None] * picked, axis=1))
    return after + residual_scale * mixture

def reference(hidden_in, seq_lengths, routes, norm1_gain, w_query, w_key, w_value, w_output, norm2_gain, w_router, expert_weights, out_cotangent):
    params = (norm1_gain.astype(jnp.float32), w_query.astype(jnp.float32), w_key.astype(jnp.float32), w_value.astype(jnp.float32), w_output.astype(jnp.float32), norm2_gain.astype(jnp.float32), w_router.astype(jnp.float32), expert_weights.astype(jnp.float32))
    hidden = hidden_in.astype(jnp.float32).reshape(DEVS, TOK_DEV, D)
    route_blocks = routes.reshape(DEVS, TOK_DEV, TOPK)

    def forward(weights_all, hidden_all):
        stepper = jax.checkpoint(lambda block_in: layer_block(weights_all, block_in))
        return lax.map(stepper, (hidden_all, seq_lengths, route_blocks))
    result, pullback = jax.vjp(forward, params, hidden)
    grad_params, grad_hidden = pullback(out_cotangent.astype(jnp.float32).reshape(DEVS, TOK_DEV, D))
    return (result.reshape(TOKENS, D).astype(jnp.bfloat16), grad_hidden.reshape(TOKENS, D), grad_params[0], grad_params[1], grad_params[2], grad_params[3], grad_params[4], grad_params[5], grad_params[6], grad_params[7])
```

```python
import jax
import jax.numpy as jnp
import numpy as np
from jax import lax
from jax.experimental import pallas as pl
from jax.experimental.pallas import tpu as pltpu
from jax.sharding import PartitionSpec as P

D = 1024
H = 16
KVH = 8
HD = 64
FF = 512
TOPK = 8
E = 16
CAP = 144
LANE = 128
QKVO = H * HD + 2 * KVH * HD + D

norm_eps = 1e-06
score_scale = 0.015625
residual_scale = 0.22
rope_base = 10000.0
masked_score = -1e30

BF = jnp.bfloat16
F32 = jnp.float32
VMEM_LIMIT = 60 * 2**20


def dot(a, b):
    return lax.dot_general(a, b, (((1,), (0,)), ((), ())), preferred_element_type=F32)


def dot_nt(a, b):
    return lax.dot_general(a, b, (((1,), (1,)), ((), ())), preferred_element_type=F32)


def dot_tn(a, b):
    return lax.dot_general(a, b, (((0,), (0,)), ((), ())), preferred_element_type=F32)


def lanes_of(rows):
    return lax.broadcasted_iota(jnp.int32, (rows, LANE), 1)


def turned(block, lane):
    return jnp.where(lane % HD < HD // 2, pltpu.roll(block, LANE - HD // 2, 1), pltpu.roll(block, HD // 2, 1))


def halves(block, low):
    zero = jnp.zeros_like(block)
    return jnp.concatenate([jnp.where(low, block, zero), jnp.where(low, zero, block)], axis=0)


def attention_forward(
    x_ref, len_ref, routes_ref, cos_ref, sin_ref, w_ref,
    q_ref, kd_ref, vd_ref, p_ref, o_ref, h1_ref, n2_ref, gd_ref, gt_ref,
):
    tokens = x_ref.shape[0]
    lane = lanes_of(tokens)
    low = lane < HD
    small = w_ref[:, QKVO:].astype(F32).T
    gain_one, gain_two = small[E : E + 1], small[E + 1 : E + 2]
    source = x_ref[...].astype(F32)
    factor = lax.rsqrt(jnp.mean(source * source, axis=1, keepdims=True) + norm_eps)
    normed = (source * factor * gain_one).astype(BF)
    cosines, sines = cos_ref[...], sin_ref[...]
    q_all = dot(normed, w_ref[:, : H * HD])
    for g in range(H // 2):
        at = slice(g * LANE, (g + 1) * LANE)
        block = q_all[:, at]
        q_ref[:, at] = (block * cosines + turned(block, lane) * sines).astype(BF)
    kv = dot(normed, w_ref[:, H * HD : H * HD + 2 * KVH * HD])
    for m in range(KVH // 2):
        block = kv[:, m * LANE : (m + 1) * LANE]
        block = block * cosines + turned(block, lane) * sines
        other = pltpu.roll(block, HD, 1)
        kd_ref[:, 2 * m * LANE : (2 * m + 1) * LANE] = jnp.where(low, block, other).astype(BF)
        kd_ref[:, (2 * m + 1) * LANE : (2 * m + 2) * LANE] = jnp.where(low, other, block).astype(BF)
        block = kv[:, KVH * HD + m * LANE : KVH * HD + (m + 1) * LANE]
        other = pltpu.roll(block, HD, 1)
        vd_ref[:, 2 * m * LANE : (2 * m + 1) * LANE] = jnp.where(low, block, other).astype(BF)
        vd_ref[:, (2 * m + 1) * LANE : (2 * m + 2) * LANE] = jnp.where(low, other, block).astype(BF)

    row = lax.broadcasted_iota(jnp.int32, (tokens, tokens), 0)
    column = lax.broadcasted_iota(jnp.int32, (tokens, tokens), 1)
    row_at = lax.broadcasted_iota(jnp.int32, (tokens, 1), 0)
    column_at = lax.broadcasted_iota(jnp.int32, (1, tokens), 1)
    row_segment = jnp.zeros((tokens, 1), jnp.int32)
    column_segment = jnp.zeros((1, tokens), jnp.int32)
    end = jnp.int32(0)
    for j in range(len_ref.shape[1]):
        end = end + len_ref[0, j]
        row_segment += (row_at >= end).astype(jnp.int32)
        column_segment += (column_at >= end).astype(jnp.int32)
    bias = jnp.where((row_segment == column_segment) & (column <= row), 0.0, masked_score)
    bias = jnp.concatenate([bias, bias], axis=0)

    for g in range(KVH):
        at = slice(g * LANE, (g + 1) * LANE)
        queries = halves(q_ref[:, at].astype(F32), low).astype(BF)
        scores = dot_nt(queries, kd_ref[:, at]) * score_scale + bias
        shifted = jnp.exp(scores - jnp.max(scores, axis=1, keepdims=True))
        weights = shifted * (1.0 / jnp.sum(shifted, axis=1, keepdims=True))
        p_ref[g] = weights
        mixed = dot(weights.astype(BF), vd_ref[:, at])
        o_ref[:, at] = jnp.where(low, mixed[:tokens], mixed[tokens:]).astype(BF)

    after = source + residual_scale * dot(o_ref[...], w_ref[:, QKVO - D : QKVO])
    h1_ref[...] = after
    factor = lax.rsqrt(jnp.mean(after * after, axis=1, keepdims=True) + norm_eps)
    normed = (after * factor * gain_two).astype(BF)
    n2_ref[...] = normed
    logits = dot(normed, w_ref[:, QKVO:])
    routed = jnp.zeros((tokens, LANE), jnp.bool_)
    for j in range(TOPK):
        routed |= routes_ref[:, j : j + 1] == lane
    top = jnp.max(jnp.where(routed, logits, masked_score), axis=1, keepdims=True)
    powers = jnp.where(routed, jnp.exp(logits - top), 0.0)
    gates = powers / jnp.sum(powers, axis=1, keepdims=True)
    gates = jnp.where(routed, gates, -1.0)
    gd_ref[...] = gates
    gt_ref[...] = gates.T[:E]


def experts(base_ref, n2_ref, do_ref, gt_ref, w_ref, yp_ref, dx_ref, xs_ref, dye_ref, dgu_ref, hx_ref):
    local = w_ref.shape[0]
    sources = gt_ref.shape[0]
    tokens = gt_ref.shape[2]
    before = lax.broadcasted_iota(jnp.int32, (tokens, tokens), 0) < lax.broadcasted_iota(jnp.int32, (tokens, tokens), 1)
    before = before.astype(F32).astype(BF)
    slot = lax.broadcasted_iota(jnp.int32, (CAP, tokens), 0).astype(F32)
    picks, gates = [], []
    for s in range(sources):
        rows = [gt_ref[s, pl.ds(base_ref[0] + i, 1), :] for i in range(local)]
        mine = jnp.concatenate(rows, axis=0) if local > 1 else rows[0]
        member = (mine >= 0.0).astype(F32)
        rank = dot(member.astype(BF), before)
        rank = jnp.where(mine >= 0.0, rank, -1.0)
        chosen = [slot == rank[i : i + 1] for i in range(local)]
        gates.append([jnp.sum(jnp.where(chosen[i], mine[i : i + 1], 0.0), axis=1, keepdims=True) for i in range(local)])
        picks.append(jnp.concatenate([c.astype(F32).astype(BF) for c in chosen], axis=0))
    dms = []
    for s in range(sources):
        at = slice(s * tokens, (s + 1) * tokens)
        taken = dot(picks[s], n2_ref[at]).astype(BF)
        grads = dot(picks[s], do_ref[at]) * residual_scale
        dms.append(grads)
        for i in range(local):
            rows = slice(i * CAP, (i + 1) * CAP)
            xs_ref[i, s * CAP : (s + 1) * CAP] = taken[rows]
            dye_ref[i, s * CAP : (s + 1) * CAP] = (gates[s][i] * grads[rows]).astype(BF)
    mixed, back, marks = [], [], []
    lane = lanes_of(CAP)
    for i in range(local):
        slots = xs_ref[i]
        gate_pre = dot_nt(slots, w_ref[i, :FF])
        up_pre = dot_nt(slots, w_ref[i, FF : 2 * FF])
        sigmoid = 1.0 / (1.0 + jnp.exp(-gate_pre))
        silu = gate_pre * sigmoid
        act = (silu * up_pre).astype(BF)
        hx_ref[i] = act
        made = dot(act, w_ref[i, 2 * FF :]).astype(BF).astype(F32)
        grad_act = dot_nt(dye_ref[i], w_ref[i, 2 * FF :])
        dgu_ref[i, :, :FF] = (grad_act * up_pre * (sigmoid * (1.0 + gate_pre * (1.0 - sigmoid)))).astype(BF)
        dgu_ref[i, :, FF:] = (grad_act * silu).astype(BF)
        grad_rows = dot(dgu_ref[i, :, :FF], w_ref[i, :FF]) + dot(dgu_ref[i, :, FF:], w_ref[i, FF : 2 * FF])
        back.append(grad_rows.astype(BF))
        for s in range(sources):
            rows = slice(s * CAP, (s + 1) * CAP)
            mixed.append((gates[s][i] * made[rows]).astype(BF))
            grad_gate = jnp.sum(dms[s][i * CAP : (i + 1) * CAP] * made[rows], axis=1, keepdims=True)
            high = grad_gate.astype(BF).astype(F32)
            expert = base_ref[0] + i
            mark = jnp.where(lane == expert, high, jnp.where(lane == expert + E, grad_gate - high, 0.0))
            marks.append(mark.astype(BF))
    for s in range(sources):
        at = slice(s * tokens, (s + 1) * tokens)
        rows = slice(s * CAP, (s + 1) * CAP)
        sent = jnp.concatenate([mixed[i * sources + s] for i in range(local)], axis=0)
        yp_ref[at] = dot_tn(picks[s], sent).astype(BF)
        sent = jnp.concatenate([back[i][rows] for i in range(local)], axis=0)
        dx_ref[at, :D] = dot_tn(picks[s], sent).astype(BF)
        sent = jnp.concatenate([marks[i * sources + s] for i in range(local)], axis=0)
        dx_ref[at, D:] = dot_tn(picks[s], sent).astype(BF)


def expert_weights_back(xs_ref, dye_ref, dgu_ref, hx_ref, out_ref):
    out_ref[0, : 2 * FF] = dot_tn(dgu_ref[0], xs_ref[0]).astype(BF)
    out_ref[0, 2 * FF :] = dot_tn(hx_ref[0], dye_ref[0]).astype(BF)


def attention_backward(
    x_ref, dout_ref, cos_ref, sin_ref, w_ref, q_ref, kd_ref, vd_ref, p_ref, o_ref, h1_ref, n2_ref, gd_ref, dx_ref,
    gin_ref, gw_ref, gs_ref, do_ref, dqkv_ref,
):
    tokens = x_ref.shape[0]
    lane = lanes_of(tokens)
    low = lane < HD
    small = w_ref[:, QKVO:].astype(F32).T
    gain_one, gain_two = small[E : E + 1], small[E + 1 : E + 2]
    after = h1_ref[...]
    factor_two = lax.rsqrt(jnp.mean(after * after, axis=1, keepdims=True) + norm_eps)
    gates = jnp.maximum(gd_ref[...], 0.0)
    tail = dx_ref[:, D:].astype(F32)
    grad_gates = jnp.where(lane < E, tail + pltpu.roll(tail, LANE - E, 1), 0.0)
    chosen = gates * (grad_gates - jnp.sum(gates * grad_gates, axis=1, keepdims=True))
    grad_logits = chosen.astype(BF)
    grad_normed = dx_ref[:, :D].astype(F32) + dot_nt(grad_logits, w_ref[:, QKVO:])
    scaled = grad_normed * gain_two
    grad_after = dout_ref[...].astype(F32) + (
        factor_two * scaled - after * factor_two**3 * jnp.mean(scaled * after, axis=1, keepdims=True)
    )
    grad_gain_two = jnp.sum(grad_normed * after * factor_two, axis=0, keepdims=True)
    grad_branch = (residual_scale * grad_after).astype(BF)
    gw_ref[:, QKVO - D :] = dot_tn(o_ref[...], grad_branch).astype(BF)
    do_ref[...] = dot_nt(grad_branch, w_ref[:, QKVO - D : QKVO]).astype(BF)
    grad_router = dot_tn(n2_ref[...], grad_logits)

    cosines, sines = cos_ref[...], sin_ref[...]
    key_back, value_back = [], []
    for g in range(KVH):
        at = slice(g * LANE, (g + 1) * LANE)
        queries = halves(q_ref[:, at].astype(F32), low).astype(BF)
        outs = halves(do_ref[:, at].astype(F32), low).astype(BF)
        weights = p_ref[g]
        grad_weights = dot_nt(outs, vd_ref[:, at])
        total = jnp.sum(weights * grad_weights, axis=1, keepdims=True)
        grad_scores = (weights * (grad_weights - total)).astype(BF)
        block = dot(grad_scores, kd_ref[:, at])
        block = jnp.where(low, block[:tokens], block[tokens:]) * score_scale
        dqkv_ref[:, at] = (block * cosines - turned(block, lane) * sines).astype(BF)
        block = dot_tn(grad_scores, queries) * score_scale
        key_back.append(block + pltpu.roll(block, HD, 1))
        block = dot_tn(weights.astype(BF), outs)
        value_back.append(block + pltpu.roll(block, HD, 1))
    for m in range(KVH // 2):
        block = jnp.where(low, key_back[2 * m], key_back[2 * m + 1])
        at = slice(H * HD + m * LANE, H * HD + (m + 1) * LANE)
        dqkv_ref[:, at] = (block * cosines - turned(block, lane) * sines).astype(BF)
        at = slice(H * HD + KVH * HD + m * LANE, H * HD + KVH * HD + (m + 1) * LANE)
        dqkv_ref[:, at] = jnp.where(low, value_back[2 * m], value_back[2 * m + 1]).astype(BF)

    source = x_ref[...].astype(F32)
    factor_one = lax.rsqrt(jnp.mean(source * source, axis=1, keepdims=True) + norm_eps)
    normed = (source * factor_one * gain_one).astype(BF)
    gw_ref[:, : QKVO - D] = dot_tn(normed, dqkv_ref[...]).astype(BF)
    grad_normed = dot_nt(dqkv_ref[...], w_ref[:, : QKVO - D])
    scaled = grad_normed * gain_one
    grad_vector = factor_one * scaled - source * factor_one**3 * jnp.mean(scaled * source, axis=1, keepdims=True)
    gin_ref[...] = grad_after + grad_vector
    grad_gain_one = jnp.sum(grad_normed * source * factor_one, axis=0, keepdims=True)
    pad = jnp.zeros((6, D), F32)
    gains = jnp.concatenate([grad_gain_one, grad_gain_two, pad], axis=0).T
    gs_ref[:, :LANE] = grad_router
    gs_ref[:, LANE:] = jnp.concatenate([gains, jnp.zeros((D, LANE - 8), F32)], axis=1)


def call(kernel, out_shape, args, scratch=(), **more):
    smem = [a.dtype == jnp.int32 and a.size <= 16 for a in args]
    return pl.pallas_call(
        kernel,
        out_shape=out_shape,
        in_specs=[pl.BlockSpec(memory_space=pltpu.SMEM if s else pltpu.VMEM) for s in smem],
        out_specs=jax.tree.map(lambda _: pl.BlockSpec(memory_space=pltpu.VMEM), out_shape),
        scratch_shapes=list(scratch),
        compiler_params=pltpu.CompilerParams(vmem_limit_bytes=VMEM_LIMIT),
        **more,
    )(*args)


def shape(dims, dtype):
    return jax.ShapeDtypeStruct(dims, dtype)


def rope_tables(seq_lengths, tokens):
    ends = jnp.sum(jnp.where(np.tri(seq_lengths.shape[1], dtype=bool), seq_lengths[0][None, :], 0), axis=1)
    token = jnp.arange(tokens, dtype=jnp.int32)
    start = jnp.max(jnp.where(token[:, None] >= ends[None, :], ends[None, :], 0), axis=1)
    position = (token - start).astype(F32)
    frequency = rope_base ** (-jnp.arange(0, HD, 2, dtype=F32) / HD)
    frequency = jnp.concatenate([frequency] * (LANE // (HD // 2)))
    sign = jnp.where(jnp.arange(LANE) % HD < HD // 2, -1.0, 1.0)
    angles = position[:, None] * frequency[None, :]
    return jnp.cos(angles), jnp.sin(angles) * sign[None, :]


def make_body(mesh):
    group = mesh.shape["fsdp"]
    local = E // group
    chunk = 2

    def body(
        hidden_in, seq_lengths, routes, norm1_gain, w_query, w_key, w_value, w_output, norm2_gain, w_router,
        expert_weights, out_cotangent,
    ):
        tokens = hidden_in.shape[0]
        rows = w_query.shape[0]
        packed = jnp.concatenate(
            [
                w_query, w_key, w_value, w_output, w_router, norm1_gain[:, None], norm2_gain[:, None],
                jnp.zeros((rows, LANE - E - 2), BF),
            ],
            axis=1,
        )
        weights = lax.all_gather(packed, "fsdp", axis=0, tiled=True)
        dout_all = lax.all_gather(out_cotangent, "fsdp", axis=0, tiled=True)
        cosines, sines = rope_tables(seq_lengths, tokens)
        q, kd, vd, p, o, h1, n2, gd, gt = call(
            attention_forward,
            (
                shape((tokens, D), BF), shape((tokens, D), BF), shape((tokens, D), BF),
                shape((KVH, 2 * tokens, tokens), F32), shape((tokens, D), BF), shape((tokens, D), F32),
                shape((tokens, D), BF), shape((tokens, LANE), F32), shape((E, tokens), F32),
            ),
            (hidden_in, seq_lengths, routes, cosines, sines, weights),
        )
        n2_all = lax.all_gather(n2, "fsdp", axis=0, tiled=True)
        gt_all = lax.all_gather(gt, "fsdp", axis=0, tiled=False)
        base = (lax.axis_index("fsdp") * local).astype(jnp.int32).reshape(1)
        whole = pl.Buffered(1)
        token_block = pl.BlockSpec((chunk * tokens, D), lambda c: (c, 0))
        slot_block = pl.BlockSpec((local, chunk * CAP, D), lambda c: (0, c, 0))
        yp, dxp, xs, dye, dgu, hx = pl.pallas_call(
            experts,
            grid=(group // chunk,),
            in_specs=[
                pl.BlockSpec(memory_space=pltpu.SMEM), token_block, token_block,
                pl.BlockSpec((chunk, E, tokens), lambda c: (c, 0, 0)),
                pl.BlockSpec((local, 3 * FF, D), lambda c: (0, 0, 0), pipeline_mode=whole),
            ],
            out_specs=[
                token_block, pl.BlockSpec((chunk * tokens, D + LANE), lambda c: (c, 0)),
                slot_block, slot_block, slot_block,
                pl.BlockSpec((local, chunk * CAP, FF), lambda c: (0, c, 0)),
            ],
            out_shape=[
                shape((group * tokens, D), BF), shape((group * tokens, D + LANE), BF),
                shape((local, group * CAP, D), BF), shape((local, group * CAP, D), BF),
                shape((local, group * CAP, D), BF), shape((local, group * CAP, FF), BF),
            ],
            compiler_params=pltpu.CompilerParams(vmem_limit_bytes=VMEM_LIMIT),
        )(base, n2_all, dout_all, gt_all, expert_weights)
        dx = lax.psum_scatter(dxp, "fsdp", scatter_dimension=0, tiled=True)
        wide = pl.BlockSpec((1, group * CAP, D), lambda i: (i, 0, 0))
        grad_experts = pl.pallas_call(
            expert_weights_back,
            grid=(local,),
            in_specs=[wide, wide, wide, pl.BlockSpec((1, group * CAP, FF), lambda i: (i, 0, 0))],
            out_specs=pl.BlockSpec((1, 3 * FF, D), lambda i: (i, 0, 0)),
            out_shape=shape((local, 3 * FF, D), BF),
            compiler_params=pltpu.CompilerParams(vmem_limit_bytes=VMEM_LIMIT),
        )(xs, dye, dgu, hx)
        moe = lax.psum_scatter(yp, "fsdp", scatter_dimension=0, tiled=True)
        layer_out = (h1 + residual_scale * moe.astype(F32)).astype(BF)
        grad_experts = lax.psum(grad_experts, "replica")
        grad_in, gw, gs = call(
            attention_backward,
            (shape((tokens, D), F32), shape((D, QKVO), BF), shape((D, 2 * LANE), F32)),
            (hidden_in, out_cotangent, cosines, sines, weights, q, kd, vd, p, o, h1, n2, gd, dx),
            [pltpu.VMEM((tokens, D), BF), pltpu.VMEM((tokens, QKVO - D), BF)],
        )
        gw = lax.psum_scatter(gw, "fsdp", scatter_dimension=0, tiled=True)
        gs = lax.psum_scatter(gs, "fsdp", scatter_dimension=0, tiled=True)
        gw, grad_experts = lax.optimization_barrier((gw, grad_experts))
        gw = lax.psum(gw, "replica").astype(F32)
        gs = lax.psum(gs, "replica")
        grad_experts = grad_experts.astype(F32)
        a, b, c = H * HD, H * HD + KVH * HD, H * HD + 2 * KVH * HD
        return (
            layer_out, grad_in, gs[:, LANE], gw[:, :a], gw[:, a:b], gw[:, b:c], gw[:, c:], gs[:, LANE + 1],
            gs[:, :E], grad_experts,
        )

    return body


def solution(mesh):
    tokens, weights = P(("replica", "fsdp"), None), P("fsdp", None)
    return jax.shard_map(
        make_body(mesh),
        mesh=mesh,
        in_specs=(
            tokens, tokens, tokens, P("fsdp"), weights, weights, weights, weights, P("fsdp"), weights,
            P("fsdp", None, None), tokens,
        ),
        out_specs=(
            tokens, tokens, P("fsdp"), weights, weights, weights, weights, P("fsdp"), weights, P("fsdp", None, None),
        ),
        check_vma=False,
    )
```

```python
import functools

import jax
import jax.numpy as jnp
import numpy as np
from jax import lax
from jax.experimental import pallas as pl
from jax.experimental.pallas import tpu as pltpu
from jax.sharding import PartitionSpec as P

D = 1024
H = 16
KVH = 8
HD = 64
FF = 512
TOPK = 8
E = 16
CAP = 144
LANE = 128
QKVO = H * HD + 2 * KVH * HD + D

norm_eps = 1e-06
score_scale = 0.015625
residual_scale = 0.22
rope_base = 10000.0
masked_score = -1e30

BF = jnp.bfloat16
F32 = jnp.float32
VMEM_LIMIT = 63 * 2**20


def dot(a, b):
    return lax.dot_general(a, b, (((1,), (0,)), ((), ())), preferred_element_type=F32)


def dot_nt(a, b):
    return lax.dot_general(a, b, (((1,), (1,)), ((), ())), preferred_element_type=F32)


def dot_tn(a, b):
    return lax.dot_general(a, b, (((0,), (0,)), ((), ())), preferred_element_type=F32)


def lanes_of(rows):
    return lax.broadcasted_iota(jnp.int32, (rows, LANE), 1)


def turned(block, lane):
    return jnp.where(lane % HD < HD // 2, pltpu.roll(block, LANE - HD // 2, 1), pltpu.roll(block, HD // 2, 1))


def halves(block, low):
    zero = jnp.zeros_like(block)
    return jnp.concatenate([jnp.where(low, block, zero), jnp.where(low, zero, block)], axis=0)


def attention_forward(
    x_ref, len_ref, routes_ref, cos_ref, sin_ref, w_ref,
    q_ref, kd_ref, vd_ref, p_ref, o_ref, h1_ref, n2_ref, gd_ref, gt_ref,
):
    tokens = x_ref.shape[0]
    lane = lanes_of(tokens)
    low = lane < HD
    small = w_ref[:, QKVO:].astype(F32).T
    gain_one, gain_two = small[E : E + 1], small[E + 1 : E + 2]
    source = x_ref[...].astype(F32)
    factor = lax.rsqrt(jnp.mean(source * source, axis=1, keepdims=True) + norm_eps)
    normed = (source * factor * gain_one).astype(BF)
    cosines, sines = cos_ref[...], sin_ref[...]
    q_all = dot(normed, w_ref[:, : H * HD])
    for g in range(H // 2):
        at = slice(g * LANE, (g + 1) * LANE)
        block = q_all[:, at]
        q_ref[:, at] = (block * cosines + turned(block, lane) * sines).astype(BF)
    kv = dot(normed, w_ref[:, H * HD : H * HD + 2 * KVH * HD])
    for m in range(KVH // 2):
        block = kv[:, m * LANE : (m + 1) * LANE]
        block = block * cosines + turned(block, lane) * sines
        other = pltpu.roll(block, HD, 1)
        kd_ref[:, 2 * m * LANE : (2 * m + 1) * LANE] = jnp.where(low, block, other).astype(BF)
        kd_ref[:, (2 * m + 1) * LANE : (2 * m + 2) * LANE] = jnp.where(low, other, block).astype(BF)
        block = kv[:, KVH * HD + m * LANE : KVH * HD + (m + 1) * LANE]
        other = pltpu.roll(block, HD, 1)
        vd_ref[:, 2 * m * LANE : (2 * m + 1) * LANE] = jnp.where(low, block, other).astype(BF)
        vd_ref[:, (2 * m + 1) * LANE : (2 * m + 2) * LANE] = jnp.where(low, other, block).astype(BF)

    row = lax.broadcasted_iota(jnp.int32, (tokens, tokens), 0)
    column = lax.broadcasted_iota(jnp.int32, (tokens, tokens), 1)
    row_at = lax.broadcasted_iota(jnp.int32, (tokens, 1), 0)
    column_at = lax.broadcasted_iota(jnp.int32, (1, tokens), 1)
    row_segment = jnp.zeros((tokens, 1), jnp.int32)
    column_segment = jnp.zeros((1, tokens), jnp.int32)
    end = jnp.int32(0)
    for j in range(len_ref.shape[1]):
        end = end + len_ref[0, j]
        row_segment += (row_at >= end).astype(jnp.int32)
        column_segment += (column_at >= end).astype(jnp.int32)
    bias = jnp.where((row_segment == column_segment) & (column <= row), 0.0, masked_score)
    bias = jnp.concatenate([bias, bias], axis=0)

    for g in range(KVH):
        at = slice(g * LANE, (g + 1) * LANE)
        queries = halves(q_ref[:, at].astype(F32), low).astype(BF)
        scores = dot_nt(queries, kd_ref[:, at]) * score_scale + bias
        shifted = jnp.exp(scores - jnp.max(scores, axis=1, keepdims=True))
        weights = shifted * (1.0 / jnp.sum(shifted, axis=1, keepdims=True))
        p_ref[g] = weights
        mixed = dot(weights.astype(BF), vd_ref[:, at])
        o_ref[:, at] = jnp.where(low, mixed[:tokens], mixed[tokens:]).astype(BF)

    after = source + residual_scale * dot(o_ref[...], w_ref[:, QKVO - D : QKVO])
    h1_ref[...] = after
    factor = lax.rsqrt(jnp.mean(after * after, axis=1, keepdims=True) + norm_eps)
    normed = (after * factor * gain_two).astype(BF)
    n2_ref[...] = normed
    logits = dot(normed, w_ref[:, QKVO:])
    routed = jnp.zeros((tokens, LANE), jnp.bool_)
    for j in range(TOPK):
        routed |= routes_ref[:, j : j + 1] == lane
    top = jnp.max(jnp.where(routed, logits, masked_score), axis=1, keepdims=True)
    powers = jnp.where(routed, jnp.exp(logits - top), 0.0)
    gates = powers / jnp.sum(powers, axis=1, keepdims=True)
    gates = jnp.where(routed, gates, -1.0)
    gd_ref[...] = gates
    gt_ref[...] = gates.T[:E]


def experts(base_ref, n2_ref, do_ref, gt_ref, w_ref, yp_ref, dx_ref, xs_ref, dye_ref, dgu_ref, hx_ref):
    local = w_ref.shape[0]
    sources = gt_ref.shape[0]
    tokens = gt_ref.shape[2]
    before = lax.broadcasted_iota(jnp.int32, (tokens, tokens), 0) < lax.broadcasted_iota(jnp.int32, (tokens, tokens), 1)
    before = before.astype(F32).astype(BF)
    slot = lax.broadcasted_iota(jnp.int32, (CAP, tokens), 0).astype(F32)
    picks, gates = [], []
    for s in range(sources):
        rows = [gt_ref[s, pl.ds(base_ref[0] + i, 1), :] for i in range(local)]
        mine = jnp.concatenate(rows, axis=0) if local > 1 else rows[0]
        member = (mine >= 0.0).astype(F32)
        rank = dot(member.astype(BF), before)
        rank = jnp.where(mine >= 0.0, rank, -1.0)
        chosen = [slot == rank[i : i + 1] for i in range(local)]
        gates.append([jnp.sum(jnp.where(chosen[i], mine[i : i + 1], 0.0), axis=1, keepdims=True) for i in range(local)])
        picks.append(jnp.concatenate([c.astype(F32).astype(BF) for c in chosen], axis=0))
    dms = []
    for s in range(sources):
        at = slice(s * tokens, (s + 1) * tokens)
        taken = dot(picks[s], n2_ref[at]).astype(BF)
        grads = dot(picks[s], do_ref[at]) * residual_scale
        dms.append(grads)
        for i in range(local):
            rows = slice(i * CAP, (i + 1) * CAP)
            xs_ref[i, s * CAP : (s + 1) * CAP] = taken[rows]
            dye_ref[i, s * CAP : (s + 1) * CAP] = (gates[s][i] * grads[rows]).astype(BF)
    mixed, back, marks = [], [], []
    lane = lanes_of(CAP)
    for i in range(local):
        slots = xs_ref[i]
        gate_pre = dot_nt(slots, w_ref[i, :FF])
        up_pre = dot_nt(slots, w_ref[i, FF : 2 * FF])
        sigmoid = 1.0 / (1.0 + jnp.exp(-gate_pre))
        silu = gate_pre * sigmoid
        act = (silu * up_pre).astype(BF)
        hx_ref[i] = act
        made = dot(act, w_ref[i, 2 * FF :]).astype(BF).astype(F32)
        grad_act = dot_nt(dye_ref[i], w_ref[i, 2 * FF :])
        dgu_ref[i, :, :FF] = (grad_act * up_pre * (sigmoid * (1.0 + gate_pre * (1.0 - sigmoid)))).astype(BF)
        dgu_ref[i, :, FF:] = (grad_act * silu).astype(BF)
        grad_rows = dot(dgu_ref[i, :, :FF], w_ref[i, :FF]) + dot(dgu_ref[i, :, FF:], w_ref[i, FF : 2 * FF])
        back.append(grad_rows.astype(BF))
        for s in range(sources):
            rows = slice(s * CAP, (s + 1) * CAP)
            mixed.append((gates[s][i] * made[rows]).astype(BF))
            grad_gate = jnp.sum(dms[s][i * CAP : (i + 1) * CAP] * made[rows], axis=1, keepdims=True)
            high = grad_gate.astype(BF).astype(F32)
            expert = base_ref[0] + i
            mark = jnp.where(lane == expert, high, jnp.where(lane == expert + E, grad_gate - high, 0.0))
            marks.append(mark.astype(BF))
    for s in range(sources):
        at = slice(s * tokens, (s + 1) * tokens)
        rows = slice(s * CAP, (s + 1) * CAP)
        sent = jnp.concatenate([mixed[i * sources + s] for i in range(local)], axis=0)
        yp_ref[at] = dot_tn(picks[s], sent).astype(BF)
        sent = jnp.concatenate([back[i][rows] for i in range(local)], axis=0)
        dx_ref[at, :D] = dot_tn(picks[s], sent).astype(BF)
        sent = jnp.concatenate([marks[i * sources + s] for i in range(local)], axis=0)
        dx_ref[at, D:] = dot_tn(picks[s], sent).astype(BF)


def expert_weights_back(xs_ref, dye_ref, dgu_ref, hx_ref, out_ref):
    out_ref[0, : 2 * FF] = dot_tn(dgu_ref[0], xs_ref[0]).astype(BF)
    out_ref[0, 2 * FF :] = dot_tn(hx_ref[0], dye_ref[0]).astype(BF)


def attention_backward(
    x_ref, dout_ref, cos_ref, sin_ref, w_ref, q_ref, kd_ref, vd_ref, p_ref, o_ref, h1_ref, n2_ref, gd_ref, dx_ref,
    gin_ref, gw_ref, do_ref, dqkv_ref,
):
    tokens = x_ref.shape[0]
    lane = lanes_of(tokens)
    low = lane < HD

    def put(at, value):
        gw_ref[:, :, :, at] = value.astype(BF).reshape(*gw_ref.shape[:3], value.shape[1])

    small = w_ref[:, QKVO:].astype(F32).T
    gain_one, gain_two = small[E : E + 1], small[E + 1 : E + 2]
    after = h1_ref[...]
    factor_two = lax.rsqrt(jnp.mean(after * after, axis=1, keepdims=True) + norm_eps)
    gates = jnp.maximum(gd_ref[...], 0.0)
    tail = dx_ref[:, D:].astype(F32)
    grad_gates = jnp.where(lane < E, tail + pltpu.roll(tail, LANE - E, 1), 0.0)
    chosen = gates * (grad_gates - jnp.sum(gates * grad_gates, axis=1, keepdims=True))
    grad_logits = chosen.astype(BF)
    grad_normed = dx_ref[:, :D].astype(F32) + dot_nt(grad_logits, w_ref[:, QKVO:])
    scaled = grad_normed * gain_two
    grad_after = dout_ref[...].astype(F32) + (
        factor_two * scaled - after * factor_two**3 * jnp.mean(scaled * after, axis=1, keepdims=True)
    )
    grad_gain_two = jnp.sum(grad_normed * after * factor_two, axis=0, keepdims=True)
    grad_branch = (residual_scale * grad_after).astype(BF)
    put(slice(QKVO - D, QKVO), dot_tn(o_ref[...], grad_branch))
    do_ref[...] = dot_nt(grad_branch, w_ref[:, QKVO - D : QKVO]).astype(BF)
    grad_router = dot_tn(n2_ref[...], grad_logits)

    cosines, sines = cos_ref[...], sin_ref[...]
    key_back, value_back = [], []
    for g in range(KVH):
        at = slice(g * LANE, (g + 1) * LANE)
        queries = halves(q_ref[:, at].astype(F32), low).astype(BF)
        outs = halves(do_ref[:, at].astype(F32), low).astype(BF)
        weights = p_ref[g]
        grad_weights = dot_nt(outs, vd_ref[:, at])
        total = jnp.sum(weights * grad_weights, axis=1, keepdims=True)
        grad_scores = (weights * (grad_weights - total)).astype(BF)
        block = dot(grad_scores, kd_ref[:, at])
        block = jnp.where(low, block[:tokens], block[tokens:]) * score_scale
        dqkv_ref[:, at] = (block * cosines - turned(block, lane) * sines).astype(BF)
        block = dot_tn(grad_scores, queries) * score_scale
        key_back.append(block + pltpu.roll(block, HD, 1))
        block = dot_tn(weights.astype(BF), outs)
        value_back.append(block + pltpu.roll(block, HD, 1))
    for m in range(KVH // 2):
        block = jnp.where(low, key_back[2 * m], key_back[2 * m + 1])
        at = slice(H * HD + m * LANE, H * HD + (m + 1) * LANE)
        dqkv_ref[:, at] = (block * cosines - turned(block, lane) * sines).astype(BF)
        at = slice(H * HD + KVH * HD + m * LANE, H * HD + KVH * HD + (m + 1) * LANE)
        dqkv_ref[:, at] = jnp.where(low, value_back[2 * m], value_back[2 * m + 1]).astype(BF)

    source = x_ref[...].astype(F32)
    factor_one = lax.rsqrt(jnp.mean(source * source, axis=1, keepdims=True) + norm_eps)
    normed = (source * factor_one * gain_one).astype(BF)
    put(slice(0, QKVO - D), dot_tn(normed, dqkv_ref[...]))
    grad_normed = dot_nt(dqkv_ref[...], w_ref[:, : QKVO - D])
    scaled = grad_normed * gain_one
    grad_vector = factor_one * scaled - source * factor_one**3 * jnp.mean(scaled * source, axis=1, keepdims=True)
    gin_ref[...] = grad_after + grad_vector
    grad_gain_one = jnp.sum(grad_normed * source * factor_one, axis=0, keepdims=True)
    gains = jnp.concatenate([grad_gain_one, grad_gain_two, jnp.zeros((6, D), F32)], axis=0).T
    at = lanes_of(D)
    extra = jnp.where(at == E, gains[:, 0:1], jnp.where(at == E + 1, gains[:, 1:2], grad_router))
    put(slice(QKVO, QKVO + LANE), extra)


def add_rows(target, first, second, rows, step):
    def some(i, carry):
        at = pl.ds(pl.multiple_of(i * step, step), step)
        target(at, first(at).astype(F32) + second(at).astype(F32))
        return carry

    lax.fori_loop(0, rows // step, some, 0)


class Copies:
    def __init__(self):
        self.sent = []

    def make(self, src, dst, send, recv, device):
        return pltpu.make_async_remote_copy(
            src_ref=src, dst_ref=dst, send_sem=send, recv_sem=recv, device_id=device, device_id_type=pl.DeviceIdType.MESH
        )


def tail(
    replicas, chips,
    x_ref, dout_ref, cos_ref, sin_ref, w_ref, q_ref, kd_ref, vd_ref, p_ref, o_ref, h1_ref, n2_ref, gd_ref, dx_ref, ge_ref,
    gin_ref, gexp_ref, gproj_ref,
    do_ref, dqkv_ref, gw_ref, core_ref, up_ref, down_ref, parts_ref, smalls_ref, result_ref, *rest,
):
    bits = replicas.bit_length() - 1
    jobs = ge_ref.shape[0] * bits
    arrived = rest[:bits]
    kept = rest[bits : 2 * bits - 1] if bits else ()
    rest = rest[2 * bits - 1 if bits else 0 :]
    (ar_send, ar_recv, core_send, core_recv, up_send, up_recv, down_send, down_recv,
     part_send, part_recv, small_send, small_recv, result_send, result_recv) = rest
    r, f = lax.axis_index("replica"), lax.axis_index("fsdp")
    z, c = f // 2, f % 2
    mate = (r, z * 2 + 1 - c)
    above, below = (r, f + 2), (r, f - 2)
    rows = gw_ref.shape[2]
    make = Copies().make

    barrier = pltpu.get_barrier_semaphore()
    expected = 1 + (replicas - 1) + jnp.where(z > 0, 1, 0) + jnp.where(z < chips - 1, 1, 0)
    pl.semaphore_signal(barrier, inc=1, device_id=mate, device_id_type=pl.DeviceIdType.MESH)
    for d in range(1, replicas):
        pl.semaphore_signal(barrier, inc=1, device_id=((r + d) % replicas, f), device_id_type=pl.DeviceIdType.MESH)

    @pl.when(z > 0)
    def _():
        pl.semaphore_signal(barrier, inc=1, device_id=below, device_id_type=pl.DeviceIdType.MESH)

    @pl.when(z < chips - 1)
    def _():
        pl.semaphore_signal(barrier, inc=1, device_id=above, device_id_type=pl.DeviceIdType.MESH)

    pl.semaphore_wait(barrier, expected)

    def bit_of(b):
        return (r // (1 << b)) % 2

    def partner(b):
        return (r + (1 - 2 * bit_of(b)) * (1 << b), f)

    def halving(e):
        size = ge_ref.shape[1] // bits
        orders = [[(g + k) % bits for k in range(bits)] for g in range(bits)]
        starts = [[] for _ in range(bits)]
        for g in range(bits):
            at = g * size
            for k in range(bits):
                starts[g].append(at)
                at = at + bit_of(orders[g][k]) * (size >> (k + 1))
            starts[g].append(at)
        copies = {}

        def source(g, k, at, length):
            return ge_ref.at[e, pl.ds(g * size + at, length)] if k == 0 else kept[k - 1].at[e * bits + g, pl.ds(at, length)]

        def exchange(g, k):
            half = size >> (k + 1)
            give = pl.multiple_of((1 - bit_of(orders[g][k])) * half, half)
            copies[g, k] = make(
                source(g, k, give, half), arrived[k].at[e * bits + g], ar_send.at[e * bits + g, k],
                ar_recv.at[e * bits + g, k], partner(orders[g][k]),
            )
            copies[g, k].start()

        def spread(g, k):
            half = size >> (k + 1)
            at = pl.ds(pl.multiple_of(starts[g][k + 1], half), half)
            copies[g, bits + k] = make(
                gexp_ref.at[e, at], gexp_ref.at[e, at], ar_send.at[e * bits + g, bits + k],
                ar_recv.at[e * bits + g, bits + k], partner(orders[g][k]),
            )
            copies[g, bits + k].start()

        for g in range(bits):
            exchange(g, 0)
        yield
        for k in range(bits):
            half = size >> (k + 1)
            for g in range(bits):
                copies[g, k].wait_recv()
                keep = pl.multiple_of(bit_of(orders[g][k]) * half, half)
                own = source(g, k, keep, half)
                there = arrived[k].at[e * bits + g]
                if k < bits - 1:
                    into = kept[k].at[e * bits + g]
                else:
                    into = gexp_ref.at[e, pl.ds(pl.multiple_of(starts[g][bits], half), half)]

                def write(at, value, into=into):
                    into[at] = value.astype(BF)

                add_rows(write, lambda at: own[at], lambda at: there[at], half, min(half, 64))
                if k < bits - 1:
                    exchange(g, k + 1)
                else:
                    spread(g, k)
            yield
        for k in range(bits - 1, -1, -1):
            for g in range(bits):
                copies[g, bits + k].wait_recv()
                if k > 0:
                    spread(g, k - 1)
            yield
        for copy in copies.values():
            copy.wait_send()

    def line():
        crossing = make(gw_ref.at[:, 1 - c], core_ref, core_send.at[0], core_recv.at[0], mate)
        crossing.start()
        yield
        crossing.wait_recv()

        def add_block(block, other):
            def write(at, value):
                gw_ref[block, c, at] = value.astype(BF)

            add_rows(write, lambda at: gw_ref[block, c, at], lambda at: other[block, at], rows, 16)

        def send(block, up):
            there, send_sem, recv_sem = (up_ref, up_send, up_recv) if up else (down_ref, down_send, down_recv)
            return make(
                gw_ref.at[block, c], there.at[block], send_sem.at[block], recv_sem.at[block], above if up else below
            )

        for k in range(chips):
            add_block(k, core_ref)
        for k in range(chips - 1):
            owner = chips - 1 - k

            @pl.when(z == 0)
            def _():
                send(owner, True).start()

            @pl.when(z == chips - 1)
            def _():
                send(k, False).start()

        yield
        for k in range(chips - 2):
            owner = chips - 1 - k

            @pl.when((z > 0) & (z < owner))
            def _():
                send(owner, True).wait_recv()
                add_block(owner, up_ref)
                send(owner, True).start()

            @pl.when((z < chips - 1) & (z > k))
            def _():
                send(k, False).wait_recv()
                add_block(k, down_ref)
                send(k, False).start()

            yield

        @pl.when(z > 0)
        def _():
            send(z, True).wait_recv()
            add_block(z, up_ref)

        @pl.when(z < chips - 1)
        def _():
            send(z, False).wait_recv()
            add_block(z, down_ref)

        wide = QKVO // replicas

        def columns(part):
            return pl.ds(pl.multiple_of(part * wide, LANE), wide)

        own = gw_ref.at[z, c]

        def part_copy(d):
            to = (r + d) % replicas
            return make(own.at[:, columns(to)], parts_ref.at[r], part_send.at[d], part_recv.at[r], (to, f))

        def small_copy(d):
            to = (r + d) % replicas
            return make(own.at[:, pl.ds(QKVO, LANE)], smalls_ref.at[r], small_send.at[d], small_recv.at[r], (to, f))

        for d in range(1, replicas):
            part_copy(d).start()
            small_copy(d).start()
        parts_ref[r] = own[:, columns(r)]
        smalls_ref[r] = own[:, pl.ds(QKVO, LANE)]
        yield
        for d in range(1, replicas):
            peer = (r + d) % replicas
            make(parts_ref.at[peer], parts_ref.at[peer], part_send.at[d], part_recv.at[peer], (peer, f)).wait_recv()
            make(smalls_ref.at[peer], smalls_ref.at[peer], small_send.at[d], small_recv.at[peer], (peer, f)).wait_recv()
        total = parts_ref[0].astype(F32)
        small = smalls_ref[0].astype(F32)
        for k in range(1, replicas):
            total = total + parts_ref[k].astype(F32)
            small = small + smalls_ref[k].astype(F32)
        result_ref[r] = total.astype(BF)
        gproj_ref[:, QKVO:] = small

        def result_copy(d):
            to = (r + d) % replicas
            return make(result_ref.at[r], result_ref.at[r], result_send.at[d], result_recv.at[r], (to, f))

        for d in range(1, replicas):
            result_copy(d).start()
        yield
        for d in range(1, replicas):
            peer = (r + d) % replicas
            make(result_ref.at[peer], result_ref.at[peer], result_send.at[d], result_recv.at[peer], (peer, f)).wait_recv()
        for k in range(replicas):
            gproj_ref[:, k * wide : (k + 1) * wide] = result_ref[k].astype(F32)
        crossing.wait_send()
        for k in range(chips):

            @pl.when(z < k)
            def _():
                send(k, True).wait_send()

            @pl.when(z > k)
            def _():
                send(k, False).wait_send()

        for d in range(1, replicas):
            part_copy(d).wait_send()
            small_copy(d).wait_send()
            result_copy(d).wait_send()

    experts_sums = [halving(e) for e in range(ge_ref.shape[0])] if bits else []
    for e, sums in enumerate(experts_sums):
        next(sums)
    if not bits:
        gexp_ref[...] = ge_ref[...]
    attention_backward(
        x_ref, dout_ref, cos_ref, sin_ref, w_ref, q_ref, kd_ref, vd_ref, p_ref, o_ref, h1_ref, n2_ref, gd_ref, dx_ref,
        gin_ref, gw_ref, do_ref, dqkv_ref,
    )
    projections = line()
    first, last = experts_sums[:1], experts_sums[1:]
    order = [[projections], first, [projections], last, [projections], first, last, [projections], first, last]
    order += [[projections], first, [projections], last, [projections]]
    order += [[projections] + experts_sums] * (chips + 2 * bits)
    for turn in order:
        for process in turn:
            next(process, None)


def call(kernel, out_shape, args, scratch=(), **params):
    smem = [a.dtype == jnp.int32 and a.size <= 16 for a in args]
    return pl.pallas_call(
        kernel,
        out_shape=out_shape,
        in_specs=[pl.BlockSpec(memory_space=pltpu.SMEM if s else pltpu.VMEM) for s in smem],
        out_specs=jax.tree.map(lambda _: pl.BlockSpec(memory_space=pltpu.VMEM), out_shape),
        scratch_shapes=list(scratch),
        compiler_params=pltpu.CompilerParams(
            vmem_limit_bytes=VMEM_LIMIT, has_side_effects="collective_id" in params, **params
        ),
    )(*args)


def shape(dims, dtype):
    return jax.ShapeDtypeStruct(dims, dtype)


def rope_tables(seq_lengths, tokens):
    ends = jnp.sum(jnp.where(np.tri(seq_lengths.shape[1], dtype=bool), seq_lengths[0][None, :], 0), axis=1)
    token = jnp.arange(tokens, dtype=jnp.int32)
    start = jnp.max(jnp.where(token[:, None] >= ends[None, :], ends[None, :], 0), axis=1)
    position = (token - start).astype(F32)
    frequency = rope_base ** (-jnp.arange(0, HD, 2, dtype=F32) / HD)
    frequency = jnp.concatenate([frequency] * (LANE // (HD // 2)))
    sign = jnp.where(jnp.arange(LANE) % HD < HD // 2, -1.0, 1.0)
    angles = position[:, None] * frequency[None, :]
    return jnp.cos(angles), jnp.sin(angles) * sign[None, :]


def make_body(mesh):
    group, replicas = mesh.shape["fsdp"], mesh.shape["replica"]
    local = E // group
    chunk = 2

    def body(
        hidden_in, seq_lengths, routes, norm1_gain, w_query, w_key, w_value, w_output, norm2_gain, w_router,
        expert_weights, out_cotangent,
    ):
        tokens = hidden_in.shape[0]
        rows = w_query.shape[0]
        packed = jnp.concatenate(
            [
                w_query, w_key, w_value, w_output, w_router, norm1_gain[:, None], norm2_gain[:, None],
                jnp.zeros((rows, LANE - E - 2), BF),
            ],
            axis=1,
        )
        weights = lax.all_gather(packed, "fsdp", axis=0, tiled=True)
        dout_all = lax.all_gather(out_cotangent, "fsdp", axis=0, tiled=True)
        cosines, sines = rope_tables(seq_lengths, tokens)
        q, kd, vd, p, o, h1, n2, gd, gt = call(
            attention_forward,
            (
                shape((tokens, D), BF), shape((tokens, D), BF), shape((tokens, D), BF),
                shape((KVH, 2 * tokens, tokens), F32), shape((tokens, D), BF), shape((tokens, D), F32),
                shape((tokens, D), BF), shape((tokens, LANE), F32), shape((E, tokens), F32),
            ),
            (hidden_in, seq_lengths, routes, cosines, sines, weights),
        )
        n2_all = lax.all_gather(n2, "fsdp", axis=0, tiled=True)
        gt_all = lax.all_gather(gt, "fsdp", axis=0, tiled=False)
        base = (lax.axis_index("fsdp") * local).astype(jnp.int32).reshape(1)
        whole = pl.Buffered(1)
        token_block = pl.BlockSpec((chunk * tokens, D), lambda c: (c, 0))
        slot_block = pl.BlockSpec((local, chunk * CAP, D), lambda c: (0, c, 0))
        yp, dxp, xs, dye, dgu, hx = pl.pallas_call(
            experts,
            grid=(group // chunk,),
            in_specs=[
                pl.BlockSpec(memory_space=pltpu.SMEM), token_block, token_block,
                pl.BlockSpec((chunk, E, tokens), lambda c: (c, 0, 0)),
                pl.BlockSpec((local, 3 * FF, D), lambda c: (0, 0, 0), pipeline_mode=whole),
            ],
            out_specs=[
                token_block, pl.BlockSpec((chunk * tokens, D + LANE), lambda c: (c, 0)),
                slot_block, slot_block, slot_block,
                pl.BlockSpec((local, chunk * CAP, FF), lambda c: (0, c, 0)),
            ],
            out_shape=[
                shape((group * tokens, D), BF), shape((group * tokens, D + LANE), BF),
                shape((local, group * CAP, D), BF), shape((local, group * CAP, D), BF),
                shape((local, group * CAP, D), BF), shape((local, group * CAP, FF), BF),
            ],
            compiler_params=pltpu.CompilerParams(vmem_limit_bytes=VMEM_LIMIT),
        )(base, n2_all, dout_all, gt_all, expert_weights)
        dx = lax.psum_scatter(dxp, "fsdp", scatter_dimension=0, tiled=True)
        wide = pl.BlockSpec((1, group * CAP, D), lambda i: (i, 0, 0))
        grad_experts = pl.pallas_call(
            expert_weights_back,
            grid=(local,),
            in_specs=[wide, wide, wide, pl.BlockSpec((1, group * CAP, FF), lambda i: (i, 0, 0))],
            out_specs=pl.BlockSpec((1, 3 * FF, D), lambda i: (i, 0, 0)),
            out_shape=shape((local, 3 * FF, D), BF),
            compiler_params=pltpu.CompilerParams(vmem_limit_bytes=VMEM_LIMIT),
        )(xs, dye, dgu, hx)
        moe = lax.psum_scatter(yp, "fsdp", scatter_dimension=0, tiled=True)
        layer_out = (h1 + residual_scale * moe.astype(F32)).astype(BF)
        bits = replicas.bit_length() - 1
        rows = D // group
        size = 3 * FF // bits if bits else 0
        dma = pltpu.SemaphoreType.DMA
        grad_in, grad_experts, gw = call(
            functools.partial(tail, replicas, group // 2),
            (shape((tokens, D), F32), shape((local, 3 * FF, D), BF), shape((rows, QKVO + LANE), F32)),
            (hidden_in, out_cotangent, cosines, sines, weights, q, kd, vd, p, o, h1, n2, gd, dx, grad_experts),
            [
                pltpu.VMEM((tokens, D), BF), pltpu.VMEM((tokens, QKVO - D), BF),
                pltpu.VMEM((group // 2, 2, rows, QKVO + LANE), BF), pltpu.VMEM((group // 2, rows, QKVO + LANE), BF),
                pltpu.VMEM((group // 2, rows, QKVO + LANE), BF), pltpu.VMEM((group // 2, rows, QKVO + LANE), BF),
                pltpu.VMEM((replicas, rows, QKVO // replicas), BF), pltpu.VMEM((replicas, rows, LANE), BF),
                pltpu.VMEM((replicas, rows, QKVO // replicas), BF),
            ]
            + [pltpu.VMEM((local * bits, size >> (k + 1), D), BF) for k in range(bits)]
            + [pltpu.VMEM((local * bits, size >> (k + 1), D), BF) for k in range(bits - 1)]
            + [dma((max(local * bits, 1), max(2 * bits, 1)))] * 2 + [dma((1,))] * 2 + [dma((group // 2,))] * 4
            + [dma((replicas,))] * 6,
            collective_id=0,
        )
        a, b, c = H * HD, H * HD + KVH * HD, H * HD + 2 * KVH * HD
        return (
            layer_out, grad_in, gw[:, QKVO + E], gw[:, :a], gw[:, a:b], gw[:, b:c], gw[:, c:QKVO], gw[:, QKVO + E + 1],
            gw[:, QKVO : QKVO + E], grad_experts.astype(F32),
        )

    return body


def solution(mesh):
    tokens, weights = P(("replica", "fsdp"), None), P("fsdp", None)
    return jax.shard_map(
        make_body(mesh),
        mesh=mesh,
        in_specs=(
            tokens, tokens, tokens, P("fsdp"), weights, weights, weights, weights, P("fsdp"), weights,
            P("fsdp", None, None), tokens,
        ),
        out_specs=(
            tokens, tokens, P("fsdp"), weights, weights, weights, weights, P("fsdp"), weights, P("fsdp", None, None),
        ),
        check_vma=False,
    )
```

```python
import functools

import jax
import jax.numpy as jnp
import numpy as np
from jax import lax
from jax.experimental import pallas as pl
from jax.experimental.pallas import tpu as pltpu
from jax.sharding import PartitionSpec as P

D = 1024
H = 16
KVH = 8
HD = 64
FF = 512
TOPK = 8
E = 16
CAP = 144
LANE = 128
QKVO = H * HD + 2 * KVH * HD + D

norm_eps = 1e-06
score_scale = 0.015625
residual_scale = 0.22
rope_base = 10000.0
masked_score = -1e30

BF = jnp.bfloat16
F32 = jnp.float32
VMEM_LIMIT = 63 * 2**20


def dot(a, b):
    return lax.dot_general(a, b, (((1,), (0,)), ((), ())), preferred_element_type=F32)


def dot_nt(a, b):
    return lax.dot_general(a, b, (((1,), (1,)), ((), ())), preferred_element_type=F32)


def dot_tn(a, b):
    return lax.dot_general(a, b, (((0,), (0,)), ((), ())), preferred_element_type=F32)


def lanes_of(rows):
    return lax.broadcasted_iota(jnp.int32, (rows, LANE), 1)


def turned(block, lane):
    return jnp.where(lane % HD < HD // 2, pltpu.roll(block, LANE - HD // 2, 1), pltpu.roll(block, HD // 2, 1))


def halves(block, low):
    zero = jnp.zeros_like(block)
    return jnp.concatenate([jnp.where(low, block, zero), jnp.where(low, zero, block)], axis=0)


def attention_forward(
    x_ref, len_ref, routes_ref, cos_ref, sin_ref, w_ref,
    q_ref, kd_ref, vd_ref, p_ref, o_ref, h1_ref, n2_ref, gd_ref, gt_ref,
):
    tokens = x_ref.shape[0]
    lane = lanes_of(tokens)
    low = lane < HD
    small = w_ref[:, QKVO:].astype(F32).T
    gain_one, gain_two = small[E : E + 1], small[E + 1 : E + 2]
    source = x_ref[...].astype(F32)
    factor = lax.rsqrt(jnp.mean(source * source, axis=1, keepdims=True) + norm_eps)
    normed = (source * factor * gain_one).astype(BF)
    cosines, sines = cos_ref[...], sin_ref[...]
    q_all = dot(normed, w_ref[:, : H * HD])
    for g in range(H // 2):
        at = slice(g * LANE, (g + 1) * LANE)
        block = q_all[:, at]
        q_ref[:, at] = (block * cosines + turned(block, lane) * sines).astype(BF)
    kv = dot(normed, w_ref[:, H * HD : H * HD + 2 * KVH * HD])
    for m in range(KVH // 2):
        block = kv[:, m * LANE : (m + 1) * LANE]
        block = block * cosines + turned(block, lane) * sines
        other = pltpu.roll(block, HD, 1)
        kd_ref[:, 2 * m * LANE : (2 * m + 1) * LANE] = jnp.where(low, block, other).astype(BF)
        kd_ref[:, (2 * m + 1) * LANE : (2 * m + 2) * LANE] = jnp.where(low, other, block).astype(BF)
        block = kv[:, KVH * HD + m * LANE : KVH * HD + (m + 1) * LANE]
        other = pltpu.roll(block, HD, 1)
        vd_ref[:, 2 * m * LANE : (2 * m + 1) * LANE] = jnp.where(low, block, other).astype(BF)
        vd_ref[:, (2 * m + 1) * LANE : (2 * m + 2) * LANE] = jnp.where(low, other, block).astype(BF)

    row = lax.broadcasted_iota(jnp.int32, (tokens, tokens), 0)
    column = lax.broadcasted_iota(jnp.int32, (tokens, tokens), 1)
    row_at = lax.broadcasted_iota(jnp.int32, (tokens, 1), 0)
    column_at = lax.broadcasted_iota(jnp.int32, (1, tokens), 1)
    row_segment = jnp.zeros((tokens, 1), jnp.int32)
    column_segment = jnp.zeros((1, tokens), jnp.int32)
    end = jnp.int32(0)
    for j in range(len_ref.shape[1]):
        end = end + len_ref[0, j]
        row_segment += (row_at >= end).astype(jnp.int32)
        column_segment += (column_at >= end).astype(jnp.int32)
    bias = jnp.where((row_segment == column_segment) & (column <= row), 0.0, masked_score)
    bias = jnp.concatenate([bias, bias], axis=0)

    for g in range(KVH):
        at = slice(g * LANE, (g + 1) * LANE)
        queries = halves(q_ref[:, at].astype(F32), low).astype(BF)
        scores = dot_nt(queries, kd_ref[:, at]) * score_scale + bias
        shifted = jnp.exp(scores - jnp.max(scores, axis=1, keepdims=True))
        weights = shifted * (1.0 / jnp.sum(shifted, axis=1, keepdims=True))
        p_ref[g] = weights
        mixed = dot(weights.astype(BF), vd_ref[:, at])
        o_ref[:, at] = jnp.where(low, mixed[:tokens], mixed[tokens:]).astype(BF)

    after = source + residual_scale * dot(o_ref[...], w_ref[:, QKVO - D : QKVO])
    h1_ref[...] = after
    factor = lax.rsqrt(jnp.mean(after * after, axis=1, keepdims=True) + norm_eps)
    normed = (after * factor * gain_two).astype(BF)
    n2_ref[...] = normed
    logits = dot(normed, w_ref[:, QKVO:])
    routed = jnp.zeros((tokens, LANE), jnp.bool_)
    for j in range(TOPK):
        routed |= routes_ref[:, j : j + 1] == lane
    top = jnp.max(jnp.where(routed, logits, masked_score), axis=1, keepdims=True)
    powers = jnp.where(routed, jnp.exp(logits - top), 0.0)
    gates = powers / jnp.sum(powers, axis=1, keepdims=True)
    gates = jnp.where(routed, gates, -1.0)
    gd_ref[...] = gates
    gt_ref[...] = gates.T[:E]


def middle(
    chips, n2_ref, gt_ref, do_hbm, w_hbm,
    dx_ref, yp_hbm, ge_ref,
    n2_all, gt_all, do_buf, w_ref, xs_ref, dye_ref, dgu_ref, hx_ref, dxp_ref, yps_ref, core_ref, from_ref,
    n2_up, n2_down, n2_mate, n2_recv, gt_up, gt_down, gt_mate, gt_recv,
    core_send, core_recv, far_send, far_recv, do_sem, yp_sem, w_sem,
):
    local = w_ref.shape[0]
    tokens = n2_ref.shape[0]
    r, f = lax.axis_index("replica"), lax.axis_index("fsdp")
    z, c = f // 2, f % 2
    mate, above, below = (r, z * 2 + 1 - c), (r, f + 2), (r, f - 2)
    make = Copies().make

    pltpu.make_async_copy(w_hbm, w_ref, w_sem.at[0]).start()

    def do_copy(zc, slot):
        return pltpu.make_async_copy(do_hbm.at[zc], do_buf.at[slot], do_sem.at[slot])

    do_copy(z, 0).start()

    barrier = pltpu.get_barrier_semaphore()
    pl.semaphore_signal(barrier, inc=1, device_id=mate, device_id_type=pl.DeviceIdType.MESH)
    for k in range(1, chips):
        to = (r, (z + k) % chips * 2 + c)
        pl.semaphore_signal(barrier, inc=1, device_id=to, device_id_type=pl.DeviceIdType.MESH)
    n2_all[z, c] = n2_ref[...]
    gt_all[z, c] = gt_ref[...]
    pl.semaphore_wait(barrier, chips)

    def pass_on(zb, how):
        to = {"up": above, "down": below, "mate": mate}[how]
        sems = {"up": (n2_up, gt_up), "down": (n2_down, gt_down), "mate": (n2_mate, gt_mate)}[how]
        return [
            make(ref.at[zb, c], ref.at[zb, c], sem.at[zb], recv.at[zb, c], to)
            for ref, sem, recv in ((gt_all, sems[1], gt_recv), (n2_all, sems[0], n2_recv))
        ]

    def got(zb, core):
        for ref, sem, recv in ((gt_all, gt_mate, gt_recv), (n2_all, n2_mate, n2_recv)):
            make(ref.at[zb, core], ref.at[zb, core], sem.at[zb], recv.at[zb, core], mate).wait_recv()

    def start(copies):
        for copy in copies:
            copy.start()

    @pl.when(z < chips - 1)
    def _():
        start(pass_on(z, "up"))

    @pl.when(z > 0)
    def _():
        start(pass_on(z, "down"))

    start(pass_on(z, "mate"))
    inner = jnp.minimum(z, chips - 1 - z)

    def place(t):
        k = (t + 1) // 2
        near = jnp.where(t % 2 == 1, z - k, z + k)
        return jnp.where(t <= 2 * inner, near, jnp.where(2 * z < chips - 1, t, chips - 1 - t))

    before = lax.broadcasted_iota(jnp.int32, (tokens, tokens), 0) < lax.broadcasted_iota(jnp.int32, (tokens, tokens), 1)
    before = before.astype(F32).astype(BF)
    slot_index = lax.broadcasted_iota(jnp.int32, (CAP, tokens), 0).astype(F32)
    lane = lanes_of(CAP)
    pair = 2 * CAP

    def far_copy(zc, slot, t):
        return make(
            dxp_ref.at[slot, c], from_ref.at[z], far_send.at[t], far_recv.at[z], (r, zc * 2 + c)
        )

    def core_copy(zc, slot, t):
        return make(dxp_ref.at[slot, 1 - c], core_ref.at[zc], core_send.at[t], core_recv.at[zc], mate)

    def yp_copy(zc, slot):
        return pltpu.make_async_copy(yps_ref.at[slot], yp_hbm.at[zc], yp_sem.at[slot])

    def chunk(t, carry):
        zc = place(t)
        slot = t % 2
        k = jnp.where(zc > z, zc - z, z - zc)
        both = (t % 2 == 1) & (t <= 2 * inner)
        single = t > 2 * inner

        @pl.when(both | (single & (zc < z)))
        def _():
            got(z - k, c)

            @pl.when(z < chips - 1)
            def _():
                start(pass_on(z - k, "up"))

            start(pass_on(z - k, "mate"))

        @pl.when(both | (single & (zc > z)))
        def _():
            got(z + k, c)

            @pl.when(z > 0)
            def _():
                start(pass_on(z + k, "down"))

            start(pass_on(z + k, "mate"))

        got(zc, 1 - c)

        @pl.when(t < chips - 1)
        def _():
            do_copy(place(t + 1), 1 - slot).start()

        do_copy(zc, slot).wait()

        @pl.when(t == 0)
        def _():
            pltpu.make_async_copy(w_hbm, w_ref, w_sem.at[0]).wait()

        @pl.when(t >= 2)
        def _():
            core_copy(z, slot, t - 2).wait_send()
            yp_copy(z, slot).wait()

        @pl.when(t >= 3)
        def _():
            far_copy(z, slot, t - 2).wait_send()

        picks, gates, dms = [], [], []
        at_chip = pl.multiple_of(zc * pair, 16)
        for core in range(2):
            rows = [gt_all[zc, core, pl.ds(f * local + i, 1), :] for i in range(local)]
            mine = jnp.concatenate(rows, axis=0) if local > 1 else rows[0]
            rank = jnp.where(mine >= 0.0, dot((mine >= 0.0).astype(F32).astype(BF), before), -1.0)
            chosen = [slot_index == rank[i : i + 1] for i in range(local)]
            gates.append([jnp.sum(jnp.where(chosen[i], mine[i : i + 1], 0.0), axis=1, keepdims=True) for i in range(local)])
            picks.append(jnp.concatenate([one.astype(F32).astype(BF) for one in chosen], axis=0))
            taken = dot(picks[core], n2_all[zc, core]).astype(BF)
            grads = dot(picks[core], do_buf[slot, core]) * residual_scale
            dms.append(grads)
            at = pl.ds(pl.multiple_of(at_chip + core * CAP, 16), CAP)
            for i in range(local):
                part = slice(i * CAP, (i + 1) * CAP)
                xs_ref[i, at] = taken[part]
                dye_ref[i, at] = (gates[core][i] * grads[part]).astype(BF)
        at = pl.ds(at_chip, pair)
        mades, backs, marks = [], [], []
        for i in range(local):
            slots = xs_ref[i, at]
            gate_pre = dot_nt(slots, w_ref[i, :FF])
            up_pre = dot_nt(slots, w_ref[i, FF : 2 * FF])
            grad_act = dot_nt(dye_ref[i, at], w_ref[i, 2 * FF :])
            sigmoid = 1.0 / (1.0 + jnp.exp(-gate_pre))
            silu = gate_pre * sigmoid
            act = (silu * up_pre).astype(BF)
            hx_ref[i, at] = act
            grad_gate = (grad_act * up_pre * (sigmoid * (1.0 + gate_pre * (1.0 - sigmoid)))).astype(BF)
            grad_up = (grad_act * silu).astype(BF)
            dgu_ref[i, at, :FF] = grad_gate
            dgu_ref[i, at, FF:] = grad_up
            made = dot(act, w_ref[i, 2 * FF :]).astype(BF).astype(F32)
            mades.append(made)
            backs.append((dot(grad_gate, w_ref[i, :FF]) + dot(grad_up, w_ref[i, FF : 2 * FF])).astype(BF))
            for core in range(2):
                part = slice(core * CAP, (core + 1) * CAP)
                value = jnp.sum(dms[core][i * CAP : (i + 1) * CAP] * made[part], axis=1, keepdims=True)
                high = value.astype(BF).astype(F32)
                expert = f * local + i
                mark = jnp.where(lane == expert, high, jnp.where(lane == expert + E, value - high, 0.0))
                marks.append(mark.astype(BF))
        for core in range(2):
            part = slice(core * CAP, (core + 1) * CAP)
            sent = jnp.concatenate([backs[i][part] for i in range(local)], axis=0)
            dxp_ref[slot, core, :, :D] = dot_tn(picks[core], sent).astype(BF)
            sent = jnp.concatenate([marks[2 * i + core] for i in range(local)], axis=0)
            dxp_ref[slot, core, :, D:] = dot_tn(picks[core], sent).astype(BF)
        core_copy(zc, slot, t).start()
        for core in range(2):
            part = slice(core * CAP, (core + 1) * CAP)
            sent = jnp.concatenate([(gates[core][i] * mades[i][part]).astype(BF) for i in range(local)], axis=0)
            yps_ref[slot, core] = dot_tn(picks[core], sent).astype(BF)
        yp_copy(zc, slot).start()
        core_copy(zc, slot, t).wait_recv()
        total = dxp_ref[slot, c].astype(F32) + core_ref[zc].astype(F32)

        @pl.when(t == 0)
        def _():
            dx_ref[...] = total

        @pl.when(t > 0)
        def _():
            dxp_ref[slot, c] = total.astype(BF)
            far_copy(zc, slot, t).start()

        return carry

    lax.fori_loop(0, chips, chunk, 0)
    for i in range(local):
        ge_ref[i, : 2 * FF] = dot_tn(dgu_ref[i], xs_ref[i]).astype(BF)
        ge_ref[i, 2 * FF :] = dot_tn(hx_ref[i], dye_ref[i]).astype(BF)
    for k in range(chips):

        @pl.when(z != k)
        def _():
            make(from_ref.at[k], from_ref.at[k], far_send.at[k], far_recv.at[k], (r, k * 2 + c)).wait_recv()
            dx_ref[...] += from_ref[k].astype(F32)

    for t in range(max(chips - 2, 0), chips):
        core_copy(z, t % 2, t).wait_send()
        yp_copy(z, t % 2).wait()
        if t > 0:
            far_copy(z, t % 2, t).wait_send()
    for k in range(chips):

        @pl.when((z >= k) & (z < chips - 1))
        def _():
            for copy in pass_on(k, "up"):
                copy.wait_send()

        @pl.when((z <= k) & (z > 0))
        def _():
            for copy in pass_on(k, "down"):
                copy.wait_send()

        for copy in pass_on(k, "mate"):
            copy.wait_send()


def attention_backward(
    x_ref, dout_ref, cos_ref, sin_ref, w_ref, q_ref, kd_ref, vd_ref, p_hbm, o_ref, h1_ref, n2_ref, gd_ref, dx_ref,
    gin_ref, gw_ref, do_ref, dqkv_ref, p_ref, p_sem,
):
    tokens = x_ref.shape[0]
    lane = lanes_of(tokens)
    low = lane < HD

    def p_copy(g):
        return pltpu.make_async_copy(p_hbm.at[g], p_ref.at[g % 2], p_sem.at[g % 2])

    p_copy(0).start()

    def put(at, value):
        gw_ref[:, :, :, at] = value.astype(BF).reshape(*gw_ref.shape[:3], value.shape[1])

    small = w_ref[:, QKVO:].astype(F32).T
    gain_one, gain_two = small[E : E + 1], small[E + 1 : E + 2]
    after = h1_ref[...]
    factor_two = lax.rsqrt(jnp.mean(after * after, axis=1, keepdims=True) + norm_eps)
    gates = jnp.maximum(gd_ref[...], 0.0)
    tail = dx_ref[:, D:].astype(F32)
    grad_gates = jnp.where(lane < E, tail + pltpu.roll(tail, LANE - E, 1), 0.0)
    chosen = gates * (grad_gates - jnp.sum(gates * grad_gates, axis=1, keepdims=True))
    grad_logits = chosen.astype(BF)
    grad_normed = dx_ref[:, :D].astype(F32) + dot_nt(grad_logits, w_ref[:, QKVO:])
    scaled = grad_normed * gain_two
    grad_after = dout_ref[...].astype(F32) + (
        factor_two * scaled - after * factor_two**3 * jnp.mean(scaled * after, axis=1, keepdims=True)
    )
    grad_gain_two = jnp.sum(grad_normed * after * factor_two, axis=0, keepdims=True)
    grad_branch = (residual_scale * grad_after).astype(BF)
    put(slice(QKVO - D, QKVO), dot_tn(o_ref[...], grad_branch))
    do_ref[...] = dot_nt(grad_branch, w_ref[:, QKVO - D : QKVO]).astype(BF)
    grad_router = dot_tn(n2_ref[...], grad_logits)

    cosines, sines = cos_ref[...], sin_ref[...]
    key_back, value_back = [], []
    for g in range(KVH):
        at = slice(g * LANE, (g + 1) * LANE)
        queries = halves(q_ref[:, at].astype(F32), low).astype(BF)
        outs = halves(do_ref[:, at].astype(F32), low).astype(BF)
        if g + 1 < KVH:
            p_copy(g + 1).start()
        p_copy(g).wait()
        weights = p_ref[g % 2]
        grad_weights = dot_nt(outs, vd_ref[:, at])
        total = jnp.sum(weights * grad_weights, axis=1, keepdims=True)
        grad_scores = (weights * (grad_weights - total)).astype(BF)
        block = dot(grad_scores, kd_ref[:, at])
        block = jnp.where(low, block[:tokens], block[tokens:]) * score_scale
        dqkv_ref[:, at] = (block * cosines - turned(block, lane) * sines).astype(BF)
        block = dot_tn(grad_scores, queries) * score_scale
        key_back.append(block + pltpu.roll(block, HD, 1))
        block = dot_tn(weights.astype(BF), outs)
        value_back.append(block + pltpu.roll(block, HD, 1))
    for m in range(KVH // 2):
        block = jnp.where(low, key_back[2 * m], key_back[2 * m + 1])
        at = slice(H * HD + m * LANE, H * HD + (m + 1) * LANE)
        dqkv_ref[:, at] = (block * cosines - turned(block, lane) * sines).astype(BF)
        at = slice(H * HD + KVH * HD + m * LANE, H * HD + KVH * HD + (m + 1) * LANE)
        dqkv_ref[:, at] = jnp.where(low, value_back[2 * m], value_back[2 * m + 1]).astype(BF)

    source = x_ref[...].astype(F32)
    factor_one = lax.rsqrt(jnp.mean(source * source, axis=1, keepdims=True) + norm_eps)
    normed = (source * factor_one * gain_one).astype(BF)
    put(slice(0, QKVO - D), dot_tn(normed, dqkv_ref[...]))
    grad_normed = dot_nt(dqkv_ref[...], w_ref[:, : QKVO - D])
    scaled = grad_normed * gain_one
    grad_vector = factor_one * scaled - source * factor_one**3 * jnp.mean(scaled * source, axis=1, keepdims=True)
    gin_ref[...] = grad_after + grad_vector
    grad_gain_one = jnp.sum(grad_normed * source * factor_one, axis=0, keepdims=True)
    gains = jnp.concatenate([grad_gain_one, grad_gain_two, jnp.zeros((6, D), F32)], axis=0).T
    at = lanes_of(D)
    extra = jnp.where(at == E, gains[:, 0:1], jnp.where(at == E + 1, gains[:, 1:2], grad_router))
    put(slice(QKVO, QKVO + LANE), extra)


def add_rows(target, first, second, rows, step):
    def some(i, carry):
        at = pl.ds(pl.multiple_of(i * step, step), step)
        target(at, first(at).astype(F32) + second(at).astype(F32))
        return carry

    lax.fori_loop(0, rows // step, some, 0)


class Copies:
    def __init__(self):
        self.sent = []

    def make(self, src, dst, send, recv, device):
        return pltpu.make_async_remote_copy(
            src_ref=src, dst_ref=dst, send_sem=send, recv_sem=recv, device_id=device, device_id_type=pl.DeviceIdType.MESH
        )


def tail(
    replicas, chips,
    x_ref, dout_ref, cos_ref, sin_ref, w_ref, q_ref, kd_ref, vd_ref, o_ref, h1_ref, n2_ref, gd_ref, dx_ref, ge_ref, p_hbm,
    gin_ref, gexp_ref, gproj_ref,
    p_ref, p_sem, do_ref, dqkv_ref, gw_ref, core_ref, up_ref, down_ref, parts_ref, smalls_ref, result_ref, *rest,
):
    bits = replicas.bit_length() - 1
    jobs = ge_ref.shape[0] * bits
    arrived = rest[:bits]
    kept = rest[bits : 2 * bits - 1] if bits else ()
    rest = rest[2 * bits - 1 if bits else 0 :]
    (ar_send, ar_recv, core_send, core_recv, up_send, up_recv, down_send, down_recv,
     part_send, part_recv, small_send, small_recv, result_send, result_recv) = rest
    r, f = lax.axis_index("replica"), lax.axis_index("fsdp")
    z, c = f // 2, f % 2
    mate = (r, z * 2 + 1 - c)
    above, below = (r, f + 2), (r, f - 2)
    rows = gw_ref.shape[2]
    make = Copies().make

    barrier = pltpu.get_barrier_semaphore()
    expected = 1 + (replicas - 1) + jnp.where(z > 0, 1, 0) + jnp.where(z < chips - 1, 1, 0)
    pl.semaphore_signal(barrier, inc=1, device_id=mate, device_id_type=pl.DeviceIdType.MESH)
    for d in range(1, replicas):
        pl.semaphore_signal(barrier, inc=1, device_id=((r + d) % replicas, f), device_id_type=pl.DeviceIdType.MESH)

    @pl.when(z > 0)
    def _():
        pl.semaphore_signal(barrier, inc=1, device_id=below, device_id_type=pl.DeviceIdType.MESH)

    @pl.when(z < chips - 1)
    def _():
        pl.semaphore_signal(barrier, inc=1, device_id=above, device_id_type=pl.DeviceIdType.MESH)

    pl.semaphore_wait(barrier, expected)

    def bit_of(b):
        return (r // (1 << b)) % 2

    def partner(b):
        return (r + (1 - 2 * bit_of(b)) * (1 << b), f)

    def halving(e):
        size = ge_ref.shape[1] // bits
        orders = [[(g + k) % bits for k in range(bits)] for g in range(bits)]
        starts = [[] for _ in range(bits)]
        for g in range(bits):
            at = g * size
            for k in range(bits):
                starts[g].append(at)
                at = at + bit_of(orders[g][k]) * (size >> (k + 1))
            starts[g].append(at)
        copies = {}

        def source(g, k, at, length):
            return ge_ref.at[e, pl.ds(g * size + at, length)] if k == 0 else kept[k - 1].at[e * bits + g, pl.ds(at, length)]

        def exchange(g, k):
            half = size >> (k + 1)
            give = pl.multiple_of((1 - bit_of(orders[g][k])) * half, half)
            copies[g, k] = make(
                source(g, k, give, half), arrived[k].at[e * bits + g], ar_send.at[e * bits + g, k],
                ar_recv.at[e * bits + g, k], partner(orders[g][k]),
            )
            copies[g, k].start()

        def spread(g, k):
            half = size >> (k + 1)
            at = pl.ds(pl.multiple_of(starts[g][k + 1], half), half)
            copies[g, bits + k] = make(
                gexp_ref.at[e, at], gexp_ref.at[e, at], ar_send.at[e * bits + g, bits + k],
                ar_recv.at[e * bits + g, bits + k], partner(orders[g][k]),
            )
            copies[g, bits + k].start()

        for g in range(bits):
            exchange(g, 0)
        yield
        for k in range(bits):
            half = size >> (k + 1)
            for g in range(bits):
                copies[g, k].wait_recv()
                keep = pl.multiple_of(bit_of(orders[g][k]) * half, half)
                own = source(g, k, keep, half)
                there = arrived[k].at[e * bits + g]
                if k < bits - 1:
                    into = kept[k].at[e * bits + g]
                else:
                    into = gexp_ref.at[e, pl.ds(pl.multiple_of(starts[g][bits], half), half)]

                def write(at, value, into=into):
                    into[at] = value.astype(BF)

                add_rows(write, lambda at: own[at], lambda at: there[at], half, min(half, 64))
                if k < bits - 1:
                    exchange(g, k + 1)
                else:
                    spread(g, k)
            yield
        for k in range(bits - 1, -1, -1):
            for g in range(bits):
                copies[g, bits + k].wait_recv()
                if k > 0:
                    spread(g, k - 1)
            yield
        for copy in copies.values():
            copy.wait_send()

    def line():
        crossing = make(gw_ref.at[:, 1 - c], core_ref, core_send.at[0], core_recv.at[0], mate)
        crossing.start()
        yield
        crossing.wait_recv()

        def add_block(block, other):
            def write(at, value):
                gw_ref[block, c, at] = value.astype(BF)

            add_rows(write, lambda at: gw_ref[block, c, at], lambda at: other[block, at], rows, 16)

        def send(block, up):
            there, send_sem, recv_sem = (up_ref, up_send, up_recv) if up else (down_ref, down_send, down_recv)
            return make(
                gw_ref.at[block, c], there.at[block], send_sem.at[block], recv_sem.at[block], above if up else below
            )

        for k in range(chips):
            add_block(k, core_ref)
        for k in range(chips - 1):
            owner = chips - 1 - k

            @pl.when(z == 0)
            def _():
                send(owner, True).start()

            @pl.when(z == chips - 1)
            def _():
                send(k, False).start()

        yield
        for k in range(chips - 2):
            owner = chips - 1 - k

            @pl.when((z > 0) & (z < owner))
            def _():
                send(owner, True).wait_recv()
                add_block(owner, up_ref)
                send(owner, True).start()

            @pl.when((z < chips - 1) & (z > k))
            def _():
                send(k, False).wait_recv()
                add_block(k, down_ref)
                send(k, False).start()

            yield

        @pl.when(z > 0)
        def _():
            send(z, True).wait_recv()
            add_block(z, up_ref)

        @pl.when(z < chips - 1)
        def _():
            send(z, False).wait_recv()
            add_block(z, down_ref)

        wide = QKVO // replicas

        def columns(part):
            return pl.ds(pl.multiple_of(part * wide, LANE), wide)

        own = gw_ref.at[z, c]

        def part_copy(d):
            to = (r + d) % replicas
            return make(own.at[:, columns(to)], parts_ref.at[r], part_send.at[d], part_recv.at[r], (to, f))

        def small_copy(d):
            to = (r + d) % replicas
            return make(own.at[:, pl.ds(QKVO, LANE)], smalls_ref.at[r], small_send.at[d], small_recv.at[r], (to, f))

        for d in range(1, replicas):
            part_copy(d).start()
            small_copy(d).start()
        parts_ref[r] = own[:, columns(r)]
        smalls_ref[r] = own[:, pl.ds(QKVO, LANE)]
        yield
        for d in range(1, replicas):
            peer = (r + d) % replicas
            make(parts_ref.at[peer], parts_ref.at[peer], part_send.at[d], part_recv.at[peer], (peer, f)).wait_recv()
            make(smalls_ref.at[peer], smalls_ref.at[peer], small_send.at[d], small_recv.at[peer], (peer, f)).wait_recv()
        total = parts_ref[0].astype(F32)
        small = smalls_ref[0].astype(F32)
        for k in range(1, replicas):
            total = total + parts_ref[k].astype(F32)
            small = small + smalls_ref[k].astype(F32)
        result_ref[r] = total.astype(BF)
        gproj_ref[:, QKVO:] = small

        def result_copy(d):
            to = (r + d) % replicas
            return make(result_ref.at[r], result_ref.at[r], result_send.at[d], result_recv.at[r], (to, f))

        for d in range(1, replicas):
            result_copy(d).start()
        yield
        for d in range(1, replicas):
            peer = (r + d) % replicas
            make(result_ref.at[peer], result_ref.at[peer], result_send.at[d], result_recv.at[peer], (peer, f)).wait_recv()
        for k in range(replicas):
            gproj_ref[:, k * wide : (k + 1) * wide] = result_ref[k].astype(F32)
        crossing.wait_send()
        for k in range(chips):

            @pl.when(z < k)
            def _():
                send(k, True).wait_send()

            @pl.when(z > k)
            def _():
                send(k, False).wait_send()

        for d in range(1, replicas):
            part_copy(d).wait_send()
            small_copy(d).wait_send()
            result_copy(d).wait_send()

    experts_sums = [halving(e) for e in range(ge_ref.shape[0])] if bits else []
    for e, sums in enumerate(experts_sums):
        next(sums)
    if not bits:
        gexp_ref[...] = ge_ref[...]
    attention_backward(
        x_ref, dout_ref, cos_ref, sin_ref, w_ref, q_ref, kd_ref, vd_ref, p_hbm, o_ref, h1_ref, n2_ref, gd_ref, dx_ref,
        gin_ref, gw_ref, do_ref, dqkv_ref, p_ref, p_sem,
    )
    projections = line()
    first, last = experts_sums[:1], experts_sums[1:]
    order = [[projections], first, [projections], last, [projections], first, last, [projections], first, last]
    order += [[projections], first, [projections], last, [projections]]
    order += [[projections] + experts_sums] * (chips + 2 * bits)
    for turn in order:
        for process in turn:
            next(process, None)


def call(kernel, out_shape, args, scratch=(), outside=0, **params):
    spaces = [pltpu.SMEM if a.dtype == jnp.int32 and a.size <= 16 else pltpu.VMEM for a in args]
    spaces[len(args) - outside :] = [pl.ANY] * outside
    return pl.pallas_call(
        kernel,
        out_shape=out_shape,
        in_specs=[pl.BlockSpec(memory_space=space) for space in spaces],
        out_specs=jax.tree.map(lambda _: pl.BlockSpec(memory_space=pltpu.VMEM), out_shape),
        scratch_shapes=list(scratch),
        compiler_params=pltpu.CompilerParams(
            vmem_limit_bytes=VMEM_LIMIT, has_side_effects="collective_id" in params, **params
        ),
    )(*args)


def shape(dims, dtype):
    return jax.ShapeDtypeStruct(dims, dtype)


def rope_tables(seq_lengths, tokens):
    ends = jnp.sum(jnp.where(np.tri(seq_lengths.shape[1], dtype=bool), seq_lengths[0][None, :], 0), axis=1)
    token = jnp.arange(tokens, dtype=jnp.int32)
    start = jnp.max(jnp.where(token[:, None] >= ends[None, :], ends[None, :], 0), axis=1)
    position = (token - start).astype(F32)
    frequency = rope_base ** (-jnp.arange(0, HD, 2, dtype=F32) / HD)
    frequency = jnp.concatenate([frequency] * (LANE // (HD // 2)))
    sign = jnp.where(jnp.arange(LANE) % HD < HD // 2, -1.0, 1.0)
    angles = position[:, None] * frequency[None, :]
    return jnp.cos(angles), jnp.sin(angles) * sign[None, :]


def make_body(mesh):
    group, replicas = mesh.shape["fsdp"], mesh.shape["replica"]
    local = E // group

    def body(
        hidden_in, seq_lengths, routes, norm1_gain, w_query, w_key, w_value, w_output, norm2_gain, w_router,
        expert_weights, out_cotangent,
    ):
        tokens = hidden_in.shape[0]
        rows = w_query.shape[0]
        packed = jnp.concatenate(
            [
                w_query, w_key, w_value, w_output, w_router, norm1_gain[:, None], norm2_gain[:, None],
                jnp.zeros((rows, LANE - E - 2), BF),
            ],
            axis=1,
        )
        weights = lax.all_gather(packed, "fsdp", axis=0, tiled=True)
        dout_all = lax.all_gather(out_cotangent, "fsdp", axis=0, tiled=True)
        cosines, sines = rope_tables(seq_lengths, tokens)
        q, kd, vd, p, o, h1, n2, gd, gt = call(
            attention_forward,
            (
                shape((tokens, D), BF), shape((tokens, D), BF), shape((tokens, D), BF),
                shape((KVH, 2 * tokens, tokens), F32), shape((tokens, D), BF), shape((tokens, D), F32),
                shape((tokens, D), BF), shape((tokens, LANE), F32), shape((E, tokens), F32),
            ),
            (hidden_in, seq_lengths, routes, cosines, sines, weights),
        )
        chips = group // 2
        dma = pltpu.SemaphoreType.DMA
        anywhere = pl.BlockSpec(memory_space=pl.ANY)
        inside = pl.BlockSpec(memory_space=pltpu.VMEM)
        wide = D + LANE
        dx, yp, grad_experts = pl.pallas_call(
            functools.partial(middle, chips),
            in_specs=[inside, inside, anywhere, anywhere],
            out_specs=[inside, anywhere, inside],
            out_shape=[
                shape((tokens, wide), F32), shape((chips, 2, tokens, D), BF), shape((local, 3 * FF, D), BF),
            ],
            scratch_shapes=[
                pltpu.VMEM((chips, 2, tokens, D), BF), pltpu.VMEM((chips, 2, E, tokens), F32),
                pltpu.VMEM((2, 2, tokens, D), BF), pltpu.VMEM((local, 3 * FF, D), BF),
                pltpu.VMEM((local, group * CAP, D), BF), pltpu.VMEM((local, group * CAP, D), BF),
                pltpu.VMEM((local, group * CAP, D), BF), pltpu.VMEM((local, group * CAP, FF), BF),
                pltpu.VMEM((2, 2, tokens, wide), BF), pltpu.VMEM((2, 2, tokens, D), BF),
                pltpu.VMEM((chips, tokens, wide), BF), pltpu.VMEM((chips, tokens, wide), BF),
            ]
            + ([dma((chips,))] * 3 + [dma((chips, 2))]) * 2 + [dma((chips,))] * 4 + [dma((2,)), dma((2,)), dma((1,))],
            compiler_params=pltpu.CompilerParams(vmem_limit_bytes=VMEM_LIMIT, has_side_effects=True, collective_id=1),
        )(n2, gt, dout_all.reshape(chips, 2, tokens, D), expert_weights)
        moe = lax.psum_scatter(yp.reshape(group * tokens, D), "fsdp", scatter_dimension=0, tiled=True)
        layer_out = (h1 + residual_scale * moe.astype(F32)).astype(BF)
        bits = replicas.bit_length() - 1
        rows = D // group
        size = 3 * FF // bits if bits else 0
        grad_in, grad_experts, gw = call(
            functools.partial(tail, replicas, group // 2),
            (shape((tokens, D), F32), shape((local, 3 * FF, D), BF), shape((rows, QKVO + LANE), F32)),
            (hidden_in, out_cotangent, cosines, sines, weights, q, kd, vd, o, h1, n2, gd, dx, grad_experts, p),
            [
                pltpu.VMEM((2, 2 * tokens, tokens), F32), dma((2,)),
                pltpu.VMEM((tokens, D), BF), pltpu.VMEM((tokens, QKVO - D), BF),
                pltpu.VMEM((group // 2, 2, rows, QKVO + LANE), BF), pltpu.VMEM((group // 2, rows, QKVO + LANE), BF),
                pltpu.VMEM((group // 2, rows, QKVO + LANE), BF), pltpu.VMEM((group // 2, rows, QKVO + LANE), BF),
                pltpu.VMEM((replicas, rows, QKVO // replicas), BF), pltpu.VMEM((replicas, rows, LANE), BF),
                pltpu.VMEM((replicas, rows, QKVO // replicas), BF),
            ]
            + [pltpu.VMEM((local * bits, size >> (k + 1), D), BF) for k in range(bits)]
            + [pltpu.VMEM((local * bits, size >> (k + 1), D), BF) for k in range(bits - 1)]
            + [dma((max(local * bits, 1), max(2 * bits, 1)))] * 2 + [dma((1,))] * 2 + [dma((group // 2,))] * 4
            + [dma((replicas,))] * 6,
            outside=1,
            collective_id=0,
        )
        a, b, c = H * HD, H * HD + KVH * HD, H * HD + 2 * KVH * HD
        return (
            layer_out, grad_in, gw[:, QKVO + E], gw[:, :a], gw[:, a:b], gw[:, b:c], gw[:, c:QKVO], gw[:, QKVO + E + 1],
            gw[:, QKVO : QKVO + E], grad_experts.astype(F32),
        )

    return body


def solution(mesh):
    tokens, weights = P(("replica", "fsdp"), None), P("fsdp", None)
    return jax.shard_map(
        make_body(mesh),
        mesh=mesh,
        in_specs=(
            tokens, tokens, tokens, P("fsdp"), weights, weights, weights, weights, P("fsdp"), weights,
            P("fsdp", None, None), tokens,
        ),
        out_specs=(
            tokens, tokens, P("fsdp"), weights, weights, weights, weights, P("fsdp"), weights, P("fsdp", None, None),
        ),
        check_vma=False,
    )
```

```python
import functools

import jax
import jax.numpy as jnp
import numpy as np
from jax import lax
from jax.experimental import pallas as pl
from jax.experimental.pallas import tpu as pltpu
from jax.sharding import PartitionSpec as P

D = 1024
H = 16
KVH = 8
HD = 64
FF = 512
TOPK = 8
E = 16
CAP = 144
LANE = 128
QKV = H * HD + 2 * KVH * HD
QKVO = QKV + D
W_O = QKV + LANE

norm_eps = 1e-06
score_scale = 0.015625
residual_scale = 0.22
rope_base = 10000.0
masked_score = -1e30

BF = jnp.bfloat16
F32 = jnp.float32
VMEM_LIMIT = 63 * 2**20


def dot(a, b):
    return lax.dot_general(a, b, (((1,), (0,)), ((), ())), preferred_element_type=F32)


def dot_nt(a, b):
    return lax.dot_general(a, b, (((1,), (1,)), ((), ())), preferred_element_type=F32)


def dot_tn(a, b):
    return lax.dot_general(a, b, (((0,), (0,)), ((), ())), preferred_element_type=F32)


def lanes_of(rows):
    return lax.broadcasted_iota(jnp.int32, (rows, LANE), 1)


def turned(block, lane):
    return jnp.where(lane % HD < HD // 2, pltpu.roll(block, LANE - HD // 2, 1), pltpu.roll(block, HD // 2, 1))


def halves(block, low):
    zero = jnp.zeros_like(block)
    return jnp.concatenate([jnp.where(low, block, zero), jnp.where(low, zero, block)], axis=0)


def rope_table(tokens):
    frequency = np.float32(rope_base) ** (-np.arange(0, HD, 2, dtype=np.float32) / np.float32(HD))
    frequency = np.tile(frequency.astype(np.float32), LANE // (HD // 2))
    angles = (np.arange(tokens, dtype=np.float32)[:, None] * frequency[None, :]).astype(np.float64)
    sign = np.where(np.arange(LANE) % HD < HD // 2, -1.0, 1.0)
    pieces = []
    for values in (np.cos(angles), np.sin(angles) * sign[None, :]):
        rest = values.astype(np.float32)
        for _ in range(3):
            piece = rest.astype(BF)
            pieces.append(piece)
            rest = rest - piece.astype(np.float32)
    return np.concatenate(pieces, axis=1)


class Copies:
    def make(self, src, dst, send, recv, device):
        return pltpu.make_async_remote_copy(
            src_ref=src, dst_ref=dst, send_sem=send, recv_sem=recv, device_id=device, device_id_type=pl.DeviceIdType.MESH
        )


def meet(devices, expected):
    barrier = pltpu.get_barrier_semaphore()
    for condition, device in devices:

        def signal(device=device):
            pl.semaphore_signal(barrier, inc=1, device_id=device, device_id_type=pl.DeviceIdType.MESH)

        if condition is True:
            signal()
        else:
            pl.when(condition)(signal)
    pl.semaphore_wait(barrier, expected)


def front(
    replicas, chips,
    x_ref, len_ref, routes_ref, table_ref, wq_ref, wk_ref, wv_ref, wo_ref, wr_ref, g1_ref, g2_ref, dout_ref,
    w_all, q_ref, kd_ref, vd_ref, o_ref, h1_ref, n2_ref, gd_ref, gt_ref, cos_ref, sin_ref, p_hbm, do_all,
    p_ref, p_sem, own_sem, z_up, z_down, z_recv, xy_send, xy_recv, mate_send, mate_recv, do_send, do_recv,
):
    tokens = x_ref.shape[0]
    r, f = lax.axis_index("replica"), lax.axis_index("fsdp")
    z, c = f // 2, f % 2
    mate, above, below = (r, z * 2 + 1 - c), (r, f + 2), (r, f - 2)
    make = Copies().make
    peers = [(True, mate), (z > 0, below), (z < chips - 1, above)]
    peers += [(True, ((r + d) % replicas, f)) for d in range(1, replicas)]

    own_dout = pltpu.make_async_copy(dout_ref, do_all.at[z, c], own_sem.at[0])
    own_dout.start()
    rows = wq_ref.shape[0]
    packed = [wr_ref[...].astype(F32), g1_ref[...].astype(F32), g2_ref[...].astype(F32)]
    packed = jnp.concatenate(packed + [jnp.zeros((LANE - E - 2, rows), F32)], axis=0)
    own = w_all.at[z, c]
    own[:, : H * HD] = wq_ref[...]
    own[:, H * HD : H * HD + KVH * HD] = wk_ref[...]
    own[:, H * HD + KVH * HD : QKV] = wv_ref[...]
    own[:, QKV:W_O] = packed.T.astype(BF)
    own[:, W_O:] = wo_ref[...]
    meet(peers, 1 + (replicas - 1) + jnp.where(z > 0, 1, 0) + jnp.where(z < chips - 1, 1, 0))

    def part(kind):
        if kind == 0:
            return pl.ds(pl.multiple_of(r * (QKV // replicas), LANE), QKV // replicas)
        if kind == 1:
            return pl.ds(QKV, LANE)
        return pl.ds(pl.multiple_of(W_O + r * (D // replicas), LANE), D // replicas)

    def along(zb, kind, up):
        ref = w_all.at[zb, c, :, part(kind)]
        return make(ref, ref, (z_up if up else z_down).at[kind, zb], z_recv.at[kind, zb], above if up else below)

    def across(zb, kind, d):
        ref = w_all.at[zb, c, :, part(kind)]
        return make(ref, ref, xy_send.at[kind, zb, d], xy_recv.at[kind, zb, r], ((r + d) % replicas, f))

    def wait_across(zb, kind):
        for d in range(1, replicas):
            peer = (r + d) % replicas
            ref = w_all.at[zb, c, :, part(kind)]
            make(ref, ref, xy_send.at[kind, zb, d], xy_recv.at[kind, zb, peer], (peer, f)).wait_recv()

    def to_mate(zb, core, late):
        ref = w_all.at[zb, core, :, pl.ds(W_O, D) if late else pl.ds(0, W_O)]
        return make(ref, ref, mate_send.at[late, zb], mate_recv.at[late, zb], mate)

    def dout_copy(zb, core, way):
        source = do_all.at[zb, core]
        return make(source, do_all.at[zb, core], do_send.at[way, zb], do_recv.at[zb, core], (above, below, mate)[way])

    def both_sides(k, act):
        @pl.when(z >= k)
        def _():
            act(z - k, True)

        @pl.when(z < chips - k)
        def _():
            act(z + k, False)

    def onward(up):
        return z < chips - 1 if up else z > 0

    for kind in range(3):
        both_sides(1, lambda zb, low: along(z, kind, not low).start())
    for late in range(2):
        to_mate(z, c, late).start()

    source = x_ref[...].astype(F32)
    factor = lax.rsqrt(jnp.mean(source * source, axis=1, keepdims=True) + norm_eps)
    lane = lanes_of(tokens)
    low_lane = lane < HD
    row = lax.broadcasted_iota(jnp.int32, (tokens, tokens), 0)
    column = lax.broadcasted_iota(jnp.int32, (tokens, tokens), 1)
    row_at = lax.broadcasted_iota(jnp.int32, (tokens, 1), 0)
    column_at = lax.broadcasted_iota(jnp.int32, (1, tokens), 1)
    row_segment = jnp.zeros((tokens, 1), jnp.int32)
    row_start = jnp.zeros((tokens, 1), jnp.int32)
    column_segment = jnp.zeros((1, tokens), jnp.int32)
    end = jnp.int32(0)
    for j in range(len_ref.shape[1]):
        end = end + len_ref[0, j]
        row_segment += (row_at >= end).astype(jnp.int32)
        row_start = jnp.maximum(row_start, jnp.where(row_at >= end, end, 0))
        column_segment += (column_at >= end).astype(jnp.int32)
    place = (column == row - row_start).astype(F32).astype(BF)
    found = dot(place, table_ref[...])
    found = [found[:, i * LANE : (i + 1) * LANE] for i in range(6)]
    cosines, sines = found[0] + found[1] + found[2], found[3] + found[4] + found[5]
    cos_ref[...] = cosines
    sin_ref[...] = sines

    own_dout.wait()
    for k in range(1, chips):
        for kind in range(3):

            def arrive(zb, low, kind=kind):
                along(zb, kind, low).wait_recv()

                @pl.when(onward(low))
                def _():
                    along(zb, kind, low).start()

                if kind != 1:
                    for d in range(1, replicas):
                        across(zb, kind, d).start()

            both_sides(k, arrive)
        if k == 1:
            both_sides(1, lambda zb, low: dout_copy(z, c, 1 if low else 0).start())
            dout_copy(z, c, 2).start()

    def share(k, late):
        def act(zb, low):
            wait_across(zb, 2 if late else 0)
            to_mate(zb, c, late).start()

        both_sides(k, act)

    for k in range(1, chips):
        share(k, 0)
    for k in range(chips):
        to_mate(k, 1 - c, 0).wait_recv()

    def columns(start, size):
        return w_all[:, :, :, start : start + size].reshape(D, size)

    small = columns(QKV, LANE)
    gains = small.astype(F32).T
    gain_one, gain_two = gains[E : E + 1], gains[E + 1 : E + 2]
    normed = (source * factor * gain_one).astype(BF)
    q_all = dot(normed, columns(0, H * HD))
    for g in range(H // 2):
        at = slice(g * LANE, (g + 1) * LANE)
        block = q_all[:, at]
        q_ref[:, at] = (block * cosines + turned(block, lane) * sines).astype(BF)
    kv = dot(normed, columns(H * HD, 2 * KVH * HD))
    for m in range(KVH // 2):
        block = kv[:, m * LANE : (m + 1) * LANE]
        block = block * cosines + turned(block, lane) * sines
        other = pltpu.roll(block, HD, 1)
        kd_ref[:, 2 * m * LANE : (2 * m + 1) * LANE] = jnp.where(low_lane, block, other).astype(BF)
        kd_ref[:, (2 * m + 1) * LANE : (2 * m + 2) * LANE] = jnp.where(low_lane, other, block).astype(BF)
        block = kv[:, KVH * HD + m * LANE : KVH * HD + (m + 1) * LANE]
        other = pltpu.roll(block, HD, 1)
        vd_ref[:, 2 * m * LANE : (2 * m + 1) * LANE] = jnp.where(low_lane, block, other).astype(BF)
        vd_ref[:, (2 * m + 1) * LANE : (2 * m + 2) * LANE] = jnp.where(low_lane, other, block).astype(BF)
    bias = jnp.where((row_segment == column_segment) & (column <= row), 0.0, masked_score)
    bias = jnp.concatenate([bias, bias], axis=0)

    def p_copy(g):
        return pltpu.make_async_copy(p_ref.at[g % 2], p_hbm.at[g], p_sem.at[g % 2])

    for g in range(KVH):
        at = slice(g * LANE, (g + 1) * LANE)
        queries = halves(q_ref[:, at].astype(F32), low_lane).astype(BF)
        scores = dot_nt(queries, kd_ref[:, at]) * score_scale + bias
        shifted = jnp.exp(scores - jnp.max(scores, axis=1, keepdims=True))
        weights = shifted * (1.0 / jnp.sum(shifted, axis=1, keepdims=True))
        if g >= 2:
            p_copy(g - 2).wait()
        p_ref[g % 2] = weights
        p_copy(g).start()
        mixed = dot(weights.astype(BF), vd_ref[:, at])
        o_ref[:, at] = jnp.where(low_lane, mixed[:tokens], mixed[tokens:]).astype(BF)

    for k in range(1, chips):
        share(k, 1)

    def dout_arrive(zb, low):
        dout_copy(zb, c, 0 if low else 1).wait_recv()

        @pl.when(onward(low))
        def _():
            dout_copy(zb, c, 0 if low else 1).start()

        dout_copy(zb, c, 2).start()

    if chips > 1:
        both_sides(1, dout_arrive)
    for k in range(chips):
        to_mate(k, 1 - c, 1).wait_recv()
    after = source + residual_scale * dot(o_ref[...], columns(W_O, D))
    h1_ref[...] = after
    factor = lax.rsqrt(jnp.mean(after * after, axis=1, keepdims=True) + norm_eps)
    normed = (after * factor * gain_two).astype(BF)
    n2_ref[...] = normed
    logits = dot(normed, small).T[:E]
    expert = lax.broadcasted_iota(jnp.int32, (E, tokens), 0)
    routed = routes_ref[0:1] == expert
    for j in range(1, TOPK):
        routed |= routes_ref[j : j + 1] == expert
    top = jnp.max(jnp.where(routed, logits, masked_score), axis=0, keepdims=True)
    powers = jnp.where(routed, jnp.exp(logits - top), 0.0)
    gates = powers / jnp.sum(powers, axis=0, keepdims=True)
    gates = jnp.where(routed, gates, -1.0)
    gt_ref[...] = gates
    gd_ref[...] = jnp.concatenate([gates, jnp.full((LANE - E, tokens), -1.0, F32)], axis=0).T

    for k in range(2, chips):
        both_sides(k, dout_arrive)
    for k in range(chips):
        dout_copy(k, 1 - c, 2).wait_recv()
    for g in (KVH - 2, KVH - 1):
        p_copy(g).wait()
    for k in range(chips):
        for late in range(2):
            to_mate(k, c, late).wait_send()
        dout_copy(k, c, 2).wait_send()

        @pl.when((z >= k) & (z < chips - 1))
        def _():
            dout_copy(k, c, 0).wait_send()
            for kind in range(3):
                along(k, kind, True).wait_send()

        @pl.when((z <= k) & (z > 0))
        def _():
            dout_copy(k, c, 1).wait_send()
            for kind in range(3):
                along(k, kind, False).wait_send()

        @pl.when(z != k)
        def _():
            for d in range(1, replicas):
                for kind in (0, 2):
                    across(k, kind, d).wait_send()


def middle(
    chips, n2_ref, gt_ref, do_hbm, w_hbm,
    dx_ref, yp_hbm, ge_ref,
    n2_all, gt_all, do_buf, w_ref, xs_ref, dye_ref, dgu_ref, hx_ref, dxp_ref, yps_ref, core_ref, from_ref,
    n2_up, n2_down, n2_mate, n2_recv, gt_up, gt_down, gt_mate, gt_recv,
    core_send, core_recv, far_send, far_recv, do_sem, yp_sem, w_sem,
):
    local = w_ref.shape[0]
    tokens = n2_ref.shape[0]
    r, f = lax.axis_index("replica"), lax.axis_index("fsdp")
    z, c = f // 2, f % 2
    mate, above, below = (r, z * 2 + 1 - c), (r, f + 2), (r, f - 2)
    make = Copies().make

    pltpu.make_async_copy(w_hbm, w_ref, w_sem.at[0]).start()

    def do_copy(zc, slot):
        return pltpu.make_async_copy(do_hbm.at[zc], do_buf.at[slot], do_sem.at[slot])

    do_copy(z, 0).start()

    barrier = pltpu.get_barrier_semaphore()
    pl.semaphore_signal(barrier, inc=1, device_id=mate, device_id_type=pl.DeviceIdType.MESH)
    for k in range(1, chips):
        to = (r, (z + k) % chips * 2 + c)
        pl.semaphore_signal(barrier, inc=1, device_id=to, device_id_type=pl.DeviceIdType.MESH)
    n2_all[z, c] = n2_ref[...]
    gt_all[z, c] = gt_ref[...]
    pl.semaphore_wait(barrier, chips)

    def pass_on(zb, how):
        to = {"up": above, "down": below, "mate": mate}[how]
        sems = {"up": (n2_up, gt_up), "down": (n2_down, gt_down), "mate": (n2_mate, gt_mate)}[how]
        return [
            make(ref.at[zb, c], ref.at[zb, c], sem.at[zb], recv.at[zb, c], to)
            for ref, sem, recv in ((gt_all, sems[1], gt_recv), (n2_all, sems[0], n2_recv))
        ]

    def got(zb, core):
        for ref, sem, recv in ((gt_all, gt_mate, gt_recv), (n2_all, n2_mate, n2_recv)):
            make(ref.at[zb, core], ref.at[zb, core], sem.at[zb], recv.at[zb, core], mate).wait_recv()

    def start(copies):
        for copy in copies:
            copy.start()

    @pl.when(z < chips - 1)
    def _():
        start(pass_on(z, "up"))

    @pl.when(z > 0)
    def _():
        start(pass_on(z, "down"))

    start(pass_on(z, "mate"))
    inner = jnp.minimum(z, chips - 1 - z)

    def place(t):
        k = (t + 1) // 2
        near = jnp.where(t % 2 == 1, z - k, z + k)
        return jnp.where(t <= 2 * inner, near, jnp.where(2 * z < chips - 1, t, chips - 1 - t))

    before = lax.broadcasted_iota(jnp.int32, (tokens, tokens), 0) < lax.broadcasted_iota(jnp.int32, (tokens, tokens), 1)
    before = before.astype(F32).astype(BF)
    slot_index = lax.broadcasted_iota(jnp.int32, (CAP, tokens), 0).astype(F32)
    lane = lanes_of(CAP)
    pair = 2 * CAP

    def far_copy(zc, slot, t):
        return make(
            dxp_ref.at[slot, c], from_ref.at[z], far_send.at[t], far_recv.at[z], (r, zc * 2 + c)
        )

    def core_copy(zc, slot, t):
        return make(dxp_ref.at[slot, 1 - c], core_ref.at[zc], core_send.at[t], core_recv.at[zc], mate)

    def yp_copy(zc, slot):
        return pltpu.make_async_copy(yps_ref.at[slot], yp_hbm.at[zc], yp_sem.at[slot])

    def chunk(t, carry):
        zc = place(t)
        slot = t % 2
        k = jnp.where(zc > z, zc - z, z - zc)
        both = (t % 2 == 1) & (t <= 2 * inner)
        single = t > 2 * inner

        @pl.when(both | (single & (zc < z)))
        def _():
            got(z - k, c)

            @pl.when(z < chips - 1)
            def _():
                start(pass_on(z - k, "up"))

            start(pass_on(z - k, "mate"))

        @pl.when(both | (single & (zc > z)))
        def _():
            got(z + k, c)

            @pl.when(z > 0)
            def _():
                start(pass_on(z + k, "down"))

            start(pass_on(z + k, "mate"))

        got(zc, 1 - c)

        @pl.when(t < chips - 1)
        def _():
            do_copy(place(t + 1), 1 - slot).start()

        do_copy(zc, slot).wait()

        @pl.when(t == 0)
        def _():
            pltpu.make_async_copy(w_hbm, w_ref, w_sem.at[0]).wait()

        @pl.when(t >= 2)
        def _():
            core_copy(z, slot, t - 2).wait_send()
            yp_copy(z, slot).wait()

        @pl.when(t >= 3)
        def _():
            far_copy(z, slot, t - 2).wait_send()

        picks, gates, dms = [], [], []
        at_chip = pl.multiple_of(zc * pair, 16)
        for core in range(2):
            rows = [gt_all[zc, core, pl.ds(f * local + i, 1), :] for i in range(local)]
            mine = jnp.concatenate(rows, axis=0) if local > 1 else rows[0]
            rank = jnp.where(mine >= 0.0, dot((mine >= 0.0).astype(F32).astype(BF), before), -1.0)
            chosen = [slot_index == rank[i : i + 1] for i in range(local)]
            gates.append([jnp.sum(jnp.where(chosen[i], mine[i : i + 1], 0.0), axis=1, keepdims=True) for i in range(local)])
            picks.append(jnp.concatenate([one.astype(F32).astype(BF) for one in chosen], axis=0))
            taken = dot(picks[core], n2_all[zc, core]).astype(BF)
            grads = dot(picks[core], do_buf[slot, core]) * residual_scale
            dms.append(grads)
            at = pl.ds(pl.multiple_of(at_chip + core * CAP, 16), CAP)
            for i in range(local):
                part = slice(i * CAP, (i + 1) * CAP)
                xs_ref[i, at] = taken[part]
                dye_ref[i, at] = (gates[core][i] * grads[part]).astype(BF)
        at = pl.ds(at_chip, pair)
        mades, backs, marks = [], [], []
        for i in range(local):
            slots = xs_ref[i, at]
            gate_pre = dot_nt(slots, w_ref[i, :FF])
            up_pre = dot_nt(slots, w_ref[i, FF : 2 * FF])
            grad_act = dot_nt(dye_ref[i, at], w_ref[i, 2 * FF :])
            sigmoid = 1.0 / (1.0 + jnp.exp(-gate_pre))
            silu = gate_pre * sigmoid
            act = (silu * up_pre).astype(BF)
            hx_ref[i, at] = act
            grad_gate = (grad_act * up_pre * (sigmoid * (1.0 + gate_pre * (1.0 - sigmoid)))).astype(BF)
            grad_up = (grad_act * silu).astype(BF)
            dgu_ref[i, at, :FF] = grad_gate
            dgu_ref[i, at, FF:] = grad_up
            made = dot(act, w_ref[i, 2 * FF :]).astype(BF).astype(F32)
            mades.append(made)
            backs.append((dot(grad_gate, w_ref[i, :FF]) + dot(grad_up, w_ref[i, FF : 2 * FF])).astype(BF))
            for core in range(2):
                part = slice(core * CAP, (core + 1) * CAP)
                value = jnp.sum(dms[core][i * CAP : (i + 1) * CAP] * made[part], axis=1, keepdims=True)
                high = value.astype(BF).astype(F32)
                expert = f * local + i
                mark = jnp.where(lane == expert, high, jnp.where(lane == expert + E, value - high, 0.0))
                marks.append(mark.astype(BF))
        for core in range(2):
            part = slice(core * CAP, (core + 1) * CAP)
            sent = jnp.concatenate([backs[i][part] for i in range(local)], axis=0)
            dxp_ref[slot, core, :, :D] = dot_tn(picks[core], sent).astype(BF)
            sent = jnp.concatenate([marks[2 * i + core] for i in range(local)], axis=0)
            dxp_ref[slot, core, :, D:] = dot_tn(picks[core], sent).astype(BF)
        core_copy(zc, slot, t).start()
        for core in range(2):
            part = slice(core * CAP, (core + 1) * CAP)
            sent = jnp.concatenate([(gates[core][i] * mades[i][part]).astype(BF) for i in range(local)], axis=0)
            yps_ref[slot, core] = dot_tn(picks[core], sent).astype(BF)
        yp_copy(zc, slot).start()
        core_copy(zc, slot, t).wait_recv()
        total = dxp_ref[slot, c].astype(F32) + core_ref[zc].astype(F32)

        @pl.when(t == 0)
        def _():
            dx_ref[...] = total

        @pl.when(t > 0)
        def _():
            dxp_ref[slot, c] = total.astype(BF)
            far_copy(zc, slot, t).start()

        return carry

    lax.fori_loop(0, chips, chunk, 0)
    for i in range(local):
        ge_ref[i, : 2 * FF] = dot_tn(dgu_ref[i], xs_ref[i]).astype(BF)
        ge_ref[i, 2 * FF :] = dot_tn(hx_ref[i], dye_ref[i]).astype(BF)
    for k in range(chips):

        @pl.when(z != k)
        def _():
            make(from_ref.at[k], from_ref.at[k], far_send.at[k], far_recv.at[k], (r, k * 2 + c)).wait_recv()
            dx_ref[...] += from_ref[k].astype(F32)

    for t in range(max(chips - 2, 0), chips):
        core_copy(z, t % 2, t).wait_send()
        yp_copy(z, t % 2).wait()
        if t > 0:
            far_copy(z, t % 2, t).wait_send()
    for k in range(chips):

        @pl.when((z >= k) & (z < chips - 1))
        def _():
            for copy in pass_on(k, "up"):
                copy.wait_send()

        @pl.when((z <= k) & (z > 0))
        def _():
            for copy in pass_on(k, "down"):
                copy.wait_send()

        for copy in pass_on(k, "mate"):
            copy.wait_send()


def attention_backward(
    x_ref, dout_ref, cos_ref, sin_ref, w_ref, q_ref, kd_ref, vd_ref, p_hbm, o_ref, h1_ref, n2_ref, gd_ref, dx_ref,
    gin_ref, gw_ref, do_ref, dqkv_ref, p_ref, p_sem,
):
    tokens = x_ref.shape[0]
    lane = lanes_of(tokens)
    low = lane < HD

    def p_copy(g):
        return pltpu.make_async_copy(p_hbm.at[g], p_ref.at[g % 2], p_sem.at[g % 2])

    p_copy(0).start()

    def put(at, value):
        gw_ref[:, :, :, at] = value.astype(BF).reshape(*gw_ref.shape[:3], value.shape[1])

    small = w_ref[:, QKV:W_O].astype(F32).T
    gain_one, gain_two = small[E : E + 1], small[E + 1 : E + 2]
    after = h1_ref[...]
    factor_two = lax.rsqrt(jnp.mean(after * after, axis=1, keepdims=True) + norm_eps)
    gates = jnp.maximum(gd_ref[...], 0.0)
    tail = dx_ref[:, D:].astype(F32)
    grad_gates = jnp.where(lane < E, tail + pltpu.roll(tail, LANE - E, 1), 0.0)
    chosen = gates * (grad_gates - jnp.sum(gates * grad_gates, axis=1, keepdims=True))
    grad_logits = chosen.astype(BF)
    grad_normed = dx_ref[:, :D].astype(F32) + dot_nt(grad_logits, w_ref[:, QKV:W_O])
    scaled = grad_normed * gain_two
    grad_after = dout_ref[...].astype(F32) + (
        factor_two * scaled - after * factor_two**3 * jnp.mean(scaled * after, axis=1, keepdims=True)
    )
    grad_gain_two = jnp.sum(grad_normed * after * factor_two, axis=0, keepdims=True)
    grad_branch = (residual_scale * grad_after).astype(BF)
    put(slice(QKVO - D, QKVO), dot_tn(o_ref[...], grad_branch))
    do_ref[...] = dot_nt(grad_branch, w_ref[:, W_O:]).astype(BF)
    grad_router = dot_tn(n2_ref[...], grad_logits)

    cosines, sines = cos_ref[...], sin_ref[...]
    key_back, value_back = [], []
    for g in range(KVH):
        at = slice(g * LANE, (g + 1) * LANE)
        queries = halves(q_ref[:, at].astype(F32), low).astype(BF)
        outs = halves(do_ref[:, at].astype(F32), low).astype(BF)
        if g + 1 < KVH:
            p_copy(g + 1).start()
        p_copy(g).wait()
        weights = p_ref[g % 2]
        grad_weights = dot_nt(outs, vd_ref[:, at])
        total = jnp.sum(weights * grad_weights, axis=1, keepdims=True)
        grad_scores = (weights * (grad_weights - total)).astype(BF)
        block = dot(grad_scores, kd_ref[:, at])
        block = jnp.where(low, block[:tokens], block[tokens:]) * score_scale
        dqkv_ref[:, at] = (block * cosines - turned(block, lane) * sines).astype(BF)
        block = dot_tn(grad_scores, queries) * score_scale
        key_back.append(block + pltpu.roll(block, HD, 1))
        block = dot_tn(weights.astype(BF), outs)
        value_back.append(block + pltpu.roll(block, HD, 1))
    for m in range(KVH // 2):
        block = jnp.where(low, key_back[2 * m], key_back[2 * m + 1])
        at = slice(H * HD + m * LANE, H * HD + (m + 1) * LANE)
        dqkv_ref[:, at] = (block * cosines - turned(block, lane) * sines).astype(BF)
        at = slice(H * HD + KVH * HD + m * LANE, H * HD + KVH * HD + (m + 1) * LANE)
        dqkv_ref[:, at] = jnp.where(low, value_back[2 * m], value_back[2 * m + 1]).astype(BF)

    source = x_ref[...].astype(F32)
    factor_one = lax.rsqrt(jnp.mean(source * source, axis=1, keepdims=True) + norm_eps)
    normed = (source * factor_one * gain_one).astype(BF)
    put(slice(0, QKVO - D), dot_tn(normed, dqkv_ref[...]))
    grad_normed = dot_nt(dqkv_ref[...], w_ref[:, :QKV])
    scaled = grad_normed * gain_one
    grad_vector = factor_one * scaled - source * factor_one**3 * jnp.mean(scaled * source, axis=1, keepdims=True)
    gin_ref[...] = grad_after + grad_vector
    grad_gain_one = jnp.sum(grad_normed * source * factor_one, axis=0, keepdims=True)
    gains = jnp.concatenate([grad_gain_one, grad_gain_two, jnp.zeros((6, D), F32)], axis=0).T
    at = lanes_of(D)
    extra = jnp.where(at == E, gains[:, 0:1], jnp.where(at == E + 1, gains[:, 1:2], grad_router))
    put(slice(QKVO, QKVO + LANE), extra)


def add_rows(target, first, second, rows, step):
    def some(i, carry):
        at = pl.ds(pl.multiple_of(i * step, step), step)
        target(at, first(at).astype(F32) + second(at).astype(F32))
        return carry

    lax.fori_loop(0, rows // step, some, 0)


def tail(
    replicas, chips,
    x_ref, dout_ref, cos_ref, sin_ref, w_ref, q_ref, kd_ref, vd_ref, o_ref, h1_ref, n2_ref, gd_ref, dx_ref, ge_ref, p_hbm,
    gin_ref, gexp_ref, gproj_ref,
    p_ref, p_sem, do_ref, dqkv_ref, gw_ref, core_ref, up_ref, down_ref, parts_ref, smalls_ref, result_ref, *rest,
):
    bits = replicas.bit_length() - 1
    jobs = ge_ref.shape[0] * bits
    arrived = rest[:bits]
    kept = rest[bits : 2 * bits - 1] if bits else ()
    rest = rest[2 * bits - 1 if bits else 0 :]
    (ar_send, ar_recv, core_send, core_recv, up_send, up_recv, down_send, down_recv,
     part_send, part_recv, small_send, small_recv, result_send, result_recv) = rest
    r, f = lax.axis_index("replica"), lax.axis_index("fsdp")
    z, c = f // 2, f % 2
    mate = (r, z * 2 + 1 - c)
    above, below = (r, f + 2), (r, f - 2)
    rows = gw_ref.shape[2]
    make = Copies().make

    barrier = pltpu.get_barrier_semaphore()
    expected = 1 + (replicas - 1) + jnp.where(z > 0, 1, 0) + jnp.where(z < chips - 1, 1, 0)
    pl.semaphore_signal(barrier, inc=1, device_id=mate, device_id_type=pl.DeviceIdType.MESH)
    for d in range(1, replicas):
        pl.semaphore_signal(barrier, inc=1, device_id=((r + d) % replicas, f), device_id_type=pl.DeviceIdType.MESH)

    @pl.when(z > 0)
    def _():
        pl.semaphore_signal(barrier, inc=1, device_id=below, device_id_type=pl.DeviceIdType.MESH)

    @pl.when(z < chips - 1)
    def _():
        pl.semaphore_signal(barrier, inc=1, device_id=above, device_id_type=pl.DeviceIdType.MESH)

    pl.semaphore_wait(barrier, expected)

    def bit_of(b):
        return (r // (1 << b)) % 2

    def partner(b):
        return (r + (1 - 2 * bit_of(b)) * (1 << b), f)

    def halving(e):
        size = ge_ref.shape[1] // bits
        orders = [[(g + k) % bits for k in range(bits)] for g in range(bits)]
        starts = [[] for _ in range(bits)]
        for g in range(bits):
            at = g * size
            for k in range(bits):
                starts[g].append(at)
                at = at + bit_of(orders[g][k]) * (size >> (k + 1))
            starts[g].append(at)
        copies = {}

        def source(g, k, at, length):
            return ge_ref.at[e, pl.ds(g * size + at, length)] if k == 0 else kept[k - 1].at[e * bits + g, pl.ds(at, length)]

        def exchange(g, k):
            half = size >> (k + 1)
            give = pl.multiple_of((1 - bit_of(orders[g][k])) * half, half)
            copies[g, k] = make(
                source(g, k, give, half), arrived[k].at[e * bits + g], ar_send.at[e * bits + g, k],
                ar_recv.at[e * bits + g, k], partner(orders[g][k]),
            )
            copies[g, k].start()

        def spread(g, k):
            half = size >> (k + 1)
            at = pl.ds(pl.multiple_of(starts[g][k + 1], half), half)
            copies[g, bits + k] = make(
                gexp_ref.at[e, at], gexp_ref.at[e, at], ar_send.at[e * bits + g, bits + k],
                ar_recv.at[e * bits + g, bits + k], partner(orders[g][k]),
            )
            copies[g, bits + k].start()

        for g in range(bits):
            exchange(g, 0)
        yield
        for k in range(bits):
            half = size >> (k + 1)
            for g in range(bits):
                copies[g, k].wait_recv()
                keep = pl.multiple_of(bit_of(orders[g][k]) * half, half)
                own = source(g, k, keep, half)
                there = arrived[k].at[e * bits + g]
                if k < bits - 1:
                    into = kept[k].at[e * bits + g]
                else:
                    into = gexp_ref.at[e, pl.ds(pl.multiple_of(starts[g][bits], half), half)]

                def write(at, value, into=into):
                    into[at] = value.astype(BF)

                add_rows(write, lambda at: own[at], lambda at: there[at], half, min(half, 64))
                if k < bits - 1:
                    exchange(g, k + 1)
                else:
                    spread(g, k)
            yield
        for k in range(bits - 1, -1, -1):
            for g in range(bits):
                copies[g, bits + k].wait_recv()
                if k > 0:
                    spread(g, k - 1)
            yield
        for copy in copies.values():
            copy.wait_send()

    def line():
        crossing = make(gw_ref.at[:, 1 - c], core_ref, core_send.at[0], core_recv.at[0], mate)
        crossing.start()
        yield
        crossing.wait_recv()

        def add_block(block, other):
            def write(at, value):
                gw_ref[block, c, at] = value.astype(BF)

            add_rows(write, lambda at: gw_ref[block, c, at], lambda at: other[block, at], rows, 16)

        def send(block, up):
            there, send_sem, recv_sem = (up_ref, up_send, up_recv) if up else (down_ref, down_send, down_recv)
            return make(
                gw_ref.at[block, c], there.at[block], send_sem.at[block], recv_sem.at[block], above if up else below
            )

        for k in range(chips):
            add_block(k, core_ref)
        for k in range(chips - 1):
            owner = chips - 1 - k

            @pl.when(z == 0)
            def _():
                send(owner, True).start()

            @pl.when(z == chips - 1)
            def _():
                send(k, False).start()

        yield
        for k in range(chips - 2):
            owner = chips - 1 - k

            @pl.when((z > 0) & (z < owner))
            def _():
                send(owner, True).wait_recv()
                add_block(owner, up_ref)
                send(owner, True).start()

            @pl.when((z < chips - 1) & (z > k))
            def _():
                send(k, False).wait_recv()
                add_block(k, down_ref)
                send(k, False).start()

            yield

        @pl.when(z > 0)
        def _():
            send(z, True).wait_recv()
            add_block(z, up_ref)

        @pl.when(z < chips - 1)
        def _():
            send(z, False).wait_recv()
            add_block(z, down_ref)

        wide = QKVO // replicas

        def columns(part):
            return pl.ds(pl.multiple_of(part * wide, LANE), wide)

        own = gw_ref.at[z, c]

        def part_copy(d):
            to = (r + d) % replicas
            return make(own.at[:, columns(to)], parts_ref.at[r], part_send.at[d], part_recv.at[r], (to, f))

        def small_copy(d):
            to = (r + d) % replicas
            return make(own.at[:, pl.ds(QKVO, LANE)], smalls_ref.at[r], small_send.at[d], small_recv.at[r], (to, f))

        for d in range(1, replicas):
            part_copy(d).start()
            small_copy(d).start()
        parts_ref[r] = own[:, columns(r)]
        smalls_ref[r] = own[:, pl.ds(QKVO, LANE)]
        yield
        for d in range(1, replicas):
            peer = (r + d) % replicas
            make(parts_ref.at[peer], parts_ref.at[peer], part_send.at[d], part_recv.at[peer], (peer, f)).wait_recv()
            make(smalls_ref.at[peer], smalls_ref.at[peer], small_send.at[d], small_recv.at[peer], (peer, f)).wait_recv()
        total = parts_ref[0].astype(F32)
        small = smalls_ref[0].astype(F32)
        for k in range(1, replicas):
            total = total + parts_ref[k].astype(F32)
            small = small + smalls_ref[k].astype(F32)
        result_ref[r] = total.astype(BF)
        gproj_ref[:, QKVO:] = small

        def result_copy(d):
            to = (r + d) % replicas
            return make(result_ref.at[r], result_ref.at[r], result_send.at[d], result_recv.at[r], (to, f))

        for d in range(1, replicas):
            result_copy(d).start()
        yield
        for d in range(1, replicas):
            peer = (r + d) % replicas
            make(result_ref.at[peer], result_ref.at[peer], result_send.at[d], result_recv.at[peer], (peer, f)).wait_recv()
        for k in range(replicas):
            gproj_ref[:, k * wide : (k + 1) * wide] = result_ref[k].astype(F32)
        crossing.wait_send()
        for k in range(chips):

            @pl.when(z < k)
            def _():
                send(k, True).wait_send()

            @pl.when(z > k)
            def _():
                send(k, False).wait_send()

        for d in range(1, replicas):
            part_copy(d).wait_send()
            small_copy(d).wait_send()
            result_copy(d).wait_send()

    experts_sums = [halving(e) for e in range(ge_ref.shape[0])] if bits else []
    for e, sums in enumerate(experts_sums):
        next(sums)
    if not bits:
        gexp_ref[...] = ge_ref[...]
    attention_backward(
        x_ref, dout_ref, cos_ref, sin_ref, w_ref, q_ref, kd_ref, vd_ref, p_hbm, o_ref, h1_ref, n2_ref, gd_ref, dx_ref,
        gin_ref, gw_ref, do_ref, dqkv_ref, p_ref, p_sem,
    )
    projections = line()
    first, last = experts_sums[:1], experts_sums[1:]
    order = [[projections], first, [projections], last, [projections], first, last, [projections], first, last]
    order += [[projections], first, [projections], last, [projections]]
    order += [[projections] + experts_sums] * (chips + 2 * bits)
    for turn in order:
        for process in turn:
            next(process, None)


def call(kernel, out_shape, args, scratch=(), outside=0, out_outside=0, **params):
    spaces = [pltpu.SMEM if a.dtype == jnp.int32 and a.size <= 16 else pltpu.VMEM for a in args]
    spaces[len(args) - outside :] = [pl.ANY] * outside
    return pl.pallas_call(
        kernel,
        out_shape=out_shape,
        in_specs=[pl.BlockSpec(memory_space=space) for space in spaces],
        out_specs=[
            pl.BlockSpec(memory_space=pltpu.VMEM if i < len(out_shape) - out_outside else pl.ANY)
            for i in range(len(out_shape))
        ],
        scratch_shapes=list(scratch),
        compiler_params=pltpu.CompilerParams(
            vmem_limit_bytes=VMEM_LIMIT, has_side_effects="collective_id" in params, **params
        ),
    )(*args)


def shape(dims, dtype):
    return jax.ShapeDtypeStruct(dims, dtype)


def make_body(mesh):
    group, replicas = mesh.shape["fsdp"], mesh.shape["replica"]
    local = E // group

    def body(
        hidden_in, seq_lengths, routes, norm1_gain, w_query, w_key, w_value, w_output, norm2_gain, w_router,
        expert_weights, out_cotangent,
    ):
        tokens = hidden_in.shape[0]
        rows = w_query.shape[0]
        chips = group // 2
        dma = pltpu.SemaphoreType.DMA
        weights, q, kd, vd, o, h1, n2, gd, gt, cosines, sines, p, dout_all = call(
            functools.partial(front, replicas, chips),
            (
                shape((chips, 2, rows, W_O + D), BF), shape((tokens, D), BF), shape((tokens, D), BF),
                shape((tokens, D), BF), shape((tokens, D), BF), shape((tokens, D), F32), shape((tokens, D), BF),
                shape((tokens, LANE), F32), shape((E, tokens), F32), shape((tokens, LANE), F32),
                shape((tokens, LANE), F32), shape((KVH, 2 * tokens, tokens), F32), shape((chips, 2, tokens, D), BF),
            ),
            (
                hidden_in, seq_lengths, routes.T, rope_table(tokens), w_query, w_key, w_value, w_output, w_router.T,
                norm1_gain[None], norm2_gain[None], out_cotangent,
            ),
            [
                pltpu.VMEM((2, 2 * tokens, tokens), F32), dma((2,)), dma((1,)), dma((3, chips)), dma((3, chips)),
                dma((3, chips)), dma((3, chips, replicas)), dma((3, chips, replicas)), dma((2, chips)),
                dma((2, chips)), dma((3, chips)), dma((chips, 2)),
            ],
            out_outside=2,
            collective_id=2,
        )
        weights = weights.reshape(D, W_O + D)
        anywhere = pl.BlockSpec(memory_space=pl.ANY)
        inside = pl.BlockSpec(memory_space=pltpu.VMEM)
        wide = D + LANE
        dx, yp, grad_experts = pl.pallas_call(
            functools.partial(middle, chips),
            in_specs=[inside, inside, anywhere, anywhere],
            out_specs=[inside, anywhere, inside],
            out_shape=[
                shape((tokens, wide), F32), shape((chips, 2, tokens, D), BF), shape((local, 3 * FF, D), BF),
            ],
            scratch_shapes=[
                pltpu.VMEM((chips, 2, tokens, D), BF), pltpu.VMEM((chips, 2, E, tokens), F32),
                pltpu.VMEM((2, 2, tokens, D), BF), pltpu.VMEM((local, 3 * FF, D), BF),
                pltpu.VMEM((local, group * CAP, D), BF), pltpu.VMEM((local, group * CAP, D), BF),
                pltpu.VMEM((local, group * CAP, D), BF), pltpu.VMEM((local, group * CAP, FF), BF),
                pltpu.VMEM((2, 2, tokens, wide), BF), pltpu.VMEM((2, 2, tokens, D), BF),
                pltpu.VMEM((chips, tokens, wide), BF), pltpu.VMEM((chips, tokens, wide), BF),
            ]
            + ([dma((chips,))] * 3 + [dma((chips, 2))]) * 2 + [dma((chips,))] * 4 + [dma((2,)), dma((2,)), dma((1,))],
            compiler_params=pltpu.CompilerParams(vmem_limit_bytes=VMEM_LIMIT, has_side_effects=True, collective_id=1),
        )(n2, gt, dout_all, expert_weights)
        moe = lax.psum_scatter(yp.reshape(group * tokens, D), "fsdp", scatter_dimension=0, tiled=True)
        layer_out = (h1 + residual_scale * moe.astype(F32)).astype(BF)
        bits = replicas.bit_length() - 1
        size = 3 * FF // bits if bits else 0
        grad_in, grad_experts, gw = call(
            functools.partial(tail, replicas, group // 2),
            (shape((tokens, D), F32), shape((local, 3 * FF, D), BF), shape((rows, QKVO + LANE), F32)),
            (hidden_in, out_cotangent, cosines, sines, weights, q, kd, vd, o, h1, n2, gd, dx, grad_experts, p),
            [
                pltpu.VMEM((2, 2 * tokens, tokens), F32), dma((2,)),
                pltpu.VMEM((tokens, D), BF), pltpu.VMEM((tokens, QKVO - D), BF),
                pltpu.VMEM((group // 2, 2, rows, QKVO + LANE), BF), pltpu.VMEM((group // 2, rows, QKVO + LANE), BF),
                pltpu.VMEM((group // 2, rows, QKVO + LANE), BF), pltpu.VMEM((group // 2, rows, QKVO + LANE), BF),
                pltpu.VMEM((replicas, rows, QKVO // replicas), BF), pltpu.VMEM((replicas, rows, LANE), BF),
                pltpu.VMEM((replicas, rows, QKVO // replicas), BF),
            ]
            + [pltpu.VMEM((local * bits, size >> (k + 1), D), BF) for k in range(bits)]
            + [pltpu.VMEM((local * bits, size >> (k + 1), D), BF) for k in range(bits - 1)]
            + [dma((max(local * bits, 1), max(2 * bits, 1)))] * 2 + [dma((1,))] * 2 + [dma((group // 2,))] * 4
            + [dma((replicas,))] * 6,
            outside=1,
            collective_id=0,
        )
        a, b, c = H * HD, H * HD + KVH * HD, H * HD + 2 * KVH * HD
        return (
            layer_out, grad_in, gw[:, QKVO + E], gw[:, :a], gw[:, a:b], gw[:, b:c], gw[:, c:QKVO], gw[:, QKVO + E + 1],
            gw[:, QKVO : QKVO + E], grad_experts.astype(F32),
        )

    return body


def solution(mesh):
    tokens, weights = P(("replica", "fsdp"), None), P("fsdp", None)
    return jax.shard_map(
        make_body(mesh),
        mesh=mesh,
        in_specs=(
            tokens, tokens, tokens, P("fsdp"), weights, weights, weights, weights, P("fsdp"), weights,
            P("fsdp", None, None), tokens,
        ),
        out_specs=(
            tokens, tokens, P("fsdp"), weights, weights, weights, weights, P("fsdp"), weights, P("fsdp", None, None),
        ),
        check_vma=False,
    )
```

```python
import functools

import jax
import jax.numpy as jnp
import numpy as np
from jax import lax
from jax.experimental import pallas as pl
from jax.experimental.pallas import tpu as pltpu
from jax.sharding import PartitionSpec as P

D = 1024
H = 16
KVH = 8
HD = 64
FF = 512
TOPK = 8
E = 16
CAP = 144
LANE = 128
QKV = H * HD + 2 * KVH * HD
QKVO = QKV + D
W_O = QKV + LANE

norm_eps = 1e-06
score_scale = 0.015625
residual_scale = 0.22
rope_base = 10000.0
masked_score = -1e30

BF = jnp.bfloat16
F32 = jnp.float32
VMEM_LIMIT = 63 * 2**20


def dot(a, b):
    return lax.dot_general(a, b, (((1,), (0,)), ((), ())), preferred_element_type=F32)


def dot_nt(a, b):
    return lax.dot_general(a, b, (((1,), (1,)), ((), ())), preferred_element_type=F32)


def dot_tn(a, b):
    return lax.dot_general(a, b, (((0,), (0,)), ((), ())), preferred_element_type=F32)


def lanes_of(rows):
    return lax.broadcasted_iota(jnp.int32, (rows, LANE), 1)


def turned(block, lane):
    return jnp.where(lane % HD < HD // 2, pltpu.roll(block, LANE - HD // 2, 1), pltpu.roll(block, HD // 2, 1))


def halves(block, low):
    zero = jnp.zeros_like(block)
    return jnp.concatenate([jnp.where(low, block, zero), jnp.where(low, zero, block)], axis=0)


def rope_table(tokens):
    frequency = np.float32(rope_base) ** (-np.arange(0, HD, 2, dtype=np.float32) / np.float32(HD))
    frequency = np.tile(frequency.astype(np.float32), LANE // (HD // 2))
    angles = (np.arange(tokens, dtype=np.float32)[:, None] * frequency[None, :]).astype(np.float64)
    sign = np.where(np.arange(LANE) % HD < HD // 2, -1.0, 1.0)
    pieces = []
    for values in (np.cos(angles), np.sin(angles) * sign[None, :]):
        rest = values.astype(np.float32)
        for _ in range(3):
            piece = rest.astype(BF)
            pieces.append(piece)
            rest = rest - piece.astype(np.float32)
    return np.concatenate(pieces, axis=1)


class Copies:
    def make(self, src, dst, send, recv, device):
        return pltpu.make_async_remote_copy(
            src_ref=src, dst_ref=dst, send_sem=send, recv_sem=recv, device_id=device, device_id_type=pl.DeviceIdType.MESH
        )


def meet(devices, expected):
    barrier = pltpu.get_barrier_semaphore()
    for condition, device in devices:

        def signal(device=device):
            pl.semaphore_signal(barrier, inc=1, device_id=device, device_id_type=pl.DeviceIdType.MESH)

        if condition is True:
            signal()
        else:
            pl.when(condition)(signal)
    pl.semaphore_wait(barrier, expected)


def front(
    replicas, chips,
    x_ref, len_ref, routes_ref, table_ref, wq_ref, wk_ref, wv_ref, wo_ref, wr_ref, g1_ref, g2_ref, dout_ref,
    w_all, q_ref, kd_ref, vd_ref, o_ref, h1_ref, n2_ref, gd_ref, gt_ref, cos_ref, sin_ref, p_hbm, do_all,
    p_ref, p_sem, own_sem, z_up, z_down, z_recv, xy_send, xy_recv, mate_send, mate_recv, do_send, do_recv,
):
    tokens = x_ref.shape[0]
    r, f = lax.axis_index("replica"), lax.axis_index("fsdp")
    z, c = f // 2, f % 2
    mate, above, below = (r, z * 2 + 1 - c), (r, f + 2), (r, f - 2)
    make = Copies().make
    peers = [(True, mate), (z > 0, below), (z < chips - 1, above)]
    peers += [(True, ((r + d) % replicas, f)) for d in range(1, replicas)]

    own_dout = pltpu.make_async_copy(dout_ref, do_all.at[z, c], own_sem.at[0])
    own_dout.start()
    rows = wq_ref.shape[0]
    packed = [wr_ref[...].astype(F32), g1_ref[...].astype(F32), g2_ref[...].astype(F32)]
    packed = jnp.concatenate(packed + [jnp.zeros((LANE - E - 2, rows), F32)], axis=0)
    own = w_all.at[z, c]
    own[:, : H * HD] = wq_ref[...]
    own[:, H * HD : H * HD + KVH * HD] = wk_ref[...]
    own[:, H * HD + KVH * HD : QKV] = wv_ref[...]
    own[:, QKV:W_O] = packed.T.astype(BF)
    own[:, W_O:] = wo_ref[...]
    meet(peers, 1 + (replicas - 1) + jnp.where(z > 0, 1, 0) + jnp.where(z < chips - 1, 1, 0))

    def part(kind):
        if kind == 0:
            return pl.ds(pl.multiple_of(r * (QKV // replicas), LANE), QKV // replicas)
        if kind == 1:
            return pl.ds(QKV, LANE)
        return pl.ds(pl.multiple_of(W_O + r * (D // replicas), LANE), D // replicas)

    def along(zb, kind, up):
        ref = w_all.at[zb, c, :, part(kind)]
        return make(ref, ref, (z_up if up else z_down).at[kind, zb], z_recv.at[kind, zb], above if up else below)

    def across(zb, kind, d):
        ref = w_all.at[zb, c, :, part(kind)]
        return make(ref, ref, xy_send.at[kind, zb, d], xy_recv.at[kind, zb, r], ((r + d) % replicas, f))

    def wait_across(zb, kind):
        for d in range(1, replicas):
            peer = (r + d) % replicas
            ref = w_all.at[zb, c, :, part(kind)]
            make(ref, ref, xy_send.at[kind, zb, d], xy_recv.at[kind, zb, peer], (peer, f)).wait_recv()

    def to_mate(zb, core, late):
        ref = w_all.at[zb, core, :, pl.ds(W_O, D) if late else pl.ds(0, W_O)]
        return make(ref, ref, mate_send.at[late, zb], mate_recv.at[late, zb], mate)

    def dout_copy(zb, core, way):
        source = do_all.at[zb, core]
        return make(source, do_all.at[zb, core], do_send.at[way, zb], do_recv.at[zb, core], (above, below, mate)[way])

    def both_sides(k, act):
        @pl.when(z >= k)
        def _():
            act(z - k, True)

        @pl.when(z < chips - k)
        def _():
            act(z + k, False)

    def onward(up):
        return z < chips - 1 if up else z > 0

    for kind in range(3):
        both_sides(1, lambda zb, low: along(z, kind, not low).start())
    for late in range(2):
        to_mate(z, c, late).start()

    source = x_ref[...].astype(F32)
    factor = lax.rsqrt(jnp.mean(source * source, axis=1, keepdims=True) + norm_eps)
    lane = lanes_of(tokens)
    low_lane = lane < HD
    row = lax.broadcasted_iota(jnp.int32, (tokens, tokens), 0)
    column = lax.broadcasted_iota(jnp.int32, (tokens, tokens), 1)
    row_at = lax.broadcasted_iota(jnp.int32, (tokens, 1), 0)
    column_at = lax.broadcasted_iota(jnp.int32, (1, tokens), 1)
    row_segment = jnp.zeros((tokens, 1), jnp.int32)
    row_start = jnp.zeros((tokens, 1), jnp.int32)
    column_segment = jnp.zeros((1, tokens), jnp.int32)
    end = jnp.int32(0)
    for j in range(len_ref.shape[1]):
        end = end + len_ref[0, j]
        row_segment += (row_at >= end).astype(jnp.int32)
        row_start = jnp.maximum(row_start, jnp.where(row_at >= end, end, 0))
        column_segment += (column_at >= end).astype(jnp.int32)
    place = (column == row - row_start).astype(F32).astype(BF)
    found = dot(place, table_ref[...])
    found = [found[:, i * LANE : (i + 1) * LANE] for i in range(6)]
    cosines, sines = found[0] + found[1] + found[2], found[3] + found[4] + found[5]
    cos_ref[...] = cosines
    sin_ref[...] = sines

    own_dout.wait()
    for k in range(1, chips):
        for kind in range(3):

            def arrive(zb, low, kind=kind):
                along(zb, kind, low).wait_recv()

                @pl.when(onward(low))
                def _():
                    along(zb, kind, low).start()

                if kind != 1:
                    for d in range(1, replicas):
                        across(zb, kind, d).start()

            both_sides(k, arrive)
        if k == 1:
            both_sides(1, lambda zb, low: dout_copy(z, c, 1 if low else 0).start())
            dout_copy(z, c, 2).start()

    def share(k, late):
        def act(zb, low):
            wait_across(zb, 2 if late else 0)
            to_mate(zb, c, late).start()

        both_sides(k, act)

    for k in range(1, chips):
        share(k, 0)
    for k in range(chips):
        to_mate(k, 1 - c, 0).wait_recv()

    def columns(start, size):
        return w_all[:, :, :, start : start + size].reshape(D, size)

    small = columns(QKV, LANE)
    gains = small.astype(F32).T
    gain_one, gain_two = gains[E : E + 1], gains[E + 1 : E + 2]
    normed = (source * factor * gain_one).astype(BF)
    q_all = dot(normed, columns(0, H * HD))
    for g in range(H // 2):
        at = slice(g * LANE, (g + 1) * LANE)
        block = q_all[:, at]
        q_ref[:, at] = (block * cosines + turned(block, lane) * sines).astype(BF)
    kv = dot(normed, columns(H * HD, 2 * KVH * HD))
    for m in range(KVH // 2):
        block = kv[:, m * LANE : (m + 1) * LANE]
        block = block * cosines + turned(block, lane) * sines
        other = pltpu.roll(block, HD, 1)
        kd_ref[:, 2 * m * LANE : (2 * m + 1) * LANE] = jnp.where(low_lane, block, other).astype(BF)
        kd_ref[:, (2 * m + 1) * LANE : (2 * m + 2) * LANE] = jnp.where(low_lane, other, block).astype(BF)
        block = kv[:, KVH * HD + m * LANE : KVH * HD + (m + 1) * LANE]
        other = pltpu.roll(block, HD, 1)
        vd_ref[:, 2 * m * LANE : (2 * m + 1) * LANE] = jnp.where(low_lane, block, other).astype(BF)
        vd_ref[:, (2 * m + 1) * LANE : (2 * m + 2) * LANE] = jnp.where(low_lane, other, block).astype(BF)
    bias = jnp.where((row_segment == column_segment) & (column <= row), 0.0, masked_score)
    bias = jnp.concatenate([bias, bias], axis=0)

    def p_copy(g):
        return pltpu.make_async_copy(p_ref.at[g % 2], p_hbm.at[g], p_sem.at[g % 2])

    for g in range(KVH):
        at = slice(g * LANE, (g + 1) * LANE)
        queries = halves(q_ref[:, at].astype(F32), low_lane).astype(BF)
        scores = dot_nt(queries, kd_ref[:, at]) * score_scale + bias
        shifted = jnp.exp(scores - jnp.max(scores, axis=1, keepdims=True))
        weights = shifted * (1.0 / jnp.sum(shifted, axis=1, keepdims=True))
        if g >= 2:
            p_copy(g - 2).wait()
        p_ref[g % 2] = weights
        p_copy(g).start()
        mixed = dot(weights.astype(BF), vd_ref[:, at])
        o_ref[:, at] = jnp.where(low_lane, mixed[:tokens], mixed[tokens:]).astype(BF)

    for k in range(1, chips):
        share(k, 1)

    def dout_arrive(zb, low):
        dout_copy(zb, c, 0 if low else 1).wait_recv()

        @pl.when(onward(low))
        def _():
            dout_copy(zb, c, 0 if low else 1).start()

        dout_copy(zb, c, 2).start()

    if chips > 1:
        both_sides(1, dout_arrive)
    for k in range(chips):
        to_mate(k, 1 - c, 1).wait_recv()
    after = source + residual_scale * dot(o_ref[...], columns(W_O, D))
    h1_ref[...] = after
    factor = lax.rsqrt(jnp.mean(after * after, axis=1, keepdims=True) + norm_eps)
    normed = (after * factor * gain_two).astype(BF)
    n2_ref[...] = normed
    logits = dot(normed, small).T[:E]
    expert = lax.broadcasted_iota(jnp.int32, (E, tokens), 0)
    routed = routes_ref[0:1] == expert
    for j in range(1, TOPK):
        routed |= routes_ref[j : j + 1] == expert
    top = jnp.max(jnp.where(routed, logits, masked_score), axis=0, keepdims=True)
    powers = jnp.where(routed, jnp.exp(logits - top), 0.0)
    gates = powers / jnp.sum(powers, axis=0, keepdims=True)
    gates = jnp.where(routed, gates, -1.0)
    gt_ref[...] = gates
    gd_ref[...] = jnp.concatenate([gates, jnp.full((LANE - E, tokens), -1.0, F32)], axis=0).T

    for k in range(2, chips):
        both_sides(k, dout_arrive)
    for k in range(chips):
        dout_copy(k, 1 - c, 2).wait_recv()
    for g in (KVH - 2, KVH - 1):
        p_copy(g).wait()
    for k in range(chips):
        for late in range(2):
            to_mate(k, c, late).wait_send()
        dout_copy(k, c, 2).wait_send()

        @pl.when((z >= k) & (z < chips - 1))
        def _():
            dout_copy(k, c, 0).wait_send()
            for kind in range(3):
                along(k, kind, True).wait_send()

        @pl.when((z <= k) & (z > 0))
        def _():
            dout_copy(k, c, 1).wait_send()
            for kind in range(3):
                along(k, kind, False).wait_send()

        @pl.when(z != k)
        def _():
            for d in range(1, replicas):
                for kind in (0, 2):
                    across(k, kind, d).wait_send()


def middle(
    chips, n2_ref, gt_ref, do_hbm, w_hbm,
    dx_ref, yp_hbm, ge_ref,
    n2_all, gt_all, do_buf, w_ref, xs_ref, dye_ref, dgu_ref, hx_ref, dxp_ref, yps_ref, core_ref, from_ref,
    n2_up, n2_down, n2_mate, n2_recv, gt_up, gt_down, gt_mate, gt_recv,
    core_send, core_recv, far_send, far_recv, do_sem, yp_sem, w_sem,
):
    local = w_ref.shape[0]
    tokens = n2_ref.shape[0]
    r, f = lax.axis_index("replica"), lax.axis_index("fsdp")
    z, c = f // 2, f % 2
    mate, above, below = (r, z * 2 + 1 - c), (r, f + 2), (r, f - 2)
    make = Copies().make

    pltpu.make_async_copy(w_hbm, w_ref, w_sem.at[0]).start()

    def do_copy(zc, slot):
        return pltpu.make_async_copy(do_hbm.at[zc], do_buf.at[slot], do_sem.at[slot])

    do_copy(z, 0).start()

    barrier = pltpu.get_barrier_semaphore()
    pl.semaphore_signal(barrier, inc=1, device_id=mate, device_id_type=pl.DeviceIdType.MESH)
    for k in range(1, chips):
        to = (r, (z + k) % chips * 2 + c)
        pl.semaphore_signal(barrier, inc=1, device_id=to, device_id_type=pl.DeviceIdType.MESH)
    n2_all[z, c] = n2_ref[...]
    gt_all[z, c] = gt_ref[...]
    pl.semaphore_wait(barrier, chips)

    def pass_on(zb, how):
        to = {"up": above, "down": below, "mate": mate}[how]
        sems = {"up": (n2_up, gt_up), "down": (n2_down, gt_down), "mate": (n2_mate, gt_mate)}[how]
        return [
            make(ref.at[zb, c], ref.at[zb, c], sem.at[zb], recv.at[zb, c], to)
            for ref, sem, recv in ((gt_all, sems[1], gt_recv), (n2_all, sems[0], n2_recv))
        ]

    def got(zb, core):
        for ref, sem, recv in ((gt_all, gt_mate, gt_recv), (n2_all, n2_mate, n2_recv)):
            make(ref.at[zb, core], ref.at[zb, core], sem.at[zb], recv.at[zb, core], mate).wait_recv()

    def start(copies):
        for copy in copies:
            copy.start()

    @pl.when(z < chips - 1)
    def _():
        start(pass_on(z, "up"))

    @pl.when(z > 0)
    def _():
        start(pass_on(z, "down"))

    start(pass_on(z, "mate"))
    inner = jnp.minimum(z, chips - 1 - z)

    def place(t):
        k = (t + 1) // 2
        near = jnp.where(t % 2 == 1, z - k, z + k)
        return jnp.where(t <= 2 * inner, near, jnp.where(2 * z < chips - 1, t, chips - 1 - t))

    before = lax.broadcasted_iota(jnp.int32, (tokens, tokens), 0) < lax.broadcasted_iota(jnp.int32, (tokens, tokens), 1)
    before = before.astype(F32).astype(BF)
    slot_index = lax.broadcasted_iota(jnp.int32, (CAP, tokens), 0).astype(F32)
    lane = lanes_of(CAP)
    pair = 2 * CAP

    def far_copy(zc, slot, t):
        return make(
            dxp_ref.at[slot, c], from_ref.at[z], far_send.at[t], far_recv.at[z], (r, zc * 2 + c)
        )

    def core_copy(zc, slot, t):
        return make(dxp_ref.at[slot, 1 - c], core_ref.at[zc], core_send.at[t], core_recv.at[zc], mate)

    def yp_copy(zc, slot):
        return pltpu.make_async_copy(yps_ref.at[slot], yp_hbm.at[zc], yp_sem.at[slot])

    def chunk(t, carry):
        zc = place(t)
        slot = t % 2
        k = jnp.where(zc > z, zc - z, z - zc)
        both = (t % 2 == 1) & (t <= 2 * inner)
        single = t > 2 * inner

        @pl.when(both | (single & (zc < z)))
        def _():
            got(z - k, c)

            @pl.when(z < chips - 1)
            def _():
                start(pass_on(z - k, "up"))

            start(pass_on(z - k, "mate"))

        @pl.when(both | (single & (zc > z)))
        def _():
            got(z + k, c)

            @pl.when(z > 0)
            def _():
                start(pass_on(z + k, "down"))

            start(pass_on(z + k, "mate"))

        got(zc, 1 - c)

        @pl.when(t < chips - 1)
        def _():
            do_copy(place(t + 1), 1 - slot).start()

        do_copy(zc, slot).wait()

        @pl.when(t == 0)
        def _():
            pltpu.make_async_copy(w_hbm, w_ref, w_sem.at[0]).wait()

        @pl.when(t >= 2)
        def _():
            core_copy(z, slot, t - 2).wait_send()
            yp_copy(z, slot).wait()

        @pl.when(t >= 3)
        def _():
            far_copy(z, slot, t - 2).wait_send()

        picks, gates, dms = [], [], []
        at_chip = pl.multiple_of(zc * pair, 16)
        for core in range(2):
            rows = [gt_all[zc, core, pl.ds(f * local + i, 1), :] for i in range(local)]
            mine = jnp.concatenate(rows, axis=0) if local > 1 else rows[0]
            rank = jnp.where(mine >= 0.0, dot((mine >= 0.0).astype(F32).astype(BF), before), -1.0)
            chosen = [slot_index == rank[i : i + 1] for i in range(local)]
            gates.append([jnp.sum(jnp.where(chosen[i], mine[i : i + 1], 0.0), axis=1, keepdims=True) for i in range(local)])
            picks.append(jnp.concatenate([one.astype(F32).astype(BF) for one in chosen], axis=0))
            taken = dot(picks[core], n2_all[zc, core]).astype(BF)
            grads = dot(picks[core], do_buf[slot, core]) * residual_scale
            dms.append(grads)
            at = pl.ds(pl.multiple_of(at_chip + core * CAP, 16), CAP)
            for i in range(local):
                part = slice(i * CAP, (i + 1) * CAP)
                xs_ref[i, at] = taken[part]
                dye_ref[i, at] = (gates[core][i] * grads[part]).astype(BF)
        at = pl.ds(at_chip, pair)
        mades, backs, marks = [], [], []
        for i in range(local):
            slots = xs_ref[i, at]
            gate_pre = dot_nt(slots, w_ref[i, :FF])
            up_pre = dot_nt(slots, w_ref[i, FF : 2 * FF])
            grad_act = dot_nt(dye_ref[i, at], w_ref[i, 2 * FF :])
            sigmoid = 1.0 / (1.0 + jnp.exp(-gate_pre))
            silu = gate_pre * sigmoid
            act = (silu * up_pre).astype(BF)
            hx_ref[i, at] = act
            grad_gate = (grad_act * up_pre * (sigmoid * (1.0 + gate_pre * (1.0 - sigmoid)))).astype(BF)
            grad_up = (grad_act * silu).astype(BF)
            dgu_ref[i, at, :FF] = grad_gate
            dgu_ref[i, at, FF:] = grad_up
            made = dot(act, w_ref[i, 2 * FF :]).astype(BF).astype(F32)
            mades.append(made)
            backs.append((dot(grad_gate, w_ref[i, :FF]) + dot(grad_up, w_ref[i, FF : 2 * FF])).astype(BF))
            for core in range(2):
                part = slice(core * CAP, (core + 1) * CAP)
                value = jnp.sum(dms[core][i * CAP : (i + 1) * CAP] * made[part], axis=1, keepdims=True)
                high = value.astype(BF).astype(F32)
                expert = f * local + i
                mark = jnp.where(lane == expert, high, jnp.where(lane == expert + E, value - high, 0.0))
                marks.append(mark.astype(BF))
        for core in range(2):
            part = slice(core * CAP, (core + 1) * CAP)
            sent = jnp.concatenate([backs[i][part] for i in range(local)], axis=0)
            dxp_ref[slot, core, :, :D] = dot_tn(picks[core], sent).astype(BF)
            sent = jnp.concatenate([marks[2 * i + core] for i in range(local)], axis=0)
            dxp_ref[slot, core, :, D:] = dot_tn(picks[core], sent).astype(BF)
        core_copy(zc, slot, t).start()
        for core in range(2):
            part = slice(core * CAP, (core + 1) * CAP)
            sent = jnp.concatenate([(gates[core][i] * mades[i][part]).astype(BF) for i in range(local)], axis=0)
            yps_ref[slot, core] = dot_tn(picks[core], sent).astype(BF)
        yp_copy(zc, slot).start()
        core_copy(zc, slot, t).wait_recv()
        total = dxp_ref[slot, c].astype(F32) + core_ref[zc].astype(F32)

        @pl.when(t == 0)
        def _():
            dx_ref[...] = total

        @pl.when(t > 0)
        def _():
            dxp_ref[slot, c] = total.astype(BF)
            far_copy(zc, slot, t).start()

        return carry

    lax.fori_loop(0, chips, chunk, 0)
    for i in range(local):
        ge_ref[i, : 2 * FF] = dot_tn(dgu_ref[i], xs_ref[i]).astype(BF)
        ge_ref[i, 2 * FF :] = dot_tn(hx_ref[i], dye_ref[i]).astype(BF)
    for k in range(chips):

        @pl.when(z != k)
        def _():
            make(from_ref.at[k], from_ref.at[k], far_send.at[k], far_recv.at[k], (r, k * 2 + c)).wait_recv()
            dx_ref[...] += from_ref[k].astype(F32)

    for t in range(max(chips - 2, 0), chips):
        core_copy(z, t % 2, t).wait_send()
        yp_copy(z, t % 2).wait()
        if t > 0:
            far_copy(z, t % 2, t).wait_send()
    for k in range(chips):

        @pl.when((z >= k) & (z < chips - 1))
        def _():
            for copy in pass_on(k, "up"):
                copy.wait_send()

        @pl.when((z <= k) & (z > 0))
        def _():
            for copy in pass_on(k, "down"):
                copy.wait_send()

        for copy in pass_on(k, "mate"):
            copy.wait_send()


def attention_backward(
    x_ref, dout_ref, cos_ref, sin_ref, w_ref, q_ref, kd_ref, vd_ref, p_hbm, o_ref, h1_ref, n2_ref, gd_ref, dx_ref,
    gin_ref, gw_ref, do_ref, dqkv_ref, p_ref, p_sem,
):
    tokens = x_ref.shape[0]
    lane = lanes_of(tokens)
    low = lane < HD

    def p_copy(g):
        return pltpu.make_async_copy(p_hbm.at[g], p_ref.at[g % 2], p_sem.at[g % 2])

    p_copy(0).start()

    def put(at, value):
        gw_ref[:, :, :, at] = value.astype(BF).reshape(*gw_ref.shape[:3], value.shape[1])

    small = w_ref[:, QKV:W_O].astype(F32).T
    gain_one, gain_two = small[E : E + 1], small[E + 1 : E + 2]
    after = h1_ref[...]
    factor_two = lax.rsqrt(jnp.mean(after * after, axis=1, keepdims=True) + norm_eps)
    gates = jnp.maximum(gd_ref[...], 0.0)
    tail = dx_ref[:, D:].astype(F32)
    grad_gates = jnp.where(lane < E, tail + pltpu.roll(tail, LANE - E, 1), 0.0)
    chosen = gates * (grad_gates - jnp.sum(gates * grad_gates, axis=1, keepdims=True))
    grad_logits = chosen.astype(BF)
    grad_normed = dx_ref[:, :D].astype(F32) + dot_nt(grad_logits, w_ref[:, QKV:W_O])
    scaled = grad_normed * gain_two
    grad_after = dout_ref[...].astype(F32) + (
        factor_two * scaled - after * factor_two**3 * jnp.mean(scaled * after, axis=1, keepdims=True)
    )
    grad_gain_two = jnp.sum(grad_normed * after * factor_two, axis=0, keepdims=True)
    grad_branch = (residual_scale * grad_after).astype(BF)
    put(slice(QKVO - D, QKVO), dot_tn(o_ref[...], grad_branch))
    do_ref[...] = dot_nt(grad_branch, w_ref[:, W_O:]).astype(BF)
    grad_router = dot_tn(n2_ref[...], grad_logits)
    yield

    cosines, sines = cos_ref[...], sin_ref[...]
    key_back, value_back = [], []
    for g in range(KVH):
        at = slice(g * LANE, (g + 1) * LANE)
        queries = halves(q_ref[:, at].astype(F32), low).astype(BF)
        outs = halves(do_ref[:, at].astype(F32), low).astype(BF)
        if g + 1 < KVH:
            p_copy(g + 1).start()
        p_copy(g).wait()
        weights = p_ref[g % 2]
        grad_weights = dot_nt(outs, vd_ref[:, at])
        total = jnp.sum(weights * grad_weights, axis=1, keepdims=True)
        grad_scores = (weights * (grad_weights - total)).astype(BF)
        block = dot(grad_scores, kd_ref[:, at])
        block = jnp.where(low, block[:tokens], block[tokens:]) * score_scale
        dqkv_ref[:, at] = (block * cosines - turned(block, lane) * sines).astype(BF)
        block = dot_tn(grad_scores, queries) * score_scale
        key_back.append(block + pltpu.roll(block, HD, 1))
        block = dot_tn(weights.astype(BF), outs)
        value_back.append(block + pltpu.roll(block, HD, 1))
    for m in range(KVH // 2):
        block = jnp.where(low, key_back[2 * m], key_back[2 * m + 1])
        at = slice(H * HD + m * LANE, H * HD + (m + 1) * LANE)
        dqkv_ref[:, at] = (block * cosines - turned(block, lane) * sines).astype(BF)
        at = slice(H * HD + KVH * HD + m * LANE, H * HD + KVH * HD + (m + 1) * LANE)
        dqkv_ref[:, at] = jnp.where(low, value_back[2 * m], value_back[2 * m + 1]).astype(BF)
    yield

    source = x_ref[...].astype(F32)
    factor_one = lax.rsqrt(jnp.mean(source * source, axis=1, keepdims=True) + norm_eps)
    normed = (source * factor_one * gain_one).astype(BF)
    put(slice(0, QKVO - D), dot_tn(normed, dqkv_ref[...]))
    grad_normed = dot_nt(dqkv_ref[...], w_ref[:, :QKV])
    scaled = grad_normed * gain_one
    grad_vector = factor_one * scaled - source * factor_one**3 * jnp.mean(scaled * source, axis=1, keepdims=True)
    gin_ref[...] = grad_after + grad_vector
    grad_gain_one = jnp.sum(grad_normed * source * factor_one, axis=0, keepdims=True)
    gains = jnp.concatenate([grad_gain_one, grad_gain_two, jnp.zeros((6, D), F32)], axis=0).T
    at = lanes_of(D)
    extra = jnp.where(at == E, gains[:, 0:1], jnp.where(at == E + 1, gains[:, 1:2], grad_router))
    put(slice(QKVO, QKVO + LANE), extra)


def add_rows(target, first, second, rows, step):
    def some(i, carry):
        at = pl.ds(pl.multiple_of(i * step, step), step)
        target[at] = (first[at].astype(F32) + second[at].astype(F32)).astype(target.dtype)
        return carry

    lax.fori_loop(0, rows // step, some, 0)


def tail(
    replicas, chips,
    x_ref, dout_ref, cos_ref, sin_ref, q_ref, kd_ref, vd_ref, o_ref, h1_ref, n2_ref, gd_ref, dx_ref,
    w_hbm, ge_hbm, yp_hbm, p_hbm,
    gin_ref, out_ref, gexp_ref, gproj_ref,
    w_ref, p_ref, do_ref, dqkv_ref, gw_ref, gw_core, gw_up, gw_down, y_ref, y_core, y_up, y_down,
    parts_ref, smalls_ref, result_ref, *rest,
):
    bits = replicas.bit_length() - 1
    arrived, rest = rest[:bits], rest[bits:]
    kept, rest = rest[: max(bits - 1, 1)], rest[max(bits - 1, 1) :]
    (load_sem, p_sem, y_load, ge_load, ar_send, ar_recv, y_core_sem, y_up_send, y_up_recv, y_down_send, y_down_recv,
     gw_core_sem, gw_up_send, gw_up_recv, gw_down_send, gw_down_recv,
     part_send, part_recv, small_send, small_recv, result_send, result_recv) = rest
    r, f = lax.axis_index("replica"), lax.axis_index("fsdp")
    z, c = f // 2, f % 2
    mate, above, below = (r, z * 2 + 1 - c), (r, f + 2), (r, f - 2)
    rows, tokens = gw_ref.shape[2], x_ref.shape[0]
    local = ge_hbm.shape[0]
    make = Copies().make

    load_w = pltpu.make_async_copy(w_hbm, w_ref, load_sem.at[0])
    load_y = [pltpu.make_async_copy(yp_hbm.at[k, c], y_ref.at[k], y_load.at[k]) for k in range(chips)]
    peers = [(True, mate), (z > 0, below), (z < chips - 1, above)]
    peers += [(True, ((r + d) % replicas, f)) for d in range(1, replicas)]
    meet(peers, 1 + (replicas - 1) + jnp.where(z > 0, 1, 0) + jnp.where(z < chips - 1, 1, 0))

    def bit_of(b):
        return (r // (1 << b)) % 2

    def partner(b):
        return (r + (1 - 2 * bit_of(b)) * (1 << b), f)

    def halving(e):
        size = ge_hbm.shape[1] // bits
        orders = [[(g + k) % bits for k in range(bits)] for g in range(bits)]
        starts = [[] for _ in range(bits)]
        for g in range(bits):
            at = g * size
            for k in range(bits):
                starts[g].append(at)
                at = at + bit_of(orders[g][k]) * (size >> (k + 1))
            starts[g].append(at)
        copies, loads = {}, {}

        def region(g, k):
            half = size >> (k + 1)
            return pl.ds(pl.multiple_of(starts[g][k + 1], half), half)

        def exchange(g, k):
            half = size >> (k + 1)
            give = (1 - bit_of(orders[g][k])) * half
            if k:
                source = kept[k - 1].at[e * bits + g, pl.ds(pl.multiple_of(give, half), half)]
            else:
                source = ge_hbm.at[e, pl.ds(pl.multiple_of(g * size + give, half), half)]
            copies[g, k] = make(
                source, arrived[k].at[e * bits + g],
                ar_send.at[e * bits + g, k], ar_recv.at[e * bits + g, k], partner(orders[g][k]),
            )
            copies[g, k].start()

        def spread(g, k):
            ref = gexp_ref.at[e, region(g, k)]
            copies[g, bits + k] = make(
                ref, ref, ar_send.at[e * bits + g, bits + k], ar_recv.at[e * bits + g, bits + k], partner(orders[g][k])
            )
            copies[g, bits + k].start()

        for g in range(bits):
            exchange(g, 0)
        for g in range(bits):
            loads[g] = pltpu.make_async_copy(
                ge_hbm.at[e, region(g, 0)], kept[0].at[e * bits + g], ge_load.at[e * bits + g]
            )
            loads[g].start()
        yield
        for k in range(bits):
            half = size >> (k + 1)
            for g in range(bits):
                if k == 0:
                    loads[g].wait()
                copies[g, k].wait_recv()
                job = e * bits + g
                own = kept[max(k - 1, 0)].at[job]
                if k:
                    own = own.at[pl.ds(pl.multiple_of(bit_of(orders[g][k]) * half, half), half)]
                into = kept[k].at[job] if k < bits - 1 else gexp_ref.at[e, region(g, k)]
                add_rows(into, own, arrived[k].at[job], half, min(half, 64))
                if k < bits - 1:
                    exchange(g, k + 1)
                else:
                    spread(g, k)
            yield
        for k in range(bits - 1, -1, -1):
            for g in range(bits):
                copies[g, bits + k].wait_recv()
                if k > 0:
                    spread(g, k - 1)
            yield
        for copy in copies.values():
            copy.wait_send()

    def line(for_mate, core_ref, own, ready, up_ref, down_ref, core_sem, up_send, up_recv, down_send, down_recv, step):
        size = core_ref.shape[1]
        crossing = make(for_mate, core_ref, core_sem.at[0], core_sem.at[1], mate)
        crossing.start()
        yield
        crossing.wait_recv()

        def add_block(block, other):
            add_rows(own(block), own(block), other.at[block], size, step)

        def send(block, up):
            there, send_sem, recv_sem = (up_ref, up_send, up_recv) if up else (down_ref, down_send, down_recv)
            return make(own(block), there.at[block], send_sem.at[block], recv_sem.at[block], above if up else below)

        ready()
        nearby = [k for pair in zip(range(chips - 1, -1, -1), range(chips)) for k in pair][:chips]
        for k in nearby:
            add_block(k, core_ref)

            @pl.when((z == 0) & (k > 0))
            def _():
                send(k, True).start()

            @pl.when((z == chips - 1) & (k < chips - 1))
            def _():
                send(k, False).start()

        yield
        for k in range(chips - 2):
            owner = chips - 1 - k

            @pl.when((z > 0) & (z < owner))
            def _():
                send(owner, True).wait_recv()
                add_block(owner, up_ref)
                send(owner, True).start()

            @pl.when((z < chips - 1) & (z > k))
            def _():
                send(k, False).wait_recv()
                add_block(k, down_ref)
                send(k, False).start()

            yield

        @pl.when(z > 0)
        def _():
            send(z, True).wait_recv()
            add_block(z, up_ref)

        @pl.when(z < chips - 1)
        def _():
            send(z, False).wait_recv()
            add_block(z, down_ref)

        crossing.wait_send()
        for k in range(chips):

            @pl.when(z < k)
            def _():
                send(k, True).wait_send()

            @pl.when(z > k)
            def _():
                send(k, False).wait_send()

    def mixture():
        yield from line(
            yp_hbm.at[:, 1 - c], y_core, lambda k: y_ref.at[k], lambda: [copy.wait() for copy in load_y], y_up, y_down,
            y_core_sem, y_up_send, y_up_recv, y_down_send, y_down_recv, 32,
        )
        out_ref[...] = (h1_ref[...] + residual_scale * y_ref[z].astype(F32)).astype(BF)

    def projection():
        yield from line(
            gw_ref.at[:, 1 - c], gw_core, lambda k: gw_ref.at[k, c], lambda: None, gw_up, gw_down,
            gw_core_sem, gw_up_send, gw_up_recv, gw_down_send, gw_down_recv, 16,
        )
        wide = QKVO // replicas

        def columns(part):
            return pl.ds(pl.multiple_of(part * wide, LANE), wide)

        own = gw_ref.at[z, c]

        def part_copy(d):
            to = (r + d) % replicas
            return make(own.at[:, columns(to)], parts_ref.at[r], part_send.at[d], part_recv.at[r], (to, f))

        def small_copy(d):
            to = (r + d) % replicas
            return make(own.at[:, pl.ds(QKVO, LANE)], smalls_ref.at[r], small_send.at[d], small_recv.at[r], (to, f))

        for d in range(1, replicas):
            part_copy(d).start()
            small_copy(d).start()
        parts_ref[r] = own[:, columns(r)]
        smalls_ref[r] = own[:, pl.ds(QKVO, LANE)]
        yield
        for d in range(1, replicas):
            peer = (r + d) % replicas
            make(parts_ref.at[peer], parts_ref.at[peer], part_send.at[d], part_recv.at[peer], (peer, f)).wait_recv()
            make(smalls_ref.at[peer], smalls_ref.at[peer], small_send.at[d], small_recv.at[peer], (peer, f)).wait_recv()
        total = parts_ref[0].astype(F32)
        small = smalls_ref[0].astype(F32)
        for k in range(1, replicas):
            total = total + parts_ref[k].astype(F32)
            small = small + smalls_ref[k].astype(F32)
        result_ref[r] = total.astype(BF)
        gproj_ref[:, QKVO:] = small

        def result_copy(d):
            to = (r + d) % replicas
            return make(result_ref.at[r], result_ref.at[r], result_send.at[d], result_recv.at[r], (to, f))

        for d in range(1, replicas):
            result_copy(d).start()
        yield
        for d in range(1, replicas):
            peer = (r + d) % replicas
            make(result_ref.at[peer], result_ref.at[peer], result_send.at[d], result_recv.at[peer], (peer, f)).wait_recv()
        for k in range(replicas):
            gproj_ref[:, k * wide : (k + 1) * wide] = result_ref[k].astype(F32)
        for d in range(1, replicas):
            part_copy(d).wait_send()
            small_copy(d).wait_send()
            result_copy(d).wait_send()

    sums = [halving(e) for e in range(local)] if bits else []
    first, last = sums[:1], sums[1:]
    moe, grads = [mixture()], [projection()]

    def go(*turns):
        for turn in turns:
            for process in turn:
                next(process, None)

    go(sums, moe)
    load_w.start()
    for copy in load_y:
        copy.start()
    if not bits:
        pltpu.sync_copy(ge_hbm, gexp_ref)
    load_w.wait()
    backward = attention_backward(
        x_ref, dout_ref, cos_ref, sin_ref, w_ref, q_ref, kd_ref, vd_ref, p_hbm, o_ref, h1_ref, n2_ref, gd_ref, dx_ref,
        gin_ref, gw_ref, do_ref, dqkv_ref, p_ref, p_sem,
    )
    next(backward)
    go(moe)
    next(backward)
    go(first, moe)
    next(backward, None)
    go(grads, moe, grads, last, first, moe, last, first, grads, last, grads, first, grads, last, grads, grads)
    go(*[moe + grads + sums] * (2 * chips + 2 * bits + 4))


def finish(gexp_ref, gproj_ref, gin_ref, out_ref, *outs):
    layer, grad_in, gains_one, query, key, value, output, gains_two, router, expert = outs
    expert[...] = gexp_ref[...].astype(F32)

    @pl.when(pl.program_id(0) == 0)
    def _():
        layer[...] = out_ref[...]
        grad_in[...] = gin_ref[...]
        a, b, c = H * HD, H * HD + KVH * HD, QKV
        query[...] = gproj_ref[:, :a]
        key[...] = gproj_ref[:, a:b]
        value[...] = gproj_ref[:, b:c]
        output[...] = gproj_ref[:, c:QKVO]
        small = gproj_ref[:, QKVO:].T
        router[...] = small[:E]
        gains_one[...] = small[E : E + 1]
        gains_two[...] = small[E + 1 : E + 2]


def call(kernel, out_shape, args, scratch=(), outside=0, out_outside=0, **params):
    spaces = [pltpu.SMEM if a.dtype == jnp.int32 and a.size <= 16 else pltpu.VMEM for a in args]
    spaces[len(args) - outside :] = [pl.ANY] * outside
    return pl.pallas_call(
        kernel,
        out_shape=out_shape,
        in_specs=[pl.BlockSpec(memory_space=space) for space in spaces],
        out_specs=[
            pl.BlockSpec(memory_space=pltpu.VMEM if i < len(out_shape) - out_outside else pl.ANY)
            for i in range(len(out_shape))
        ],
        scratch_shapes=list(scratch),
        compiler_params=pltpu.CompilerParams(
            vmem_limit_bytes=VMEM_LIMIT, has_side_effects="collective_id" in params, **params
        ),
    )(*args)


def shape(dims, dtype):
    return jax.ShapeDtypeStruct(dims, dtype)


def make_body(mesh):
    group, replicas = mesh.shape["fsdp"], mesh.shape["replica"]
    local = E // group

    def body(
        hidden_in, seq_lengths, routes, norm1_gain, w_query, w_key, w_value, w_output, norm2_gain, w_router,
        expert_weights, out_cotangent,
    ):
        tokens = hidden_in.shape[0]
        rows = w_query.shape[0]
        chips = group // 2
        dma = pltpu.SemaphoreType.DMA
        weights, q, kd, vd, o, h1, n2, gd, gt, cosines, sines, p, dout_all = call(
            functools.partial(front, replicas, chips),
            (
                shape((chips, 2, rows, W_O + D), BF), shape((tokens, D), BF), shape((tokens, D), BF),
                shape((tokens, D), BF), shape((tokens, D), BF), shape((tokens, D), F32), shape((tokens, D), BF),
                shape((tokens, LANE), F32), shape((E, tokens), F32), shape((tokens, LANE), F32),
                shape((tokens, LANE), F32), shape((KVH, 2 * tokens, tokens), F32), shape((chips, 2, tokens, D), BF),
            ),
            (
                hidden_in, seq_lengths, routes.T, rope_table(tokens), w_query, w_key, w_value, w_output, w_router.T,
                norm1_gain[None], norm2_gain[None], out_cotangent,
            ),
            [
                pltpu.VMEM((2, 2 * tokens, tokens), F32), dma((2,)), dma((1,)), dma((3, chips)), dma((3, chips)),
                dma((3, chips)), dma((3, chips, replicas)), dma((3, chips, replicas)), dma((2, chips)),
                dma((2, chips)), dma((3, chips)), dma((chips, 2)),
            ],
            out_outside=2,
            collective_id=2,
        )
        weights = weights.reshape(D, W_O + D)
        anywhere = pl.BlockSpec(memory_space=pl.ANY)
        inside = pl.BlockSpec(memory_space=pltpu.VMEM)
        wide = D + LANE
        dx, yp, grad_experts = pl.pallas_call(
            functools.partial(middle, chips),
            in_specs=[inside, inside, anywhere, anywhere],
            out_specs=[inside, anywhere, inside],
            out_shape=[
                shape((tokens, wide), F32), shape((chips, 2, tokens, D), BF), shape((local, 3 * FF, D), BF),
            ],
            scratch_shapes=[
                pltpu.VMEM((chips, 2, tokens, D), BF), pltpu.VMEM((chips, 2, E, tokens), F32),
                pltpu.VMEM((2, 2, tokens, D), BF), pltpu.VMEM((local, 3 * FF, D), BF),
                pltpu.VMEM((local, group * CAP, D), BF), pltpu.VMEM((local, group * CAP, D), BF),
                pltpu.VMEM((local, group * CAP, D), BF), pltpu.VMEM((local, group * CAP, FF), BF),
                pltpu.VMEM((2, 2, tokens, wide), BF), pltpu.VMEM((2, 2, tokens, D), BF),
                pltpu.VMEM((chips, tokens, wide), BF), pltpu.VMEM((chips, tokens, wide), BF),
            ]
            + ([dma((chips,))] * 3 + [dma((chips, 2))]) * 2 + [dma((chips,))] * 4 + [dma((2,)), dma((2,)), dma((1,))],
            compiler_params=pltpu.CompilerParams(vmem_limit_bytes=VMEM_LIMIT, has_side_effects=True, collective_id=1),
        )(n2, gt, dout_all, expert_weights)
        bits = replicas.bit_length() - 1
        size = 3 * FF // bits if bits else 0
        width = QKVO + LANE
        grad_in, layer_out, grad_experts, gw = call(
            functools.partial(tail, replicas, chips),
            (
                shape((tokens, D), F32), shape((tokens, D), BF), shape((local, 3 * FF, D), BF), shape((rows, width), F32),
            ),
            (hidden_in, out_cotangent, cosines, sines, q, kd, vd, o, h1, n2, gd, dx, weights, grad_experts, yp, p),
            [
                pltpu.VMEM((D, W_O + D), BF), pltpu.VMEM((2, 2 * tokens, tokens), F32), pltpu.VMEM((tokens, D), BF),
                pltpu.VMEM((tokens, QKV), BF), pltpu.VMEM((chips, 2, rows, width), BF),
            ]
            + [pltpu.VMEM((chips, rows, width), BF)] * 3 + [pltpu.VMEM((chips, tokens, D), BF)] * 4
            + [
                pltpu.VMEM((replicas, rows, QKVO // replicas), BF), pltpu.VMEM((replicas, rows, LANE), BF),
                pltpu.VMEM((replicas, rows, QKVO // replicas), BF),
            ]
            + [pltpu.VMEM((local * bits, size >> (k + 1), D), BF) for k in range(bits)]
            + [pltpu.VMEM((max(local * bits, 1), max(size >> (k + 1), 16), D), BF) for k in range(max(bits - 1, 1))]
            + [dma((1,)), dma((2,)), dma((chips,)), dma((max(local * bits, 1),))]
            + [dma((max(local * bits, 1), max(2 * bits, 1)))] * 2
            + ([dma((2,))] + [dma((chips,))] * 4) * 2 + [dma((replicas,))] * 6,
            outside=4,
            collective_id=0,
        )
        steps = 8
        block = local * 3 * FF // steps
        fixed = [
            shape((tokens, D), BF), shape((tokens, D), F32), shape((1, rows), F32), shape((rows, H * HD), F32),
            shape((rows, KVH * HD), F32), shape((rows, KVH * HD), F32), shape((rows, D), F32), shape((1, rows), F32),
            shape((E, rows), F32),
        ]

        def still(a):
            return pl.BlockSpec(a.shape, lambda i: (0, 0))

        expert_block = pl.BlockSpec((block, D), lambda i: (i, 0))
        outs = pl.pallas_call(
            finish,
            grid=(steps,),
            in_specs=[expert_block, still(gw), still(grad_in), still(layer_out)],
            out_specs=[still(a) for a in fixed] + [expert_block],
            out_shape=fixed + [shape((local * 3 * FF, D), F32)],
            compiler_params=pltpu.CompilerParams(vmem_limit_bytes=32 * 2**20),
        )(grad_experts.reshape(local * 3 * FF, D), gw, grad_in, layer_out)
        return (
            outs[0], outs[1], outs[2][0], outs[3], outs[4], outs[5], outs[6], outs[7][0], outs[8].T,
            outs[9].reshape(local, 3 * FF, D),
        )

    return body


def solution(mesh):
    tokens, weights = P(("replica", "fsdp"), None), P("fsdp", None)
    return jax.shard_map(
        make_body(mesh),
        mesh=mesh,
        in_specs=(
            tokens, tokens, tokens, P("fsdp"), weights, weights, weights, weights, P("fsdp"), weights,
            P("fsdp", None, None), tokens,
        ),
        out_specs=(
            tokens, tokens, P("fsdp"), weights, weights, weights, weights, P("fsdp"), weights, P("fsdp", None, None),
        ),
        check_vma=False,
    )
```

```python
import functools

import jax
import jax.numpy as jnp
import numpy as np
from jax import lax
from jax.experimental import pallas as pl
from jax.experimental.pallas import tpu as pltpu
from jax.sharding import PartitionSpec as P

D = 1024
H = 16
KVH = 8
HD = 64
FF = 512
TOPK = 8
E = 16
CAP = 144
LANE = 128
QKV = H * HD + 2 * KVH * HD
QKVO = QKV + D
W_O = QKV + LANE

norm_eps = 1e-06
score_scale = 0.015625
residual_scale = 0.22
rope_base = 10000.0
masked_score = -1e30

BF = jnp.bfloat16
F32 = jnp.float32
VMEM_LIMIT = 63 * 2**20


def dot(a, b):
    return lax.dot_general(a, b, (((1,), (0,)), ((), ())), preferred_element_type=F32)


def dot_nt(a, b):
    return lax.dot_general(a, b, (((1,), (1,)), ((), ())), preferred_element_type=F32)


def dot_tn(a, b):
    return lax.dot_general(a, b, (((0,), (0,)), ((), ())), preferred_element_type=F32)


def lanes_of(rows):
    return lax.broadcasted_iota(jnp.int32, (rows, LANE), 1)


def turned(block, lane):
    return jnp.where(lane % HD < HD // 2, pltpu.roll(block, LANE - HD // 2, 1), pltpu.roll(block, HD // 2, 1))


def halves(block, low):
    zero = jnp.zeros_like(block)
    return jnp.concatenate([jnp.where(low, block, zero), jnp.where(low, zero, block)], axis=0)


def rope_table(tokens):
    frequency = np.float32(rope_base) ** (-np.arange(0, HD, 2, dtype=np.float32) / np.float32(HD))
    frequency = np.tile(frequency.astype(np.float32), LANE // (HD // 2))
    angles = (np.arange(tokens, dtype=np.float32)[:, None] * frequency[None, :]).astype(np.float64)
    sign = np.where(np.arange(LANE) % HD < HD // 2, -1.0, 1.0)
    pieces = []
    for values in (np.cos(angles), np.sin(angles) * sign[None, :]):
        rest = values.astype(np.float32)
        for _ in range(3):
            piece = rest.astype(BF)
            pieces.append(piece)
            rest = rest - piece.astype(np.float32)
    return np.concatenate(pieces, axis=1)


class Copies:
    def make(self, src, dst, send, recv, device):
        return pltpu.make_async_remote_copy(
            src_ref=src, dst_ref=dst, send_sem=send, recv_sem=recv, device_id=device, device_id_type=pl.DeviceIdType.MESH
        )


def meet(devices, expected):
    barrier = pltpu.get_barrier_semaphore()
    for condition, device in devices:

        def signal(device=device):
            pl.semaphore_signal(barrier, inc=1, device_id=device, device_id_type=pl.DeviceIdType.MESH)

        if condition is True:
            signal()
        else:
            pl.when(condition)(signal)
    pl.semaphore_wait(barrier, expected)


def front(
    replicas, chips,
    x_ref, len_ref, routes_ref, table_ref, wq_ref, wk_ref, wv_ref, wo_ref, wr_ref, g1_ref, g2_ref, dout_ref,
    w_all, q_ref, kd_ref, vd_ref, o_ref, h1_ref, n2_ref, gd_ref, gt_ref, cos_ref, sin_ref, p_hbm, do_all,
    p_ref, p_sem, own_sem, z_up, z_down, z_recv, xy_send, xy_recv, mate_send, mate_recv, do_send, do_recv,
):
    tokens = x_ref.shape[0]
    r, f = lax.axis_index("replica"), lax.axis_index("fsdp")
    z, c = f // 2, f % 2
    mate, above, below = (r, z * 2 + 1 - c), (r, f + 2), (r, f - 2)
    make = Copies().make
    peers = [(True, mate), (z > 0, below), (z < chips - 1, above)]
    peers += [(True, ((r + d) % replicas, f)) for d in range(1, replicas)]

    own_dout = pltpu.make_async_copy(dout_ref, do_all.at[z, c], own_sem.at[0])
    own_dout.start()
    rows = wq_ref.shape[0]
    packed = [wr_ref[...].astype(F32), g1_ref[...].astype(F32), g2_ref[...].astype(F32)]
    packed = jnp.concatenate(packed + [jnp.zeros((LANE - E - 2, rows), F32)], axis=0)
    own = w_all.at[z, c]
    own[:, : H * HD] = wq_ref[...]
    own[:, H * HD : H * HD + KVH * HD] = wk_ref[...]
    own[:, H * HD + KVH * HD : QKV] = wv_ref[...]
    own[:, QKV:W_O] = packed.T.astype(BF)
    own[:, W_O:] = wo_ref[...]
    meet(peers, 1 + (replicas - 1) + jnp.where(z > 0, 1, 0) + jnp.where(z < chips - 1, 1, 0))

    def part(kind):
        if kind == 0:
            return pl.ds(pl.multiple_of(r * (QKV // replicas), LANE), QKV // replicas)
        if kind == 1:
            return pl.ds(QKV, LANE)
        return pl.ds(pl.multiple_of(W_O + r * (D // replicas), LANE), D // replicas)

    def along(zb, kind, up):
        ref = w_all.at[zb, c, :, part(kind)]
        return make(ref, ref, (z_up if up else z_down).at[kind, zb], z_recv.at[kind, zb], above if up else below)

    def across(zb, kind, d):
        ref = w_all.at[zb, c, :, part(kind)]
        return make(ref, ref, xy_send.at[kind, zb, d], xy_recv.at[kind, zb, r], ((r + d) % replicas, f))

    def wait_across(zb, kind):
        for d in range(1, replicas):
            peer = (r + d) % replicas
            ref = w_all.at[zb, c, :, part(kind)]
            make(ref, ref, xy_send.at[kind, zb, d], xy_recv.at[kind, zb, peer], (peer, f)).wait_recv()

    def to_mate(zb, core, late):
        ref = w_all.at[zb, core, :, pl.ds(W_O, D) if late else pl.ds(0, W_O)]
        return make(ref, ref, mate_send.at[late, zb], mate_recv.at[late, zb], mate)

    def dout_copy(zb, core, way):
        source = do_all.at[zb, core]
        return make(source, do_all.at[zb, core], do_send.at[way, zb], do_recv.at[zb, core], (above, below, mate)[way])

    def both_sides(k, act):
        @pl.when(z >= k)
        def _():
            act(z - k, True)

        @pl.when(z < chips - k)
        def _():
            act(z + k, False)

    def onward(up):
        return z < chips - 1 if up else z > 0

    for kind in range(3):
        both_sides(1, lambda zb, low: along(z, kind, not low).start())
    for late in range(2):
        to_mate(z, c, late).start()

    source = x_ref[...].astype(F32)
    factor = lax.rsqrt(jnp.mean(source * source, axis=1, keepdims=True) + norm_eps)
    lane = lanes_of(tokens)
    low_lane = lane < HD
    row = lax.broadcasted_iota(jnp.int32, (tokens, tokens), 0)
    column = lax.broadcasted_iota(jnp.int32, (tokens, tokens), 1)
    row_at = lax.broadcasted_iota(jnp.int32, (tokens, 1), 0)
    column_at = lax.broadcasted_iota(jnp.int32, (1, tokens), 1)
    row_segment = jnp.zeros((tokens, 1), jnp.int32)
    row_start = jnp.zeros((tokens, 1), jnp.int32)
    column_segment = jnp.zeros((1, tokens), jnp.int32)
    end = jnp.int32(0)
    for j in range(len_ref.shape[1]):
        end = end + len_ref[0, j]
        row_segment += (row_at >= end).astype(jnp.int32)
        row_start = jnp.maximum(row_start, jnp.where(row_at >= end, end, 0))
        column_segment += (column_at >= end).astype(jnp.int32)
    place = (column == row - row_start).astype(F32).astype(BF)
    found = dot(place, table_ref[...])
    found = [found[:, i * LANE : (i + 1) * LANE] for i in range(6)]
    cosines, sines = found[0] + found[1] + found[2], found[3] + found[4] + found[5]
    cos_ref[...] = cosines
    sin_ref[...] = sines

    own_dout.wait()
    for k in range(1, chips):
        for kind in range(3):

            def arrive(zb, low, kind=kind):
                along(zb, kind, low).wait_recv()

                @pl.when(onward(low))
                def _():
                    along(zb, kind, low).start()

                if kind != 1:
                    for d in range(1, replicas):
                        across(zb, kind, d).start()

            both_sides(k, arrive)
        if k == 1:
            both_sides(1, lambda zb, low: dout_copy(z, c, 1 if low else 0).start())
            dout_copy(z, c, 2).start()

    def share(k, late):
        def act(zb, low):
            wait_across(zb, 2 if late else 0)
            to_mate(zb, c, late).start()

        both_sides(k, act)

    def dout_arrive(zb, low):
        dout_copy(zb, c, 0 if low else 1).wait_recv()

        @pl.when(onward(low))
        def _():
            dout_copy(zb, c, 0 if low else 1).start()

        dout_copy(zb, c, 2).start()

    for k in range(1, chips):
        share(k, 0)
    if chips > 1:
        both_sides(1, dout_arrive)
    for k in range(chips):
        to_mate(k, 1 - c, 0).wait_recv()

    def columns(start, size):
        return w_all[:, :, :, start : start + size].reshape(D, size)

    small = columns(QKV, LANE)
    gains = small.astype(F32).T
    gain_one, gain_two = gains[E : E + 1], gains[E + 1 : E + 2]
    normed = (source * factor * gain_one).astype(BF)
    q_all = dot(normed, columns(0, H * HD))
    for g in range(H // 2):
        at = slice(g * LANE, (g + 1) * LANE)
        block = q_all[:, at]
        q_ref[:, at] = (block * cosines + turned(block, lane) * sines).astype(BF)
    kv = dot(normed, columns(H * HD, 2 * KVH * HD))
    for m in range(KVH // 2):
        block = kv[:, m * LANE : (m + 1) * LANE]
        block = block * cosines + turned(block, lane) * sines
        other = pltpu.roll(block, HD, 1)
        kd_ref[:, 2 * m * LANE : (2 * m + 1) * LANE] = jnp.where(low_lane, block, other).astype(BF)
        kd_ref[:, (2 * m + 1) * LANE : (2 * m + 2) * LANE] = jnp.where(low_lane, other, block).astype(BF)
        block = kv[:, KVH * HD + m * LANE : KVH * HD + (m + 1) * LANE]
        other = pltpu.roll(block, HD, 1)
        vd_ref[:, 2 * m * LANE : (2 * m + 1) * LANE] = jnp.where(low_lane, block, other).astype(BF)
        vd_ref[:, (2 * m + 1) * LANE : (2 * m + 2) * LANE] = jnp.where(low_lane, other, block).astype(BF)
    bias = jnp.where((row_segment == column_segment) & (column <= row), 0.0, masked_score)
    bias = jnp.concatenate([bias, bias], axis=0)

    def p_copy(g):
        return pltpu.make_async_copy(p_ref.at[g % 2], p_hbm.at[g], p_sem.at[g % 2])

    for g in range(KVH):
        at = slice(g * LANE, (g + 1) * LANE)
        queries = halves(q_ref[:, at].astype(F32), low_lane).astype(BF)
        scores = dot_nt(queries, kd_ref[:, at]) * score_scale + bias
        shifted = jnp.exp(scores - jnp.max(scores, axis=1, keepdims=True))
        weights = shifted * (1.0 / jnp.sum(shifted, axis=1, keepdims=True))
        if g >= 2:
            p_copy(g - 2).wait()
        p_ref[g % 2] = weights
        p_copy(g).start()
        mixed = dot(weights.astype(BF), vd_ref[:, at])
        o_ref[:, at] = jnp.where(low_lane, mixed[:tokens], mixed[tokens:]).astype(BF)

    if chips > 2:
        both_sides(2, dout_arrive)
    for k in range(1, chips):
        share(k, 1)

    for k in range(chips):
        to_mate(k, 1 - c, 1).wait_recv()
    after = source + residual_scale * dot(o_ref[...], columns(W_O, D))
    h1_ref[...] = after
    factor = lax.rsqrt(jnp.mean(after * after, axis=1, keepdims=True) + norm_eps)
    normed = (after * factor * gain_two).astype(BF)
    n2_ref[...] = normed
    logits = dot(normed, small).T[:E]
    expert = lax.broadcasted_iota(jnp.int32, (E, tokens), 0)
    routed = routes_ref[0:1] == expert
    for j in range(1, TOPK):
        routed |= routes_ref[j : j + 1] == expert
    top = jnp.max(jnp.where(routed, logits, masked_score), axis=0, keepdims=True)
    powers = jnp.where(routed, jnp.exp(logits - top), 0.0)
    gates = powers / jnp.sum(powers, axis=0, keepdims=True)
    gates = jnp.where(routed, gates, -1.0)
    gt_ref[...] = gates
    gd_ref[...] = jnp.concatenate([gates, jnp.full((LANE - E, tokens), -1.0, F32)], axis=0).T

    for k in range(3, chips):
        both_sides(k, dout_arrive)
    for k in range(chips):
        dout_copy(k, 1 - c, 2).wait_recv()
    for g in (KVH - 2, KVH - 1):
        p_copy(g).wait()
    for k in range(chips):
        for late in range(2):
            to_mate(k, c, late).wait_send()
        dout_copy(k, c, 2).wait_send()

        @pl.when((z >= k) & (z < chips - 1))
        def _():
            dout_copy(k, c, 0).wait_send()
            for kind in range(3):
                along(k, kind, True).wait_send()

        @pl.when((z <= k) & (z > 0))
        def _():
            dout_copy(k, c, 1).wait_send()
            for kind in range(3):
                along(k, kind, False).wait_send()

        @pl.when(z != k)
        def _():
            for d in range(1, replicas):
                for kind in (0, 2):
                    across(k, kind, d).wait_send()


def attention_backward(
    x_ref, dout_ref, cos_ref, sin_ref, w_ref, q_ref, kd_ref, vd_ref, p_hbm, o_ref, h1_ref, n2_ref, gd_ref, dx_ref, dgate,
    gin_ref, gw_ref, do_ref, dqkv_ref, p_ref, p_sem,
):
    tokens = x_ref.shape[0]
    lane = lanes_of(tokens)
    low = lane < HD

    def p_copy(g):
        return pltpu.make_async_copy(p_hbm.at[g], p_ref.at[g % 2], p_sem.at[g % 2])

    p_copy(0).start()

    def put(at, value):
        gw_ref[:, :, :, at] = value.astype(BF).reshape(*gw_ref.shape[:3], value.shape[1])

    small = w_ref[:, QKV:W_O].astype(F32).T
    gain_one, gain_two = small[E : E + 1], small[E + 1 : E + 2]
    after = h1_ref[...]
    factor_two = lax.rsqrt(jnp.mean(after * after, axis=1, keepdims=True) + norm_eps)
    gates = jnp.maximum(gd_ref[...], 0.0)
    grad_gates = dgate()
    chosen = gates * (grad_gates - jnp.sum(gates * grad_gates, axis=1, keepdims=True))
    grad_logits = chosen.astype(BF)
    grad_normed = dx_ref[...] + dot_nt(grad_logits, w_ref[:, QKV:W_O])
    scaled = grad_normed * gain_two
    grad_after = dout_ref[...].astype(F32) + (
        factor_two * scaled - after * factor_two**3 * jnp.mean(scaled * after, axis=1, keepdims=True)
    )
    grad_gain_two = jnp.sum(grad_normed * after * factor_two, axis=0, keepdims=True)
    grad_branch = (residual_scale * grad_after).astype(BF)
    put(slice(QKVO - D, QKVO), dot_tn(o_ref[...], grad_branch))
    do_ref[...] = dot_nt(grad_branch, w_ref[:, W_O:]).astype(BF)
    grad_router = dot_tn(n2_ref[...], grad_logits)
    yield

    cosines, sines = cos_ref[...], sin_ref[...]
    key_back, value_back = [], []
    for g in range(KVH):
        at = slice(g * LANE, (g + 1) * LANE)
        queries = halves(q_ref[:, at].astype(F32), low).astype(BF)
        outs = halves(do_ref[:, at].astype(F32), low).astype(BF)
        if g + 1 < KVH:
            p_copy(g + 1).start()
        p_copy(g).wait()
        weights = p_ref[g % 2]
        grad_weights = dot_nt(outs, vd_ref[:, at])
        total = jnp.sum(weights * grad_weights, axis=1, keepdims=True)
        grad_scores = (weights * (grad_weights - total)).astype(BF)
        block = dot(grad_scores, kd_ref[:, at])
        block = jnp.where(low, block[:tokens], block[tokens:]) * score_scale
        dqkv_ref[:, at] = (block * cosines - turned(block, lane) * sines).astype(BF)
        block = dot_tn(grad_scores, queries) * score_scale
        key_back.append(block + pltpu.roll(block, HD, 1))
        block = dot_tn(weights.astype(BF), outs)
        value_back.append(block + pltpu.roll(block, HD, 1))
    for m in range(KVH // 2):
        block = jnp.where(low, key_back[2 * m], key_back[2 * m + 1])
        at = slice(H * HD + m * LANE, H * HD + (m + 1) * LANE)
        dqkv_ref[:, at] = (block * cosines - turned(block, lane) * sines).astype(BF)
        at = slice(H * HD + KVH * HD + m * LANE, H * HD + KVH * HD + (m + 1) * LANE)
        dqkv_ref[:, at] = jnp.where(low, value_back[2 * m], value_back[2 * m + 1]).astype(BF)
    yield

    source = x_ref[...].astype(F32)
    factor_one = lax.rsqrt(jnp.mean(source * source, axis=1, keepdims=True) + norm_eps)
    normed = (source * factor_one * gain_one).astype(BF)
    put(slice(0, QKVO - D), dot_tn(normed, dqkv_ref[...]))
    grad_normed = dot_nt(dqkv_ref[...], w_ref[:, :QKV])
    scaled = grad_normed * gain_one
    grad_vector = factor_one * scaled - source * factor_one**3 * jnp.mean(scaled * source, axis=1, keepdims=True)
    gin_ref[...] = grad_after + grad_vector
    grad_gain_one = jnp.sum(grad_normed * source * factor_one, axis=0, keepdims=True)
    gains = jnp.concatenate([grad_gain_one, grad_gain_two, jnp.zeros((6, D), F32)], axis=0).T
    at = lanes_of(D)
    extra = jnp.where(at == E, gains[:, 0:1], jnp.where(at == E + 1, gains[:, 1:2], grad_router))
    put(slice(QKVO, QKVO + LANE), extra)


def add_rows(target, first, second, rows, step):
    def some(i, carry):
        at = pl.ds(pl.multiple_of(i * step, step), step)
        target[at] = (first[at].astype(F32) + second[at].astype(F32)).astype(target.dtype)
        return carry

    lax.fori_loop(0, rows // step, some, 0)


def back(
    replicas, chips,
    x_ref, dout_ref, cos_ref, sin_ref, h1_ref, n2_ref, gd_ref, gt_ref,
    do_hbm, we_hbm, w_hbm, q_hbm, kd_hbm, vd_hbm, o_hbm, p_hbm,
    gin_ref, out_ref, result_ref, total_ref, ge_hbm, y_core, y_up, y_down, gw_up, gw_down, *rest,
):
    bits = replicas.bit_length() - 1
    roomy = chips <= 4
    arrived, rest = rest[:bits], rest[bits:]
    if not roomy:
        core_ref, from_ref, rest = rest[0], rest[1], rest[2:]
    (ge_ref, n2_all, gt_all, via_ref, pair_ref, dx_ref, dgt_ref, dgt_all, y_ref, gw_core, parts_ref, smalls_ref), rest = rest[:12], rest[12:]
    if roomy:
        core_ref, from_ref, rest = rest[0], rest[1], rest[2:]
    (n2_up, n2_down, n2_mate, n2_recv, gt_up, gt_down, gt_mate, gt_recv,
     core_send, core_recv, far_send, far_recv, pair_send, via_recv, dgt_send, dgt_recv, yc_send, yc_recv,
     do_sem, we_sem, load_sem, stage_sem, ge_sem, p_sem, ar_send, ar_recv, ar_free,
     y_up_send, y_up_recv, y_down_send, y_down_recv, gw_core_sem, gw_up_send, gw_up_recv, gw_down_send, gw_down_recv,
     part_send, part_recv, small_send, small_recv, result_send, result_recv) = rest
    local, tokens, rows = ge_ref.shape[0], x_ref.shape[0], gw_core.shape[1]
    r, f = lax.axis_index("replica"), lax.axis_index("fsdp")
    z, c = f // 2, f % 2
    mate, above, below = (r, z * 2 + 1 - c), (r, f + 2), (r, f - 2)
    make = Copies().make

    load_experts = pltpu.make_async_copy(we_hbm, ge_ref, we_sem.at[0])
    load_experts.start()
    n2_all[z, c] = n2_ref[...]
    gt_all[z, c] = gt_ref[...]
    peers = [(True, mate)]
    for k in range(1, chips):
        to = (z + k) % chips
        peers += [(True, (r, to * 2 + c)), (True, (r, to * 2 + 1 - c))]
    peers += [(True, ((r + d) % replicas, f)) for d in range(1, replicas)]
    meet(peers, len(peers))

    def bit_of(b):
        return (r // (1 << b)) % 2

    def partner(b):
        return (r + (1 - 2 * bit_of(b)) * (1 << b), f)

    stages = {}

    def landed(ref, name):
        stage, sem = stages[name]
        if ref.shape != stage.shape:
            stage = stage.at[pl.ds(0, ref.shape[0])]
        copy = pltpu.make_async_copy(ref, stage, sem)
        copy.start()
        copy.wait()
        return stage

    def halving(e):
        size = ge_ref.shape[1] // bits
        orders = [[(g + k) % bits for k in range(bits)] for g in range(bits)]
        starts = [[] for _ in range(bits)]
        for g in range(bits):
            at = g * size
            for k in range(bits):
                starts[g].append(at)
                at = at + bit_of(orders[g][k]) * (size >> (k + 1))
            starts[g].append(at)

        def region(g, k):
            half = size >> (k + 1)
            return ge_ref.at[e, pl.ds(pl.multiple_of(starts[g][k + 1], half), half)]

        def exchange(g, k):
            half, job = size >> (k + 1), e * bits + g
            give = pl.multiple_of(starts[g][k] + (1 - bit_of(orders[g][k])) * half, half)
            return make(
                ge_ref.at[e, pl.ds(give, half)], arrived[k].at[job], ar_send.at[job, k], ar_recv.at[job, k],
                partner(orders[g][k]),
            )

        def spread(g, k):
            job, ref = e * bits + g, region(g, k)
            return make(ref, ref, ar_send.at[job, bits + k], ar_recv.at[job, bits + k], partner(orders[g][k]))

        def spread_once_free(g, k):
            pl.semaphore_wait(ar_free.at[e * bits + g, k], 1)
            spread(g, k).start()

        yield
        for g in range(bits):
            exchange(g, 0).start()
        yield
        for k in range(bits):
            half = size >> (k + 1)
            for g in range(bits):
                job = e * bits + g
                exchange(g, k).wait_recv()
                own = region(g, k)
                add_rows(own, own, landed(arrived[k].at[job], "halves"), half, min(half, 64))
                if k < bits - 1:
                    exchange(g, k + 1).start()
                exchange(g, k).wait_send()
                pl.semaphore_signal(
                    ar_free.at[job, k], inc=1, device_id=partner(orders[g][k]), device_id_type=pl.DeviceIdType.MESH
                )
                if k == bits - 1:
                    spread_once_free(g, k)
            yield
        for k in range(bits - 1, -1, -1):
            for g in range(bits):
                spread(g, k).wait_recv()
                if k > 0:
                    spread_once_free(g, k - 1)
            yield
        for g in range(bits):
            for k in range(bits):
                spread(g, k).wait_send()
        pltpu.make_async_copy(ge_ref.at[e], ge_hbm.at[e], ge_sem.at[e]).start()

    sums = [halving(e) for e in range(local)] if bits else []
    first, last = sums[:1], sums[1:]
    for process in sums:
        next(process)

    def pass_on(zb, how):
        to = {"up": above, "down": below, "mate": mate}[how]
        sems = {"up": (n2_up, gt_up), "down": (n2_down, gt_down), "mate": (n2_mate, gt_mate)}[how]
        return [
            make(ref.at[zb, c], ref.at[zb, c], sem.at[zb], recv.at[zb, c], to)
            for ref, sem, recv in ((gt_all, sems[1], gt_recv), (n2_all, sems[0], n2_recv))
        ]

    def got(zb, core):
        for ref, sem, recv in ((gt_all, gt_mate, gt_recv), (n2_all, n2_mate, n2_recv)):
            make(ref.at[zb, core], ref.at[zb, core], sem.at[zb], recv.at[zb, core], mate).wait_recv()

    def start(copies):
        for copy in copies:
            copy.start()

    @pl.when(z < chips - 1)
    def _():
        start(pass_on(z, "up"))

    @pl.when(z > 0)
    def _():
        start(pass_on(z, "down"))

    start(pass_on(z, "mate"))
    inner = jnp.minimum(z, chips - 1 - z)

    def place(t):
        k = (t + 1) // 2
        near = jnp.where(t % 2 == 1, z - k, z + k)
        return jnp.where(t <= 2 * inner, near, jnp.where(2 * z < chips - 1, t, chips - 1 - t))

    def far(zc):
        return jnp.where(zc > z, zc - z, z - zc)

    def side_of(zc):
        return jnp.where(zc > z, 1, 0)

    def relay(k, low, high):
        @pl.when(low)
        def _():
            got(z - k, c)

            @pl.when(z < chips - 1)
            def _():
                start(pass_on(z - k, "up"))

            start(pass_on(z - k, "mate"))

        @pl.when(high)
        def _():
            got(z + k, c)

            @pl.when(z > 0)
            def _():
                start(pass_on(z + k, "down"))

            start(pass_on(z + k, "mate"))

    def early(t):
        return (t >= 2) & (t % 2 == 0) & (t <= 2 * inner) & (t < chips - 1)

    def pair_copy(side):
        owner = z + 2 * side - 1
        return make(pair_ref.at[side], from_ref.at[z], pair_send.at[side], far_recv.at[z], (r, owner * 2 + c))

    def experts_and_sums(do_buf, xs_ref, dye_ref, dgu_ref, hx_ref, dxp_ref, yps_ref, core_stage):
        stages["core"] = (core_stage, stage_sem.at[0])
        before = lax.broadcasted_iota(jnp.int32, (tokens, tokens), 0) < lax.broadcasted_iota(jnp.int32, (tokens, tokens), 1)
        before = before.astype(F32).astype(BF)
        slot_index = lax.broadcasted_iota(jnp.int32, (CAP, tokens), 0).astype(F32)
        pair = 2 * CAP

        def do_copy(zc, slot):
            return pltpu.make_async_copy(do_hbm.at[zc], do_buf.at[slot], do_sem.at[slot])

        def core_copy(zc, slot, t):
            return make(dxp_ref.at[slot, 1 - c], core_ref.at[zc], core_send.at[t], core_recv.at[zc], mate)

        def y_copy(zc, slot, t):
            return make(yps_ref.at[slot], y_core.at[zc], yc_send.at[t], yc_recv.at[zc], mate)

        def via_copy(zc, slot, t):
            side = side_of(zc)
            return make(
                dxp_ref.at[slot, c], via_ref.at[side], far_send.at[t], via_recv.at[side], (r, (z + 2 * side - 1) * 2 + c)
            )

        def far_copy(zc, slot, t):
            return make(dxp_ref.at[slot, c], from_ref.at[z], far_send.at[t], far_recv.at[z], (r, zc * 2 + c))

        def dgt_copy(zc, core, t):
            return make(dgt_ref.at[t, core], dgt_all.at[f], dgt_send.at[t, core], dgt_recv.at[f], (r, zc * 2 + core))

        def free_slot(t, slot):
            core_copy(z, slot, t).wait_send()
            y_copy(z, slot, t).wait_send()

            @pl.when(far(place(t)) >= 2)
            def _():
                far_copy(z, slot, t).wait_send()

        do_copy(z, 0).start()

        def chunk(t, carry):
            zc = place(t)
            slot = t % 2
            k = far(zc)
            both = (t % 2 == 1) & (t <= 2 * inner)
            single = (t > 2 * inner) & jnp.logical_not(early(t - 1))
            relay(k, both | (single & (zc < z)), both | (single & (zc > z)))
            got(zc, 1 - c)

            @pl.when(t < chips - 1)
            def _():
                do_copy(place(t + 1), 1 - slot).start()

            do_copy(zc, slot).wait()

            @pl.when(t == 0)
            def _():
                load_experts.wait()

            @pl.when(t >= 2)
            def _():
                free_slot(t - 2, slot)

            picks, gates, dms = [], [], []
            at_chip = pl.multiple_of(zc * pair, 16)
            for core in range(2):
                mine = [gt_all[zc, core, pl.ds(f * local + i, 1), :] for i in range(local)]
                mine = jnp.concatenate(mine, axis=0) if local > 1 else mine[0]
                rank = jnp.where(mine >= 0.0, dot((mine >= 0.0).astype(F32).astype(BF), before), -1.0)
                chosen = [slot_index == rank[i : i + 1] for i in range(local)]
                gates.append([jnp.sum(jnp.where(chosen[i], mine[i : i + 1], 0.0), axis=1, keepdims=True) for i in range(local)])
                picks.append([one.astype(F32) for one in chosen])
                pick = jnp.concatenate([one.astype(BF) for one in picks[core]], axis=0)
                taken = dot(pick, n2_all[zc, core]).astype(BF)
                grads = dot(pick, do_buf[slot, core]) * residual_scale
                dms.append(grads)
                at = pl.ds(pl.multiple_of(at_chip + core * CAP, 16), CAP)
                for i in range(local):
                    part = slice(i * CAP, (i + 1) * CAP)
                    xs_ref[i, at] = taken[part]
                    dye_ref[i, at] = (gates[core][i] * grads[part]).astype(BF)
            at = pl.ds(at_chip, pair)
            mades, backs, values = [], [], []
            for i in range(local):
                slots = xs_ref[i, at]
                gate_pre = dot_nt(slots, ge_ref[i, :FF])
                up_pre = dot_nt(slots, ge_ref[i, FF : 2 * FF])
                grad_act = dot_nt(dye_ref[i, at], ge_ref[i, 2 * FF :])
                sigmoid = 1.0 / (1.0 + jnp.exp(-gate_pre))
                silu = gate_pre * sigmoid
                act = (silu * up_pre).astype(BF)
                hx_ref[i, at] = act
                grad_gate = (grad_act * up_pre * (sigmoid * (1.0 + gate_pre * (1.0 - sigmoid)))).astype(BF)
                grad_up = (grad_act * silu).astype(BF)
                dgu_ref[i, at, :FF] = grad_gate
                dgu_ref[i, at, FF:] = grad_up
                backs.append((dot(grad_gate, ge_ref[i, :FF]) + dot(grad_up, ge_ref[i, FF : 2 * FF])).astype(BF))
                made = dot(act, ge_ref[i, 2 * FF :]).astype(BF).astype(F32)
                mades.append(made)
                for core in range(2):
                    part = slice(core * CAP, (core + 1) * CAP)
                    value = jnp.sum(dms[core][i * CAP : (i + 1) * CAP] * made[part], axis=1, keepdims=True)
                    values.append(jnp.sum(picks[core][i] * value, axis=0, keepdims=True))
            for core in range(2):
                pick = jnp.concatenate([one.astype(BF) for one in picks[core]], axis=0)
                part = slice(core * CAP, (core + 1) * CAP)
                sent = jnp.concatenate([backs[i][part] for i in range(local)], axis=0)
                dxp_ref[slot, core] = dot_tn(pick, sent).astype(BF)
                for i in range(local):
                    dgt_ref[t, core, i : i + 1] = values[2 * i + core]
            core_copy(zc, slot, t).start()
            for core in range(2):

                @pl.when((t > 0) | (c != core))
                def _():
                    dgt_copy(zc, core, t).start()

            @pl.when(early(t))
            def _():
                k_next = t // 2 + 1
                relay(k_next, z >= k_next, z + k_next < chips)

            for core in range(2):
                pick = jnp.concatenate([one.astype(BF) for one in picks[core]], axis=0)
                part = slice(core * CAP, (core + 1) * CAP)
                sent = jnp.concatenate([(gates[core][i] * mades[i][part]).astype(BF) for i in range(local)], axis=0)
                mixed = dot_tn(pick, sent).astype(BF)

                @pl.when(c == core)
                def _():
                    y_ref[zc] = mixed

                @pl.when(c != core)
                def _():
                    yps_ref[slot] = mixed

            y_copy(zc, slot, t).start()
            core_copy(zc, slot, t).wait_recv()
            there = core_ref.at[zc] if roomy else landed(core_ref.at[zc], "core")
            own = dxp_ref.at[slot, c]

            @pl.when(k == 0)
            def _():
                dx_ref[...] = own[...].astype(F32) + there[...].astype(F32)

            @pl.when(k == 1)
            def _():
                side = side_of(zc)
                add_rows(pair_ref.at[side], own, there, tokens, 64)

                @pl.when((z == 0) | (z == chips - 1))
                def _():
                    pair_copy(side).start()

            @pl.when(k >= 2)
            def _():
                add_rows(own, own, there, tokens, 64)

                @pl.when(k == 2)
                def _():
                    via_copy(zc, slot, t).start()

                @pl.when(k > 2)
                def _():
                    far_copy(zc, slot, t).start()

            return carry

        lax.fori_loop(0, chips, chunk, 0)

        @pl.when((z > 0) & (z < chips - 1))
        def _():
            for side in range(2):
                make(via_ref.at[side], via_ref.at[side], far_send.at[0], via_recv.at[side], mate).wait_recv()
                add_rows(pair_ref.at[side], pair_ref.at[side], via_ref.at[side], tokens, 64)
                pair_copy(side).start()

        for i in range(local):
            ge_ref[i, : 2 * FF] = dot_tn(dgu_ref[i], xs_ref[i]).astype(BF)
            ge_ref[i, 2 * FF :] = dot_tn(hx_ref[i], dye_ref[i]).astype(BF)
            if bits:
                next(sums[i])
        for t in range(max(chips - 2, 0), chips):
            free_slot(t, t % 2)
        for t in range(chips):
            for core in range(2):

                @pl.when((t > 0) | (c != core))
                def _():
                    dgt_copy(z, core, t).wait_send()

    slots = chips * 2 * CAP
    pl.run_scoped(
        experts_and_sums,
        pltpu.VMEM((2, 2, tokens, D), BF), pltpu.VMEM((local, slots, D), BF), pltpu.VMEM((local, slots, D), BF),
        pltpu.VMEM((local, slots, 2 * FF), BF), pltpu.VMEM((local, slots, FF), BF), pltpu.VMEM((2, 2, tokens, D), BF),
        pltpu.VMEM((2, tokens, D), BF), pltpu.VMEM((16 if roomy else tokens, D), BF),
    )

    def line(own, size, step, core_add, name, up_ref, down_ref, up_send, up_recv, down_send, down_recv):
        def add_block(block, other):
            add_rows(own(block), own(block), landed(other.at[block], name), size, step)

        def send(block, up):
            there, send_sem, recv_sem = (up_ref, up_send, up_recv) if up else (down_ref, down_send, down_recv)
            return make(own(block), there.at[block], send_sem.at[block], recv_sem.at[block], above if up else below)

        nearby = [k for both in zip(range(chips - 1, -1, -1), range(chips)) for k in both][:chips]
        for k in nearby:
            core_add(k)

            @pl.when((z == 0) & (k > 0))
            def _():
                send(k, True).start()

            @pl.when((z == chips - 1) & (k < chips - 1))
            def _():
                send(k, False).start()

        yield
        for k in range(chips - 2):
            owner = chips - 1 - k

            @pl.when((z > 0) & (z < owner))
            def _():
                send(owner, True).wait_recv()
                add_block(owner, up_ref)
                send(owner, True).start()

            @pl.when((z < chips - 1) & (z > k))
            def _():
                send(k, False).wait_recv()
                add_block(k, down_ref)
                send(k, False).start()

            yield

        @pl.when(z > 0)
        def _():
            send(z, True).wait_recv()
            add_block(z, up_ref)

        @pl.when(z < chips - 1)
        def _():
            send(z, False).wait_recv()
            add_block(z, down_ref)

        for k in range(chips):

            @pl.when(z < k)
            def _():
                send(k, True).wait_send()

            @pl.when(z > k)
            def _():
                send(k, False).wait_send()

    def mixture():
        def core_add(k):
            make(y_core.at[k], y_core.at[k], yc_send.at[k], yc_recv.at[k], mate).wait_recv()
            add_rows(y_ref.at[k], y_ref.at[k], landed(y_core.at[k], "tokens"), tokens, 32)

        yield from line(
            lambda k: y_ref.at[k], tokens, 32, core_add, "tokens", y_up, y_down, y_up_send, y_up_recv, y_down_send,
            y_down_recv,
        )
        out_ref[...] = (h1_ref[...] + residual_scale * y_ref[z].astype(F32)).astype(BF)

    def attention(w_ref, q_ref, kd_ref, vd_ref, o_ref, p_ref, do_ref, dqkv_ref, gw_ref, halves_stage, tokens_stage, rows_stage):
        stages["halves"] = (halves_stage, stage_sem.at[1])
        stages["tokens"] = (tokens_stage, stage_sem.at[2])
        stages["rows"] = (rows_stage, stage_sem.at[3])
        loads = [
            pltpu.make_async_copy(source, target, load_sem.at[i])
            for i, (source, target) in enumerate(
                ((w_hbm, w_ref), (o_hbm, o_ref), (q_hbm, q_ref), (kd_hbm, kd_ref), (vd_hbm, vd_ref))
            )
        ]
        start(loads)

        def projection():
            crossing = make(gw_ref.at[:, 1 - c], gw_core, gw_core_sem.at[0], gw_core_sem.at[1], mate)
            crossing.start()
            yield
            crossing.wait_recv()

            def own(k):
                return gw_ref.at[k, c]

            yield from line(
                own, rows, 16, lambda k: add_rows(own(k), own(k), gw_core.at[k], rows, 16), "rows", gw_up, gw_down,
                gw_up_send, gw_up_recv, gw_down_send, gw_down_recv,
            )
            crossing.wait_send()
            wide = QKVO // replicas

            def columns(part):
                return pl.ds(pl.multiple_of(part * wide, LANE), wide)

            mine = gw_ref.at[z, c]

            def part_copy(d):
                to = (r + d) % replicas
                return make(mine.at[:, columns(to)], parts_ref.at[r], part_send.at[d], part_recv.at[r], (to, f))

            def small_copy(d):
                to = (r + d) % replicas
                return make(mine.at[:, pl.ds(QKVO, LANE)], smalls_ref.at[r], small_send.at[d], small_recv.at[r], (to, f))

            for d in range(1, replicas):
                part_copy(d).start()
                small_copy(d).start()
            parts_ref[r] = mine[:, columns(r)]
            smalls_ref[r] = mine[:, pl.ds(QKVO, LANE)]
            yield
            for d in range(1, replicas):
                peer = (r + d) % replicas
                make(parts_ref.at[peer], parts_ref.at[peer], part_send.at[d], part_recv.at[peer], (peer, f)).wait_recv()
                make(smalls_ref.at[peer], smalls_ref.at[peer], small_send.at[d], small_recv.at[peer], (peer, f)).wait_recv()
            total = parts_ref[0].astype(F32)
            small = smalls_ref[0].astype(F32)
            for k in range(1, replicas):
                total = total + parts_ref[k].astype(F32)
                small = small + smalls_ref[k].astype(F32)
            result_ref[r] = total.astype(BF)
            total_ref[...] = small

            def result_copy(d):
                to = (r + d) % replicas
                return make(result_ref.at[r], result_ref.at[r], result_send.at[d], result_recv.at[r], (to, f))

            for d in range(1, replicas):
                result_copy(d).start()
            yield
            for d in range(1, replicas):
                peer = (r + d) % replicas
                make(
                    result_ref.at[peer], result_ref.at[peer], result_send.at[d], result_recv.at[peer], (peer, f)
                ).wait_recv()
            for d in range(1, replicas):
                part_copy(d).wait_send()
                small_copy(d).wait_send()
                result_copy(d).wait_send()

        moe, grads = [mixture()], [projection()]

        def go(*turns):
            for turn in turns:
                for process in turn:
                    next(process, None)

        def dgate():
            found = [dgt_all[k, :local] for k in range(2 * chips)]
            return jnp.concatenate(found + [jnp.zeros((LANE - E, tokens), F32)], axis=0).T

        for k in range(chips):

            @pl.when((z == k + 1) | (z + 1 == k) | (z > k + 2) | (z + 2 < k))
            def _():
                make(from_ref.at[k], from_ref.at[k], far_send.at[0], far_recv.at[k], mate).wait_recv()
                there = from_ref.at[k] if roomy else landed(from_ref.at[k], "tokens")
                add_rows(dx_ref, dx_ref, there, tokens, 64)

        for k in range(2 * chips):

            @pl.when(f == k)
            def _():
                for core in range(2):

                    @pl.when(c == core)
                    def _():
                        dgt_all[k] = dgt_ref[0, core]

            @pl.when(f != k)
            def _():
                make(dgt_all.at[k], dgt_all.at[k], dgt_send.at[0, 0], dgt_recv.at[k], mate).wait_recv()

        go(moe)
        for load in loads:
            load.wait()
        backward = attention_backward(
            x_ref, dout_ref, cos_ref, sin_ref, w_ref, q_ref, kd_ref, vd_ref, p_hbm, o_ref, h1_ref, n2_ref, gd_ref, dx_ref,
            dgate, gin_ref, gw_ref, do_ref, dqkv_ref, p_ref, p_sem,
        )
        next(backward)
        go(first)
        next(backward)
        go(moe)
        next(backward, None)
        go(grads, last, moe, grads, first, moe, last, first, grads, last, grads, first, grads, last, grads, grads)
        go(*[moe + grads + sums] * (2 * chips + 2 * bits + 4))

    size = ge_ref.shape[1] // max(bits, 1)
    pl.run_scoped(
        attention,
        pltpu.VMEM((D, W_O + D), BF), pltpu.VMEM((tokens, D), BF), pltpu.VMEM((tokens, D), BF), pltpu.VMEM((tokens, D), BF),
        pltpu.VMEM((tokens, D), BF), pltpu.VMEM((2, 2 * tokens, tokens), F32), pltpu.VMEM((tokens, D), BF),
        pltpu.VMEM((tokens, QKV), BF), pltpu.VMEM((chips, 2, rows, QKVO + LANE), BF), pltpu.VMEM((size // 2, D), BF),
        pltpu.VMEM((tokens, D), BF), pltpu.VMEM((rows, QKVO + LANE), BF),
    )

    for e in range(local):
        copy = pltpu.make_async_copy(ge_ref.at[e], ge_hbm.at[e], ge_sem.at[e])
        if not bits:
            copy.start()
        copy.wait()
    for side in range(2):

        @pl.when(z > 0 if side == 0 else z < chips - 1)
        def _():
            pair_copy(side).wait_send()

    for k in range(chips):

        @pl.when((z >= k) & (z < chips - 1))
        def _():
            for copy in pass_on(k, "up"):
                copy.wait_send()

        @pl.when((z <= k) & (z > 0))
        def _():
            for copy in pass_on(k, "down"):
                copy.wait_send()

        for copy in pass_on(k, "mate"):
            copy.wait_send()


def finish(gexp_ref, result_ref, total_ref, gin_ref, out_ref, *outs):
    layer, grad_in, gains_one, query, key, value, output, gains_two, router, expert = outs
    expert[...] = gexp_ref[...].astype(F32)

    @pl.when(pl.program_id(0) == 0)
    def _():
        layer[...] = out_ref[...]
        grad_in[...] = gin_ref[...]
        wide = result_ref.shape[2]
        start = 0
        for ref in (query, key, value, output):
            for at in range(0, ref.shape[1], LANE):
                part, column = divmod(start + at, wide)
                ref[:, at : at + LANE] = result_ref[part, :, column : column + LANE].astype(F32)
            start += ref.shape[1]
        small = total_ref[...].T
        router[...] = small[:E]
        gains_one[...] = small[E : E + 1]
        gains_two[...] = small[E + 1 : E + 2]


def call(kernel, out_shape, args, scratch=(), outside=0, out_outside=0, **params):
    spaces = [pltpu.SMEM if a.dtype == jnp.int32 and a.size <= 16 else pltpu.VMEM for a in args]
    spaces[len(args) - outside :] = [pl.ANY] * outside
    return pl.pallas_call(
        kernel,
        out_shape=out_shape,
        in_specs=[pl.BlockSpec(memory_space=space) for space in spaces],
        out_specs=[
            pl.BlockSpec(memory_space=pltpu.VMEM if i < len(out_shape) - out_outside else pl.ANY)
            for i in range(len(out_shape))
        ],
        scratch_shapes=list(scratch),
        compiler_params=pltpu.CompilerParams(
            vmem_limit_bytes=VMEM_LIMIT, has_side_effects="collective_id" in params, **params
        ),
    )(*args)


def shape(dims, dtype):
    return jax.ShapeDtypeStruct(dims, dtype)


def make_body(mesh):
    group, replicas = mesh.shape["fsdp"], mesh.shape["replica"]
    local = E // group

    def body(
        hidden_in, seq_lengths, routes, norm1_gain, w_query, w_key, w_value, w_output, norm2_gain, w_router,
        expert_weights, out_cotangent,
    ):
        tokens = hidden_in.shape[0]
        rows = w_query.shape[0]
        chips = group // 2
        dma = pltpu.SemaphoreType.DMA
        weights, q, kd, vd, o, h1, n2, gd, gt, cosines, sines, p, dout_all = call(
            functools.partial(front, replicas, chips),
            (
                shape((chips, 2, rows, W_O + D), BF), shape((tokens, D), BF), shape((tokens, D), BF),
                shape((tokens, D), BF), shape((tokens, D), BF), shape((tokens, D), F32), shape((tokens, D), BF),
                shape((tokens, LANE), F32), shape((E, tokens), F32), shape((tokens, LANE), F32),
                shape((tokens, LANE), F32), shape((KVH, 2 * tokens, tokens), F32), shape((chips, 2, tokens, D), BF),
            ),
            (
                hidden_in, seq_lengths, routes.T, rope_table(tokens), w_query, w_key, w_value, w_output, w_router.T,
                norm1_gain[None], norm2_gain[None], out_cotangent,
            ),
            [
                pltpu.VMEM((2, 2 * tokens, tokens), F32), dma((2,)), dma((1,)), dma((3, chips)), dma((3, chips)),
                dma((3, chips)), dma((3, chips, replicas)), dma((3, chips, replicas)), dma((2, chips)),
                dma((2, chips)), dma((3, chips)), dma((chips, 2)),
            ],
            out_outside=2,
            collective_id=2,
        )
        weights = weights.reshape(D, W_O + D)
        bits = replicas.bit_length() - 1
        size = 3 * FF // bits if bits else 0
        width = QKVO + LANE
        roomy = chips <= 4
        landing = [shape((local * bits, size >> (k + 1), D), BF) for k in range(bits)]
        blocks = [shape((chips, tokens, D), BF)] * 2
        if not roomy:
            landing += blocks
        landing_sems = [dma((chips,))] * 4
        outs = call(
            functools.partial(back, replicas, chips),
            [
                shape((tokens, D), F32), shape((tokens, D), BF), shape((replicas, rows, QKVO // replicas), BF),
                shape((rows, LANE), F32), shape((local, 3 * FF, D), BF),
            ]
            + [shape((chips, tokens, D), BF)] * 3 + [shape((chips, rows, width), BF)] * 2 + landing,
            (
                hidden_in, out_cotangent, cosines, sines, h1, n2, gd, gt,
                dout_all, expert_weights, weights, q, kd, vd, o, p,
            ),
            [
                pltpu.VMEM((local, 3 * FF, D), BF), pltpu.VMEM((chips, 2, tokens, D), BF),
                pltpu.VMEM((chips, 2, E, tokens), F32), pltpu.VMEM((2, tokens, D), BF), pltpu.VMEM((2, tokens, D), BF),
                pltpu.VMEM((tokens, D), F32), pltpu.VMEM((chips, 2, 8, tokens), F32), pltpu.VMEM((group, 8, tokens), F32),
                pltpu.VMEM((chips, tokens, D), BF), pltpu.VMEM((chips, rows, width), BF),
                pltpu.VMEM((replicas, rows, QKVO // replicas), BF), pltpu.VMEM((replicas, rows, LANE), BF),
            ]
            + ([pltpu.VMEM(b.shape, b.dtype) for b in blocks] if roomy else [])
            + ([dma((chips,))] * 3 + [dma((chips, 2))]) * 2 + [dma((chips,))] * 4 + [dma((2,))] * 2
            + [dma((chips, 2)), dma((group,)), dma((chips,)), dma((chips,))]
            + [dma((2,)), dma((1,)), dma((5,)), dma((4,)), dma((local,)), dma((2,))]
            + [dma((max(local * bits, 1), max(2 * bits, 1)))] * 2
            + [pltpu.SemaphoreType.REGULAR((max(local * bits, 1), max(bits, 1)))]
            + landing_sems + [dma((2,))] + landing_sems + [dma((replicas,))] * 6,
            outside=8,
            out_outside=6 + len(landing),
            collective_id=0,
        )
        grad_in, layer_out, result, total, grad_experts = outs[:5]
        steps = 8
        block = local * 3 * FF // steps
        fixed = [
            shape((tokens, D), BF), shape((tokens, D), F32), shape((1, rows), F32), shape((rows, H * HD), F32),
            shape((rows, KVH * HD), F32), shape((rows, KVH * HD), F32), shape((rows, D), F32), shape((1, rows), F32),
            shape((E, rows), F32),
        ]

        def still(a):
            return pl.BlockSpec(a.shape, lambda i: (0, 0))

        expert_block = pl.BlockSpec((block, D), lambda i: (i, 0))
        outs = pl.pallas_call(
            finish,
            grid=(steps,),
            in_specs=[
                expert_block, pl.BlockSpec(result.shape, lambda i: (0, 0, 0)), still(total), still(grad_in), still(layer_out)
            ],
            out_specs=[still(a) for a in fixed] + [expert_block],
            out_shape=fixed + [shape((local * 3 * FF, D), F32)],
            compiler_params=pltpu.CompilerParams(vmem_limit_bytes=VMEM_LIMIT),
        )(grad_experts.reshape(local * 3 * FF, D), result, total, grad_in, layer_out)
        return (
            outs[0], outs[1], outs[2][0], outs[3], outs[4], outs[5], outs[6], outs[7][0], outs[8].T,
            outs[9].reshape(local, 3 * FF, D),
        )

    return body


def solution(mesh):
    tokens, weights = P(("replica", "fsdp"), None), P("fsdp", None)
    return jax.shard_map(
        make_body(mesh),
        mesh=mesh,
        in_specs=(
            tokens, tokens, tokens, P("fsdp"), weights, weights, weights, weights, P("fsdp"), weights,
            P("fsdp", None, None), tokens,
        ),
        out_specs=(
            tokens, tokens, P("fsdp"), weights, weights, weights, weights, P("fsdp"), weights, P("fsdp", None, None),
        ),
        check_vma=False,
    )
```

```python
import functools

import jax
import jax.numpy as jnp
import numpy as np
from jax import lax
from jax.experimental import pallas as pl
from jax.experimental.pallas import tpu as pltpu
from jax.sharding import PartitionSpec as P

D = 1024
H = 16
KVH = 8
HD = 64
FF = 512
TOPK = 8
E = 16
CAP = 144
LANE = 128
QKV = H * HD + 2 * KVH * HD
QKVO = QKV + D
W_O = QKV + LANE

norm_eps = 1e-06
score_scale = 0.015625
residual_scale = 0.22
rope_base = 10000.0
masked_score = -1e30

BF = jnp.bfloat16
F32 = jnp.float32
VMEM_LIMIT = 63 * 2**20


def dot(a, b):
    return lax.dot_general(a, b, (((1,), (0,)), ((), ())), preferred_element_type=F32)


def dot_nt(a, b):
    return lax.dot_general(a, b, (((1,), (1,)), ((), ())), preferred_element_type=F32)


def dot_tn(a, b):
    return lax.dot_general(a, b, (((0,), (0,)), ((), ())), preferred_element_type=F32)


def lanes_of(rows):
    return lax.broadcasted_iota(jnp.int32, (rows, LANE), 1)


def turned(block, lane):
    return jnp.where(lane % HD < HD // 2, pltpu.roll(block, LANE - HD // 2, 1), pltpu.roll(block, HD // 2, 1))


def halves(block, low):
    zero = jnp.zeros_like(block)
    return jnp.concatenate([jnp.where(low, block, zero), jnp.where(low, zero, block)], axis=0)


def rope_table(tokens):
    frequency = np.float32(rope_base) ** (-np.arange(0, HD, 2, dtype=np.float32) / np.float32(HD))
    frequency = np.tile(frequency.astype(np.float32), LANE // (HD // 2))
    angles = (np.arange(tokens, dtype=np.float32)[:, None] * frequency[None, :]).astype(np.float64)
    sign = np.where(np.arange(LANE) % HD < HD // 2, -1.0, 1.0)
    pieces = []
    for values in (np.cos(angles), np.sin(angles) * sign[None, :]):
        rest = values.astype(np.float32)
        for _ in range(3):
            piece = rest.astype(BF)
            pieces.append(piece)
            rest = rest - piece.astype(np.float32)
    return np.concatenate(pieces, axis=1)


class Copies:
    def make(self, src, dst, send, recv, device):
        return pltpu.make_async_remote_copy(
            src_ref=src, dst_ref=dst, send_sem=send, recv_sem=recv, device_id=device, device_id_type=pl.DeviceIdType.MESH
        )


def meet(devices, expected):
    barrier = pltpu.get_barrier_semaphore()
    for condition, device in devices:

        def signal(device=device):
            pl.semaphore_signal(barrier, inc=1, device_id=device, device_id_type=pl.DeviceIdType.MESH)

        if condition is True:
            signal()
        else:
            pl.when(condition)(signal)
    pl.semaphore_wait(barrier, expected)


def front(
    replicas, chips,
    x_ref, len_ref, routes_ref, table_ref, wq_ref, wk_ref, wv_ref, wo_ref, wr_ref, g1_ref, g2_ref, dout_ref,
    w_all, q_ref, kd_ref, vd_ref, o_ref, h1_ref, n2_ref, gd_ref, gt_ref, cos_ref, sin_ref, p_hbm, do_all,
    p_ref, p_sem, own_sem, z_up, z_down, z_recv, xy_send, xy_recv, mate_send, mate_recv, do_send, do_recv,
):
    tokens = x_ref.shape[0]
    r, f = lax.axis_index("replica"), lax.axis_index("fsdp")
    z, c = f // 2, f % 2
    mate, above, below = (r, z * 2 + 1 - c), (r, f + 2), (r, f - 2)
    make = Copies().make
    peers = [(True, mate), (z > 0, below), (z < chips - 1, above)]
    peers += [(True, ((r + d) % replicas, f)) for d in range(1, replicas)]

    own_dout = pltpu.make_async_copy(dout_ref, do_all.at[z, c], own_sem.at[0])
    own_dout.start()
    rows = wq_ref.shape[0]
    packed = [wr_ref[...].astype(F32), g1_ref[...].astype(F32), g2_ref[...].astype(F32)]
    packed = jnp.concatenate(packed + [jnp.zeros((LANE - E - 2, rows), F32)], axis=0)
    own = w_all.at[z, c]
    own[:, : H * HD] = wq_ref[...]
    own[:, H * HD : H * HD + KVH * HD] = wk_ref[...]
    own[:, H * HD + KVH * HD : QKV] = wv_ref[...]
    own[:, QKV:W_O] = packed.T.astype(BF)
    own[:, W_O:] = wo_ref[...]
    meet(peers, 1 + (replicas - 1) + jnp.where(z > 0, 1, 0) + jnp.where(z < chips - 1, 1, 0))

    def part(kind):
        if kind == 0:
            return pl.ds(pl.multiple_of(r * (QKV // replicas), LANE), QKV // replicas)
        if kind == 1:
            return pl.ds(QKV, LANE)
        return pl.ds(pl.multiple_of(W_O + r * (D // replicas), LANE), D // replicas)

    def along(zb, kind, up):
        ref = w_all.at[zb, c, :, part(kind)]
        return make(ref, ref, (z_up if up else z_down).at[kind, zb], z_recv.at[kind, zb], above if up else below)

    def across(zb, kind, d):
        ref = w_all.at[zb, c, :, part(kind)]
        return make(ref, ref, xy_send.at[kind, zb, d], xy_recv.at[kind, zb, r], ((r + d) % replicas, f))

    def wait_across(zb, kind):
        for d in range(1, replicas):
            peer = (r + d) % replicas
            ref = w_all.at[zb, c, :, part(kind)]
            make(ref, ref, xy_send.at[kind, zb, d], xy_recv.at[kind, zb, peer], (peer, f)).wait_recv()

    def to_mate(zb, core, late):
        ref = w_all.at[zb, core, :, pl.ds(W_O, D) if late else pl.ds(0, W_O)]
        return make(ref, ref, mate_send.at[late, zb], mate_recv.at[late, zb], mate)

    def dout_copy(zb, core, way):
        source = do_all.at[zb, core]
        return make(source, do_all.at[zb, core], do_send.at[way, zb], do_recv.at[zb, core], (above, below, mate)[way])

    def both_sides(k, act):
        @pl.when(z >= k)
        def _():
            act(z - k, True)

        @pl.when(z < chips - k)
        def _():
            act(z + k, False)

    def onward(up):
        return z < chips - 1 if up else z > 0

    for kind in range(3):
        both_sides(1, lambda zb, low: along(z, kind, not low).start())
    for late in range(2):
        to_mate(z, c, late).start()

    source = x_ref[...].astype(F32)
    factor = lax.rsqrt(jnp.mean(source * source, axis=1, keepdims=True) + norm_eps)
    lane = lanes_of(tokens)
    low_lane = lane < HD
    row = lax.broadcasted_iota(jnp.int32, (tokens, tokens), 0)
    column = lax.broadcasted_iota(jnp.int32, (tokens, tokens), 1)
    row_at = lax.broadcasted_iota(jnp.int32, (tokens, 1), 0)
    column_at = lax.broadcasted_iota(jnp.int32, (1, tokens), 1)
    row_segment = jnp.zeros((tokens, 1), jnp.int32)
    row_start = jnp.zeros((tokens, 1), jnp.int32)
    column_segment = jnp.zeros((1, tokens), jnp.int32)
    end = jnp.int32(0)
    for j in range(len_ref.shape[1]):
        end = end + len_ref[0, j]
        row_segment += (row_at >= end).astype(jnp.int32)
        row_start = jnp.maximum(row_start, jnp.where(row_at >= end, end, 0))
        column_segment += (column_at >= end).astype(jnp.int32)
    place = (column == row - row_start).astype(F32).astype(BF)
    found = dot(place, table_ref[...])
    found = [found[:, i * LANE : (i + 1) * LANE] for i in range(6)]
    cosines, sines = found[0] + found[1] + found[2], found[3] + found[4] + found[5]
    cos_ref[...] = cosines
    sin_ref[...] = sines

    own_dout.wait()
    for k in range(1, chips):
        for kind in range(3):

            def arrive(zb, low, kind=kind):
                along(zb, kind, low).wait_recv()

                @pl.when(onward(low))
                def _():
                    along(zb, kind, low).start()

                if kind != 1:
                    for d in range(1, replicas):
                        across(zb, kind, d).start()

            both_sides(k, arrive)
        if k == 1:
            both_sides(1, lambda zb, low: dout_copy(z, c, 1 if low else 0).start())
            dout_copy(z, c, 2).start()

    def share(k, late):
        def act(zb, low):
            wait_across(zb, 2 if late else 0)
            to_mate(zb, c, late).start()

        both_sides(k, act)

    def dout_arrive(zb, low):
        dout_copy(zb, c, 0 if low else 1).wait_recv()

        @pl.when(onward(low))
        def _():
            dout_copy(zb, c, 0 if low else 1).start()

        dout_copy(zb, c, 2).start()

    for k in range(1, chips):
        share(k, 0)
    if chips > 1:
        both_sides(1, dout_arrive)
    for k in range(chips):
        to_mate(k, 1 - c, 0).wait_recv()

    def columns(start, size):
        return w_all[:, :, :, start : start + size].reshape(D, size)

    small = columns(QKV, LANE)
    gains = small.astype(F32).T
    gain_one, gain_two = gains[E : E + 1], gains[E + 1 : E + 2]
    normed = (source * factor * gain_one).astype(BF)
    q_all = dot(normed, columns(0, H * HD))
    for g in range(H // 2):
        at = slice(g * LANE, (g + 1) * LANE)
        block = q_all[:, at]
        q_ref[:, at] = (block * cosines + turned(block, lane) * sines).astype(BF)
    kv = dot(normed, columns(H * HD, 2 * KVH * HD))
    for m in range(KVH // 2):
        block = kv[:, m * LANE : (m + 1) * LANE]
        block = block * cosines + turned(block, lane) * sines
        other = pltpu.roll(block, HD, 1)
        kd_ref[:, 2 * m * LANE : (2 * m + 1) * LANE] = jnp.where(low_lane, block, other).astype(BF)
        kd_ref[:, (2 * m + 1) * LANE : (2 * m + 2) * LANE] = jnp.where(low_lane, other, block).astype(BF)
        block = kv[:, KVH * HD + m * LANE : KVH * HD + (m + 1) * LANE]
        other = pltpu.roll(block, HD, 1)
        vd_ref[:, 2 * m * LANE : (2 * m + 1) * LANE] = jnp.where(low_lane, block, other).astype(BF)
        vd_ref[:, (2 * m + 1) * LANE : (2 * m + 2) * LANE] = jnp.where(low_lane, other, block).astype(BF)
    bias = jnp.where((row_segment == column_segment) & (column <= row), 0.0, masked_score)
    bias = jnp.concatenate([bias, bias], axis=0)

    def p_copy(g):
        return pltpu.make_async_copy(p_ref.at[g % 2], p_hbm.at[g], p_sem.at[g % 2])

    for g in range(KVH):
        at = slice(g * LANE, (g + 1) * LANE)
        queries = halves(q_ref[:, at].astype(F32), low_lane).astype(BF)
        scores = dot_nt(queries, kd_ref[:, at]) * score_scale + bias
        shifted = jnp.exp(scores - jnp.max(scores, axis=1, keepdims=True))
        weights = shifted * (1.0 / jnp.sum(shifted, axis=1, keepdims=True))
        if g >= 2:
            p_copy(g - 2).wait()
        p_ref[g % 2] = weights
        p_copy(g).start()
        mixed = dot(weights.astype(BF), vd_ref[:, at])
        o_ref[:, at] = jnp.where(low_lane, mixed[:tokens], mixed[tokens:]).astype(BF)

    if chips > 2:
        both_sides(2, dout_arrive)
    for k in range(1, chips):
        share(k, 1)

    for k in range(chips):
        to_mate(k, 1 - c, 1).wait_recv()
    after = source + residual_scale * dot(o_ref[...], columns(W_O, D))
    h1_ref[...] = after
    factor = lax.rsqrt(jnp.mean(after * after, axis=1, keepdims=True) + norm_eps)
    normed = (after * factor * gain_two).astype(BF)
    n2_ref[...] = normed
    logits = dot(normed, small).T[:E]
    expert = lax.broadcasted_iota(jnp.int32, (E, tokens), 0)
    routed = routes_ref[0:1] == expert
    for j in range(1, TOPK):
        routed |= routes_ref[j : j + 1] == expert
    top = jnp.max(jnp.where(routed, logits, masked_score), axis=0, keepdims=True)
    powers = jnp.where(routed, jnp.exp(logits - top), 0.0)
    gates = powers / jnp.sum(powers, axis=0, keepdims=True)
    gates = jnp.where(routed, gates, -1.0)
    gt_ref[...] = gates
    gd_ref[...] = jnp.concatenate([gates, jnp.full((LANE - E, tokens), -1.0, F32)], axis=0).T

    for k in range(3, chips):
        both_sides(k, dout_arrive)
    for k in range(chips):
        dout_copy(k, 1 - c, 2).wait_recv()
    for g in (KVH - 2, KVH - 1):
        p_copy(g).wait()
    for k in range(chips):
        for late in range(2):
            to_mate(k, c, late).wait_send()
        dout_copy(k, c, 2).wait_send()

        @pl.when((z >= k) & (z < chips - 1))
        def _():
            dout_copy(k, c, 0).wait_send()
            for kind in range(3):
                along(k, kind, True).wait_send()

        @pl.when((z <= k) & (z > 0))
        def _():
            dout_copy(k, c, 1).wait_send()
            for kind in range(3):
                along(k, kind, False).wait_send()

        @pl.when(z != k)
        def _():
            for d in range(1, replicas):
                for kind in (0, 2):
                    across(k, kind, d).wait_send()


def attention_backward(
    x_ref, dout_ref, cos_ref, sin_ref, w_ref, q_ref, kd_ref, vd_ref, p_hbm, o_ref, h1_ref, n2_ref, gd_ref, dx_ref, dgate,
    gin_ref, gq_ref, go_ref, do_ref, dqkv_ref, p_ref, p_sem,
):
    tokens = x_ref.shape[0]
    lane = lanes_of(tokens)
    low = lane < HD

    def p_copy(g):
        return pltpu.make_async_copy(p_hbm.at[g], p_ref.at[g % 2], p_sem.at[g % 2])

    p_copy(0).start()

    def put(ref, at, value):
        ref[:, :, :, at] = value.astype(BF).reshape(*ref.shape[:3], value.shape[1])

    small = w_ref[:, QKV:W_O].astype(F32).T
    gain_one, gain_two = small[E : E + 1], small[E + 1 : E + 2]
    after = h1_ref[...]
    factor_two = lax.rsqrt(jnp.mean(after * after, axis=1, keepdims=True) + norm_eps)
    gates = jnp.maximum(gd_ref[...], 0.0)
    grad_gates = dgate()
    chosen = gates * (grad_gates - jnp.sum(gates * grad_gates, axis=1, keepdims=True))
    grad_logits = chosen.astype(BF)
    grad_normed = dx_ref[...] + dot_nt(grad_logits, w_ref[:, QKV:W_O])
    scaled = grad_normed * gain_two
    grad_after = dout_ref[...].astype(F32) + (
        factor_two * scaled - after * factor_two**3 * jnp.mean(scaled * after, axis=1, keepdims=True)
    )
    grad_gain_two = jnp.sum(grad_normed * after * factor_two, axis=0, keepdims=True)
    grad_branch = (residual_scale * grad_after).astype(BF)
    put(go_ref, slice(0, D), dot_tn(o_ref[...], grad_branch))
    do_ref[...] = dot_nt(grad_branch, w_ref[:, W_O:]).astype(BF)
    grad_router = dot_tn(n2_ref[...], grad_logits)
    yield

    cosines, sines = cos_ref[...], sin_ref[...]
    key_back, value_back = [], []
    for g in range(KVH):
        at = slice(g * LANE, (g + 1) * LANE)
        queries = halves(q_ref[:, at].astype(F32), low).astype(BF)
        outs = halves(do_ref[:, at].astype(F32), low).astype(BF)
        if g + 1 < KVH:
            p_copy(g + 1).start()
        p_copy(g).wait()
        weights = p_ref[g % 2]
        grad_weights = dot_nt(outs, vd_ref[:, at])
        total = jnp.sum(weights * grad_weights, axis=1, keepdims=True)
        grad_scores = (weights * (grad_weights - total)).astype(BF)
        block = dot(grad_scores, kd_ref[:, at])
        block = jnp.where(low, block[:tokens], block[tokens:]) * score_scale
        dqkv_ref[:, at] = (block * cosines - turned(block, lane) * sines).astype(BF)
        block = dot_tn(grad_scores, queries) * score_scale
        key_back.append(block + pltpu.roll(block, HD, 1))
        block = dot_tn(weights.astype(BF), outs)
        value_back.append(block + pltpu.roll(block, HD, 1))
    for m in range(KVH // 2):
        block = jnp.where(low, key_back[2 * m], key_back[2 * m + 1])
        at = slice(H * HD + m * LANE, H * HD + (m + 1) * LANE)
        dqkv_ref[:, at] = (block * cosines - turned(block, lane) * sines).astype(BF)
        at = slice(H * HD + KVH * HD + m * LANE, H * HD + KVH * HD + (m + 1) * LANE)
        dqkv_ref[:, at] = jnp.where(low, value_back[2 * m], value_back[2 * m + 1]).astype(BF)
    yield

    source = x_ref[...].astype(F32)
    factor_one = lax.rsqrt(jnp.mean(source * source, axis=1, keepdims=True) + norm_eps)
    normed = (source * factor_one * gain_one).astype(BF)
    put(gq_ref, slice(0, QKV), dot_tn(normed, dqkv_ref[...]))
    grad_normed = dot_nt(dqkv_ref[...], w_ref[:, :QKV])
    scaled = grad_normed * gain_one
    grad_vector = factor_one * scaled - source * factor_one**3 * jnp.mean(scaled * source, axis=1, keepdims=True)
    gin_ref[...] = grad_after + grad_vector
    grad_gain_one = jnp.sum(grad_normed * source * factor_one, axis=0, keepdims=True)
    gains = jnp.concatenate([grad_gain_one, grad_gain_two, jnp.zeros((6, D), F32)], axis=0).T
    at = lanes_of(D)
    extra = jnp.where(at == E, gains[:, 0:1], jnp.where(at == E + 1, gains[:, 1:2], grad_router))
    put(gq_ref, slice(QKV, W_O), extra)


def add_rows(target, first, second, rows, step):
    def some(i, carry):
        at = pl.ds(pl.multiple_of(i * step, step), step)
        target[at] = (first[at].astype(F32) + second[at].astype(F32)).astype(target.dtype)
        return carry

    lax.fori_loop(0, rows // step, some, 0)


def back(
    replicas, chips,
    x_ref, dout_ref, cos_ref, sin_ref, h1_ref, n2_ref, gd_ref, gt_ref,
    do_hbm, we_hbm, w_hbm, q_hbm, kd_hbm, vd_hbm, o_hbm, p_hbm,
    gin_ref, out_ref, rq_ref, ro_ref, total_ref, ge_hbm, y_via, y_from, q_via, q_from, o_via, o_from, *rest,
):
    bits = replicas.bit_length() - 1
    roomy = chips <= 4
    arrived, rest = rest[:bits], rest[bits:]
    if not roomy:
        (core_ref, from_ref, y_core), rest = rest[:3], rest[3:]
    (ge_ref, n2_all, gt_all, via_ref, pair_ref, dx_ref, dgt_ref, dgt_all, y_ref, q_core, o_core, pq_ref, po_ref, smalls_ref), rest = (
        rest[:14], rest[14:]
    )
    if roomy:
        (core_ref, from_ref, y_core), rest = rest[:3], rest[3:]
    (n2_up, n2_down, n2_mate, n2_recv, gt_up, gt_down, gt_mate, gt_recv,
     core_send, core_recv, far_send, far_recv, pair_send, via_recv, dgt_send, dgt_recv, yc_send, yc_recv,
     do_sem, we_sem, load_sem, stage_sem, ge_sem, p_sem, ar_send, ar_recv, ar_free,
     *sum_sems, part_send, part_recv, small_send, small_recv, result_send, result_recv) = rest
    y_sems, q_sems, o_sems = sum_sems[:3], sum_sems[3:7], sum_sems[7:]
    local, tokens, rows = ge_ref.shape[0], x_ref.shape[0], q_core.shape[1]
    r, f = lax.axis_index("replica"), lax.axis_index("fsdp")
    z, c = f // 2, f % 2
    mate, above, below = (r, z * 2 + 1 - c), (r, f + 2), (r, f - 2)
    make = Copies().make

    load_experts = pltpu.make_async_copy(we_hbm, ge_ref, we_sem.at[0])
    load_experts.start()
    n2_all[z, c] = n2_ref[...]
    gt_all[z, c] = gt_ref[...]
    peers = [(True, mate)]
    for k in range(1, chips):
        to = (z + k) % chips
        peers += [(True, (r, to * 2 + c)), (True, (r, to * 2 + 1 - c))]
    peers += [(True, ((r + d) % replicas, f)) for d in range(1, replicas)]
    meet(peers, len(peers))

    def bit_of(b):
        return (r // (1 << b)) % 2

    def partner(b):
        return (r + (1 - 2 * bit_of(b)) * (1 << b), f)

    stages = {}

    def landed(ref, name):
        stage, sem = stages[name]
        if ref.shape != stage.shape:
            stage = stage.at[pl.ds(0, ref.shape[0])]
        copy = pltpu.make_async_copy(ref, stage, sem)
        copy.start()
        copy.wait()
        return stage

    def halving(e):
        size = ge_ref.shape[1] // bits
        orders = [[(g + k) % bits for k in range(bits)] for g in range(bits)]
        starts = [[] for _ in range(bits)]
        for g in range(bits):
            at = g * size
            for k in range(bits):
                starts[g].append(at)
                at = at + bit_of(orders[g][k]) * (size >> (k + 1))
            starts[g].append(at)

        def region(g, k):
            half = size >> (k + 1)
            return ge_ref.at[e, pl.ds(pl.multiple_of(starts[g][k + 1], half), half)]

        def exchange(g, k):
            half, job = size >> (k + 1), e * bits + g
            give = pl.multiple_of(starts[g][k] + (1 - bit_of(orders[g][k])) * half, half)
            return make(
                ge_ref.at[e, pl.ds(give, half)], arrived[k].at[job], ar_send.at[job, k], ar_recv.at[job, k],
                partner(orders[g][k]),
            )

        def spread(g, k):
            job, ref = e * bits + g, region(g, k)
            return make(ref, ref, ar_send.at[job, bits + k], ar_recv.at[job, bits + k], partner(orders[g][k]))

        def spread_once_free(g, k):
            pl.semaphore_wait(ar_free.at[e * bits + g, k], 1)
            spread(g, k).start()

        yield
        for g in range(bits):
            exchange(g, 0).start()
        yield
        for k in range(bits):
            half = size >> (k + 1)
            for g in range(bits):
                job = e * bits + g
                exchange(g, k).wait_recv()
                own = region(g, k)
                add_rows(own, own, landed(arrived[k].at[job], "halves"), half, min(half, 64))
                if k < bits - 1:
                    exchange(g, k + 1).start()
                exchange(g, k).wait_send()
                pl.semaphore_signal(
                    ar_free.at[job, k], inc=1, device_id=partner(orders[g][k]), device_id_type=pl.DeviceIdType.MESH
                )
                if k == bits - 1:
                    spread_once_free(g, k)
            yield
        for k in range(bits - 1, -1, -1):
            for g in range(bits):
                spread(g, k).wait_recv()
                if k > 0:
                    spread_once_free(g, k - 1)
            yield
        for g in range(bits):
            for k in range(bits):
                spread(g, k).wait_send()
        pltpu.make_async_copy(ge_ref.at[e], ge_hbm.at[e], ge_sem.at[e]).start()

    sums = [halving(e) for e in range(local)] if bits else []
    first, last = sums[:1], sums[1:]
    for process in sums:
        next(process)

    def pass_on(zb, how):
        to = {"up": above, "down": below, "mate": mate}[how]
        sems = {"up": (n2_up, gt_up), "down": (n2_down, gt_down), "mate": (n2_mate, gt_mate)}[how]
        return [
            make(ref.at[zb, c], ref.at[zb, c], sem.at[zb], recv.at[zb, c], to)
            for ref, sem, recv in ((gt_all, sems[1], gt_recv), (n2_all, sems[0], n2_recv))
        ]

    def got(zb, core):
        for ref, sem, recv in ((gt_all, gt_mate, gt_recv), (n2_all, n2_mate, n2_recv)):
            make(ref.at[zb, core], ref.at[zb, core], sem.at[zb], recv.at[zb, core], mate).wait_recv()

    def start(copies):
        for copy in copies:
            copy.start()

    @pl.when(z < chips - 1)
    def _():
        start(pass_on(z, "up"))

    @pl.when(z > 0)
    def _():
        start(pass_on(z, "down"))

    start(pass_on(z, "mate"))
    inner = jnp.minimum(z, chips - 1 - z)

    def place(t):
        k = (t + 1) // 2
        near = jnp.where(t % 2 == 1, z - k, z + k)
        return jnp.where(t <= 2 * inner, near, jnp.where(2 * z < chips - 1, t, chips - 1 - t))

    def far(zc):
        return jnp.where(zc > z, zc - z, z - zc)

    def side_of(zc):
        return jnp.where(zc > z, 1, 0)

    def relay(k, low, high):
        @pl.when(low)
        def _():
            got(z - k, c)

            @pl.when(z < chips - 1)
            def _():
                start(pass_on(z - k, "up"))

            start(pass_on(z - k, "mate"))

        @pl.when(high)
        def _():
            got(z + k, c)

            @pl.when(z > 0)
            def _():
                start(pass_on(z + k, "down"))

            start(pass_on(z + k, "mate"))

    def early(t):
        return (t >= 2) & (t % 2 == 0) & (t <= 2 * inner) & (t < chips - 1)

    def pair_copy(side):
        owner = z + 2 * side - 1
        return make(pair_ref.at[side], from_ref.at[z], pair_send.at[side], far_recv.at[z], (r, owner * 2 + c))

    def experts_and_sums(do_buf, xs_ref, dye_ref, dgu_ref, hx_ref, dxp_ref, yps_ref, core_stage):
        stages["core"] = (core_stage, stage_sem.at[0])
        before = lax.broadcasted_iota(jnp.int32, (tokens, tokens), 0) < lax.broadcasted_iota(jnp.int32, (tokens, tokens), 1)
        before = before.astype(F32).astype(BF)
        slot_index = lax.broadcasted_iota(jnp.int32, (CAP, tokens), 0).astype(F32)
        pair = 2 * CAP

        def do_copy(zc, slot):
            return pltpu.make_async_copy(do_hbm.at[zc], do_buf.at[slot], do_sem.at[slot])

        def core_copy(zc, slot, t):
            return make(dxp_ref.at[slot, 1 - c], core_ref.at[zc], core_send.at[t], core_recv.at[zc], mate)

        def y_copy(zc, slot, t):
            return make(yps_ref.at[slot], y_core.at[zc], yc_send.at[t], yc_recv.at[zc], mate)

        def via_copy(zc, slot, t):
            side = side_of(zc)
            return make(
                dxp_ref.at[slot, c], via_ref.at[side], far_send.at[t], via_recv.at[side], (r, (z + 2 * side - 1) * 2 + c)
            )

        def far_copy(zc, slot, t):
            return make(dxp_ref.at[slot, c], from_ref.at[z], far_send.at[t], far_recv.at[z], (r, zc * 2 + c))

        def dgt_copy(zc, core, t):
            return make(dgt_ref.at[t, core], dgt_all.at[f], dgt_send.at[t, core], dgt_recv.at[f], (r, zc * 2 + core))

        def free_slot(t, slot):
            core_copy(z, slot, t).wait_send()
            y_copy(z, slot, t).wait_send()

            @pl.when(far(place(t)) >= 2)
            def _():
                far_copy(z, slot, t).wait_send()

        def add_ye(zc):
            make(y_core.at[zc], y_core.at[zc], yc_send.at[0], yc_recv.at[zc], mate).wait_recv()
            there = y_core.at[zc] if roomy else landed(y_core.at[zc], "core")
            add_rows(y_ref.at[zc], y_ref.at[zc], there, tokens, 64)

        do_copy(z, 0).start()

        def chunk(t, carry):
            zc = place(t)
            slot = t % 2

            @pl.when(t > 0)
            def _():
                add_ye(place(t - 1))

            k = far(zc)
            both = (t % 2 == 1) & (t <= 2 * inner)
            single = (t > 2 * inner) & jnp.logical_not(early(t - 1))
            relay(k, both | (single & (zc < z)), both | (single & (zc > z)))
            got(zc, 1 - c)

            @pl.when(t < chips - 1)
            def _():
                do_copy(place(t + 1), 1 - slot).start()

            do_copy(zc, slot).wait()

            @pl.when(t == 0)
            def _():
                load_experts.wait()

            @pl.when(t >= 2)
            def _():
                free_slot(t - 2, slot)

            picks, gates, dms = [], [], []
            at_chip = pl.multiple_of(zc * pair, 16)
            for core in range(2):
                mine = [gt_all[zc, core, pl.ds(f * local + i, 1), :] for i in range(local)]
                mine = jnp.concatenate(mine, axis=0) if local > 1 else mine[0]
                rank = jnp.where(mine >= 0.0, dot((mine >= 0.0).astype(F32).astype(BF), before), -1.0)
                chosen = [slot_index == rank[i : i + 1] for i in range(local)]
                gates.append([jnp.sum(jnp.where(chosen[i], mine[i : i + 1], 0.0), axis=1, keepdims=True) for i in range(local)])
                picks.append([one.astype(F32) for one in chosen])
                pick = jnp.concatenate([one.astype(BF) for one in picks[core]], axis=0)
                taken = dot(pick, n2_all[zc, core]).astype(BF)
                grads = dot(pick, do_buf[slot, core]) * residual_scale
                dms.append(grads)
                at = pl.ds(pl.multiple_of(at_chip + core * CAP, 16), CAP)
                for i in range(local):
                    part = slice(i * CAP, (i + 1) * CAP)
                    xs_ref[i, at] = taken[part]
                    dye_ref[i, at] = (gates[core][i] * grads[part]).astype(BF)
            at = pl.ds(at_chip, pair)
            mades, backs, values = [], [], []
            for i in range(local):
                slots = xs_ref[i, at]
                gate_pre = dot_nt(slots, ge_ref[i, :FF])
                up_pre = dot_nt(slots, ge_ref[i, FF : 2 * FF])
                grad_act = dot_nt(dye_ref[i, at], ge_ref[i, 2 * FF :])
                sigmoid = 1.0 / (1.0 + jnp.exp(-gate_pre))
                silu = gate_pre * sigmoid
                act = (silu * up_pre).astype(BF)
                hx_ref[i, at] = act
                grad_gate = (grad_act * up_pre * (sigmoid * (1.0 + gate_pre * (1.0 - sigmoid)))).astype(BF)
                grad_up = (grad_act * silu).astype(BF)
                dgu_ref[i, at, :FF] = grad_gate
                dgu_ref[i, at, FF:] = grad_up
                backs.append((dot(grad_gate, ge_ref[i, :FF]) + dot(grad_up, ge_ref[i, FF : 2 * FF])).astype(BF))
                made = dot(act, ge_ref[i, 2 * FF :]).astype(BF).astype(F32)
                mades.append(made)
                for core in range(2):
                    part = slice(core * CAP, (core + 1) * CAP)
                    value = jnp.sum(dms[core][i * CAP : (i + 1) * CAP] * made[part], axis=1, keepdims=True)
                    values.append(jnp.sum(picks[core][i] * value, axis=0, keepdims=True))
            for core in range(2):
                pick = jnp.concatenate([one.astype(BF) for one in picks[core]], axis=0)
                part = slice(core * CAP, (core + 1) * CAP)
                sent = jnp.concatenate([backs[i][part] for i in range(local)], axis=0)
                dxp_ref[slot, core] = dot_tn(pick, sent).astype(BF)
                for i in range(local):
                    dgt_ref[t, core, i : i + 1] = values[2 * i + core]
            core_copy(zc, slot, t).start()
            for core in range(2):

                @pl.when((t > 0) | (c != core))
                def _():
                    dgt_copy(zc, core, t).start()

            @pl.when(early(t))
            def _():
                k_next = t // 2 + 1
                relay(k_next, z >= k_next, z + k_next < chips)

            for core in range(2):
                pick = jnp.concatenate([one.astype(BF) for one in picks[core]], axis=0)
                part = slice(core * CAP, (core + 1) * CAP)
                sent = jnp.concatenate([(gates[core][i] * mades[i][part]).astype(BF) for i in range(local)], axis=0)
                mixed = dot_tn(pick, sent).astype(BF)

                @pl.when(c == core)
                def _():
                    y_ref[zc] = mixed

                @pl.when(c != core)
                def _():
                    yps_ref[slot] = mixed

            y_copy(zc, slot, t).start()
            core_copy(zc, slot, t).wait_recv()
            there = core_ref.at[zc] if roomy else landed(core_ref.at[zc], "core")
            own = dxp_ref.at[slot, c]

            @pl.when(k == 0)
            def _():
                dx_ref[...] = own[...].astype(F32) + there[...].astype(F32)

            @pl.when(k == 1)
            def _():
                side = side_of(zc)
                add_rows(pair_ref.at[side], own, there, tokens, 64)

                @pl.when((z == 0) | (z == chips - 1))
                def _():
                    pair_copy(side).start()

            @pl.when(k >= 2)
            def _():
                add_rows(own, own, there, tokens, 64)

                @pl.when(k == 2)
                def _():
                    via_copy(zc, slot, t).start()

                @pl.when(k > 2)
                def _():
                    far_copy(zc, slot, t).start()

            return carry

        lax.fori_loop(0, chips, chunk, 0)

        @pl.when((z > 0) & (z < chips - 1))
        def _():
            for side in range(2):
                make(via_ref.at[side], via_ref.at[side], far_send.at[0], via_recv.at[side], mate).wait_recv()
                add_rows(pair_ref.at[side], pair_ref.at[side], via_ref.at[side], tokens, 64)
                pair_copy(side).start()

        for i in range(local):
            ge_ref[i, : 2 * FF] = dot_tn(dgu_ref[i], xs_ref[i]).astype(BF)
            ge_ref[i, 2 * FF :] = dot_tn(hx_ref[i], dye_ref[i]).astype(BF)
            if bits:
                next(sums[i])
        add_ye(place(chips - 1))
        for t in range(max(chips - 2, 0), chips):
            free_slot(t, t % 2)
        for t in range(chips):
            for core in range(2):

                @pl.when((t > 0) | (c != core))
                def _():
                    dgt_copy(z, core, t).wait_send()

    slots = chips * 2 * CAP
    pl.run_scoped(
        experts_and_sums,
        pltpu.VMEM((2, 2, tokens, D), BF), pltpu.VMEM((local, slots, D), BF), pltpu.VMEM((local, slots, D), BF),
        pltpu.VMEM((local, slots, 2 * FF), BF), pltpu.VMEM((local, slots, FF), BF), pltpu.VMEM((2, 2, tokens, D), BF),
        pltpu.VMEM((2, tokens, D), BF), pltpu.VMEM((16 if roomy else tokens, D), BF),
    )

    def line(own, size, step, core_add, name, via, arrive, send_sem, via_recv, from_recv):
        def direct(k):
            return make(own(k), arrive.at[z], send_sem.at[k], from_recv.at[z], (r, k * 2 + c))

        def passing(k, side):
            return make(own(k), via.at[side], send_sem.at[k], via_recv.at[side], (r, (z + 2 * side - 1) * 2 + c))

        for d in range(chips - 1, 0, -1):
            for side in range(2):
                owner = z + (d if side else -d)

                @pl.when((owner >= 0) & (owner < chips))
                def _():
                    core_add(owner)
                    if d > 2:
                        direct(owner).start()
                    elif d == 2:
                        passing(owner, side).start()
                    else:
                        pl.when((z == 0) | (z == chips - 1))(lambda: direct(owner).start())

        core_add(z)
        yield

        @pl.when((z > 0) & (z < chips - 1))
        def _():
            for side in range(2):
                owner = z + 2 * side - 1
                make(via.at[side], via.at[side], send_sem.at[0], via_recv.at[side], mate).wait_recv()
                add_rows(own(owner), own(owner), landed(via.at[side], name), size, step)
                direct(owner).start()

        yield
        for k in range(chips):

            @pl.when((z == k + 1) | (z + 1 == k) | (z > k + 2) | (z + 2 < k))
            def _():
                make(arrive.at[k], arrive.at[k], send_sem.at[0], from_recv.at[k], mate).wait_recv()
                add_rows(own(z), own(z), landed(arrive.at[k], name), size, step)

        for k in range(chips):

            @pl.when(z != k)
            def _():
                direct(k).wait_send()

    def mixture():
        yield from line(lambda k: y_ref.at[k], tokens, 64, lambda k: None, "tokens", y_via, y_from, *y_sems)
        out_ref[...] = (h1_ref[...] + residual_scale * y_ref[z].astype(F32)).astype(BF)

    def attention(w_ref, q_ref, kd_ref, vd_ref, o_ref, p_ref, do_ref, dqkv_ref, gq_ref, go_ref, halves_stage, tokens_stage, q_stage, o_stage):
        stages["halves"] = (halves_stage, stage_sem.at[1])
        stages["tokens"] = (tokens_stage, stage_sem.at[2])
        stages["q"] = (q_stage, stage_sem.at[3])
        stages["o"] = (o_stage, stage_sem.at[4])
        loads = [
            pltpu.make_async_copy(source, target, load_sem.at[i])
            for i, (source, target) in enumerate(
                ((w_hbm, w_ref), (o_hbm, o_ref), (q_hbm, q_ref), (kd_hbm, kd_ref), (vd_hbm, vd_ref))
            )
        ]
        start(loads)

        def projection(index, name, grad_ref, core, via, arrive, sems, parts, results, wide):
            core_sem, *sems = sems
            crossing = make(grad_ref.at[:, 1 - c], core, core_sem.at[0], core_sem.at[1], mate)
            crossing.start()
            yield
            crossing.wait_recv()

            def own(k):
                return grad_ref.at[k, c]

            yield from line(
                own, rows, 16, lambda k: add_rows(own(k), own(k), core.at[k], rows, 16), name, via, arrive, *sems
            )
            crossing.wait_send()
            mine = grad_ref.at[z, c]

            def columns(part):
                return pl.ds(pl.multiple_of(part * wide, LANE), wide)

            def part_copy(d):
                to = (r + d) % replicas
                return make(
                    mine.at[:, columns(to)], parts.at[r], part_send.at[index, d], part_recv.at[index, r], (to, f)
                )

            def small_copy(d):
                to = (r + d) % replicas
                return make(mine.at[:, pl.ds(QKV, LANE)], smalls_ref.at[r], small_send.at[d], small_recv.at[r], (to, f))

            for d in range(1, replicas):
                part_copy(d).start()
                if index == 0:
                    small_copy(d).start()
            parts[r] = mine[:, columns(r)]
            if index == 0:
                smalls_ref[r] = mine[:, pl.ds(QKV, LANE)]
            yield
            for d in range(1, replicas):
                peer = (r + d) % replicas
                make(
                    parts.at[peer], parts.at[peer], part_send.at[index, d], part_recv.at[index, peer], (peer, f)
                ).wait_recv()
                if index == 0:
                    make(
                        smalls_ref.at[peer], smalls_ref.at[peer], small_send.at[d], small_recv.at[peer], (peer, f)
                    ).wait_recv()
            total = parts[0].astype(F32)
            for k in range(1, replicas):
                total = total + parts[k].astype(F32)
            results[r] = total.astype(BF)

            def result_copy(d):
                to = (r + d) % replicas
                return make(
                    results.at[r], results.at[r], result_send.at[index, d], result_recv.at[index, r], (to, f)
                )

            for d in range(1, replicas):
                result_copy(d).start()
            if index == 0:
                small = smalls_ref[0].astype(F32)
                for k in range(1, replicas):
                    small = small + smalls_ref[k].astype(F32)
                total_ref[...] = small
            yield
            for d in range(1, replicas):
                peer = (r + d) % replicas
                make(
                    results.at[peer], results.at[peer], result_send.at[index, d], result_recv.at[index, peer], (peer, f)
                ).wait_recv()
            for d in range(1, replicas):
                part_copy(d).wait_send()
                if index == 0:
                    small_copy(d).wait_send()
                result_copy(d).wait_send()

        moe = [mixture()]
        grads = [projection(0, "q", gq_ref, q_core, q_via, q_from, q_sems, pq_ref, rq_ref, QKV // replicas)]
        outs = [projection(1, "o", go_ref, o_core, o_via, o_from, o_sems, po_ref, ro_ref, D // replicas)]

        def go(*turns):
            for turn in turns:
                for process in turn:
                    next(process, None)

        def dgate():
            found = [dgt_all[k, :local] for k in range(2 * chips)]
            return jnp.concatenate(found + [jnp.zeros((LANE - E, tokens), F32)], axis=0).T

        for k in range(chips):

            @pl.when((z == k + 1) | (z + 1 == k) | (z > k + 2) | (z + 2 < k))
            def _():
                make(from_ref.at[k], from_ref.at[k], far_send.at[0], far_recv.at[k], mate).wait_recv()
                there = from_ref.at[k] if roomy else landed(from_ref.at[k], "tokens")
                add_rows(dx_ref, dx_ref, there, tokens, 64)

        for k in range(2 * chips):

            @pl.when(f == k)
            def _():
                for core in range(2):

                    @pl.when(c == core)
                    def _():
                        dgt_all[k] = dgt_ref[0, core]

            @pl.when(f != k)
            def _():
                make(dgt_all.at[k], dgt_all.at[k], dgt_send.at[0, 0], dgt_recv.at[k], mate).wait_recv()

        go(moe)
        for load in loads:
            load.wait()
        backward = attention_backward(
            x_ref, dout_ref, cos_ref, sin_ref, w_ref, q_ref, kd_ref, vd_ref, p_hbm, o_ref, h1_ref, n2_ref, gd_ref, dx_ref,
            dgate, gin_ref, gq_ref, go_ref, do_ref, dqkv_ref, p_ref, p_sem,
        )
        next(backward)
        go(outs)
        next(backward)
        go(first, outs)
        next(backward, None)
        go(grads, moe, last, grads, first, outs, last, moe, first, outs, last, grads, outs, outs, first, grads, last, grads, grads)
        go(*[moe + outs + grads + sums] * (2 * bits + 8))

    size = ge_ref.shape[1] // max(bits, 1)
    pl.run_scoped(
        attention,
        pltpu.VMEM((D, W_O + D), BF), pltpu.VMEM((tokens, D), BF), pltpu.VMEM((tokens, D), BF), pltpu.VMEM((tokens, D), BF),
        pltpu.VMEM((tokens, D), BF), pltpu.VMEM((2, 2 * tokens, tokens), F32), pltpu.VMEM((tokens, D), BF),
        pltpu.VMEM((tokens, QKV), BF), pltpu.VMEM((chips, 2, rows, W_O), BF), pltpu.VMEM((chips, 2, rows, D), BF),
        pltpu.VMEM((size // 2, D), BF), pltpu.VMEM((tokens, D), BF), pltpu.VMEM((rows, W_O), BF), pltpu.VMEM((rows, D), BF),
    )

    for e in range(local):
        copy = pltpu.make_async_copy(ge_ref.at[e], ge_hbm.at[e], ge_sem.at[e])
        if not bits:
            copy.start()
        copy.wait()
    for side in range(2):

        @pl.when(z > 0 if side == 0 else z < chips - 1)
        def _():
            pair_copy(side).wait_send()

    for k in range(chips):

        @pl.when((z >= k) & (z < chips - 1))
        def _():
            for copy in pass_on(k, "up"):
                copy.wait_send()

        @pl.when((z <= k) & (z > 0))
        def _():
            for copy in pass_on(k, "down"):
                copy.wait_send()

        for copy in pass_on(k, "mate"):
            copy.wait_send()


def finish(gexp_ref, rq_ref, ro_ref, total_ref, gin_ref, out_ref, *outs):
    layer, grad_in, gains_one, query, key, value, output, gains_two, router, expert = outs
    expert[...] = gexp_ref[...].astype(F32)

    @pl.when(pl.program_id(0) == 0)
    def _():
        layer[...] = out_ref[...]
        grad_in[...] = gin_ref[...]
        for results, targets in ((rq_ref, (query, key, value)), (ro_ref, (output,))):
            wide, start = results.shape[2], 0
            for ref in targets:
                for at in range(0, ref.shape[1], LANE):
                    part, column = divmod(start + at, wide)
                    ref[:, at : at + LANE] = results[part, :, column : column + LANE].astype(F32)
                start += ref.shape[1]
        small = total_ref[...].T
        router[...] = small[:E]
        gains_one[...] = small[E : E + 1]
        gains_two[...] = small[E + 1 : E + 2]


def call(kernel, out_shape, args, scratch=(), outside=0, out_outside=0, **params):
    spaces = [pltpu.SMEM if a.dtype == jnp.int32 and a.size <= 16 else pltpu.VMEM for a in args]
    spaces[len(args) - outside :] = [pl.ANY] * outside
    return pl.pallas_call(
        kernel,
        out_shape=out_shape,
        in_specs=[pl.BlockSpec(memory_space=space) for space in spaces],
        out_specs=[
            pl.BlockSpec(memory_space=pltpu.VMEM if i < len(out_shape) - out_outside else pl.ANY)
            for i in range(len(out_shape))
        ],
        scratch_shapes=list(scratch),
        compiler_params=pltpu.CompilerParams(
            vmem_limit_bytes=VMEM_LIMIT, has_side_effects="collective_id" in params, **params
        ),
    )(*args)


def shape(dims, dtype):
    return jax.ShapeDtypeStruct(dims, dtype)


def make_body(mesh):
    group, replicas = mesh.shape["fsdp"], mesh.shape["replica"]
    local = E // group

    def body(
        hidden_in, seq_lengths, routes, norm1_gain, w_query, w_key, w_value, w_output, norm2_gain, w_router,
        expert_weights, out_cotangent,
    ):
        tokens = hidden_in.shape[0]
        rows = w_query.shape[0]
        chips = group // 2
        dma = pltpu.SemaphoreType.DMA
        weights, q, kd, vd, o, h1, n2, gd, gt, cosines, sines, p, dout_all = call(
            functools.partial(front, replicas, chips),
            (
                shape((chips, 2, rows, W_O + D), BF), shape((tokens, D), BF), shape((tokens, D), BF),
                shape((tokens, D), BF), shape((tokens, D), BF), shape((tokens, D), F32), shape((tokens, D), BF),
                shape((tokens, LANE), F32), shape((E, tokens), F32), shape((tokens, LANE), F32),
                shape((tokens, LANE), F32), shape((KVH, 2 * tokens, tokens), F32), shape((chips, 2, tokens, D), BF),
            ),
            (
                hidden_in, seq_lengths, routes.T, rope_table(tokens), w_query, w_key, w_value, w_output, w_router.T,
                norm1_gain[None], norm2_gain[None], out_cotangent,
            ),
            [
                pltpu.VMEM((2, 2 * tokens, tokens), F32), dma((2,)), dma((1,)), dma((3, chips)), dma((3, chips)),
                dma((3, chips)), dma((3, chips, replicas)), dma((3, chips, replicas)), dma((2, chips)),
                dma((2, chips)), dma((3, chips)), dma((chips, 2)),
            ],
            out_outside=2,
            collective_id=2,
        )
        weights = weights.reshape(D, W_O + D)
        bits = replicas.bit_length() - 1
        size = 3 * FF // bits if bits else 0
        roomy = chips <= 4
        landing = [shape((local * bits, size >> (k + 1), D), BF) for k in range(bits)]
        blocks = [shape((chips, tokens, D), BF)] * 3
        if not roomy:
            landing += blocks
        outs = call(
            functools.partial(back, replicas, chips),
            [
                shape((tokens, D), F32), shape((tokens, D), BF), shape((replicas, rows, QKV // replicas), BF),
                shape((replicas, rows, D // replicas), BF), shape((rows, LANE), F32), shape((local, 3 * FF, D), BF),
                shape((2, tokens, D), BF), shape((chips, tokens, D), BF), shape((2, rows, W_O), BF),
                shape((chips, rows, W_O), BF), shape((2, rows, D), BF), shape((chips, rows, D), BF),
            ]
            + landing,
            (
                hidden_in, out_cotangent, cosines, sines, h1, n2, gd, gt,
                dout_all, expert_weights, weights, q, kd, vd, o, p,
            ),
            [
                pltpu.VMEM((local, 3 * FF, D), BF), pltpu.VMEM((chips, 2, tokens, D), BF),
                pltpu.VMEM((chips, 2, E, tokens), F32), pltpu.VMEM((2, tokens, D), BF), pltpu.VMEM((2, tokens, D), BF),
                pltpu.VMEM((tokens, D), F32), pltpu.VMEM((chips, 2, 8, tokens), F32), pltpu.VMEM((group, 8, tokens), F32),
                pltpu.VMEM((chips, tokens, D), BF), pltpu.VMEM((chips, rows, W_O), BF), pltpu.VMEM((chips, rows, D), BF),
                pltpu.VMEM((replicas, rows, QKV // replicas), BF), pltpu.VMEM((replicas, rows, D // replicas), BF),
                pltpu.VMEM((replicas, rows, LANE), BF),
            ]
            + ([pltpu.VMEM(b.shape, b.dtype) for b in blocks] if roomy else [])
            + ([dma((chips,))] * 3 + [dma((chips, 2))]) * 2 + [dma((chips,))] * 4 + [dma((2,))] * 2
            + [dma((chips, 2)), dma((group,)), dma((chips,)), dma((chips,))]
            + [dma((2,)), dma((1,)), dma((5,)), dma((5,)), dma((local,)), dma((2,))]
            + [dma((max(local * bits, 1), max(2 * bits, 1)))] * 2
            + [pltpu.SemaphoreType.REGULAR((max(local * bits, 1), max(bits, 1)))]
            + [dma((chips,)), dma((2,)), dma((chips,))] + [dma((2,)), dma((chips,)), dma((2,)), dma((chips,))] * 2
            + [dma((2, replicas))] * 2 + [dma((replicas,))] * 2 + [dma((2, replicas))] * 2,
            outside=8,
            out_outside=7 + len(landing),
            collective_id=0,
        )
        grad_in, layer_out, result_q, result_o, total, grad_experts = outs[:6]
        steps = 8
        block = local * 3 * FF // steps
        fixed = [
            shape((tokens, D), BF), shape((tokens, D), F32), shape((1, rows), F32), shape((rows, H * HD), F32),
            shape((rows, KVH * HD), F32), shape((rows, KVH * HD), F32), shape((rows, D), F32), shape((1, rows), F32),
            shape((E, rows), F32),
        ]

        def still(a):
            return pl.BlockSpec(a.shape, lambda i: (0,) * len(a.shape))

        expert_block = pl.BlockSpec((block, D), lambda i: (i, 0))
        outs = pl.pallas_call(
            finish,
            grid=(steps,),
            in_specs=[
                expert_block, still(result_q), still(result_o), still(total), still(grad_in), still(layer_out)
            ],
            out_specs=[still(a) for a in fixed] + [expert_block],
            out_shape=fixed + [shape((local * 3 * FF, D), F32)],
            compiler_params=pltpu.CompilerParams(vmem_limit_bytes=VMEM_LIMIT),
        )(grad_experts.reshape(local * 3 * FF, D), result_q, result_o, total, grad_in, layer_out)
        return (
            outs[0], outs[1], outs[2][0], outs[3], outs[4], outs[5], outs[6], outs[7][0], outs[8].T,
            outs[9].reshape(local, 3 * FF, D),
        )

    return body


def solution(mesh):
    tokens, weights = P(("replica", "fsdp"), None), P("fsdp", None)
    return jax.shard_map(
        make_body(mesh),
        mesh=mesh,
        in_specs=(
            tokens, tokens, tokens, P("fsdp"), weights, weights, weights, weights, P("fsdp"), weights,
            P("fsdp", None, None), tokens,
        ),
        out_specs=(
            tokens, tokens, P("fsdp"), weights, weights, weights, weights, P("fsdp"), weights, P("fsdp", None, None),
        ),
        check_vma=False,
    )
```

```python
import functools

import jax
import jax.numpy as jnp
import numpy as np
from jax import lax
from jax.experimental import pallas as pl
from jax.experimental.pallas import tpu as pltpu
from jax.sharding import PartitionSpec as P

D = 1024
H = 16
KVH = 8
HD = 64
FF = 512
TOPK = 8
E = 16
CAP = 144
LANE = 128
QKV = H * HD + 2 * KVH * HD
QKVO = QKV + D
W_O = QKV + LANE

norm_eps = 1e-06
score_scale = 0.015625
residual_scale = 0.22
rope_base = 10000.0
masked_score = -1e30

BF = jnp.bfloat16
F32 = jnp.float32
VMEM_LIMIT = 63 * 2**20


def dot(a, b):
    return lax.dot_general(a, b, (((1,), (0,)), ((), ())), preferred_element_type=F32)


def dot_nt(a, b):
    return lax.dot_general(a, b, (((1,), (1,)), ((), ())), preferred_element_type=F32)


def dot_tn(a, b):
    return lax.dot_general(a, b, (((0,), (0,)), ((), ())), preferred_element_type=F32)


def lanes_of(rows):
    return lax.broadcasted_iota(jnp.int32, (rows, LANE), 1)


def turned(block, lane):
    return jnp.where(lane % HD < HD // 2, pltpu.roll(block, LANE - HD // 2, 1), pltpu.roll(block, HD // 2, 1))


def halves(block, low):
    zero = jnp.zeros_like(block)
    return jnp.concatenate([jnp.where(low, block, zero), jnp.where(low, zero, block)], axis=0)


def rope_table(tokens):
    frequency = np.float32(rope_base) ** (-np.arange(0, HD, 2, dtype=np.float32) / np.float32(HD))
    frequency = np.tile(frequency.astype(np.float32), LANE // (HD // 2))
    angles = (np.arange(tokens, dtype=np.float32)[:, None] * frequency[None, :]).astype(np.float64)
    sign = np.where(np.arange(LANE) % HD < HD // 2, -1.0, 1.0)
    pieces = []
    for values in (np.cos(angles), np.sin(angles) * sign[None, :]):
        rest = values.astype(np.float32)
        for _ in range(3):
            piece = rest.astype(BF)
            pieces.append(piece)
            rest = rest - piece.astype(np.float32)
    return np.concatenate(pieces, axis=1)


class Copies:
    def make(self, src, dst, send, recv, device):
        return pltpu.make_async_remote_copy(
            src_ref=src, dst_ref=dst, send_sem=send, recv_sem=recv, device_id=device, device_id_type=pl.DeviceIdType.MESH
        )


def meet(devices, expected):
    barrier = pltpu.get_barrier_semaphore()
    for condition, device in devices:

        def signal(device=device):
            pl.semaphore_signal(barrier, inc=1, device_id=device, device_id_type=pl.DeviceIdType.MESH)

        if condition is True:
            signal()
        else:
            pl.when(condition)(signal)
    pl.semaphore_wait(barrier, expected)


def attention_backward(
    x_ref, dout_ref, cos_ref, sin_ref, columns, q_ref, kd_ref, vd_ref, p_hbm, o_ref, h1_ref, n2_ref, gd_ref, dx_ref, dgate,
    gin_ref, gq_ref, gkv_ref, go_ref, do_ref, dqkv_ref, p_ref, p_sem,
):
    tokens = x_ref.shape[0]
    lane = lanes_of(tokens)
    low = lane < HD

    def p_copy(g):
        return pltpu.make_async_copy(p_hbm.at[g], p_ref.at[g % 2], p_sem.at[g % 2])

    p_copy(0).start()

    def put(ref, at, value):
        ref[:, :, :, at] = value.astype(BF).reshape(*ref.shape[:3], value.shape[1])

    small = columns(QKV, LANE).astype(F32).T
    gain_one, gain_two = small[E : E + 1], small[E + 1 : E + 2]
    after = h1_ref[...]
    factor_two = lax.rsqrt(jnp.mean(after * after, axis=1, keepdims=True) + norm_eps)
    gates = jnp.maximum(gd_ref[...], 0.0)
    grad_gates = dgate()
    chosen = gates * (grad_gates - jnp.sum(gates * grad_gates, axis=1, keepdims=True))
    grad_logits = chosen.astype(BF)
    grad_normed = dx_ref[...] + dot_nt(grad_logits, columns(QKV, LANE))
    scaled = grad_normed * gain_two
    grad_after = dout_ref[...].astype(F32) + (
        factor_two * scaled - after * factor_two**3 * jnp.mean(scaled * after, axis=1, keepdims=True)
    )
    grad_gain_two = jnp.sum(grad_normed * after * factor_two, axis=0, keepdims=True)
    gin_ref[...] = grad_after
    grad_branch = (residual_scale * grad_after).astype(BF)
    for at in range(0, D, FF):
        put(go_ref, slice(at, at + FF), dot_tn(o_ref[...], grad_branch[:, at : at + FF]))
    do_ref[...] = dot_nt(grad_branch, columns(W_O, D)).astype(BF)
    grad_router = dot_tn(n2_ref[...], grad_logits)
    yield

    cosines, sines = cos_ref[...], sin_ref[...]
    key_back, value_back = [], []
    for g in range(KVH):
        at = slice(g * LANE, (g + 1) * LANE)
        queries = halves(q_ref[:, at].astype(F32), low).astype(BF)
        outs = halves(do_ref[:, at].astype(F32), low).astype(BF)
        if g + 1 < KVH:
            p_copy(g + 1).start()
        p_copy(g).wait()
        weights = p_ref[g % 2]
        grad_weights = dot_nt(outs, vd_ref[:, at])
        total = jnp.sum(weights * grad_weights, axis=1, keepdims=True)
        grad_scores = (weights * (grad_weights - total)).astype(BF)
        block = dot(grad_scores, kd_ref[:, at])
        block = jnp.where(low, block[:tokens], block[tokens:]) * score_scale
        dqkv_ref[:, at] = (block * cosines - turned(block, lane) * sines).astype(BF)
        block = dot_tn(grad_scores, queries) * score_scale
        key_back.append(block + pltpu.roll(block, HD, 1))
        block = dot_tn(weights.astype(BF), outs)
        value_back.append(block + pltpu.roll(block, HD, 1))
    for m in range(KVH // 2):
        block = jnp.where(low, key_back[2 * m], key_back[2 * m + 1])
        at = slice(H * HD + m * LANE, H * HD + (m + 1) * LANE)
        dqkv_ref[:, at] = (block * cosines - turned(block, lane) * sines).astype(BF)
        at = slice(H * HD + KVH * HD + m * LANE, H * HD + KVH * HD + (m + 1) * LANE)
        dqkv_ref[:, at] = jnp.where(low, value_back[2 * m], value_back[2 * m + 1]).astype(BF)
    yield

    source = x_ref[...].astype(F32)
    factor_one = lax.rsqrt(jnp.mean(source * source, axis=1, keepdims=True) + norm_eps)
    normed = (source * factor_one * gain_one).astype(BF)
    for at in range(0, H * HD, FF):
        put(gq_ref, slice(at, at + FF), dot_tn(normed, dqkv_ref[:, at : at + FF]))
    yield
    grad_normed = dot_nt(dqkv_ref[...], columns(0, QKV))
    scaled = grad_normed * gain_one
    grad_vector = factor_one * scaled - source * factor_one**3 * jnp.mean(scaled * source, axis=1, keepdims=True)
    gin_ref[...] += grad_vector
    grad_gain_one = jnp.sum(grad_normed * source * factor_one, axis=0, keepdims=True)
    gains = jnp.concatenate([grad_gain_one, grad_gain_two, jnp.zeros((6, D), F32)], axis=0).T
    at = lanes_of(D)
    extra = jnp.where(at == E, gains[:, 0:1], jnp.where(at == E + 1, gains[:, 1:2], grad_router))
    put(gkv_ref, slice(D, D + LANE), extra)
    for at in range(0, QKV - H * HD, FF):
        put(gkv_ref, slice(at, at + FF), dot_tn(normed, dqkv_ref[:, H * HD + at : H * HD + at + FF]))


def add_rows(target, first, second, rows, step):
    def some(i, carry):
        at = pl.ds(pl.multiple_of(i * step, step), step)
        target[at] = (first[at].astype(F32) + second[at].astype(F32)).astype(target.dtype)
        return carry

    lax.fori_loop(0, rows // step, some, 0)


def layer(
    replicas, chips,
    x_ref, len_ref, routes_ref, table_ref, wq_ref, wk_ref, wv_ref, wo_ref, wr_ref, g1_ref, g2_ref, dout_ref, we_hbm,
    gin_ref, out_ref, results_ref, total_ref, ge_hbm, p_hbm, heads_hbm, do_all, y_via, y_from, kv_via, kv_from, q_via, q_from,
    o_via, o_from, *rest,
):
    bits = replicas.bit_length() - 1
    roomy = chips <= 4
    arrived, y_core, rest = rest[:bits], rest[bits], rest[bits + 1 :]
    if not roomy:
        (core_ref, from_ref), rest = rest[:2], rest[2:]
    (w_all, h1_ref, gd_ref, cos_ref, sin_ref), rest = rest[:5], rest[5:]
    (heads_sem, own_sem, z_up, z_down, z_recv, xy_send, xy_recv, mate_send, mate_recv, do_send, do_recv), rest = rest[:11], rest[11:]
    (ge_ref, n2_all, gt_all, via_ref, pair_ref, dgt_ref, dgt_all, y_ref, kv_core, q_core, o_core, parts_ref, smalls_ref), rest = (
        rest[:13], rest[13:]
    )
    dx_ref = gin_ref
    if roomy:
        (core_ref, from_ref), rest = rest[:2], rest[2:]
    (n2_up, n2_down, n2_mate, n2_recv, gt_up, gt_down, gt_mate, gt_recv,
     core_send, core_recv, far_send, far_recv, pair_send, via_recv, dgt_send, dgt_recv, yc_send, yc_recv,
     do_sem, we_sem, stage_sem, ge_sem, p_sem, ar_send, ar_recv, ar_free,
     *sum_sems, part_send, part_recv, small_send, small_recv, result_send, result_recv) = rest
    y_sems, kv_sems, q_sems, o_sems = sum_sems[:3], sum_sems[3:7], sum_sems[7:11], sum_sems[11:]
    local, tokens, rows = ge_ref.shape[0], x_ref.shape[0], q_core.shape[1]
    r, f = lax.axis_index("replica"), lax.axis_index("fsdp")
    z, c = f // 2, f % 2
    mate, above, below = (r, z * 2 + 1 - c), (r, f + 2), (r, f - 2)
    make = Copies().make

    load_experts = pltpu.make_async_copy(we_hbm, ge_ref, we_sem.at[0])
    load_experts.start()
    own_dout = pltpu.make_async_copy(dout_ref, do_all.at[z, c], own_sem.at[0])
    own_dout.start()
    packed = [wr_ref[...].astype(F32), g1_ref[...].astype(F32), g2_ref[...].astype(F32)]
    packed = jnp.concatenate(packed + [jnp.zeros((LANE - E - 2, rows), F32)], axis=0)
    own = w_all.at[z, c]
    own[:, : H * HD] = wq_ref[...]
    own[:, H * HD : H * HD + KVH * HD] = wk_ref[...]
    own[:, H * HD + KVH * HD : QKV] = wv_ref[...]
    own[:, QKV:W_O] = packed.T.astype(BF)
    own[:, W_O:] = wo_ref[...]
    peers = [(True, mate)]
    for k in range(1, chips):
        to = (z + k) % chips
        peers += [(True, (r, to * 2 + c)), (True, (r, to * 2 + 1 - c))]
    peers += [(True, ((r + d) % replicas, f)) for d in range(1, replicas)]
    meet(peers, len(peers))

    def part(kind):
        if kind == 0:
            return pl.ds(pl.multiple_of(r * (QKV // replicas), LANE), QKV // replicas)
        if kind == 1:
            return pl.ds(QKV, LANE)
        return pl.ds(pl.multiple_of(W_O + r * (D // replicas), LANE), D // replicas)

    def along(zb, kind, up):
        ref = w_all.at[zb, c, :, part(kind)]
        return make(ref, ref, (z_up if up else z_down).at[kind, zb], z_recv.at[kind, zb], above if up else below)

    def across(zb, kind, d):
        ref = w_all.at[zb, c, :, part(kind)]
        return make(ref, ref, xy_send.at[kind, zb, d], xy_recv.at[kind, zb, r], ((r + d) % replicas, f))

    def wait_across(zb, kind):
        for d in range(1, replicas):
            peer = (r + d) % replicas
            ref = w_all.at[zb, c, :, part(kind)]
            make(ref, ref, xy_send.at[kind, zb, d], xy_recv.at[kind, zb, peer], (peer, f)).wait_recv()

    def to_mate(zb, core, late):
        ref = w_all.at[zb, core, :, pl.ds(W_O, D) if late else pl.ds(0, W_O)]
        return make(ref, ref, mate_send.at[late, zb], mate_recv.at[late, zb], mate)

    def dout_copy(zb, core, way):
        source = do_all.at[zb, core]
        return make(source, do_all.at[zb, core], do_send.at[way, zb], do_recv.at[zb, core], (above, below, mate)[way])

    def both_sides(k, act):
        @pl.when(z >= k)
        def _():
            act(z - k, True)

        @pl.when(z < chips - k)
        def _():
            act(z + k, False)

    def onward(up):
        return z < chips - 1 if up else z > 0

    def dout_arrive(zb, low):
        dout_copy(zb, c, 0 if low else 1).wait_recv()

        @pl.when(onward(low))
        def _():
            dout_copy(zb, c, 0 if low else 1).start()

        dout_copy(zb, c, 2).start()

    def columns(start, size):
        return w_all.reshape(D, W_O + D)[:, start : start + size]

    def forward(p_ref, q_ref, kd_ref, vd_ref, o_ref):
        for kind in range(3):
            both_sides(1, lambda zb, low: along(z, kind, not low).start())
        for late in range(2):
            to_mate(z, c, late).start()

        source = x_ref[...].astype(F32)
        factor = lax.rsqrt(jnp.mean(source * source, axis=1, keepdims=True) + norm_eps)
        lane = lanes_of(tokens)
        low_lane = lane < HD
        row = lax.broadcasted_iota(jnp.int32, (tokens, tokens), 0)
        column = lax.broadcasted_iota(jnp.int32, (tokens, tokens), 1)
        row_at = lax.broadcasted_iota(jnp.int32, (tokens, 1), 0)
        column_at = lax.broadcasted_iota(jnp.int32, (1, tokens), 1)
        row_segment = jnp.zeros((tokens, 1), jnp.int32)
        row_start = jnp.zeros((tokens, 1), jnp.int32)
        column_segment = jnp.zeros((1, tokens), jnp.int32)
        end = jnp.int32(0)
        for j in range(len_ref.shape[1]):
            end = end + len_ref[0, j]
            row_segment += (row_at >= end).astype(jnp.int32)
            row_start = jnp.maximum(row_start, jnp.where(row_at >= end, end, 0))
            column_segment += (column_at >= end).astype(jnp.int32)
        place = (column == row - row_start).astype(F32).astype(BF)
        found = dot(place, table_ref[...])
        found = [found[:, i * LANE : (i + 1) * LANE] for i in range(6)]
        cosines, sines = found[0] + found[1] + found[2], found[3] + found[4] + found[5]
        cos_ref[...] = cosines
        sin_ref[...] = sines

        own_dout.wait()
        for k in range(1, chips):
            for kind in range(3):

                def arrive(zb, low, kind=kind):
                    along(zb, kind, low).wait_recv()

                    @pl.when(onward(low))
                    def _():
                        along(zb, kind, low).start()

                    if kind != 1:
                        for d in range(1, replicas):
                            across(zb, kind, d).start()

                both_sides(k, arrive)
            if k == 1:
                both_sides(1, lambda zb, low: dout_copy(z, c, 1 if low else 0).start())
                dout_copy(z, c, 2).start()

        def share(k, late):
            def act(zb, low):
                wait_across(zb, 2 if late else 0)
                to_mate(zb, c, late).start()

            both_sides(k, act)

        for k in range(1, chips):
            share(k, 0)
        if chips > 1:
            both_sides(1, dout_arrive)
        for k in range(chips):
            to_mate(k, 1 - c, 0).wait_recv()

        small = columns(QKV, LANE)
        gains = small.astype(F32).T
        gain_one, gain_two = gains[E : E + 1], gains[E + 1 : E + 2]
        normed = (source * factor * gain_one).astype(BF)
        q_all = dot(normed, columns(0, H * HD))
        for g in range(H // 2):
            at = slice(g * LANE, (g + 1) * LANE)
            block = q_all[:, at]
            q_ref[:, at] = (block * cosines + turned(block, lane) * sines).astype(BF)
        kv = dot(normed, columns(H * HD, 2 * KVH * HD))
        for m in range(KVH // 2):
            block = kv[:, m * LANE : (m + 1) * LANE]
            block = block * cosines + turned(block, lane) * sines
            other = pltpu.roll(block, HD, 1)
            kd_ref[:, 2 * m * LANE : (2 * m + 1) * LANE] = jnp.where(low_lane, block, other).astype(BF)
            kd_ref[:, (2 * m + 1) * LANE : (2 * m + 2) * LANE] = jnp.where(low_lane, other, block).astype(BF)
            block = kv[:, KVH * HD + m * LANE : KVH * HD + (m + 1) * LANE]
            other = pltpu.roll(block, HD, 1)
            vd_ref[:, 2 * m * LANE : (2 * m + 1) * LANE] = jnp.where(low_lane, block, other).astype(BF)
            vd_ref[:, (2 * m + 1) * LANE : (2 * m + 2) * LANE] = jnp.where(low_lane, other, block).astype(BF)
        saves = [
            pltpu.make_async_copy(ref, heads_hbm.at[i], heads_sem.at[i]) for i, ref in enumerate((q_ref, kd_ref, vd_ref, o_ref))
        ]
        for save in saves[:3]:
            save.start()
        bias = jnp.where((row_segment == column_segment) & (column <= row), 0.0, masked_score)
        bias = jnp.concatenate([bias, bias], axis=0)

        def p_copy(g):
            return pltpu.make_async_copy(p_ref.at[g % 2], p_hbm.at[g], p_sem.at[g % 2])

        for g in range(KVH):
            at = slice(g * LANE, (g + 1) * LANE)
            queries = halves(q_ref[:, at].astype(F32), low_lane).astype(BF)
            scores = dot_nt(queries, kd_ref[:, at]) * score_scale + bias
            shifted = jnp.exp(scores - jnp.max(scores, axis=1, keepdims=True))
            weights = shifted * (1.0 / jnp.sum(shifted, axis=1, keepdims=True))
            if g >= 2:
                p_copy(g - 2).wait()
            p_ref[g % 2] = weights
            p_copy(g).start()
            mixed = dot(weights.astype(BF), vd_ref[:, at])
            o_ref[:, at] = jnp.where(low_lane, mixed[:tokens], mixed[tokens:]).astype(BF)

        saves[3].start()
        if chips > 2:
            both_sides(2, dout_arrive)
        for k in range(1, chips):
            share(k, 1)

        for k in range(chips):
            to_mate(k, 1 - c, 1).wait_recv()
        after = source + residual_scale * dot(o_ref[...], columns(W_O, D))
        h1_ref[...] = after
        factor = lax.rsqrt(jnp.mean(after * after, axis=1, keepdims=True) + norm_eps)
        normed = (after * factor * gain_two).astype(BF)
        n2_all[z, c] = normed
        logits = dot(normed, small).T[:E]
        expert = lax.broadcasted_iota(jnp.int32, (E, tokens), 0)
        routed = routes_ref[0:1] == expert
        for j in range(1, TOPK):
            routed |= routes_ref[j : j + 1] == expert
        top = jnp.max(jnp.where(routed, logits, masked_score), axis=0, keepdims=True)
        powers = jnp.where(routed, jnp.exp(logits - top), 0.0)
        gates = powers / jnp.sum(powers, axis=0, keepdims=True)
        gates = jnp.where(routed, gates, -1.0)
        gt_all[z, c] = gates
        gd_ref[...] = jnp.concatenate([gates, jnp.full((LANE - E, tokens), -1.0, F32)], axis=0).T
        for g in (KVH - 2, KVH - 1):
            p_copy(g).wait()
        for save in saves:
            save.wait()

    pl.run_scoped(forward, pltpu.VMEM((2, 2 * tokens, tokens), F32), *[pltpu.VMEM((tokens, D), BF)] * 4)

    def bit_of(b):
        return (r // (1 << b)) % 2

    def partner(b):
        return (r + (1 - 2 * bit_of(b)) * (1 << b), f)

    stages = {}

    def landed(ref, name):
        stage, sem = stages[name]
        if ref.shape != stage.shape:
            stage = stage.at[pl.ds(0, ref.shape[0])]
        copy = pltpu.make_async_copy(ref, stage, sem)
        copy.start()
        copy.wait()
        return stage

    def halving(e):
        size = ge_ref.shape[1] // bits
        orders = [[(g + k) % bits for k in range(bits)] for g in range(bits)]
        starts = [[] for _ in range(bits)]
        for g in range(bits):
            at = g * size
            for k in range(bits):
                starts[g].append(at)
                at = at + bit_of(orders[g][k]) * (size >> (k + 1))
            starts[g].append(at)

        def region(g, k):
            half = size >> (k + 1)
            return ge_ref.at[e, pl.ds(pl.multiple_of(starts[g][k + 1], half), half)]

        def exchange(g, k):
            half, job = size >> (k + 1), e * bits + g
            give = pl.multiple_of(starts[g][k] + (1 - bit_of(orders[g][k])) * half, half)
            return make(
                ge_ref.at[e, pl.ds(give, half)], arrived[k].at[job], ar_send.at[job, k], ar_recv.at[job, k],
                partner(orders[g][k]),
            )

        def spread(g, k):
            job, ref = e * bits + g, region(g, k)
            return make(ref, ref, ar_send.at[job, bits + k], ar_recv.at[job, bits + k], partner(orders[g][k]))

        def spread_once_free(g, k):
            pl.semaphore_wait(ar_free.at[e * bits + g, k], 1)
            spread(g, k).start()

        yield
        for g in range(bits):
            exchange(g, 0).start()
        yield
        for k in range(bits):
            half = size >> (k + 1)
            for g in range(bits):
                job = e * bits + g
                exchange(g, k).wait_recv()
                own = region(g, k)
                add_rows(own, own, landed(arrived[k].at[job], "halves"), half, min(half, 64))
                if k < bits - 1:
                    exchange(g, k + 1).start()
                exchange(g, k).wait_send()
                pl.semaphore_signal(
                    ar_free.at[job, k], inc=1, device_id=partner(orders[g][k]), device_id_type=pl.DeviceIdType.MESH
                )
                if k == bits - 1:
                    spread_once_free(g, k)
            yield
        for k in range(bits - 1, -1, -1):
            for g in range(bits):
                spread(g, k).wait_recv()
                if k > 0:
                    spread_once_free(g, k - 1)
            yield
        for g in range(bits):
            for k in range(bits):
                spread(g, k).wait_send()
        pltpu.make_async_copy(ge_ref.at[e], ge_hbm.at[e], ge_sem.at[e]).start()

    sums = [halving(e) for e in range(local)] if bits else []
    first, last = sums[:1], sums[1:]
    for process in sums:
        next(process)

    def pass_on(zb, how):
        to = {"up": above, "down": below, "mate": mate}[how]
        sems = {"up": (n2_up, gt_up), "down": (n2_down, gt_down), "mate": (n2_mate, gt_mate)}[how]
        return [
            make(ref.at[zb, c], ref.at[zb, c], sem.at[zb], recv.at[zb, c], to)
            for ref, sem, recv in ((gt_all, sems[1], gt_recv), (n2_all, sems[0], n2_recv))
        ]

    def got(zb, core):
        for ref, sem, recv in ((gt_all, gt_mate, gt_recv), (n2_all, n2_mate, n2_recv)):
            make(ref.at[zb, core], ref.at[zb, core], sem.at[zb], recv.at[zb, core], mate).wait_recv()

    def start(copies):
        for copy in copies:
            copy.start()

    @pl.when(z < chips - 1)
    def _():
        start(pass_on(z, "up"))

    @pl.when(z > 0)
    def _():
        start(pass_on(z, "down"))

    start(pass_on(z, "mate"))
    inner = jnp.minimum(z, chips - 1 - z)

    def place(t):
        k = (t + 1) // 2
        near = jnp.where(t % 2 == 1, z - k, z + k)
        return jnp.where(t <= 2 * inner, near, jnp.where(2 * z < chips - 1, t, chips - 1 - t))

    def far(zc):
        return jnp.where(zc > z, zc - z, z - zc)

    def side_of(zc):
        return jnp.where(zc > z, 1, 0)

    def relay(k, low, high):
        @pl.when(low)
        def _():
            pl.when(k > 2)(lambda: dout_arrive(z - k, True))
            got(z - k, c)

            @pl.when(z < chips - 1)
            def _():
                start(pass_on(z - k, "up"))

            start(pass_on(z - k, "mate"))

        @pl.when(high)
        def _():
            pl.when(k > 2)(lambda: dout_arrive(z + k, False))
            got(z + k, c)

            @pl.when(z > 0)
            def _():
                start(pass_on(z + k, "down"))

            start(pass_on(z + k, "mate"))

    def early(t):
        return (t >= 2) & (t % 2 == 0) & (t <= 2 * inner) & (t < chips - 1)

    def pair_copy(side):
        owner = z + 2 * side - 1
        return make(pair_ref.at[side], from_ref.at[z], pair_send.at[side], far_recv.at[z], (r, owner * 2 + c))

    def experts_and_sums(do_buf, xs_ref, dye_ref, dgu_ref, hx_ref, dxp_ref, yps_ref, core_stage):
        stages["core"] = (core_stage, stage_sem.at[0])
        before = lax.broadcasted_iota(jnp.int32, (tokens, tokens), 0) < lax.broadcasted_iota(jnp.int32, (tokens, tokens), 1)
        before = before.astype(F32).astype(BF)
        slot_index = lax.broadcasted_iota(jnp.int32, (CAP, tokens), 0).astype(F32)
        pair = 2 * CAP

        def do_copy(zc):
            return pltpu.make_async_copy(do_all.at[zc], do_buf, do_sem.at[0])

        def core_copy(zc, slot, t):
            return make(dxp_ref.at[slot, 1 - c], core_ref.at[zc], core_send.at[t], core_recv.at[zc], mate)

        def y_copy(zc, slot, t):
            return make(yps_ref.at[slot], y_core.at[zc], yc_send.at[t], yc_recv.at[zc], mate)

        def via_copy(zc, slot, t):
            side = side_of(zc)
            return make(
                dxp_ref.at[slot, c], via_ref.at[side], far_send.at[t], via_recv.at[side], (r, (z + 2 * side - 1) * 2 + c)
            )

        def far_copy(zc, slot, t):
            return make(dxp_ref.at[slot, c], from_ref.at[z], far_send.at[t], far_recv.at[z], (r, zc * 2 + c))

        def dgt_copy(zc, core, t):
            return make(dgt_ref.at[t, core], dgt_all.at[f], dgt_send.at[t, core], dgt_recv.at[f], (r, zc * 2 + core))

        def free_slot(t, slot):
            core_copy(z, slot, t).wait_send()
            y_copy(z, slot, t).wait_send()

            @pl.when(far(place(t)) >= 2)
            def _():
                far_copy(z, slot, t).wait_send()

        def add_ye(zc):
            make(y_core.at[zc], y_core.at[zc], yc_send.at[0], yc_recv.at[zc], mate).wait_recv()
            add_rows(y_ref.at[zc], y_ref.at[zc], landed(y_core.at[zc], "core"), tokens, 64)
            send_sem, _, from_recv = y_sems


        def chunk(t, carry):
            zc = place(t)
            slot = t % 2

            @pl.when(t > 0)
            def _():
                add_ye(place(t - 1))

            k = far(zc)
            both = (t % 2 == 1) & (t <= 2 * inner)
            single = (t > 2 * inner) & jnp.logical_not(early(t - 1))
            relay(k, both | (single & (zc < z)), both | (single & (zc > z)))
            dout_copy(zc, 1 - c, 2).wait_recv()
            do_copy(zc).start()
            got(zc, 1 - c)
            do_copy(zc).wait()

            @pl.when(t == 0)
            def _():
                load_experts.wait()

            @pl.when(t >= 2)
            def _():
                free_slot(t - 2, slot)

            picks, gates, dms = [], [], []
            at_chip = pl.multiple_of(zc * pair, 16)
            for core in range(2):
                mine = [gt_all[zc, core, pl.ds(f * local + i, 1), :] for i in range(local)]
                mine = jnp.concatenate(mine, axis=0) if local > 1 else mine[0]
                rank = jnp.where(mine >= 0.0, dot((mine >= 0.0).astype(F32).astype(BF), before), -1.0)
                chosen = [slot_index == rank[i : i + 1] for i in range(local)]
                gates.append([jnp.sum(jnp.where(chosen[i], mine[i : i + 1], 0.0), axis=1, keepdims=True) for i in range(local)])
                picks.append([one.astype(F32) for one in chosen])
                pick = jnp.concatenate([one.astype(BF) for one in picks[core]], axis=0)
                taken = dot(pick, n2_all[zc, core]).astype(BF)
                grads = dot(pick, do_buf[core])
                dms.append(grads.astype(BF))
                grads = grads * residual_scale
                at = pl.ds(pl.multiple_of(at_chip + core * CAP, 16), CAP)
                for i in range(local):
                    part = slice(i * CAP, (i + 1) * CAP)
                    xs_ref[i, at] = taken[part]
                    dye_ref[i, at] = (gates[core][i] * grads[part]).astype(BF)
            at = pl.ds(at_chip, pair)
            mades, backs, values = [], [], []
            for i in range(local):
                slots = xs_ref[i, at]
                gate_pre = dot_nt(slots, ge_ref[i, :FF])
                up_pre = dot_nt(slots, ge_ref[i, FF : 2 * FF])
                grad_act = dot_nt(dye_ref[i, at], ge_ref[i, 2 * FF :])
                sigmoid = 1.0 / (1.0 + jnp.exp(-gate_pre))
                silu = gate_pre * sigmoid
                act = (silu * up_pre).astype(BF)
                hx_ref[i, at] = act
                grad_gate = (grad_act * up_pre * (sigmoid * (1.0 + gate_pre * (1.0 - sigmoid)))).astype(BF)
                grad_up = (grad_act * silu).astype(BF)
                dgu_ref[i, at, :FF] = grad_gate
                dgu_ref[i, at, FF:] = grad_up
                backs.append((dot(grad_gate, ge_ref[i, :FF]) + dot(grad_up, ge_ref[i, FF : 2 * FF])).astype(BF))
                made = dot(act, ge_ref[i, 2 * FF :]).astype(BF)
                mades.append(made)
                for core in range(2):
                    part = slice(core * CAP, (core + 1) * CAP)
                    grads = dms[core][i * CAP : (i + 1) * CAP].astype(F32) * residual_scale
                    value = jnp.sum(grads * made[part].astype(F32), axis=1, keepdims=True)
                    values.append(jnp.sum(picks[core][i] * value, axis=0, keepdims=True))
            for core in range(2):
                pick = jnp.concatenate([one.astype(BF) for one in picks[core]], axis=0)
                part = slice(core * CAP, (core + 1) * CAP)
                sent = jnp.concatenate([backs[i][part] for i in range(local)], axis=0)
                dxp_ref[slot, core] = dot_tn(pick, sent).astype(BF)
                for i in range(local):
                    dgt_ref[t, core, i : i + 1] = values[2 * i + core]
            core_copy(zc, slot, t).start()
            for core in range(2):

                @pl.when((t > 0) | (c != core))
                def _():
                    dgt_copy(zc, core, t).start()

            @pl.when(early(t))
            def _():
                k_next = t // 2 + 1
                relay(k_next, z >= k_next, z + k_next < chips)

            for core in range(2):
                pick = jnp.concatenate([one.astype(BF) for one in picks[core]], axis=0)
                part = slice(core * CAP, (core + 1) * CAP)
                sent = jnp.concatenate([(gates[core][i] * mades[i][part].astype(F32)).astype(BF) for i in range(local)], axis=0)
                mixed = dot_tn(pick, sent).astype(BF)

                @pl.when(c == core)
                def _():
                    y_ref[zc] = mixed

                @pl.when(c != core)
                def _():
                    yps_ref[slot] = mixed

            y_copy(zc, slot, t).start()
            core_copy(zc, slot, t).wait_recv()
            there = core_ref.at[zc] if roomy else landed(core_ref.at[zc], "core")
            own = dxp_ref.at[slot, c]

            @pl.when(k == 0)
            def _():
                dx_ref[...] = own[...].astype(F32) + there[...].astype(F32)

            @pl.when(k == 1)
            def _():
                side = side_of(zc)
                add_rows(pair_ref.at[side], own, there, tokens, 64)

                @pl.when((z == 0) | (z == chips - 1))
                def _():
                    pair_copy(side).start()

            @pl.when(k >= 2)
            def _():
                add_rows(own, own, there, tokens, 64)

                @pl.when(k == 2)
                def _():
                    via_copy(zc, slot, t).start()

                @pl.when(k > 2)
                def _():
                    far_copy(zc, slot, t).start()

            return carry

        lax.fori_loop(0, chips, chunk, 0)

        @pl.when((z > 0) & (z < chips - 1))
        def _():
            for side in range(2):
                make(via_ref.at[side], via_ref.at[side], far_send.at[0], via_recv.at[side], mate).wait_recv()
                add_rows(pair_ref.at[side], pair_ref.at[side], via_ref.at[side], tokens, 64)
                pair_copy(side).start()

        for i in range(local):
            ge_ref[i, :FF] = dot_tn(dgu_ref[i, :, :FF], xs_ref[i]).astype(BF)
            ge_ref[i, FF : 2 * FF] = dot_tn(dgu_ref[i, :, FF:], xs_ref[i]).astype(BF)
            ge_ref[i, 2 * FF :] = dot_tn(hx_ref[i], dye_ref[i]).astype(BF)
            if bits:
                next(sums[i])
        add_ye(place(chips - 1))
        for t in range(max(chips - 2, 0), chips):
            free_slot(t, t % 2)
        for t in range(chips):
            for core in range(2):

                @pl.when((t > 0) | (c != core))
                def _():
                    dgt_copy(z, core, t).wait_send()

    slots = chips * 2 * CAP
    pl.run_scoped(
        experts_and_sums,
        pltpu.VMEM((2, tokens, D), BF), pltpu.VMEM((local, slots, D), BF), pltpu.VMEM((local, slots, D), BF),
        pltpu.VMEM((local, slots, 2 * FF), BF), pltpu.VMEM((local, slots, FF), BF), pltpu.VMEM((2, 2, tokens, D), BF),
        pltpu.VMEM((2, tokens, D), BF), pltpu.VMEM((tokens, D), BF),
    )

    def line(own, size, step, core_add, name, reach, via, arrive, send_sem, via_recv, from_recv):
        def direct(k):
            return make(own(k), arrive.at[z], send_sem.at[k], from_recv.at[z], (r, k * 2 + c))

        def passing(k, side):
            return make(own(k), via.at[side], send_sem.at[k], via_recv.at[side], (r, (z + 2 * side - 1) * 2 + c))

        def within(k):
            return (k >= 0) & (k < chips)

        for d in range(chips - 1, 0, -1):
            for side in range(2):
                way = 1 if side else -1
                owner = z + d * way

                @pl.when(within(owner))
                def _():
                    core_add(owner)
                    if d > reach + 1:
                        direct(owner).start()
                    elif d == reach + 1:
                        passing(owner, side).start()
                    elif d == reach:
                        pl.when(jnp.logical_not(within(z - way)))(lambda: direct(owner).start())

        core_add(z)
        yield
        for side in range(2):
            way = 1 if side else -1
            owner = z + reach * way

            @pl.when(within(owner) & within(z - way))
            def _():
                make(via.at[side], via.at[side], send_sem.at[0], via_recv.at[side], mate).wait_recv()
                add_rows(own(owner), own(owner), landed(via.at[side], name), size, step)
                direct(owner).start()

        yield
        for k in range(chips):

            @pl.when((z != k) & (far(k) != reach + 1))
            def _():
                make(arrive.at[k], arrive.at[k], send_sem.at[0], from_recv.at[k], mate).wait_recv()
                add_rows(own(z), own(z), landed(arrive.at[k], name), size, step)

        for k in range(chips):

            @pl.when(z != k)
            def _():
                direct(k).wait_send()

    def mixture():
        yield from line(lambda k: y_ref.at[k], tokens, 64, lambda k: None, "tokens", 1, y_via, y_from, *y_sems)
        out_ref[...] = (h1_ref[...] + residual_scale * y_ref[z].astype(F32)).astype(BF)

    def attention(q_ref, kd_ref, vd_ref, o_ref, p_ref, do_ref, dqkv_ref, gkv_ref, gq_ref, go_ref, halves_stage, tokens_stage, kv_stage, o_stage):
        loads = [
            pltpu.make_async_copy(heads_hbm.at[i], ref, heads_sem.at[i]) for i, ref in enumerate((q_ref, kd_ref, vd_ref, o_ref))
        ]
        start(loads)
        stages["halves"] = (halves_stage, stage_sem.at[1])
        stages["tokens"] = (tokens_stage, stage_sem.at[2])
        stages["kv"] = (kv_stage, stage_sem.at[3])
        stages["o"] = (o_stage, stage_sem.at[4])
        def projection(index, name, grad_ref, core, via, arrive, sems):
            core_sem, *sems = sems
            parts, results, wide = parts_ref.at[index], results_ref.at[index], D // replicas
            crossing = make(grad_ref.at[:, 1 - c], core, core_sem.at[0], core_sem.at[1], mate)
            crossing.start()
            yield
            crossing.wait_recv()

            def own(k):
                return grad_ref.at[k, c]

            yield from line(
                own, rows, 16, lambda k: add_rows(own(k), own(k), core.at[k], rows, 16), name, 1, via, arrive, *sems
            )
            crossing.wait_send()
            mine = grad_ref.at[z, c]

            def columns(part):
                return pl.ds(pl.multiple_of(part * wide, LANE), wide)

            def part_copy(d):
                to = (r + d) % replicas
                return make(
                    mine.at[:, columns(to)], parts.at[r], part_send.at[index, d], part_recv.at[index, r], (to, f)
                )

            def small_copy(d):
                to = (r + d) % replicas
                return make(mine.at[:, pl.ds(D, LANE)], smalls_ref.at[r], small_send.at[d], small_recv.at[r], (to, f))

            for d in range(1, replicas):
                part_copy(d).start()
                if index == 0:
                    small_copy(d).start()
            parts[r] = mine[:, columns(r)]
            if index == 0:
                smalls_ref[r] = mine[:, pl.ds(D, LANE)]
            yield
            for d in range(1, replicas):
                peer = (r + d) % replicas
                make(
                    parts.at[peer], parts.at[peer], part_send.at[index, d], part_recv.at[index, peer], (peer, f)
                ).wait_recv()
                if index == 0:
                    make(
                        smalls_ref.at[peer], smalls_ref.at[peer], small_send.at[d], small_recv.at[peer], (peer, f)
                    ).wait_recv()
            total = parts[0].astype(F32)
            for k in range(1, replicas):
                total = total + parts[k].astype(F32)
            results[r] = total.astype(BF)

            def result_copy(d):
                to = (r + d) % replicas
                return make(
                    results.at[r], results.at[r], result_send.at[index, d], result_recv.at[index, r], (to, f)
                )

            for d in range(1, replicas):
                result_copy(d).start()
            if index == 0:
                small = smalls_ref[0].astype(F32)
                for k in range(1, replicas):
                    small = small + smalls_ref[k].astype(F32)
                total_ref[...] = small
            yield
            for d in range(1, replicas):
                peer = (r + d) % replicas
                make(
                    results.at[peer], results.at[peer], result_send.at[index, d], result_recv.at[index, peer], (peer, f)
                ).wait_recv()
            for d in range(1, replicas):
                part_copy(d).wait_send()
                if index == 0:
                    small_copy(d).wait_send()
                result_copy(d).wait_send()

        moe = [mixture()]
        kvs = [projection(0, "kv", gkv_ref, kv_core, kv_via, kv_from, kv_sems)]
        outs = [projection(1, "o", go_ref, o_core, o_via, o_from, o_sems)]
        qs = [projection(2, "o", gq_ref, q_core, q_via, q_from, q_sems)]

        def go(*turns):
            for turn in turns:
                for process in turn:
                    next(process, None)

        def dgate():
            found = [dgt_all[k, :local] for k in range(2 * chips)]
            return jnp.concatenate(found + [jnp.zeros((LANE - E, tokens), F32)], axis=0).T

        for k in range(chips):

            @pl.when((z == k + 1) | (z + 1 == k) | (z > k + 2) | (z + 2 < k))
            def _():
                make(from_ref.at[k], from_ref.at[k], far_send.at[0], far_recv.at[k], mate).wait_recv()
                there = from_ref.at[k] if roomy else landed(from_ref.at[k], "tokens")
                add_rows(dx_ref, dx_ref, there, tokens, 64)

        for k in range(2 * chips):

            @pl.when(f == k)
            def _():
                for core in range(2):

                    @pl.when(c == core)
                    def _():
                        dgt_all[k] = dgt_ref[0, core]

            @pl.when(f != k)
            def _():
                make(dgt_all.at[k], dgt_all.at[k], dgt_send.at[0, 0], dgt_recv.at[k], mate).wait_recv()

        for load in loads:
            load.wait()
        backward = attention_backward(
            x_ref, dout_ref, cos_ref, sin_ref, columns, q_ref, kd_ref, vd_ref, p_hbm, o_ref, h1_ref, n2_all.at[z, c], gd_ref,
            dx_ref, dgate, gin_ref, gq_ref, gkv_ref, go_ref, do_ref, dqkv_ref, p_ref, p_sem,
        )
        next(backward)
        go(outs)
        next(backward)
        go(first, outs)
        next(backward)
        go(qs)
        next(backward, None)
        go(kvs, qs, kvs, last, first, moe, outs, last, first, qs, last, outs, kvs, moe, outs, qs, first, qs, outs, kvs, moe, last)
        go(kvs, qs, kvs)
        go(*[moe + outs + qs + kvs + sums] * (2 * bits + 8))

    size = ge_ref.shape[1] // max(bits, 1)
    pl.run_scoped(
        attention, *[pltpu.VMEM((tokens, D), BF)] * 4,
        pltpu.VMEM((2, 2 * tokens, tokens), F32), pltpu.VMEM((tokens, D), BF),
        pltpu.VMEM((tokens, QKV), BF), pltpu.VMEM((chips, 2, rows, D + LANE), BF), pltpu.VMEM((chips, 2, rows, D), BF),
        pltpu.VMEM((chips, 2, rows, D), BF), pltpu.VMEM((size // 2, D), BF), pltpu.VMEM((tokens, D), BF),
        pltpu.VMEM((rows, D + LANE), BF), pltpu.VMEM((rows, D), BF),
    )

    for e in range(local):
        copy = pltpu.make_async_copy(ge_ref.at[e], ge_hbm.at[e], ge_sem.at[e])
        if not bits:
            copy.start()
        copy.wait()
    for side in range(2):

        @pl.when(z > 0 if side == 0 else z < chips - 1)
        def _():
            pair_copy(side).wait_send()

    for k in range(chips):

        @pl.when((z >= k) & (z < chips - 1))
        def _():
            for copy in pass_on(k, "up"):
                copy.wait_send()

        @pl.when((z <= k) & (z > 0))
        def _():
            for copy in pass_on(k, "down"):
                copy.wait_send()

        for copy in pass_on(k, "mate"):
            copy.wait_send()

    for k in range(chips):
        for late in range(2):
            to_mate(k, c, late).wait_send()
        dout_copy(k, c, 2).wait_send()

        @pl.when((z >= k) & (z < chips - 1))
        def _():
            dout_copy(k, c, 0).wait_send()
            for kind in range(3):
                along(k, kind, True).wait_send()

        @pl.when((z <= k) & (z > 0))
        def _():
            dout_copy(k, c, 1).wait_send()
            for kind in range(3):
                along(k, kind, False).wait_send()

        @pl.when(z != k)
        def _():
            for d in range(1, replicas):
                for kind in (0, 2):
                    across(k, kind, d).wait_send()


def finish(gexp_ref, results_ref, total_ref, gin_ref, out_ref, *outs):
    layer_out, grad_in, gains_one, query, key, value, output, gains_two, router, expert = outs
    expert[...] = gexp_ref[...].astype(F32)
    layer_out[...] = out_ref[...]
    grad_in[...] = gin_ref[...]
    for index, targets in ((0, (key, value)), (1, (output,)), (2, (query,))):
        start, wide = 0, results_ref.shape[3]
        for ref in targets:
            for at in range(0, ref.shape[1], LANE):
                part, column = divmod(start + at, wide)
                ref[:, at : at + LANE] = results_ref[index, part, :, column : column + LANE].astype(F32)
            start += ref.shape[1]

    @pl.when(pl.program_id(0) == 0)
    def _():
        small = total_ref[...].T
        router[...] = small[:E]
        gains_one[...] = small[E : E + 1]
        gains_two[...] = small[E + 1 : E + 2]


def call(kernel, out_shape, args, scratch=(), outside=0, out_outside=0, **params):
    spaces = [pltpu.SMEM if a.dtype == jnp.int32 and a.size <= 16 else pltpu.VMEM for a in args]
    spaces[len(args) - outside :] = [pl.ANY] * outside
    return pl.pallas_call(
        kernel,
        out_shape=out_shape,
        in_specs=[pl.BlockSpec(memory_space=space) for space in spaces],
        out_specs=[
            pl.BlockSpec(memory_space=pltpu.VMEM if i < len(out_shape) - out_outside else pl.ANY)
            for i in range(len(out_shape))
        ],
        scratch_shapes=list(scratch),
        compiler_params=pltpu.CompilerParams(
            vmem_limit_bytes=VMEM_LIMIT, has_side_effects="collective_id" in params, **params
        ),
    )(*args)


def shape(dims, dtype):
    return jax.ShapeDtypeStruct(dims, dtype)


def make_body(mesh):
    group, replicas = mesh.shape["fsdp"], mesh.shape["replica"]
    local = E // group

    def body(
        hidden_in, seq_lengths, routes, norm1_gain, w_query, w_key, w_value, w_output, norm2_gain, w_router,
        expert_weights, out_cotangent,
    ):
        tokens = hidden_in.shape[0]
        rows = w_query.shape[0]
        chips = group // 2
        dma = pltpu.SemaphoreType.DMA
        bits = replicas.bit_length() - 1
        size = 3 * FF // bits if bits else 0
        roomy = chips <= 4
        landing = [shape((local * bits, size >> (k + 1), D), BF) for k in range(bits)]
        blocks = [shape((chips, tokens, D), BF)] * 2
        landing += [shape((chips, tokens, D), BF)]
        if not roomy:
            landing += blocks
        outs = call(
            functools.partial(layer, replicas, chips),
            [
                shape((tokens, D), F32), shape((tokens, D), BF), shape((3, replicas, rows, D // replicas), BF),
                shape((rows, LANE), F32), shape((local, 3 * FF, D), BF),
                shape((KVH, 2 * tokens, tokens), F32), shape((4, tokens, D), BF), shape((chips, 2, tokens, D), BF),
                shape((2, tokens, D), BF), shape((chips, tokens, D), BF), shape((2, rows, D + LANE), BF),
                shape((chips, rows, D + LANE), BF), shape((2, rows, D), BF), shape((chips, rows, D), BF),
                shape((2, rows, D), BF), shape((chips, rows, D), BF),
            ]
            + landing,
            (
                hidden_in, seq_lengths, routes.T, rope_table(tokens), w_query, w_key, w_value, w_output, w_router.T,
                norm1_gain[None], norm2_gain[None], out_cotangent, expert_weights,
            ),
            [
                pltpu.VMEM((chips, 2, rows, W_O + D), BF), pltpu.VMEM((tokens, D), F32),
                pltpu.VMEM((tokens, LANE), F32), pltpu.VMEM((tokens, LANE), F32), pltpu.VMEM((tokens, LANE), F32),
                dma((4,)), dma((1,)), dma((3, chips)), dma((3, chips)), dma((3, chips)), dma((3, chips, replicas)),
                dma((3, chips, replicas)), dma((2, chips)), dma((2, chips)), dma((3, chips)), dma((chips, 2)),
                pltpu.VMEM((local, 3 * FF, D), BF), pltpu.VMEM((chips, 2, tokens, D), BF),
                pltpu.VMEM((chips, 2, E, tokens), F32), pltpu.VMEM((2, tokens, D), BF), pltpu.VMEM((2, tokens, D), BF),
                pltpu.VMEM((chips, 2, 8, tokens), F32), pltpu.VMEM((group, 8, tokens), F32),
                pltpu.VMEM((chips, tokens, D), BF), pltpu.VMEM((chips, rows, D + LANE), BF), pltpu.VMEM((chips, rows, D), BF),
                pltpu.VMEM((chips, rows, D), BF), pltpu.VMEM((3, replicas, rows, D // replicas), BF),
                pltpu.VMEM((replicas, rows, LANE), BF),
            ]
            + ([pltpu.VMEM(b.shape, b.dtype) for b in blocks] if roomy else [])
            + ([dma((chips,))] * 3 + [dma((chips, 2))]) * 2 + [dma((chips,))] * 4 + [dma((2,))] * 2
            + [dma((chips, 2)), dma((group,)), dma((chips,)), dma((chips,))]
            + [dma((1,)), dma((1,)), dma((5,)), dma((local,)), dma((2,))]
            + [dma((max(local * bits, 1), max(2 * bits, 1)))] * 2
            + [pltpu.SemaphoreType.REGULAR((max(local * bits, 1), max(bits, 1)))]
            + [dma((chips,)), dma((2,)), dma((chips,))] + [dma((2,)), dma((chips,)), dma((2,)), dma((chips,))] * 3
            + [dma((3, replicas))] * 2 + [dma((replicas,))] * 2 + [dma((3, replicas))] * 2,
            outside=1,
            out_outside=12 + len(landing),
            collective_id=0,
        )
        grad_in, layer_out, results, total, grad_experts = outs[:5]
        steps = 8

        def moving(a, dim=0):
            block = tuple(n // steps if i == dim else n for i, n in enumerate(a.shape))
            return pl.BlockSpec(block, lambda i: tuple(i if at == dim else 0 for at in range(len(block))))

        def still(a):
            return pl.BlockSpec(a.shape, lambda i: (0,) * len(a.shape))

        grad_experts = grad_experts.reshape(local * 3 * FF, D)
        gain, router = shape((1, rows), F32), shape((E, rows), F32)
        wide, narrow = shape((rows, D), F32), shape((rows, KVH * HD), F32)
        out_shapes = [
            shape((tokens, D), BF), shape((tokens, D), F32), gain, wide, narrow, narrow, wide, gain, router,
            shape((local * 3 * FF, D), F32),
        ]
        outs = pl.pallas_call(
            finish,
            grid=(steps,),
            in_specs=[moving(grad_experts), moving(results, 2), still(total), moving(grad_in), moving(layer_out)],
            out_specs=[still(a) if a in (gain, router) else moving(a) for a in out_shapes],
            out_shape=out_shapes,
            compiler_params=pltpu.CompilerParams(vmem_limit_bytes=VMEM_LIMIT),
        )(grad_experts, results, total, grad_in, layer_out)
        return (
            outs[0], outs[1], outs[2][0], outs[3], outs[4], outs[5], outs[6], outs[7][0], outs[8].T,
            outs[9].reshape(local, 3 * FF, D),
        )

    return body


def solution(mesh):
    tokens, weights = P(("replica", "fsdp"), None), P("fsdp", None)
    return jax.shard_map(
        make_body(mesh),
        mesh=mesh,
        in_specs=(
            tokens, tokens, tokens, P("fsdp"), weights, weights, weights, weights, P("fsdp"), weights,
            P("fsdp", None, None), tokens,
        ),
        out_specs=(
            tokens, tokens, P("fsdp"), weights, weights, weights, weights, P("fsdp"), weights, P("fsdp", None, None),
        ),
        check_vma=False,
    )
```

```python
import functools

import jax
import jax.numpy as jnp
import numpy as np
from jax import lax
from jax.experimental import pallas as pl
from jax.experimental.pallas import tpu as pltpu
from jax.sharding import PartitionSpec as P

D = 1024
H = 16
KVH = 8
HD = 64
FF = 512
TOPK = 8
E = 16
CAP = 144
LANE = 128
QKV = H * HD + 2 * KVH * HD
QKVO = QKV + D
W_O = QKV + LANE

norm_eps = 1e-06
score_scale = 0.015625
residual_scale = 0.22
rope_base = 10000.0
masked_score = -1e30

BF = jnp.bfloat16
F32 = jnp.float32
VMEM_LIMIT = 63 * 2**20


def dot(a, b):
    return lax.dot_general(a, b, (((1,), (0,)), ((), ())), preferred_element_type=F32)


def dot_nt(a, b):
    return lax.dot_general(a, b, (((1,), (1,)), ((), ())), preferred_element_type=F32)


def dot_tn(a, b):
    return lax.dot_general(a, b, (((0,), (0,)), ((), ())), preferred_element_type=F32)


def lanes_of(rows):
    return lax.broadcasted_iota(jnp.int32, (rows, LANE), 1)


def turned(block, lane):
    return jnp.where(lane % HD < HD // 2, pltpu.roll(block, LANE - HD // 2, 1), pltpu.roll(block, HD // 2, 1))


def halves(block, low):
    zero = jnp.zeros_like(block)
    return jnp.concatenate([jnp.where(low, block, zero), jnp.where(low, zero, block)], axis=0)


def rope_table(tokens):
    frequency = np.float32(rope_base) ** (-np.arange(0, HD, 2, dtype=np.float32) / np.float32(HD))
    frequency = np.tile(frequency.astype(np.float32), LANE // (HD // 2))
    angles = (np.arange(tokens, dtype=np.float32)[:, None] * frequency[None, :]).astype(np.float64)
    sign = np.where(np.arange(LANE) % HD < HD // 2, -1.0, 1.0)
    pieces = []
    for values in (np.cos(angles), np.sin(angles) * sign[None, :]):
        rest = values.astype(np.float32)
        for _ in range(3):
            piece = rest.astype(BF)
            pieces.append(piece)
            rest = rest - piece.astype(np.float32)
    return np.concatenate(pieces, axis=1)


class Copies:
    def make(self, src, dst, send, recv, device):
        return pltpu.make_async_remote_copy(
            src_ref=src, dst_ref=dst, send_sem=send, recv_sem=recv, device_id=device, device_id_type=pl.DeviceIdType.MESH
        )


def meet(devices, expected):
    barrier = pltpu.get_barrier_semaphore()
    for condition, device in devices:

        def signal(device=device):
            pl.semaphore_signal(barrier, inc=1, device_id=device, device_id_type=pl.DeviceIdType.MESH)

        if condition is True:
            signal()
        else:
            pl.when(condition)(signal)
    pl.semaphore_wait(barrier, expected)


def attention_backward(
    x_ref, dout_ref, cos_ref, sin_ref, columns, q_ref, kd_ref, vd_ref, p_hbm, o_ref, h1_ref, n2_ref, gd_ref, dx_ref, dgate,
    gin_ref, gq_ref, gkv_ref, go_ref, do_ref, dqkv_ref, p_ref, p_sem,
):
    tokens = x_ref.shape[0]
    lane = lanes_of(tokens)
    low = lane < HD

    def p_copy(g):
        return pltpu.make_async_copy(p_hbm.at[g], p_ref.at[g % 2], p_sem.at[g % 2])

    p_copy(0).start()

    def put(ref, at, value):
        ref[:, :, :, at] = value.astype(BF).reshape(*ref.shape[:3], value.shape[1])

    small = columns(QKV, LANE).astype(F32).T
    gain_one, gain_two = small[E : E + 1], small[E + 1 : E + 2]
    after = h1_ref[...]
    factor_two = lax.rsqrt(jnp.mean(after * after, axis=1, keepdims=True) + norm_eps)
    gates = jnp.maximum(gd_ref[...], 0.0)
    grad_gates = dgate()
    chosen = gates * (grad_gates - jnp.sum(gates * grad_gates, axis=1, keepdims=True))
    grad_logits = chosen.astype(BF)
    grad_normed = dx_ref[...] + dot_nt(grad_logits, columns(QKV, LANE))
    scaled = grad_normed * gain_two
    grad_after = dout_ref[...].astype(F32) + (
        factor_two * scaled - after * factor_two**3 * jnp.mean(scaled * after, axis=1, keepdims=True)
    )
    grad_gain_two = jnp.sum(grad_normed * after * factor_two, axis=0, keepdims=True)
    gin_ref[...] = grad_after
    grad_branch = (residual_scale * grad_after).astype(BF)
    for at in range(0, D, FF):
        put(go_ref, slice(at, at + FF), dot_tn(o_ref[...], grad_branch[:, at : at + FF]))
    do_ref[...] = dot_nt(grad_branch, columns(W_O, D)).astype(BF)
    grad_router = dot_tn(n2_ref[...], grad_logits)
    yield

    cosines, sines = cos_ref[...], sin_ref[...]
    key_back, value_back = [], []
    for g in range(KVH):
        at = slice(g * LANE, (g + 1) * LANE)
        queries = halves(q_ref[:, at].astype(F32), low).astype(BF)
        outs = halves(do_ref[:, at].astype(F32), low).astype(BF)
        if g + 1 < KVH:
            p_copy(g + 1).start()
        p_copy(g).wait()
        weights = p_ref[g % 2]
        grad_weights = dot_nt(outs, vd_ref[:, at])
        total = jnp.sum(weights * grad_weights, axis=1, keepdims=True)
        grad_scores = (weights * (grad_weights - total)).astype(BF)
        block = dot(grad_scores, kd_ref[:, at])
        block = jnp.where(low, block[:tokens], block[tokens:]) * score_scale
        dqkv_ref[:, at] = (block * cosines - turned(block, lane) * sines).astype(BF)
        block = dot_tn(grad_scores, queries) * score_scale
        key_back.append(block + pltpu.roll(block, HD, 1))
        block = dot_tn(weights.astype(BF), outs)
        value_back.append(block + pltpu.roll(block, HD, 1))
        if g == KVH // 2 - 1:
            yield
    for m in range(KVH // 2):
        block = jnp.where(low, key_back[2 * m], key_back[2 * m + 1])
        at = slice(H * HD + m * LANE, H * HD + (m + 1) * LANE)
        dqkv_ref[:, at] = (block * cosines - turned(block, lane) * sines).astype(BF)
        at = slice(H * HD + KVH * HD + m * LANE, H * HD + KVH * HD + (m + 1) * LANE)
        dqkv_ref[:, at] = jnp.where(low, value_back[2 * m], value_back[2 * m + 1]).astype(BF)
    yield

    source = x_ref[...].astype(F32)
    factor_one = lax.rsqrt(jnp.mean(source * source, axis=1, keepdims=True) + norm_eps)
    normed = (source * factor_one * gain_one).astype(BF)
    for at in range(0, H * HD, FF):
        put(gq_ref, slice(at, at + FF), dot_tn(normed, dqkv_ref[:, at : at + FF]))
    yield
    grad_normed = dot_nt(dqkv_ref[...], columns(0, QKV))
    scaled = grad_normed * gain_one
    grad_vector = factor_one * scaled - source * factor_one**3 * jnp.mean(scaled * source, axis=1, keepdims=True)
    gin_ref[...] += grad_vector
    grad_gain_one = jnp.sum(grad_normed * source * factor_one, axis=0, keepdims=True)
    gains = jnp.concatenate([grad_gain_one, grad_gain_two, jnp.zeros((6, D), F32)], axis=0).T
    at = lanes_of(D)
    extra = jnp.where(at == E, gains[:, 0:1], jnp.where(at == E + 1, gains[:, 1:2], grad_router))
    put(gkv_ref, slice(D, D + LANE), extra)
    for at in range(0, QKV - H * HD, FF):
        put(gkv_ref, slice(at, at + FF), dot_tn(normed, dqkv_ref[:, H * HD + at : H * HD + at + FF]))


def add_rows(target, first, second, rows, step):
    def some(i, carry):
        at = pl.ds(pl.multiple_of(i * step, step), step)
        target[at] = (first[at].astype(F32) + second[at].astype(F32)).astype(target.dtype)
        return carry

    lax.fori_loop(0, rows // step, some, 0)


def layer(
    replicas, chips,
    x_ref, len_ref, routes_ref, table_ref, wq_ref, wk_ref, wv_ref, wo_ref, wr_ref, g1_ref, g2_ref, dout_ref, we_hbm,
    gin_ref, out_ref, results_ref, total_ref, ge_hbm, p_hbm, heads_hbm, do_all, y_via, y_from, kv_via, kv_from, q_via, q_from,
    o_via, o_from, *rest,
):
    bits = replicas.bit_length() - 1
    roomy = chips <= 4
    arrived, y_core, rest = rest[:bits], rest[bits], rest[bits + 1 :]
    if not roomy:
        (core_ref, from_ref), rest = rest[:2], rest[2:]
    (w_all, h1_ref, gd_ref, cos_ref, sin_ref), rest = rest[:5], rest[5:]
    (heads_sem, own_sem, z_up, z_down, z_recv, xy_send, xy_recv, mate_send, mate_recv, do_send, do_recv), rest = rest[:11], rest[11:]
    (ge_ref, n2_all, gt_all, via_ref, pair_ref, dgt_ref, dgt_all, y_ref, kv_core, q_core, o_core, parts_ref, smalls_ref), rest = (
        rest[:13], rest[13:]
    )
    dx_ref = gin_ref
    if roomy:
        (core_ref, from_ref), rest = rest[:2], rest[2:]
    (n2_up, n2_down, n2_mate, n2_recv, gt_up, gt_down, gt_mate, gt_recv,
     core_send, core_recv, far_send, far_recv, pair_send, via_recv, dgt_send, dgt_recv, yc_send, yc_recv,
     do_sem, we_sem, stage_sem, ge_sem, p_sem, ar_send, ar_recv, ar_free,
     *sum_sems, part_send, part_recv, small_send, small_recv, result_send, result_recv) = rest
    y_sems, kv_sems, q_sems, o_sems = sum_sems[:3], sum_sems[3:7], sum_sems[7:11], sum_sems[11:]
    local, tokens, rows = ge_ref.shape[0], x_ref.shape[0], q_core.shape[1]
    r, f = lax.axis_index("replica"), lax.axis_index("fsdp")
    z, c = f // 2, f % 2
    mate, above, below = (r, z * 2 + 1 - c), (r, f + 2), (r, f - 2)
    make = Copies().make

    load_experts = pltpu.make_async_copy(we_hbm, ge_ref, we_sem.at[0])
    load_experts.start()
    own_dout = pltpu.make_async_copy(dout_ref, do_all.at[z, c], own_sem.at[0])
    own_dout.start()
    packed = [wr_ref[...].astype(F32), g1_ref[...].astype(F32), g2_ref[...].astype(F32)]
    packed = jnp.concatenate(packed + [jnp.zeros((LANE - E - 2, rows), F32)], axis=0)
    own = w_all.at[z, c]
    own[:, : H * HD] = wq_ref[...]
    own[:, H * HD : H * HD + KVH * HD] = wk_ref[...]
    own[:, H * HD + KVH * HD : QKV] = wv_ref[...]
    own[:, QKV:W_O] = packed.T.astype(BF)
    own[:, W_O:] = wo_ref[...]
    peers = [(True, mate)]
    for k in range(1, chips):
        to = (z + k) % chips
        peers += [(True, (r, to * 2 + c)), (True, (r, to * 2 + 1 - c))]
    peers += [(True, ((r + d) % replicas, f)) for d in range(1, replicas)]
    meet(peers, len(peers))

    def part(kind):
        if kind == 0:
            return pl.ds(pl.multiple_of(r * (QKV // replicas), LANE), QKV // replicas)
        if kind == 1:
            return pl.ds(QKV, LANE)
        return pl.ds(pl.multiple_of(W_O + r * (D // replicas), LANE), D // replicas)

    def along(zb, kind, up):
        ref = w_all.at[zb, c, :, part(kind)]
        return make(ref, ref, (z_up if up else z_down).at[kind, zb], z_recv.at[kind, zb], above if up else below)

    def across(zb, kind, d):
        ref = w_all.at[zb, c, :, part(kind)]
        return make(ref, ref, xy_send.at[kind, zb, d], xy_recv.at[kind, zb, r], ((r + d) % replicas, f))

    def wait_across(zb, kind):
        for d in range(1, replicas):
            peer = (r + d) % replicas
            ref = w_all.at[zb, c, :, part(kind)]
            make(ref, ref, xy_send.at[kind, zb, d], xy_recv.at[kind, zb, peer], (peer, f)).wait_recv()

    def to_mate(zb, core, late):
        ref = w_all.at[zb, core, :, pl.ds(W_O, D) if late else pl.ds(0, W_O)]
        return make(ref, ref, mate_send.at[late, zb], mate_recv.at[late, zb], mate)

    def dout_copy(zb, core, way):
        source = do_all.at[zb, core]
        return make(source, do_all.at[zb, core], do_send.at[way, zb], do_recv.at[zb, core], (above, below, mate)[way])

    def both_sides(k, act):
        @pl.when(z >= k)
        def _():
            act(z - k, True)

        @pl.when(z < chips - k)
        def _():
            act(z + k, False)

    def onward(up):
        return z < chips - 1 if up else z > 0

    def dout_arrive(zb, low):
        dout_copy(zb, c, 0 if low else 1).wait_recv()

        @pl.when(onward(low))
        def _():
            dout_copy(zb, c, 0 if low else 1).start()

        dout_copy(zb, c, 2).start()

    def columns(start, size):
        return w_all.reshape(D, W_O + D)[:, start : start + size]

    def forward(p_ref, q_ref, kd_ref, vd_ref, o_ref):
        for kind in range(3):
            both_sides(1, lambda zb, low: along(z, kind, not low).start())
        for late in range(2):
            to_mate(z, c, late).start()

        source = x_ref[...].astype(F32)
        factor = lax.rsqrt(jnp.mean(source * source, axis=1, keepdims=True) + norm_eps)
        lane = lanes_of(tokens)
        low_lane = lane < HD
        row = lax.broadcasted_iota(jnp.int32, (tokens, tokens), 0)
        column = lax.broadcasted_iota(jnp.int32, (tokens, tokens), 1)
        row_at = lax.broadcasted_iota(jnp.int32, (tokens, 1), 0)
        column_at = lax.broadcasted_iota(jnp.int32, (1, tokens), 1)
        row_segment = jnp.zeros((tokens, 1), jnp.int32)
        row_start = jnp.zeros((tokens, 1), jnp.int32)
        column_segment = jnp.zeros((1, tokens), jnp.int32)
        end = jnp.int32(0)
        for j in range(len_ref.shape[1]):
            end = end + len_ref[0, j]
            row_segment += (row_at >= end).astype(jnp.int32)
            row_start = jnp.maximum(row_start, jnp.where(row_at >= end, end, 0))
            column_segment += (column_at >= end).astype(jnp.int32)
        place = (column == row - row_start).astype(F32).astype(BF)
        found = dot(place, table_ref[...])
        found = [found[:, i * LANE : (i + 1) * LANE] for i in range(6)]
        cosines, sines = found[0] + found[1] + found[2], found[3] + found[4] + found[5]
        cos_ref[...] = cosines
        sin_ref[...] = sines

        own_dout.wait()
        for k in range(1, chips):
            for kind in range(3):

                def arrive(zb, low, kind=kind):
                    along(zb, kind, low).wait_recv()

                    @pl.when(onward(low))
                    def _():
                        along(zb, kind, low).start()

                    if kind != 1:
                        for d in range(1, replicas):
                            across(zb, kind, d).start()

                both_sides(k, arrive)
            if k == 1:
                both_sides(1, lambda zb, low: dout_copy(z, c, 1 if low else 0).start())
                dout_copy(z, c, 2).start()

        def share(k, late):
            def act(zb, low):
                wait_across(zb, 2 if late else 0)
                to_mate(zb, c, late).start()

            both_sides(k, act)

        for k in range(1, chips):
            share(k, 0)
        if chips > 1:
            both_sides(1, dout_arrive)
        for k in range(chips):
            to_mate(k, 1 - c, 0).wait_recv()

        small = columns(QKV, LANE)
        gains = small.astype(F32).T
        gain_one, gain_two = gains[E : E + 1], gains[E + 1 : E + 2]
        normed = (source * factor * gain_one).astype(BF)
        q_all = dot(normed, columns(0, H * HD))
        for g in range(H // 2):
            at = slice(g * LANE, (g + 1) * LANE)
            block = q_all[:, at]
            q_ref[:, at] = (block * cosines + turned(block, lane) * sines).astype(BF)
        kv = dot(normed, columns(H * HD, 2 * KVH * HD))
        for m in range(KVH // 2):
            block = kv[:, m * LANE : (m + 1) * LANE]
            block = block * cosines + turned(block, lane) * sines
            other = pltpu.roll(block, HD, 1)
            kd_ref[:, 2 * m * LANE : (2 * m + 1) * LANE] = jnp.where(low_lane, block, other).astype(BF)
            kd_ref[:, (2 * m + 1) * LANE : (2 * m + 2) * LANE] = jnp.where(low_lane, other, block).astype(BF)
            block = kv[:, KVH * HD + m * LANE : KVH * HD + (m + 1) * LANE]
            other = pltpu.roll(block, HD, 1)
            vd_ref[:, 2 * m * LANE : (2 * m + 1) * LANE] = jnp.where(low_lane, block, other).astype(BF)
            vd_ref[:, (2 * m + 1) * LANE : (2 * m + 2) * LANE] = jnp.where(low_lane, other, block).astype(BF)
        saves = [
            pltpu.make_async_copy(ref, heads_hbm.at[i], heads_sem.at[i]) for i, ref in enumerate((q_ref, kd_ref, vd_ref, o_ref))
        ]
        for save in saves[:3]:
            save.start()
        bias = jnp.where((row_segment == column_segment) & (column <= row), 0.0, masked_score)
        bias = jnp.concatenate([bias, bias], axis=0)

        def p_copy(g):
            return pltpu.make_async_copy(p_ref.at[g % 2], p_hbm.at[g], p_sem.at[g % 2])

        for g in range(KVH):
            at = slice(g * LANE, (g + 1) * LANE)
            queries = halves(q_ref[:, at].astype(F32), low_lane).astype(BF)
            scores = dot_nt(queries, kd_ref[:, at]) * score_scale + bias
            shifted = jnp.exp(scores - jnp.max(scores, axis=1, keepdims=True))
            weights = shifted * (1.0 / jnp.sum(shifted, axis=1, keepdims=True))
            if g >= 2:
                p_copy(g - 2).wait()
            p_ref[g % 2] = weights
            p_copy(g).start()
            mixed = dot(weights.astype(BF), vd_ref[:, at])
            o_ref[:, at] = jnp.where(low_lane, mixed[:tokens], mixed[tokens:]).astype(BF)

        saves[3].start()
        if chips > 2:
            both_sides(2, dout_arrive)
        for k in range(1, chips):
            share(k, 1)

        for k in range(chips):
            to_mate(k, 1 - c, 1).wait_recv()
        after = source + residual_scale * dot(o_ref[...], columns(W_O, D))
        h1_ref[...] = after
        factor = lax.rsqrt(jnp.mean(after * after, axis=1, keepdims=True) + norm_eps)
        normed = (after * factor * gain_two).astype(BF)
        n2_all[z, c] = normed
        logits = dot(normed, small).T[:E]
        expert = lax.broadcasted_iota(jnp.int32, (E, tokens), 0)
        routed = routes_ref[0:1] == expert
        for j in range(1, TOPK):
            routed |= routes_ref[j : j + 1] == expert
        top = jnp.max(jnp.where(routed, logits, masked_score), axis=0, keepdims=True)
        powers = jnp.where(routed, jnp.exp(logits - top), 0.0)
        gates = powers / jnp.sum(powers, axis=0, keepdims=True)
        gates = jnp.where(routed, gates, -1.0)
        gt_all[z, c] = gates
        gd_ref[...] = jnp.concatenate([gates, jnp.full((LANE - E, tokens), -1.0, F32)], axis=0).T
        for g in (KVH - 2, KVH - 1):
            p_copy(g).wait()
        for save in saves:
            save.wait()

    pl.run_scoped(forward, pltpu.VMEM((2, 2 * tokens, tokens), F32), *[pltpu.VMEM((tokens, D), BF)] * 4)

    def bit_of(b):
        return (r // (1 << b)) % 2

    def partner(b):
        return (r + (1 - 2 * bit_of(b)) * (1 << b), f)

    stages = {}

    def landed(ref, name):
        stage, sem = stages[name]
        if ref.shape != stage.shape:
            stage = stage.at[pl.ds(0, ref.shape[0])]
        copy = pltpu.make_async_copy(ref, stage, sem)
        copy.start()
        copy.wait()
        return stage

    def halving(e):
        size = ge_ref.shape[1] // bits
        orders = [[(g + k) % bits for k in range(bits)] for g in range(bits)]
        starts = [[] for _ in range(bits)]
        for g in range(bits):
            at = g * size
            for k in range(bits):
                starts[g].append(at)
                at = at + bit_of(orders[g][k]) * (size >> (k + 1))
            starts[g].append(at)

        def region(g, k):
            half = size >> (k + 1)
            return ge_ref.at[e, pl.ds(pl.multiple_of(starts[g][k + 1], half), half)]

        def exchange(g, k):
            half, job = size >> (k + 1), e * bits + g
            give = pl.multiple_of(starts[g][k] + (1 - bit_of(orders[g][k])) * half, half)
            return make(
                ge_ref.at[e, pl.ds(give, half)], arrived[k].at[job], ar_send.at[job, k], ar_recv.at[job, k],
                partner(orders[g][k]),
            )

        def spread(g, k):
            job, ref = e * bits + g, region(g, k)
            return make(ref, ref, ar_send.at[job, bits + k], ar_recv.at[job, bits + k], partner(orders[g][k]))

        def spread_once_free(g, k):
            pl.semaphore_wait(ar_free.at[e * bits + g, k], 1)
            spread(g, k).start()

        yield
        for g in range(bits):
            exchange(g, 0).start()
        yield
        for k in range(bits):
            half = size >> (k + 1)
            for g in range(bits):
                job = e * bits + g
                exchange(g, k).wait_recv()
                own = region(g, k)
                add_rows(own, own, landed(arrived[k].at[job], "halves"), half, min(half, 64))
                if k < bits - 1:
                    exchange(g, k + 1).start()
                exchange(g, k).wait_send()
                pl.semaphore_signal(
                    ar_free.at[job, k], inc=1, device_id=partner(orders[g][k]), device_id_type=pl.DeviceIdType.MESH
                )
                if k == bits - 1:
                    spread_once_free(g, k)
            yield
        for k in range(bits - 1, -1, -1):
            for g in range(bits):
                spread(g, k).wait_recv()
                if k > 0:
                    spread_once_free(g, k - 1)
            yield
        for g in range(bits):
            for k in range(bits):
                spread(g, k).wait_send()
        pltpu.make_async_copy(ge_ref.at[e], ge_hbm.at[e], ge_sem.at[e]).start()

    sums = [halving(e) for e in range(local)] if bits else []
    first, last = sums[:1], sums[1:]
    for process in sums:
        next(process)

    def pass_on(zb, how):
        to = {"up": above, "down": below, "mate": mate}[how]
        sems = {"up": (n2_up, gt_up), "down": (n2_down, gt_down), "mate": (n2_mate, gt_mate)}[how]
        return [
            make(ref.at[zb, c], ref.at[zb, c], sem.at[zb], recv.at[zb, c], to)
            for ref, sem, recv in ((gt_all, sems[1], gt_recv), (n2_all, sems[0], n2_recv))
        ]

    def got(zb, core):
        for ref, sem, recv in ((gt_all, gt_mate, gt_recv), (n2_all, n2_mate, n2_recv)):
            make(ref.at[zb, core], ref.at[zb, core], sem.at[zb], recv.at[zb, core], mate).wait_recv()

    def start(copies):
        for copy in copies:
            copy.start()

    @pl.when(z < chips - 1)
    def _():
        start(pass_on(z, "up"))

    @pl.when(z > 0)
    def _():
        start(pass_on(z, "down"))

    start(pass_on(z, "mate"))
    inner = jnp.minimum(z, chips - 1 - z)

    def place(t):
        k = (t + 1) // 2
        near = jnp.where(t % 2 == 1, z - k, z + k)
        return jnp.where(t <= 2 * inner, near, jnp.where(2 * z < chips - 1, t, chips - 1 - t))

    def far(zc):
        return jnp.where(zc > z, zc - z, z - zc)

    def side_of(zc):
        return jnp.where(zc > z, 1, 0)

    def relay(k, low, high):
        @pl.when(low)
        def _():
            pl.when(k > 2)(lambda: dout_arrive(z - k, True))
            got(z - k, c)

            @pl.when(z < chips - 1)
            def _():
                start(pass_on(z - k, "up"))

            start(pass_on(z - k, "mate"))

        @pl.when(high)
        def _():
            pl.when(k > 2)(lambda: dout_arrive(z + k, False))
            got(z + k, c)

            @pl.when(z > 0)
            def _():
                start(pass_on(z + k, "down"))

            start(pass_on(z + k, "mate"))

    def early(t):
        return (t >= 2) & (t % 2 == 0) & (t <= 2 * inner) & (t < chips - 1)

    def pair_copy(side):
        owner = z + 2 * side - 1
        return make(pair_ref.at[side], from_ref.at[z], pair_send.at[side], far_recv.at[z], (r, owner * 2 + c))

    def experts_and_sums(do_buf, xs_ref, dye_ref, dgu_ref, hx_ref, dxp_ref, yps_ref, core_stage):
        stages["core"] = (core_stage, stage_sem.at[0])
        before = lax.broadcasted_iota(jnp.int32, (tokens, tokens), 0) < lax.broadcasted_iota(jnp.int32, (tokens, tokens), 1)
        before = before.astype(F32).astype(BF)
        slot_index = lax.broadcasted_iota(jnp.int32, (CAP, tokens), 0).astype(F32)
        pair = 2 * CAP

        def do_copy(zc):
            return pltpu.make_async_copy(do_all.at[zc], do_buf, do_sem.at[0])

        def core_copy(zc, slot, t):
            return make(dxp_ref.at[slot, 1 - c], core_ref.at[zc], core_send.at[t], core_recv.at[zc], mate)

        def y_copy(zc, slot, t):
            return make(yps_ref.at[slot], y_core.at[zc], yc_send.at[t], yc_recv.at[zc], mate)

        def via_copy(zc, slot, t):
            side = side_of(zc)
            return make(
                dxp_ref.at[slot, c], via_ref.at[side], far_send.at[t], via_recv.at[side], (r, (z + 2 * side - 1) * 2 + c)
            )

        def far_copy(zc, slot, t):
            return make(dxp_ref.at[slot, c], from_ref.at[z], far_send.at[t], far_recv.at[z], (r, zc * 2 + c))

        def dgt_copy(zc, core, t):
            return make(dgt_ref.at[t, core], dgt_all.at[f], dgt_send.at[t, core], dgt_recv.at[f], (r, zc * 2 + core))

        def free_slot(t, slot):
            core_copy(z, slot, t).wait_send()
            y_copy(z, slot, t).wait_send()

            @pl.when(far(place(t)) >= 2)
            def _():
                far_copy(z, slot, t).wait_send()

        def add_ye(zc):
            make(y_core.at[zc], y_core.at[zc], yc_send.at[0], yc_recv.at[zc], mate).wait_recv()
            add_rows(y_ref.at[zc], y_ref.at[zc], landed(y_core.at[zc], "core"), tokens, 64)
            send_sem, _, from_recv = y_sems


        def chunk(t, carry):
            zc = place(t)
            slot = t % 2

            @pl.when(t > 0)
            def _():
                add_ye(place(t - 1))

            k = far(zc)
            both = (t % 2 == 1) & (t <= 2 * inner)
            single = (t > 2 * inner) & jnp.logical_not(early(t - 1))
            relay(k, both | (single & (zc < z)), both | (single & (zc > z)))
            dout_copy(zc, 1 - c, 2).wait_recv()
            do_copy(zc).start()
            got(zc, 1 - c)
            do_copy(zc).wait()

            @pl.when(t == 0)
            def _():
                load_experts.wait()

            @pl.when(t >= 2)
            def _():
                free_slot(t - 2, slot)

            picks, gates, dms = [], [], []
            at_chip = pl.multiple_of(zc * pair, 16)
            for core in range(2):
                mine = [gt_all[zc, core, pl.ds(f * local + i, 1), :] for i in range(local)]
                mine = jnp.concatenate(mine, axis=0) if local > 1 else mine[0]
                rank = jnp.where(mine >= 0.0, dot((mine >= 0.0).astype(F32).astype(BF), before), -1.0)
                chosen = [slot_index == rank[i : i + 1] for i in range(local)]
                gates.append([jnp.sum(jnp.where(chosen[i], mine[i : i + 1], 0.0), axis=1, keepdims=True) for i in range(local)])
                picks.append([one.astype(F32) for one in chosen])
                pick = jnp.concatenate([one.astype(BF) for one in picks[core]], axis=0)
                taken = dot(pick, n2_all[zc, core]).astype(BF)
                grads = dot(pick, do_buf[core])
                dms.append(grads.astype(BF))
                grads = grads * residual_scale
                at = pl.ds(pl.multiple_of(at_chip + core * CAP, 16), CAP)
                for i in range(local):
                    part = slice(i * CAP, (i + 1) * CAP)
                    xs_ref[i, at] = taken[part]
                    dye_ref[i, at] = (gates[core][i] * grads[part]).astype(BF)
            at = pl.ds(at_chip, pair)
            mades, backs = [], []
            for i in range(local):
                slots = xs_ref[i, at]
                gate_pre = dot_nt(slots, ge_ref[i, :FF])
                up_pre = dot_nt(slots, ge_ref[i, FF : 2 * FF])
                grad_act = dot_nt(dye_ref[i, at], ge_ref[i, 2 * FF :])
                sigmoid = 1.0 / (1.0 + jnp.exp(-gate_pre))
                silu = gate_pre * sigmoid
                act = (silu * up_pre).astype(BF)
                hx_ref[i, at] = act
                grad_gate = (grad_act * up_pre * (sigmoid * (1.0 + gate_pre * (1.0 - sigmoid)))).astype(BF)
                grad_up = (grad_act * silu).astype(BF)
                dgu_ref[i, at, :FF] = grad_gate
                dgu_ref[i, at, FF:] = grad_up
                backs.append((dot(grad_gate, ge_ref[i, :FF]) + dot(grad_up, ge_ref[i, FF : 2 * FF])).astype(BF))
            for core in range(2):
                pick = jnp.concatenate([one.astype(BF) for one in picks[core]], axis=0)
                part = slice(core * CAP, (core + 1) * CAP)
                sent = jnp.concatenate([backs[i][part] for i in range(local)], axis=0)
                dxp_ref[slot, core] = dot_tn(pick, sent).astype(BF)
            core_copy(zc, slot, t).start()
            for i in range(local):
                made = dot(hx_ref[i, at], ge_ref[i, 2 * FF :]).astype(BF)
                mades.append(made)
                for core in range(2):
                    part = slice(core * CAP, (core + 1) * CAP)
                    grads = dms[core][i * CAP : (i + 1) * CAP].astype(F32) * residual_scale
                    value = jnp.sum(grads * made[part].astype(F32), axis=1, keepdims=True)
                    dgt_ref[t, core, i : i + 1] = jnp.sum(picks[core][i] * value, axis=0, keepdims=True)
            for core in range(2):

                @pl.when((t > 0) | (c != core))
                def _():
                    dgt_copy(zc, core, t).start()

            @pl.when(early(t))
            def _():
                k_next = t // 2 + 1
                relay(k_next, z >= k_next, z + k_next < chips)

            for core in range(2):
                pick = jnp.concatenate([one.astype(BF) for one in picks[core]], axis=0)
                part = slice(core * CAP, (core + 1) * CAP)
                sent = jnp.concatenate([(gates[core][i] * mades[i][part].astype(F32)).astype(BF) for i in range(local)], axis=0)
                mixed = dot_tn(pick, sent).astype(BF)

                @pl.when(c == core)
                def _():
                    y_ref[zc] = mixed

                @pl.when(c != core)
                def _():
                    yps_ref[slot] = mixed

            y_copy(zc, slot, t).start()
            core_copy(zc, slot, t).wait_recv()
            there = core_ref.at[zc] if roomy else landed(core_ref.at[zc], "core")
            own = dxp_ref.at[slot, c]

            @pl.when(k == 0)
            def _():
                dx_ref[...] = own[...].astype(F32) + there[...].astype(F32)

            @pl.when(k == 1)
            def _():
                side = side_of(zc)
                add_rows(pair_ref.at[side], own, there, tokens, 64)

                @pl.when((z == 0) | (z == chips - 1))
                def _():
                    pair_copy(side).start()

            @pl.when(k >= 2)
            def _():
                add_rows(own, own, there, tokens, 64)

                @pl.when(k == 2)
                def _():
                    via_copy(zc, slot, t).start()

                @pl.when(k > 2)
                def _():
                    far_copy(zc, slot, t).start()

            return carry

        lax.fori_loop(0, chips, chunk, 0)

        for i in range(local):
            ge_ref[i, :FF] = dot_tn(dgu_ref[i, :, :FF], xs_ref[i]).astype(BF)
            ge_ref[i, FF : 2 * FF] = dot_tn(dgu_ref[i, :, FF:], xs_ref[i]).astype(BF)
            ge_ref[i, 2 * FF :] = dot_tn(hx_ref[i], dye_ref[i]).astype(BF)
            if bits:
                next(sums[i])
            if i > 0:
                continue

            @pl.when((z > 0) & (z < chips - 1))
            def _():
                for side in range(2):
                    make(via_ref.at[side], via_ref.at[side], far_send.at[0], via_recv.at[side], mate).wait_recv()
                    add_rows(pair_ref.at[side], pair_ref.at[side], via_ref.at[side], tokens, 64)
                    pair_copy(side).start()

        add_ye(place(chips - 1))
        for t in range(max(chips - 2, 0), chips):
            free_slot(t, t % 2)
        for t in range(chips):
            for core in range(2):

                @pl.when((t > 0) | (c != core))
                def _():
                    dgt_copy(z, core, t).wait_send()

    slots = chips * 2 * CAP
    pl.run_scoped(
        experts_and_sums,
        pltpu.VMEM((2, tokens, D), BF), pltpu.VMEM((local, slots, D), BF), pltpu.VMEM((local, slots, D), BF),
        pltpu.VMEM((local, slots, 2 * FF), BF), pltpu.VMEM((local, slots, FF), BF), pltpu.VMEM((2, 2, tokens, D), BF),
        pltpu.VMEM((2, tokens, D), BF), pltpu.VMEM((tokens, D), BF),
    )

    def line(own, size, step, core_add, name, reach, via, arrive, send_sem, via_recv, from_recv):
        def direct(k):
            return make(own(k), arrive.at[z], send_sem.at[k], from_recv.at[z], (r, k * 2 + c))

        def passing(k, side):
            return make(own(k), via.at[side], send_sem.at[k], via_recv.at[side], (r, (z + 2 * side - 1) * 2 + c))

        def within(k):
            return (k >= 0) & (k < chips)

        for d in range(chips - 1, 0, -1):
            for side in range(2):
                way = 1 if side else -1
                owner = z + d * way

                @pl.when(within(owner))
                def _():
                    core_add(owner)
                    if d > reach + 1:
                        direct(owner).start()
                    elif d == reach + 1:
                        passing(owner, side).start()
                    elif d == reach:
                        pl.when(jnp.logical_not(within(z - way)))(lambda: direct(owner).start())

        core_add(z)
        yield
        for side in range(2):
            way = 1 if side else -1
            owner = z + reach * way

            @pl.when(within(owner) & within(z - way))
            def _():
                make(via.at[side], via.at[side], send_sem.at[0], via_recv.at[side], mate).wait_recv()
                add_rows(own(owner), own(owner), landed(via.at[side], name), size, step)
                direct(owner).start()

        yield
        for k in range(chips):

            @pl.when((z != k) & (far(k) != reach + 1))
            def _():
                make(arrive.at[k], arrive.at[k], send_sem.at[0], from_recv.at[k], mate).wait_recv()
                add_rows(own(z), own(z), landed(arrive.at[k], name), size, step)

        for k in range(chips):

            @pl.when(z != k)
            def _():
                direct(k).wait_send()

    def mixture():
        yield from line(lambda k: y_ref.at[k], tokens, 64, lambda k: None, "tokens", 1, y_via, y_from, *y_sems)
        out_ref[...] = (h1_ref[...] + residual_scale * y_ref[z].astype(F32)).astype(BF)

    def attention(q_ref, kd_ref, vd_ref, o_ref, p_ref, do_ref, dqkv_ref, gkv_ref, gq_ref, go_ref, halves_stage, tokens_stage, kv_stage, o_stage):
        loads = [
            pltpu.make_async_copy(heads_hbm.at[i], ref, heads_sem.at[i]) for i, ref in enumerate((q_ref, kd_ref, vd_ref, o_ref))
        ]
        start(loads)
        stages["halves"] = (halves_stage, stage_sem.at[1])
        stages["tokens"] = (tokens_stage, stage_sem.at[2])
        stages["kv"] = (kv_stage, stage_sem.at[3])
        stages["o"] = (o_stage, stage_sem.at[4])
        def projection(index, name, grad_ref, core, via, arrive, sems):
            core_sem, *sems = sems
            parts, results, wide = parts_ref.at[index], results_ref.at[index], D // replicas
            crossing = make(grad_ref.at[:, 1 - c], core, core_sem.at[0], core_sem.at[1], mate)
            crossing.start()
            yield
            crossing.wait_recv()

            def own(k):
                return grad_ref.at[k, c]

            yield from line(
                own, rows, 16, lambda k: add_rows(own(k), own(k), core.at[k], rows, 16), name, 1, via, arrive, *sems
            )
            crossing.wait_send()
            mine = grad_ref.at[z, c]

            def columns(part):
                return pl.ds(pl.multiple_of(part * wide, LANE), wide)

            def part_copy(d):
                to = (r + d) % replicas
                return make(
                    mine.at[:, columns(to)], parts.at[r], part_send.at[index, d], part_recv.at[index, r], (to, f)
                )

            def small_copy(d):
                to = (r + d) % replicas
                return make(mine.at[:, pl.ds(D, LANE)], smalls_ref.at[r], small_send.at[d], small_recv.at[r], (to, f))

            for d in range(1, replicas):
                part_copy(d).start()
                if index == 0:
                    small_copy(d).start()
            parts[r] = mine[:, columns(r)]
            if index == 0:
                smalls_ref[r] = mine[:, pl.ds(D, LANE)]
            yield
            for d in range(1, replicas):
                peer = (r + d) % replicas
                make(
                    parts.at[peer], parts.at[peer], part_send.at[index, d], part_recv.at[index, peer], (peer, f)
                ).wait_recv()
                if index == 0:
                    make(
                        smalls_ref.at[peer], smalls_ref.at[peer], small_send.at[d], small_recv.at[peer], (peer, f)
                    ).wait_recv()
            total = parts[0].astype(F32)
            for k in range(1, replicas):
                total = total + parts[k].astype(F32)
            results[r] = total.astype(BF)

            def result_copy(d):
                to = (r + d) % replicas
                return make(
                    results.at[r], results.at[r], result_send.at[index, d], result_recv.at[index, r], (to, f)
                )

            for d in range(1, replicas):
                result_copy(d).start()
            if index == 0:
                small = smalls_ref[0].astype(F32)
                for k in range(1, replicas):
                    small = small + smalls_ref[k].astype(F32)
                total_ref[...] = small
            yield
            for d in range(1, replicas):
                peer = (r + d) % replicas
                make(
                    results.at[peer], results.at[peer], result_send.at[index, d], result_recv.at[index, peer], (peer, f)
                ).wait_recv()
            for d in range(1, replicas):
                part_copy(d).wait_send()
                if index == 0:
                    small_copy(d).wait_send()
                result_copy(d).wait_send()

        moe = [mixture()]
        kvs = [projection(0, "kv", gkv_ref, kv_core, kv_via, kv_from, kv_sems)]
        outs = [projection(1, "o", go_ref, o_core, o_via, o_from, o_sems)]
        qs = [projection(2, "o", gq_ref, q_core, q_via, q_from, q_sems)]

        def go(*turns):
            for turn in turns:
                for process in turn:
                    next(process, None)

        def dgate():
            found = [dgt_all[k, :local] for k in range(2 * chips)]
            return jnp.concatenate(found + [jnp.zeros((LANE - E, tokens), F32)], axis=0).T

        for k in range(chips):

            @pl.when((z == k + 1) | (z + 1 == k) | (z > k + 2) | (z + 2 < k))
            def _():
                make(from_ref.at[k], from_ref.at[k], far_send.at[0], far_recv.at[k], mate).wait_recv()
                there = from_ref.at[k] if roomy else landed(from_ref.at[k], "tokens")
                add_rows(dx_ref, dx_ref, there, tokens, 64)

        for k in range(2 * chips):

            @pl.when(f == k)
            def _():
                for core in range(2):

                    @pl.when(c == core)
                    def _():
                        dgt_all[k] = dgt_ref[0, core]

            @pl.when(f != k)
            def _():
                make(dgt_all.at[k], dgt_all.at[k], dgt_send.at[0, 0], dgt_recv.at[k], mate).wait_recv()

        for load in loads:
            load.wait()
        backward = attention_backward(
            x_ref, dout_ref, cos_ref, sin_ref, columns, q_ref, kd_ref, vd_ref, p_hbm, o_ref, h1_ref, n2_all.at[z, c], gd_ref,
            dx_ref, dgate, gin_ref, gq_ref, gkv_ref, go_ref, do_ref, dqkv_ref, p_ref, p_sem,
        )
        next(backward)
        go(outs)
        next(backward)
        go(first)
        next(backward)
        go(outs)
        next(backward)
        go(qs)
        next(backward, None)
        go(kvs, last, qs, first, kvs, last, outs, first, moe, last, qs, outs, kvs, outs, first, qs, outs, moe, qs, kvs, moe, last)
        go(qs, kvs, kvs)
        go(*[moe + outs + qs + kvs + sums] * (2 * bits + 8))

    size = ge_ref.shape[1] // max(bits, 1)
    pl.run_scoped(
        attention, *[pltpu.VMEM((tokens, D), BF)] * 4,
        pltpu.VMEM((2, 2 * tokens, tokens), F32), pltpu.VMEM((tokens, D), BF),
        pltpu.VMEM((tokens, QKV), BF), pltpu.VMEM((chips, 2, rows, D + LANE), BF), pltpu.VMEM((chips, 2, rows, D), BF),
        pltpu.VMEM((chips, 2, rows, D), BF), pltpu.VMEM((size // 2, D), BF), pltpu.VMEM((tokens, D), BF),
        pltpu.VMEM((rows, D + LANE), BF), pltpu.VMEM((rows, D), BF),
    )

    for e in range(local):
        copy = pltpu.make_async_copy(ge_ref.at[e], ge_hbm.at[e], ge_sem.at[e])
        if not bits:
            copy.start()
        copy.wait()
    for side in range(2):

        @pl.when(z > 0 if side == 0 else z < chips - 1)
        def _():
            pair_copy(side).wait_send()

    for k in range(chips):

        @pl.when((z >= k) & (z < chips - 1))
        def _():
            for copy in pass_on(k, "up"):
                copy.wait_send()

        @pl.when((z <= k) & (z > 0))
        def _():
            for copy in pass_on(k, "down"):
                copy.wait_send()

        for copy in pass_on(k, "mate"):
            copy.wait_send()

    for k in range(chips):
        for late in range(2):
            to_mate(k, c, late).wait_send()
        dout_copy(k, c, 2).wait_send()

        @pl.when((z >= k) & (z < chips - 1))
        def _():
            dout_copy(k, c, 0).wait_send()
            for kind in range(3):
                along(k, kind, True).wait_send()

        @pl.when((z <= k) & (z > 0))
        def _():
            dout_copy(k, c, 1).wait_send()
            for kind in range(3):
                along(k, kind, False).wait_send()

        @pl.when(z != k)
        def _():
            for d in range(1, replicas):
                for kind in (0, 2):
                    across(k, kind, d).wait_send()


def finish(gexp_ref, results_ref, total_ref, gin_ref, out_ref, *outs):
    layer_out, grad_in, gains_one, query, key, value, output, gains_two, router, expert = outs
    expert[...] = gexp_ref[...].astype(F32)
    layer_out[...] = out_ref[...]
    grad_in[...] = gin_ref[...]
    for index, targets in ((0, (key, value)), (1, (output,)), (2, (query,))):
        start, wide = 0, results_ref.shape[3]
        for ref in targets:
            for at in range(0, ref.shape[1], LANE):
                part, column = divmod(start + at, wide)
                ref[:, at : at + LANE] = results_ref[index, part, :, column : column + LANE].astype(F32)
            start += ref.shape[1]

    @pl.when(pl.program_id(0) == 0)
    def _():
        small = total_ref[...].T
        router[...] = small[:E]
        gains_one[...] = small[E : E + 1]
        gains_two[...] = small[E + 1 : E + 2]


def call(kernel, out_shape, args, scratch=(), outside=0, out_outside=0, **params):
    spaces = [pltpu.SMEM if a.dtype == jnp.int32 and a.size <= 16 else pltpu.VMEM for a in args]
    spaces[len(args) - outside :] = [pl.ANY] * outside
    return pl.pallas_call(
        kernel,
        out_shape=out_shape,
        in_specs=[pl.BlockSpec(memory_space=space) for space in spaces],
        out_specs=[
            pl.BlockSpec(memory_space=pltpu.VMEM if i < len(out_shape) - out_outside else pl.ANY)
            for i in range(len(out_shape))
        ],
        scratch_shapes=list(scratch),
        compiler_params=pltpu.CompilerParams(
            vmem_limit_bytes=VMEM_LIMIT, has_side_effects="collective_id" in params, **params
        ),
    )(*args)


def shape(dims, dtype):
    return jax.ShapeDtypeStruct(dims, dtype)


def make_body(mesh):
    group, replicas = mesh.shape["fsdp"], mesh.shape["replica"]
    local = E // group

    def body(
        hidden_in, seq_lengths, routes, norm1_gain, w_query, w_key, w_value, w_output, norm2_gain, w_router,
        expert_weights, out_cotangent,
    ):
        tokens = hidden_in.shape[0]
        rows = w_query.shape[0]
        chips = group // 2
        dma = pltpu.SemaphoreType.DMA
        bits = replicas.bit_length() - 1
        size = 3 * FF // bits if bits else 0
        roomy = chips <= 4
        landing = [shape((local * bits, size >> (k + 1), D), BF) for k in range(bits)]
        blocks = [shape((chips, tokens, D), BF)] * 2
        landing += [shape((chips, tokens, D), BF)]
        if not roomy:
            landing += blocks
        outs = call(
            functools.partial(layer, replicas, chips),
            [
                shape((tokens, D), F32), shape((tokens, D), BF), shape((3, replicas, rows, D // replicas), BF),
                shape((rows, LANE), F32), shape((local, 3 * FF, D), BF),
                shape((KVH, 2 * tokens, tokens), F32), shape((4, tokens, D), BF), shape((chips, 2, tokens, D), BF),
                shape((2, tokens, D), BF), shape((chips, tokens, D), BF), shape((2, rows, D + LANE), BF),
                shape((chips, rows, D + LANE), BF), shape((2, rows, D), BF), shape((chips, rows, D), BF),
                shape((2, rows, D), BF), shape((chips, rows, D), BF),
            ]
            + landing,
            (
                hidden_in, seq_lengths, routes.T, rope_table(tokens), w_query, w_key, w_value, w_output, w_router.T,
                norm1_gain[None], norm2_gain[None], out_cotangent, expert_weights,
            ),
            [
                pltpu.VMEM((chips, 2, rows, W_O + D), BF), pltpu.VMEM((tokens, D), F32),
                pltpu.VMEM((tokens, LANE), F32), pltpu.VMEM((tokens, LANE), F32), pltpu.VMEM((tokens, LANE), F32),
                dma((4,)), dma((1,)), dma((3, chips)), dma((3, chips)), dma((3, chips)), dma((3, chips, replicas)),
                dma((3, chips, replicas)), dma((2, chips)), dma((2, chips)), dma((3, chips)), dma((chips, 2)),
                pltpu.VMEM((local, 3 * FF, D), BF), pltpu.VMEM((chips, 2, tokens, D), BF),
                pltpu.VMEM((chips, 2, E, tokens), F32), pltpu.VMEM((2, tokens, D), BF), pltpu.VMEM((2, tokens, D), BF),
                pltpu.VMEM((chips, 2, 8, tokens), F32), pltpu.VMEM((group, 8, tokens), F32),
                pltpu.VMEM((chips, tokens, D), BF), pltpu.VMEM((chips, rows, D + LANE), BF), pltpu.VMEM((chips, rows, D), BF),
                pltpu.VMEM((chips, rows, D), BF), pltpu.VMEM((3, replicas, rows, D // replicas), BF),
                pltpu.VMEM((replicas, rows, LANE), BF),
            ]
            + ([pltpu.VMEM(b.shape, b.dtype) for b in blocks] if roomy else [])
            + ([dma((chips,))] * 3 + [dma((chips, 2))]) * 2 + [dma((chips,))] * 4 + [dma((2,))] * 2
            + [dma((chips, 2)), dma((group,)), dma((chips,)), dma((chips,))]
            + [dma((1,)), dma((1,)), dma((5,)), dma((local,)), dma((2,))]
            + [dma((max(local * bits, 1), max(2 * bits, 1)))] * 2
            + [pltpu.SemaphoreType.REGULAR((max(local * bits, 1), max(bits, 1)))]
            + [dma((chips,)), dma((2,)), dma((chips,))] + [dma((2,)), dma((chips,)), dma((2,)), dma((chips,))] * 3
            + [dma((3, replicas))] * 2 + [dma((replicas,))] * 2 + [dma((3, replicas))] * 2,
            outside=1,
            out_outside=12 + len(landing),
            collective_id=0,
        )
        grad_in, layer_out, results, total, grad_experts = outs[:5]
        steps = 4

        def moving(a, dim=0):
            block = tuple(n // steps if i == dim else n for i, n in enumerate(a.shape))
            return pl.BlockSpec(block, lambda i: tuple(i if at == dim else 0 for at in range(len(block))))

        def still(a):
            return pl.BlockSpec(a.shape, lambda i: (0,) * len(a.shape))

        grad_experts = grad_experts.reshape(local * 3 * FF, D)
        gain, router = shape((1, rows), F32), shape((E, rows), F32)
        wide, narrow = shape((rows, D), F32), shape((rows, KVH * HD), F32)
        out_shapes = [
            shape((tokens, D), BF), shape((tokens, D), F32), gain, wide, narrow, narrow, wide, gain, router,
            shape((local * 3 * FF, D), F32),
        ]
        outs = pl.pallas_call(
            finish,
            grid=(steps,),
            in_specs=[moving(grad_experts), moving(results, 2), still(total), moving(grad_in), moving(layer_out)],
            out_specs=[still(a) if a in (gain, router) else moving(a) for a in out_shapes],
            out_shape=out_shapes,
            compiler_params=pltpu.CompilerParams(vmem_limit_bytes=VMEM_LIMIT),
        )(grad_experts, results, total, grad_in, layer_out)
        return (
            outs[0], outs[1], outs[2][0], outs[3], outs[4], outs[5], outs[6], outs[7][0], outs[8].T,
            outs[9].reshape(local, 3 * FF, D),
        )

    return body


def solution(mesh):
    tokens, weights = P(("replica", "fsdp"), None), P("fsdp", None)
    return jax.shard_map(
        make_body(mesh),
        mesh=mesh,
        in_specs=(
            tokens, tokens, tokens, P("fsdp"), weights, weights, weights, weights, P("fsdp"), weights,
            P("fsdp", None, None), tokens,
        ),
        out_specs=(
            tokens, tokens, P("fsdp"), weights, weights, weights, weights, P("fsdp"), weights, P("fsdp", None, None),
        ),
        check_vma=False,
    )
```

```python
import functools

import jax
import jax.numpy as jnp
import numpy as np
from jax import lax
from jax.experimental import pallas as pl
from jax.experimental.pallas import tpu as pltpu
from jax.sharding import PartitionSpec as P

D = 1024
H = 16
KVH = 8
HD = 64
FF = 512
TOPK = 8
E = 16
CAP = 144
LANE = 128
QKV = H * HD + 2 * KVH * HD
QKVO = QKV + D
W_O = QKV + LANE

norm_eps = 1e-06
score_scale = 0.015625
residual_scale = 0.22
rope_base = 10000.0
masked_score = -1e30

BF = jnp.bfloat16
F32 = jnp.float32
VMEM_LIMIT = 63 * 2**20


def dot(a, b):
    return lax.dot_general(a, b, (((1,), (0,)), ((), ())), preferred_element_type=F32)


def dot_nt(a, b):
    return lax.dot_general(a, b, (((1,), (1,)), ((), ())), preferred_element_type=F32)


def dot_tn(a, b):
    return lax.dot_general(a, b, (((0,), (0,)), ((), ())), preferred_element_type=F32)


def lanes_of(rows):
    return lax.broadcasted_iota(jnp.int32, (rows, LANE), 1)


def turned(block, lane):
    return jnp.where(lane % HD < HD // 2, pltpu.roll(block, LANE - HD // 2, 1), pltpu.roll(block, HD // 2, 1))


def halves(block, low):
    zero = jnp.zeros_like(block)
    return jnp.concatenate([jnp.where(low, block, zero), jnp.where(low, zero, block)], axis=0)


def rope_table(tokens):
    frequency = np.float32(rope_base) ** (-np.arange(0, HD, 2, dtype=np.float32) / np.float32(HD))
    frequency = np.tile(frequency.astype(np.float32), LANE // (HD // 2))
    angles = (np.arange(tokens, dtype=np.float32)[:, None] * frequency[None, :]).astype(np.float64)
    sign = np.where(np.arange(LANE) % HD < HD // 2, -1.0, 1.0)
    pieces = []
    for values in (np.cos(angles), np.sin(angles) * sign[None, :]):
        rest = values.astype(np.float32)
        for _ in range(3):
            piece = rest.astype(BF)
            pieces.append(piece)
            rest = rest - piece.astype(np.float32)
    return np.concatenate(pieces, axis=1)


class Copies:
    def make(self, src, dst, send, recv, device):
        return pltpu.make_async_remote_copy(
            src_ref=src, dst_ref=dst, send_sem=send, recv_sem=recv, device_id=device, device_id_type=pl.DeviceIdType.MESH
        )


def meet(devices, expected):
    barrier = pltpu.get_barrier_semaphore()
    for condition, device in devices:

        def signal(device=device):
            pl.semaphore_signal(barrier, inc=1, device_id=device, device_id_type=pl.DeviceIdType.MESH)

        if condition is True:
            signal()
        else:
            pl.when(condition)(signal)
    pl.semaphore_wait(barrier, expected)


def attention_backward(
    x_ref, dout_ref, cos_ref, sin_ref, columns, q_ref, kd_ref, vd_ref, p_hbm, o_ref, h1_ref, n2_ref, gd_ref, dx_ref, dgate,
    gin_ref, gq_ref, gkv_ref, go_ref, do_ref, dqkv_ref, p_ref, p_sem,
):
    tokens = x_ref.shape[0]
    lane = lanes_of(tokens)
    low = lane < HD

    def p_copy(g):
        return pltpu.make_async_copy(p_hbm.at[g], p_ref.at[g % 2], p_sem.at[g % 2])

    p_copy(0).start()

    def put(ref, at, value):
        ref[:, :, :, at] = value.astype(BF).reshape(*ref.shape[:3], value.shape[1])

    small = columns(QKV, LANE).astype(F32).T
    gain_one, gain_two = small[E : E + 1], small[E + 1 : E + 2]
    after = h1_ref[...]
    factor_two = lax.rsqrt(jnp.mean(after * after, axis=1, keepdims=True) + norm_eps)
    gates = jnp.maximum(gd_ref[...], 0.0)
    grad_gates = dgate()
    chosen = gates * (grad_gates - jnp.sum(gates * grad_gates, axis=1, keepdims=True))
    grad_logits = chosen.astype(BF)
    grad_normed = dx_ref[...] + dot_nt(grad_logits, columns(QKV, LANE))
    scaled = grad_normed * gain_two
    grad_after = dout_ref[...].astype(F32) + (
        factor_two * scaled - after * factor_two**3 * jnp.mean(scaled * after, axis=1, keepdims=True)
    )
    grad_gain_two = jnp.sum(grad_normed * after * factor_two, axis=0, keepdims=True)
    gin_ref[...] = grad_after
    grad_branch = (residual_scale * grad_after).astype(BF)
    for at in range(0, D, FF):
        put(go_ref, slice(at, at + FF), dot_tn(o_ref[...], grad_branch[:, at : at + FF]))
    do_ref[...] = dot_nt(grad_branch, columns(W_O, D)).astype(BF)
    grad_router = dot_tn(n2_ref[...], grad_logits)
    yield

    cosines, sines = cos_ref[...], sin_ref[...]
    key_back, value_back = [], []
    for g in range(KVH):
        at = slice(g * LANE, (g + 1) * LANE)
        queries = halves(q_ref[:, at].astype(F32), low).astype(BF)
        outs = halves(do_ref[:, at].astype(F32), low).astype(BF)
        if g + 1 < KVH:
            p_copy(g + 1).start()
        p_copy(g).wait()
        weights = p_ref[g % 2]
        grad_weights = dot_nt(outs, vd_ref[:, at])
        total = jnp.sum(weights * grad_weights, axis=1, keepdims=True)
        grad_scores = (weights * (grad_weights - total)).astype(BF)
        block = dot(grad_scores, kd_ref[:, at])
        block = jnp.where(low, block[:tokens], block[tokens:]) * score_scale
        dqkv_ref[:, at] = (block * cosines - turned(block, lane) * sines).astype(BF)
        block = dot_tn(grad_scores, queries) * score_scale
        key_back.append(block + pltpu.roll(block, HD, 1))
        block = dot_tn(weights.astype(BF), outs)
        value_back.append(block + pltpu.roll(block, HD, 1))
        if g == KVH // 2 - 1:
            yield
    for m in range(KVH // 2):
        block = jnp.where(low, key_back[2 * m], key_back[2 * m + 1])
        at = slice(H * HD + m * LANE, H * HD + (m + 1) * LANE)
        dqkv_ref[:, at] = (block * cosines - turned(block, lane) * sines).astype(BF)
        at = slice(H * HD + KVH * HD + m * LANE, H * HD + KVH * HD + (m + 1) * LANE)
        dqkv_ref[:, at] = jnp.where(low, value_back[2 * m], value_back[2 * m + 1]).astype(BF)
    yield

    source = x_ref[...].astype(F32)
    factor_one = lax.rsqrt(jnp.mean(source * source, axis=1, keepdims=True) + norm_eps)
    normed = (source * factor_one * gain_one).astype(BF)
    for at in range(0, H * HD, FF):
        put(gq_ref, slice(at, at + FF), dot_tn(normed, dqkv_ref[:, at : at + FF]))
    yield
    grad_normed = dot_nt(dqkv_ref[...], columns(0, QKV))
    scaled = grad_normed * gain_one
    grad_vector = factor_one * scaled - source * factor_one**3 * jnp.mean(scaled * source, axis=1, keepdims=True)
    gin_ref[...] += grad_vector
    grad_gain_one = jnp.sum(grad_normed * source * factor_one, axis=0, keepdims=True)
    gains = jnp.concatenate([grad_gain_one, grad_gain_two, jnp.zeros((6, D), F32)], axis=0).T
    at = lanes_of(D)
    extra = jnp.where(at == E, gains[:, 0:1], jnp.where(at == E + 1, gains[:, 1:2], grad_router))
    put(gkv_ref, slice(D, D + LANE), extra)
    for at in range(0, QKV - H * HD, FF):
        put(gkv_ref, slice(at, at + FF), dot_tn(normed, dqkv_ref[:, H * HD + at : H * HD + at + FF]))


def add_rows(target, first, second, rows, step):
    def some(i, carry):
        at = pl.ds(pl.multiple_of(i * step, step), step)
        target[at] = (first[at].astype(F32) + second[at].astype(F32)).astype(target.dtype)
        return carry

    lax.fori_loop(0, rows // step, some, 0)


def layer(
    replicas, chips,
    x_ref, len_ref, routes_ref, table_ref, wq_ref, wk_ref, wv_ref, wo_ref, wr_ref, g1_ref, g2_ref, dout_ref, we_hbm,
    gin_ref, out_ref, results_ref, total_ref, ge_hbm, p_hbm, heads_hbm, do_all, y_via, y_from, kv_via, kv_from, q_via, q_from,
    o_via, o_from, *rest,
):
    bits = replicas.bit_length() - 1
    roomy = chips <= 4
    arrived, y_core, rest = rest[:bits], rest[bits], rest[bits + 1 :]
    if not roomy:
        (core_ref, from_ref), rest = rest[:2], rest[2:]
    (w_all, h1_ref, gd_ref, cos_ref, sin_ref), rest = rest[:5], rest[5:]
    (heads_sem, own_sem, z_up, z_down, z_recv, xy_send, xy_recv, mate_send, mate_recv, do_send, do_recv), rest = rest[:11], rest[11:]
    (ge_ref, n2_all, gt_all, via_ref, pair_ref, dgt_ref, dgt_all, y_ref, kv_core, q_core, o_core, parts_ref, smalls_ref), rest = (
        rest[:13], rest[13:]
    )
    dx_ref = gin_ref
    if roomy:
        (core_ref, from_ref), rest = rest[:2], rest[2:]
    (n2_up, n2_down, n2_mate, n2_recv, gt_up, gt_down, gt_mate, gt_recv,
     core_send, core_recv, far_send, far_recv, pair_send, via_recv, dgt_send, dgt_recv, yc_send, yc_recv,
     do_sem, we_sem, stage_sem, ge_sem, p_sem, ar_send, ar_recv, ar_free,
     *sum_sems, part_send, part_recv, small_send, small_recv, result_send, result_recv) = rest
    y_sems, kv_sems, q_sems, o_sems = sum_sems[:3], sum_sems[3:7], sum_sems[7:11], sum_sems[11:]
    local, tokens, rows = ge_ref.shape[0], x_ref.shape[0], q_core.shape[1]
    r, f = lax.axis_index("replica"), lax.axis_index("fsdp")
    z, c = f // 2, f % 2
    mate, above, below = (r, z * 2 + 1 - c), (r, f + 2), (r, f - 2)
    make = Copies().make

    load_experts = pltpu.make_async_copy(we_hbm, ge_ref, we_sem.at[0])
    load_experts.start()
    own_dout = pltpu.make_async_copy(dout_ref, do_all.at[z, c], own_sem.at[0])
    own_dout.start()
    packed = [wr_ref[...].astype(F32), g1_ref[...].astype(F32), g2_ref[...].astype(F32)]
    packed = jnp.concatenate(packed + [jnp.zeros((LANE - E - 2, rows), F32)], axis=0)
    own = w_all.at[z, c]
    own[:, : H * HD] = wq_ref[...]
    own[:, H * HD : H * HD + KVH * HD] = wk_ref[...]
    own[:, H * HD + KVH * HD : QKV] = wv_ref[...]
    own[:, QKV:W_O] = packed.T.astype(BF)
    own[:, W_O:] = wo_ref[...]
    peers = [(True, mate)]
    for k in range(1, chips):
        to = (z + k) % chips
        peers += [(True, (r, to * 2 + c)), (True, (r, to * 2 + 1 - c))]
    peers += [(True, ((r + d) % replicas, f)) for d in range(1, replicas)]
    meet(peers, len(peers))

    def part(kind):
        if kind == 0:
            return pl.ds(pl.multiple_of(r * (QKV // replicas), LANE), QKV // replicas)
        if kind == 1:
            return pl.ds(QKV, LANE)
        return pl.ds(pl.multiple_of(W_O + r * (D // replicas), LANE), D // replicas)

    def along(zb, kind, up):
        ref = w_all.at[zb, c, :, part(kind)]
        return make(ref, ref, (z_up if up else z_down).at[kind, zb], z_recv.at[kind, zb], above if up else below)

    def across(zb, kind, d):
        ref = w_all.at[zb, c, :, part(kind)]
        return make(ref, ref, xy_send.at[kind, zb, d], xy_recv.at[kind, zb, r], ((r + d) % replicas, f))

    def wait_across(zb, kind):
        for d in range(1, replicas):
            peer = (r + d) % replicas
            ref = w_all.at[zb, c, :, part(kind)]
            make(ref, ref, xy_send.at[kind, zb, d], xy_recv.at[kind, zb, peer], (peer, f)).wait_recv()

    def to_mate(zb, core, late):
        ref = w_all.at[zb, core, :, pl.ds(W_O, D) if late else pl.ds(0, W_O)]
        return make(ref, ref, mate_send.at[late, zb], mate_recv.at[late, zb], mate)

    def dout_copy(zb, core, way):
        source = do_all.at[zb, core]
        return make(source, do_all.at[zb, core], do_send.at[way, zb], do_recv.at[zb, core], (above, below, mate)[way])

    def both_sides(k, act):
        @pl.when(z >= k)
        def _():
            act(z - k, True)

        @pl.when(z < chips - k)
        def _():
            act(z + k, False)

    def onward(up):
        return z < chips - 1 if up else z > 0

    def dout_arrive(zb, low):
        dout_copy(zb, c, 0 if low else 1).wait_recv()

        @pl.when(onward(low))
        def _():
            dout_copy(zb, c, 0 if low else 1).start()

        dout_copy(zb, c, 2).start()

    def columns(start, size):
        return w_all.reshape(D, W_O + D)[:, start : start + size]

    def forward(p_ref, q_ref, kd_ref, vd_ref, o_ref):
        for kind in range(3):
            both_sides(1, lambda zb, low: along(z, kind, not low).start())
        for late in range(2):
            to_mate(z, c, late).start()

        source = x_ref[...].astype(F32)
        factor = lax.rsqrt(jnp.mean(source * source, axis=1, keepdims=True) + norm_eps)
        lane = lanes_of(tokens)
        low_lane = lane < HD
        row = lax.broadcasted_iota(jnp.int32, (tokens, tokens), 0)
        column = lax.broadcasted_iota(jnp.int32, (tokens, tokens), 1)
        row_at = lax.broadcasted_iota(jnp.int32, (tokens, 1), 0)
        column_at = lax.broadcasted_iota(jnp.int32, (1, tokens), 1)
        row_segment = jnp.zeros((tokens, 1), jnp.int32)
        row_start = jnp.zeros((tokens, 1), jnp.int32)
        column_segment = jnp.zeros((1, tokens), jnp.int32)
        end = jnp.int32(0)
        for j in range(len_ref.shape[1]):
            end = end + len_ref[0, j]
            row_segment += (row_at >= end).astype(jnp.int32)
            row_start = jnp.maximum(row_start, jnp.where(row_at >= end, end, 0))
            column_segment += (column_at >= end).astype(jnp.int32)
        place = (column == row - row_start).astype(F32).astype(BF)
        found = dot(place, table_ref[...])
        found = [found[:, i * LANE : (i + 1) * LANE] for i in range(6)]
        cosines, sines = found[0] + found[1] + found[2], found[3] + found[4] + found[5]
        cos_ref[...] = cosines
        sin_ref[...] = sines

        own_dout.wait()
        for k in range(1, chips):
            for kind in range(3):

                def arrive(zb, low, kind=kind):
                    along(zb, kind, low).wait_recv()

                    @pl.when(onward(low))
                    def _():
                        along(zb, kind, low).start()

                    if kind != 1:
                        for d in range(1, replicas):
                            across(zb, kind, d).start()

                both_sides(k, arrive)
            if k == min(2, chips - 1):
                both_sides(1, lambda zb, low: dout_copy(z, c, 1 if low else 0).start())
                dout_copy(z, c, 2).start()

        def share(k, late):
            def act(zb, low):
                wait_across(zb, 2 if late else 0)
                to_mate(zb, c, late).start()

            both_sides(k, act)

        for k in range(1, chips):
            share(k, 0)
        if chips > 1:
            both_sides(1, dout_arrive)
        for k in range(chips):
            to_mate(k, 1 - c, 0).wait_recv()

        small = columns(QKV, LANE)
        gains = small.astype(F32).T
        gain_one, gain_two = gains[E : E + 1], gains[E + 1 : E + 2]
        normed = (source * factor * gain_one).astype(BF)
        q_all = dot(normed, columns(0, H * HD))
        for g in range(H // 2):
            at = slice(g * LANE, (g + 1) * LANE)
            block = q_all[:, at]
            q_ref[:, at] = (block * cosines + turned(block, lane) * sines).astype(BF)
        kv = dot(normed, columns(H * HD, 2 * KVH * HD))
        for m in range(KVH // 2):
            block = kv[:, m * LANE : (m + 1) * LANE]
            block = block * cosines + turned(block, lane) * sines
            other = pltpu.roll(block, HD, 1)
            kd_ref[:, 2 * m * LANE : (2 * m + 1) * LANE] = jnp.where(low_lane, block, other).astype(BF)
            kd_ref[:, (2 * m + 1) * LANE : (2 * m + 2) * LANE] = jnp.where(low_lane, other, block).astype(BF)
            block = kv[:, KVH * HD + m * LANE : KVH * HD + (m + 1) * LANE]
            other = pltpu.roll(block, HD, 1)
            vd_ref[:, 2 * m * LANE : (2 * m + 1) * LANE] = jnp.where(low_lane, block, other).astype(BF)
            vd_ref[:, (2 * m + 1) * LANE : (2 * m + 2) * LANE] = jnp.where(low_lane, other, block).astype(BF)
        saves = [
            pltpu.make_async_copy(ref, heads_hbm.at[i], heads_sem.at[i]) for i, ref in enumerate((q_ref, kd_ref, vd_ref, o_ref))
        ]
        for save in saves[:3]:
            save.start()
        bias = jnp.where((row_segment == column_segment) & (column <= row), 0.0, masked_score)
        bias = jnp.concatenate([bias, bias], axis=0)

        def p_copy(g):
            return pltpu.make_async_copy(p_ref.at[g % 2], p_hbm.at[g], p_sem.at[g % 2])

        for g in range(KVH):
            at = slice(g * LANE, (g + 1) * LANE)
            queries = halves(q_ref[:, at].astype(F32), low_lane).astype(BF)
            scores = dot_nt(queries, kd_ref[:, at]) * score_scale + bias
            shifted = jnp.exp(scores - jnp.max(scores, axis=1, keepdims=True))
            weights = shifted * (1.0 / jnp.sum(shifted, axis=1, keepdims=True))
            if g >= 2:
                p_copy(g - 2).wait()
            p_ref[g % 2] = weights
            p_copy(g).start()
            mixed = dot(weights.astype(BF), vd_ref[:, at])
            o_ref[:, at] = jnp.where(low_lane, mixed[:tokens], mixed[tokens:]).astype(BF)

        saves[3].start()
        if chips > 2:
            both_sides(2, dout_arrive)
        for k in range(1, chips):
            share(k, 1)

        for k in range(chips):
            to_mate(k, 1 - c, 1).wait_recv()
        after = source + residual_scale * dot(o_ref[...], columns(W_O, D))
        h1_ref[...] = after
        factor = lax.rsqrt(jnp.mean(after * after, axis=1, keepdims=True) + norm_eps)
        normed = (after * factor * gain_two).astype(BF)
        n2_all[z, c] = normed
        logits = dot(normed, small).T[:E]
        expert = lax.broadcasted_iota(jnp.int32, (E, tokens), 0)
        routed = routes_ref[0:1] == expert
        for j in range(1, TOPK):
            routed |= routes_ref[j : j + 1] == expert
        top = jnp.max(jnp.where(routed, logits, masked_score), axis=0, keepdims=True)
        powers = jnp.where(routed, jnp.exp(logits - top), 0.0)
        gates = powers / jnp.sum(powers, axis=0, keepdims=True)
        gates = jnp.where(routed, gates, -1.0)
        gt_all[z, c] = gates
        gd_ref[...] = jnp.concatenate([gates, jnp.full((LANE - E, tokens), -1.0, F32)], axis=0).T
        for g in (KVH - 2, KVH - 1):
            p_copy(g).wait()
        for save in saves:
            save.wait()

    pl.run_scoped(forward, pltpu.VMEM((2, 2 * tokens, tokens), F32), *[pltpu.VMEM((tokens, D), BF)] * 4)

    def bit_of(b):
        return (r // (1 << b)) % 2

    def partner(b):
        return (r + (1 - 2 * bit_of(b)) * (1 << b), f)

    stages = {}

    def landed(ref, name):
        stage, sem = stages[name]
        if ref.shape != stage.shape:
            stage = stage.at[pl.ds(0, ref.shape[0])]
        copy = pltpu.make_async_copy(ref, stage, sem)
        copy.start()
        copy.wait()
        return stage

    def halving(e):
        size = ge_ref.shape[1] // bits
        orders = [[(g + k) % bits for k in range(bits)] for g in range(bits)]
        starts = [[] for _ in range(bits)]
        for g in range(bits):
            at = g * size
            for k in range(bits):
                starts[g].append(at)
                at = at + bit_of(orders[g][k]) * (size >> (k + 1))
            starts[g].append(at)

        def region(g, k):
            half = size >> (k + 1)
            return ge_ref.at[e, pl.ds(pl.multiple_of(starts[g][k + 1], half), half)]

        def exchange(g, k):
            half, job = size >> (k + 1), e * bits + g
            give = pl.multiple_of(starts[g][k] + (1 - bit_of(orders[g][k])) * half, half)
            return make(
                ge_ref.at[e, pl.ds(give, half)], arrived[k].at[job], ar_send.at[job, k], ar_recv.at[job, k],
                partner(orders[g][k]),
            )

        def spread(g, k):
            job, ref = e * bits + g, region(g, k)
            return make(ref, ref, ar_send.at[job, bits + k], ar_recv.at[job, bits + k], partner(orders[g][k]))

        def spread_once_free(g, k):
            pl.semaphore_wait(ar_free.at[e * bits + g, k], 1)
            spread(g, k).start()

        yield
        for g in range(bits):
            exchange(g, 0).start()
        yield
        for k in range(bits):
            half = size >> (k + 1)
            for g in range(bits):
                job = e * bits + g
                exchange(g, k).wait_recv()
                own = region(g, k)
                add_rows(own, own, landed(arrived[k].at[job], "halves"), half, min(half, 64))
                if k < bits - 1:
                    exchange(g, k + 1).start()
                exchange(g, k).wait_send()
                pl.semaphore_signal(
                    ar_free.at[job, k], inc=1, device_id=partner(orders[g][k]), device_id_type=pl.DeviceIdType.MESH
                )
                if k == bits - 1:
                    spread_once_free(g, k)
            yield
        for k in range(bits - 1, -1, -1):
            for g in range(bits):
                spread(g, k).wait_recv()
                if k > 0:
                    spread_once_free(g, k - 1)
            yield
        for g in range(bits):
            for k in range(bits):
                spread(g, k).wait_send()
        pltpu.make_async_copy(ge_ref.at[e], ge_hbm.at[e], ge_sem.at[e]).start()

    sums = [halving(e) for e in range(local)] if bits else []
    first, last = sums[:1], sums[1:]
    for process in sums:
        next(process)

    def pass_on(zb, how):
        to = {"up": above, "down": below, "mate": mate}[how]
        sems = {"up": (n2_up, gt_up), "down": (n2_down, gt_down), "mate": (n2_mate, gt_mate)}[how]
        return [
            make(ref.at[zb, c], ref.at[zb, c], sem.at[zb], recv.at[zb, c], to)
            for ref, sem, recv in ((gt_all, sems[1], gt_recv), (n2_all, sems[0], n2_recv))
        ]

    def got(zb, core):
        for ref, sem, recv in ((gt_all, gt_mate, gt_recv), (n2_all, n2_mate, n2_recv)):
            make(ref.at[zb, core], ref.at[zb, core], sem.at[zb], recv.at[zb, core], mate).wait_recv()

    def start(copies):
        for copy in copies:
            copy.start()

    @pl.when(z < chips - 1)
    def _():
        start(pass_on(z, "up"))

    @pl.when(z > 0)
    def _():
        start(pass_on(z, "down"))

    start(pass_on(z, "mate"))
    inner = jnp.minimum(z, chips - 1 - z)

    def place(t):
        k = (t + 1) // 2
        near = jnp.where(t % 2 == 1, z - k, z + k)
        return jnp.where(t <= 2 * inner, near, jnp.where(2 * z < chips - 1, t, chips - 1 - t))

    def far(zc):
        return jnp.where(zc > z, zc - z, z - zc)

    def side_of(zc):
        return jnp.where(zc > z, 1, 0)

    def relay(k, low, high):
        @pl.when(low)
        def _():
            pl.when(k > 2)(lambda: dout_arrive(z - k, True))
            got(z - k, c)

            @pl.when(z < chips - 1)
            def _():
                start(pass_on(z - k, "up"))

            start(pass_on(z - k, "mate"))

        @pl.when(high)
        def _():
            pl.when(k > 2)(lambda: dout_arrive(z + k, False))
            got(z + k, c)

            @pl.when(z > 0)
            def _():
                start(pass_on(z + k, "down"))

            start(pass_on(z + k, "mate"))

    def early(t):
        return (t >= 2) & (t % 2 == 0) & (t <= 2 * inner) & (t < chips - 1)

    def pair_copy(side):
        owner = z + 2 * side - 1
        return make(pair_ref.at[side], from_ref.at[z], pair_send.at[side], far_recv.at[z], (r, owner * 2 + c))

    def experts_and_sums(do_buf, xs_ref, dye_ref, dgu_ref, hx_ref, dxp_ref, yps_ref, core_stage):
        stages["core"] = (core_stage, stage_sem.at[0])
        before = lax.broadcasted_iota(jnp.int32, (tokens, tokens), 0) < lax.broadcasted_iota(jnp.int32, (tokens, tokens), 1)
        before = before.astype(F32).astype(BF)
        slot_index = lax.broadcasted_iota(jnp.int32, (CAP, tokens), 0).astype(F32)
        pair = 2 * CAP

        def do_copy(zc):
            return pltpu.make_async_copy(do_all.at[zc], do_buf, do_sem.at[0])

        def core_copy(zc, slot, t):
            return make(dxp_ref.at[slot, 1 - c], core_ref.at[zc], core_send.at[t], core_recv.at[zc], mate)

        def y_copy(zc, slot, t):
            return make(yps_ref.at[slot], y_core.at[zc], yc_send.at[t], yc_recv.at[zc], mate)

        def via_copy(zc, slot, t):
            side = side_of(zc)
            return make(
                dxp_ref.at[slot, c], via_ref.at[side], far_send.at[t], via_recv.at[side], (r, (z + 2 * side - 1) * 2 + c)
            )

        def far_copy(zc, slot, t):
            return make(dxp_ref.at[slot, c], from_ref.at[z], far_send.at[t], far_recv.at[z], (r, zc * 2 + c))

        def dgt_copy(zc, core, t):
            return make(dgt_ref.at[t, core], dgt_all.at[f], dgt_send.at[t, core], dgt_recv.at[f], (r, zc * 2 + core))

        def free_slot(t, slot):
            core_copy(z, slot, t).wait_send()
            y_copy(z, slot, t).wait_send()

            @pl.when(far(place(t)) >= 2)
            def _():
                far_copy(z, slot, t).wait_send()

        def add_ye(zc):
            make(y_core.at[zc], y_core.at[zc], yc_send.at[0], yc_recv.at[zc], mate).wait_recv()
            add_rows(y_ref.at[zc], y_ref.at[zc], landed(y_core.at[zc], "core"), tokens, 64)
            send_sem, _, from_recv = y_sems


        def chunk(t, carry):
            zc = place(t)
            slot = t % 2

            @pl.when(t > 0)
            def _():
                add_ye(place(t - 1))

            k = far(zc)
            both = (t % 2 == 1) & (t <= 2 * inner)
            single = (t > 2 * inner) & jnp.logical_not(early(t - 1))
            relay(k, both | (single & (zc < z)), both | (single & (zc > z)))
            dout_copy(zc, 1 - c, 2).wait_recv()
            do_copy(zc).start()
            got(zc, 1 - c)
            do_copy(zc).wait()

            @pl.when(t == 0)
            def _():
                load_experts.wait()

            @pl.when(t >= 2)
            def _():
                free_slot(t - 2, slot)

            picks, gates, dms = [], [], []
            at_chip = pl.multiple_of(zc * pair, 16)
            for core in range(2):
                mine = [gt_all[zc, core, pl.ds(f * local + i, 1), :] for i in range(local)]
                mine = jnp.concatenate(mine, axis=0) if local > 1 else mine[0]
                rank = jnp.where(mine >= 0.0, dot((mine >= 0.0).astype(F32).astype(BF), before), -1.0)
                chosen = [slot_index == rank[i : i + 1] for i in range(local)]
                gates.append([jnp.sum(jnp.where(chosen[i], mine[i : i + 1], 0.0), axis=1, keepdims=True) for i in range(local)])
                picks.append([one.astype(F32) for one in chosen])
                pick = jnp.concatenate([one.astype(BF) for one in picks[core]], axis=0)
                taken = dot(pick, n2_all[zc, core]).astype(BF)
                grads = dot(pick, do_buf[core])
                dms.append(grads.astype(BF))
                grads = grads * residual_scale
                at = pl.ds(pl.multiple_of(at_chip + core * CAP, 16), CAP)
                for i in range(local):
                    part = slice(i * CAP, (i + 1) * CAP)
                    xs_ref[i, at] = taken[part]
                    dye_ref[i, at] = (gates[core][i] * grads[part]).astype(BF)
            at = pl.ds(at_chip, pair)
            mades, backs = [], []
            for i in range(local):
                slots = xs_ref[i, at]
                gate_pre = dot_nt(slots, ge_ref[i, :FF])
                up_pre = dot_nt(slots, ge_ref[i, FF : 2 * FF])
                grad_act = dot_nt(dye_ref[i, at], ge_ref[i, 2 * FF :])
                sigmoid = 1.0 / (1.0 + jnp.exp(-gate_pre))
                silu = gate_pre * sigmoid
                act = (silu * up_pre).astype(BF)
                hx_ref[i, at] = act
                grad_gate = (grad_act * up_pre * (sigmoid * (1.0 + gate_pre * (1.0 - sigmoid)))).astype(BF)
                grad_up = (grad_act * silu).astype(BF)
                dgu_ref[i, at, :FF] = grad_gate
                dgu_ref[i, at, FF:] = grad_up
                backs.append((dot(grad_gate, ge_ref[i, :FF]) + dot(grad_up, ge_ref[i, FF : 2 * FF])).astype(BF))
            for core in range(2):
                pick = jnp.concatenate([one.astype(BF) for one in picks[core]], axis=0)
                part = slice(core * CAP, (core + 1) * CAP)
                sent = jnp.concatenate([backs[i][part] for i in range(local)], axis=0)
                dxp_ref[slot, core] = dot_tn(pick, sent).astype(BF)
            core_copy(zc, slot, t).start()
            for i in range(local):
                made = dot(hx_ref[i, at], ge_ref[i, 2 * FF :]).astype(BF)
                mades.append(made)
                for core in range(2):
                    part = slice(core * CAP, (core + 1) * CAP)
                    grads = dms[core][i * CAP : (i + 1) * CAP].astype(F32) * residual_scale
                    value = jnp.sum(grads * made[part].astype(F32), axis=1, keepdims=True)
                    dgt_ref[t, core, i : i + 1] = jnp.sum(picks[core][i] * value, axis=0, keepdims=True)
            for core in range(2):

                @pl.when((t > 0) | (c != core))
                def _():
                    dgt_copy(zc, core, t).start()

            @pl.when(early(t))
            def _():
                k_next = t // 2 + 1
                relay(k_next, z >= k_next, z + k_next < chips)

            for core in range(2):
                pick = jnp.concatenate([one.astype(BF) for one in picks[core]], axis=0)
                part = slice(core * CAP, (core + 1) * CAP)
                sent = jnp.concatenate([(gates[core][i] * mades[i][part].astype(F32)).astype(BF) for i in range(local)], axis=0)
                mixed = dot_tn(pick, sent).astype(BF)

                @pl.when(c == core)
                def _():
                    y_ref[zc] = mixed

                @pl.when(c != core)
                def _():
                    yps_ref[slot] = mixed

            y_copy(zc, slot, t).start()
            core_copy(zc, slot, t).wait_recv()
            there = core_ref.at[zc] if roomy else landed(core_ref.at[zc], "core")
            own = dxp_ref.at[slot, c]

            @pl.when(k == 0)
            def _():
                dx_ref[...] = own[...].astype(F32) + there[...].astype(F32)

            @pl.when(k == 1)
            def _():
                side = side_of(zc)
                add_rows(pair_ref.at[side], own, there, tokens, 64)

                @pl.when((z == 0) | (z == chips - 1))
                def _():
                    pair_copy(side).start()

            @pl.when(k >= 2)
            def _():
                add_rows(own, own, there, tokens, 64)

                @pl.when(k == 2)
                def _():
                    via_copy(zc, slot, t).start()

                @pl.when(k > 2)
                def _():
                    far_copy(zc, slot, t).start()

            return carry

        lax.fori_loop(0, chips, chunk, 0)

        for i in range(local):
            ge_ref[i, :FF] = dot_tn(dgu_ref[i, :, :FF], xs_ref[i]).astype(BF)
            ge_ref[i, FF : 2 * FF] = dot_tn(dgu_ref[i, :, FF:], xs_ref[i]).astype(BF)
            ge_ref[i, 2 * FF :] = dot_tn(hx_ref[i], dye_ref[i]).astype(BF)
            if bits:
                next(sums[i])
            if i > 0:
                continue

            @pl.when((z > 0) & (z < chips - 1))
            def _():
                for side in range(2):
                    make(via_ref.at[side], via_ref.at[side], far_send.at[0], via_recv.at[side], mate).wait_recv()
                    add_rows(pair_ref.at[side], pair_ref.at[side], via_ref.at[side], tokens, 64)
                    pair_copy(side).start()

        add_ye(place(chips - 1))
        for t in range(max(chips - 2, 0), chips):
            free_slot(t, t % 2)
        for t in range(chips):
            for core in range(2):

                @pl.when((t > 0) | (c != core))
                def _():
                    dgt_copy(z, core, t).wait_send()

    slots = chips * 2 * CAP
    pl.run_scoped(
        experts_and_sums,
        pltpu.VMEM((2, tokens, D), BF), pltpu.VMEM((local, slots, D), BF), pltpu.VMEM((local, slots, D), BF),
        pltpu.VMEM((local, slots, 2 * FF), BF), pltpu.VMEM((local, slots, FF), BF), pltpu.VMEM((2, 2, tokens, D), BF),
        pltpu.VMEM((2, tokens, D), BF), pltpu.VMEM((tokens, D), BF),
    )

    def line(own, size, step, core_add, name, reach, via, arrive, send_sem, via_recv, from_recv):
        def direct(k):
            return make(own(k), arrive.at[z], send_sem.at[k], from_recv.at[z], (r, k * 2 + c))

        def passing(k, side):
            return make(own(k), via.at[side], send_sem.at[k], via_recv.at[side], (r, (z + 2 * side - 1) * 2 + c))

        def within(k):
            return (k >= 0) & (k < chips)

        for d in range(chips - 1, 0, -1):
            for side in range(2):
                way = 1 if side else -1
                owner = z + d * way

                @pl.when(within(owner))
                def _():
                    core_add(owner)
                    if d > reach + 1:
                        direct(owner).start()
                    elif d == reach + 1:
                        passing(owner, side).start()
                    elif d == reach:
                        pl.when(jnp.logical_not(within(z - way)))(lambda: direct(owner).start())

        core_add(z)
        yield
        for side in range(2):
            way = 1 if side else -1
            owner = z + reach * way

            @pl.when(within(owner) & within(z - way))
            def _():
                make(via.at[side], via.at[side], send_sem.at[0], via_recv.at[side], mate).wait_recv()
                add_rows(own(owner), own(owner), landed(via.at[side], name), size, step)
                direct(owner).start()

        yield
        for k in range(chips):

            @pl.when((z != k) & (far(k) != reach + 1))
            def _():
                make(arrive.at[k], arrive.at[k], send_sem.at[0], from_recv.at[k], mate).wait_recv()
                add_rows(own(z), own(z), landed(arrive.at[k], name), size, step)

        for k in range(chips):

            @pl.when(z != k)
            def _():
                direct(k).wait_send()

    def mixture():
        yield from line(lambda k: y_ref.at[k], tokens, 64, lambda k: None, "tokens", 1, y_via, y_from, *y_sems)
        out_ref[...] = (h1_ref[...] + residual_scale * y_ref[z].astype(F32)).astype(BF)

    def attention(q_ref, kd_ref, vd_ref, o_ref, p_ref, do_ref, dqkv_ref, gkv_ref, gq_ref, go_ref, halves_stage, tokens_stage, kv_stage, o_stage):
        loads = [
            pltpu.make_async_copy(heads_hbm.at[i], ref, heads_sem.at[i]) for i, ref in enumerate((q_ref, kd_ref, vd_ref, o_ref))
        ]
        start(loads)
        stages["halves"] = (halves_stage, stage_sem.at[1])
        stages["tokens"] = (tokens_stage, stage_sem.at[2])
        stages["kv"] = (kv_stage, stage_sem.at[3])
        stages["o"] = (o_stage, stage_sem.at[4])
        def projection(index, name, grad_ref, core, via, arrive, sems):
            core_sem, *sems = sems
            parts, results, wide = parts_ref.at[index], results_ref.at[index], D // replicas
            crossing = make(grad_ref.at[:, 1 - c], core, core_sem.at[0], core_sem.at[1], mate)
            crossing.start()
            yield
            crossing.wait_recv()

            def own(k):
                return grad_ref.at[k, c]

            yield from line(
                own, rows, 16, lambda k: add_rows(own(k), own(k), core.at[k], rows, 16), name, 1, via, arrive, *sems
            )
            crossing.wait_send()
            mine = grad_ref.at[z, c]

            def columns(part):
                return pl.ds(pl.multiple_of(part * wide, LANE), wide)

            def part_copy(d):
                to = (r + d) % replicas
                return make(
                    mine.at[:, columns(to)], parts.at[r], part_send.at[index, d], part_recv.at[index, r], (to, f)
                )

            def small_copy(d):
                to = (r + d) % replicas
                return make(mine.at[:, pl.ds(D, LANE)], smalls_ref.at[r], small_send.at[d], small_recv.at[r], (to, f))

            for d in range(1, replicas):
                part_copy(d).start()
                if index == 0:
                    small_copy(d).start()
            parts[r] = mine[:, columns(r)]
            if index == 0:
                smalls_ref[r] = mine[:, pl.ds(D, LANE)]
            yield
            for d in range(1, replicas):
                peer = (r + d) % replicas
                make(
                    parts.at[peer], parts.at[peer], part_send.at[index, d], part_recv.at[index, peer], (peer, f)
                ).wait_recv()
                if index == 0:
                    make(
                        smalls_ref.at[peer], smalls_ref.at[peer], small_send.at[d], small_recv.at[peer], (peer, f)
                    ).wait_recv()
            total = parts[0].astype(F32)
            for k in range(1, replicas):
                total = total + parts[k].astype(F32)
            results[r] = total.astype(BF)

            def result_copy(d):
                to = (r + d) % replicas
                return make(
                    results.at[r], results.at[r], result_send.at[index, d], result_recv.at[index, r], (to, f)
                )

            for d in range(1, replicas):
                result_copy(d).start()
            if index == 0:
                small = smalls_ref[0].astype(F32)
                for k in range(1, replicas):
                    small = small + smalls_ref[k].astype(F32)
                total_ref[...] = small
            yield
            for d in range(1, replicas):
                peer = (r + d) % replicas
                make(
                    results.at[peer], results.at[peer], result_send.at[index, d], result_recv.at[index, peer], (peer, f)
                ).wait_recv()
            for d in range(1, replicas):
                part_copy(d).wait_send()
                if index == 0:
                    small_copy(d).wait_send()
                result_copy(d).wait_send()

        moe = [mixture()]
        kvs = [projection(0, "kv", gkv_ref, kv_core, kv_via, kv_from, kv_sems)]
        outs = [projection(1, "o", go_ref, o_core, o_via, o_from, o_sems)]
        qs = [projection(2, "o", gq_ref, q_core, q_via, q_from, q_sems)]

        def go(*turns):
            for turn in turns:
                for process in turn:
                    next(process, None)

        def dgate():
            found = [dgt_all[k, :local] for k in range(2 * chips)]
            return jnp.concatenate(found + [jnp.zeros((LANE - E, tokens), F32)], axis=0).T

        for k in range(chips):

            @pl.when((z == k + 1) | (z + 1 == k) | (z > k + 2) | (z + 2 < k))
            def _():
                make(from_ref.at[k], from_ref.at[k], far_send.at[0], far_recv.at[k], mate).wait_recv()
                there = from_ref.at[k] if roomy else landed(from_ref.at[k], "tokens")
                add_rows(dx_ref, dx_ref, there, tokens, 64)

        for k in range(2 * chips):

            @pl.when(f == k)
            def _():
                for core in range(2):

                    @pl.when(c == core)
                    def _():
                        dgt_all[k] = dgt_ref[0, core]

            @pl.when(f != k)
            def _():
                make(dgt_all.at[k], dgt_all.at[k], dgt_send.at[0, 0], dgt_recv.at[k], mate).wait_recv()

        for load in loads:
            load.wait()
        backward = attention_backward(
            x_ref, dout_ref, cos_ref, sin_ref, columns, q_ref, kd_ref, vd_ref, p_hbm, o_ref, h1_ref, n2_all.at[z, c], gd_ref,
            dx_ref, dgate, gin_ref, gq_ref, gkv_ref, go_ref, do_ref, dqkv_ref, p_ref, p_sem,
        )
        next(backward)
        go(outs)
        next(backward)
        go(first)
        next(backward)
        go(outs)
        next(backward)
        go(qs)
        next(backward, None)
        go(kvs, last, qs, first, kvs, last, outs, first, moe, last, qs, outs, kvs, outs, first, qs, outs, moe, qs, kvs, moe, last)
        go(qs, kvs, kvs)
        go(*[moe + outs + qs + kvs + sums] * (2 * bits + 8))

    size = ge_ref.shape[1] // max(bits, 1)
    pl.run_scoped(
        attention, *[pltpu.VMEM((tokens, D), BF)] * 4,
        pltpu.VMEM((2, 2 * tokens, tokens), F32), pltpu.VMEM((tokens, D), BF),
        pltpu.VMEM((tokens, QKV), BF), pltpu.VMEM((chips, 2, rows, D + LANE), BF), pltpu.VMEM((chips, 2, rows, D), BF),
        pltpu.VMEM((chips, 2, rows, D), BF), pltpu.VMEM((size // 2, D), BF), pltpu.VMEM((tokens, D), BF),
        pltpu.VMEM((rows, D + LANE), BF), pltpu.VMEM((rows, D), BF),
    )

    for e in range(local):
        copy = pltpu.make_async_copy(ge_ref.at[e], ge_hbm.at[e], ge_sem.at[e])
        if not bits:
            copy.start()
        copy.wait()
    for side in range(2):

        @pl.when(z > 0 if side == 0 else z < chips - 1)
        def _():
            pair_copy(side).wait_send()

    for k in range(chips):

        @pl.when((z >= k) & (z < chips - 1))
        def _():
            for copy in pass_on(k, "up"):
                copy.wait_send()

        @pl.when((z <= k) & (z > 0))
        def _():
            for copy in pass_on(k, "down"):
                copy.wait_send()

        for copy in pass_on(k, "mate"):
            copy.wait_send()

    for k in range(chips):
        for late in range(2):
            to_mate(k, c, late).wait_send()
        dout_copy(k, c, 2).wait_send()

        @pl.when((z >= k) & (z < chips - 1))
        def _():
            dout_copy(k, c, 0).wait_send()
            for kind in range(3):
                along(k, kind, True).wait_send()

        @pl.when((z <= k) & (z > 0))
        def _():
            dout_copy(k, c, 1).wait_send()
            for kind in range(3):
                along(k, kind, False).wait_send()

        @pl.when(z != k)
        def _():
            for d in range(1, replicas):
                for kind in (0, 2):
                    across(k, kind, d).wait_send()


def finish(gexp_ref, results_ref, total_ref, gin_ref, out_ref, *outs):
    layer_out, grad_in, gains_one, query, key, value, output, gains_two, router, expert = outs
    expert[...] = gexp_ref[...].astype(F32)
    layer_out[...] = out_ref[...]
    grad_in[...] = gin_ref[...]
    for index, targets in ((0, (key, value)), (1, (output,)), (2, (query,))):
        start, wide = 0, results_ref.shape[3]
        for ref in targets:
            for at in range(0, ref.shape[1], LANE):
                part, column = divmod(start + at, wide)
                ref[:, at : at + LANE] = results_ref[index, part, :, column : column + LANE].astype(F32)
            start += ref.shape[1]

    @pl.when(pl.program_id(0) == 0)
    def _():
        small = total_ref[...].T
        router[...] = small[:E]
        gains_one[...] = small[E : E + 1]
        gains_two[...] = small[E + 1 : E + 2]


def call(kernel, out_shape, args, scratch=(), outside=0, out_outside=0, **params):
    spaces = [pltpu.SMEM if a.dtype == jnp.int32 and a.size <= 16 else pltpu.VMEM for a in args]
    spaces[len(args) - outside :] = [pl.ANY] * outside
    return pl.pallas_call(
        kernel,
        out_shape=out_shape,
        in_specs=[pl.BlockSpec(memory_space=space) for space in spaces],
        out_specs=[
            pl.BlockSpec(memory_space=pltpu.VMEM if i < len(out_shape) - out_outside else pl.ANY)
            for i in range(len(out_shape))
        ],
        scratch_shapes=list(scratch),
        compiler_params=pltpu.CompilerParams(
            vmem_limit_bytes=VMEM_LIMIT, has_side_effects="collective_id" in params, **params
        ),
    )(*args)


def shape(dims, dtype):
    return jax.ShapeDtypeStruct(dims, dtype)


def make_body(mesh):
    group, replicas = mesh.shape["fsdp"], mesh.shape["replica"]
    local = E // group

    def body(
        hidden_in, seq_lengths, routes, norm1_gain, w_query, w_key, w_value, w_output, norm2_gain, w_router,
        expert_weights, out_cotangent,
    ):
        tokens = hidden_in.shape[0]
        rows = w_query.shape[0]
        chips = group // 2
        dma = pltpu.SemaphoreType.DMA
        bits = replicas.bit_length() - 1
        size = 3 * FF // bits if bits else 0
        roomy = chips <= 4
        landing = [shape((local * bits, size >> (k + 1), D), BF) for k in range(bits)]
        blocks = [shape((chips, tokens, D), BF)] * 2
        landing += [shape((chips, tokens, D), BF)]
        if not roomy:
            landing += blocks
        outs = call(
            functools.partial(layer, replicas, chips),
            [
                shape((tokens, D), F32), shape((tokens, D), BF), shape((3, replicas, rows, D // replicas), BF),
                shape((rows, LANE), F32), shape((local, 3 * FF, D), BF),
                shape((KVH, 2 * tokens, tokens), F32), shape((4, tokens, D), BF), shape((chips, 2, tokens, D), BF),
                shape((2, tokens, D), BF), shape((chips, tokens, D), BF), shape((2, rows, D + LANE), BF),
                shape((chips, rows, D + LANE), BF), shape((2, rows, D), BF), shape((chips, rows, D), BF),
                shape((2, rows, D), BF), shape((chips, rows, D), BF),
            ]
            + landing,
            (
                hidden_in, seq_lengths, routes.T, rope_table(tokens), w_query, w_key, w_value, w_output, w_router.T,
                norm1_gain[None], norm2_gain[None], out_cotangent, expert_weights,
            ),
            [
                pltpu.VMEM((chips, 2, rows, W_O + D), BF), pltpu.VMEM((tokens, D), F32),
                pltpu.VMEM((tokens, LANE), F32), pltpu.VMEM((tokens, LANE), F32), pltpu.VMEM((tokens, LANE), F32),
                dma((4,)), dma((1,)), dma((3, chips)), dma((3, chips)), dma((3, chips)), dma((3, chips, replicas)),
                dma((3, chips, replicas)), dma((2, chips)), dma((2, chips)), dma((3, chips)), dma((chips, 2)),
                pltpu.VMEM((local, 3 * FF, D), BF), pltpu.VMEM((chips, 2, tokens, D), BF),
                pltpu.VMEM((chips, 2, E, tokens), F32), pltpu.VMEM((2, tokens, D), BF), pltpu.VMEM((2, tokens, D), BF),
                pltpu.VMEM((chips, 2, 8, tokens), F32), pltpu.VMEM((group, 8, tokens), F32),
                pltpu.VMEM((chips, tokens, D), BF), pltpu.VMEM((chips, rows, D + LANE), BF), pltpu.VMEM((chips, rows, D), BF),
                pltpu.VMEM((chips, rows, D), BF), pltpu.VMEM((3, replicas, rows, D // replicas), BF),
                pltpu.VMEM((replicas, rows, LANE), BF),
            ]
            + ([pltpu.VMEM(b.shape, b.dtype) for b in blocks] if roomy else [])
            + ([dma((chips,))] * 3 + [dma((chips, 2))]) * 2 + [dma((chips,))] * 4 + [dma((2,))] * 2
            + [dma((chips, 2)), dma((group,)), dma((chips,)), dma((chips,))]
            + [dma((1,)), dma((1,)), dma((5,)), dma((local,)), dma((2,))]
            + [dma((max(local * bits, 1), max(2 * bits, 1)))] * 2
            + [pltpu.SemaphoreType.REGULAR((max(local * bits, 1), max(bits, 1)))]
            + [dma((chips,)), dma((2,)), dma((chips,))] + [dma((2,)), dma((chips,)), dma((2,)), dma((chips,))] * 3
            + [dma((3, replicas))] * 2 + [dma((replicas,))] * 2 + [dma((3, replicas))] * 2,
            outside=1,
            out_outside=12 + len(landing),
            collective_id=0,
        )
        grad_in, layer_out, results, total, grad_experts = outs[:5]
        steps = 4

        def moving(a, dim=0):
            block = tuple(n // steps if i == dim else n for i, n in enumerate(a.shape))
            return pl.BlockSpec(block, lambda i: tuple(i if at == dim else 0 for at in range(len(block))))

        def still(a):
            return pl.BlockSpec(a.shape, lambda i: (0,) * len(a.shape))

        grad_experts = grad_experts.reshape(local * 3 * FF, D)
        gain, router = shape((1, rows), F32), shape((E, rows), F32)
        wide, narrow = shape((rows, D), F32), shape((rows, KVH * HD), F32)
        out_shapes = [
            shape((tokens, D), BF), shape((tokens, D), F32), gain, wide, narrow, narrow, wide, gain, router,
            shape((local * 3 * FF, D), F32),
        ]
        outs = pl.pallas_call(
            finish,
            grid=(steps,),
            in_specs=[moving(grad_experts), moving(results, 2), still(total), moving(grad_in), moving(layer_out)],
            out_specs=[still(a) if a in (gain, router) else moving(a) for a in out_shapes],
            out_shape=out_shapes,
            compiler_params=pltpu.CompilerParams(vmem_limit_bytes=VMEM_LIMIT),
        )(grad_experts, results, total, grad_in, layer_out)
        return (
            outs[0], outs[1], outs[2][0], outs[3], outs[4], outs[5], outs[6], outs[7][0], outs[8].T,
            outs[9].reshape(local, 3 * FF, D),
        )

    return body


def solution(mesh):
    tokens, weights = P(("replica", "fsdp"), None), P("fsdp", None)
    return jax.shard_map(
        make_body(mesh),
        mesh=mesh,
        in_specs=(
            tokens, tokens, tokens, P("fsdp"), weights, weights, weights, weights, P("fsdp"), weights,
            P("fsdp", None, None), tokens,
        ),
        out_specs=(
            tokens, tokens, P("fsdp"), weights, weights, weights, weights, P("fsdp"), weights, P("fsdp", None, None),
        ),
        check_vma=False,
    )
```

```python
import functools

import jax
import jax.numpy as jnp
import numpy as np
from jax import lax
from jax.experimental import pallas as pl
from jax.experimental.pallas import tpu as pltpu
from jax.sharding import PartitionSpec as P

D = 1024
H = 16
KVH = 8
HD = 64
FF = 512
TOPK = 8
E = 16
CAP = 144
LANE = 128
QKV = H * HD + 2 * KVH * HD
QKVO = QKV + D
W_O = QKV + LANE

norm_eps = 1e-06
score_scale = 0.015625
residual_scale = 0.22
rope_base = 10000.0
masked_score = -1e30

BF = jnp.bfloat16
F32 = jnp.float32
VMEM_LIMIT = 63 * 2**20


def dot(a, b):
    return lax.dot_general(a, b, (((1,), (0,)), ((), ())), preferred_element_type=F32)


def dot_nt(a, b):
    return lax.dot_general(a, b, (((1,), (1,)), ((), ())), preferred_element_type=F32)


def dot_tn(a, b):
    return lax.dot_general(a, b, (((0,), (0,)), ((), ())), preferred_element_type=F32)


def lanes_of(rows):
    return lax.broadcasted_iota(jnp.int32, (rows, LANE), 1)


def turned(block, lane):
    return jnp.where(lane % HD < HD // 2, pltpu.roll(block, LANE - HD // 2, 1), pltpu.roll(block, HD // 2, 1))


def halves(block, low):
    zero = jnp.zeros_like(block)
    return jnp.concatenate([jnp.where(low, block, zero), jnp.where(low, zero, block)], axis=0)


def rope_table(tokens):
    frequency = np.float32(rope_base) ** (-np.arange(0, HD, 2, dtype=np.float32) / np.float32(HD))
    frequency = np.tile(frequency.astype(np.float32), LANE // (HD // 2))
    angles = (np.arange(tokens, dtype=np.float32)[:, None] * frequency[None, :]).astype(np.float64)
    sign = np.where(np.arange(LANE) % HD < HD // 2, -1.0, 1.0)
    pieces = []
    for values in (np.cos(angles), np.sin(angles) * sign[None, :]):
        rest = values.astype(np.float32)
        for _ in range(3):
            piece = rest.astype(BF)
            pieces.append(piece)
            rest = rest - piece.astype(np.float32)
    return np.concatenate(pieces, axis=1)


class Copies:
    def make(self, src, dst, send, recv, device):
        return pltpu.make_async_remote_copy(
            src_ref=src, dst_ref=dst, send_sem=send, recv_sem=recv, device_id=device, device_id_type=pl.DeviceIdType.MESH
        )


def greet(devices):
    for device in devices:
        pl.semaphore_signal(
            pltpu.get_barrier_semaphore(), inc=1, device_id=device, device_id_type=pl.DeviceIdType.MESH
        )


def attention_backward(
    x_ref, dout_ref, cos_ref, sin_ref, columns, q_ref, kd_ref, vd_ref, p_hbm, o_ref, h1_ref, n2_ref, gd_ref, dx_ref, dgate,
    gin_ref, gq_ref, gkv_ref, go_ref, do_ref, dqkv_ref, p_ref, p_sem,
):
    tokens = x_ref.shape[0]
    lane = lanes_of(tokens)
    low = lane < HD

    def p_copy(g):
        return pltpu.make_async_copy(p_hbm.at[g], p_ref.at[g % 2], p_sem.at[g % 2])

    p_copy(0).start()

    def put(ref, at, value):
        ref[:, :, :, at] = value.astype(BF).reshape(*ref.shape[:3], value.shape[1])

    small = columns(QKV, LANE).astype(F32).T
    gain_one, gain_two = small[E : E + 1], small[E + 1 : E + 2]
    after = h1_ref[...]
    factor_two = lax.rsqrt(jnp.mean(after * after, axis=1, keepdims=True) + norm_eps)
    gates = jnp.maximum(gd_ref[...], 0.0)
    grad_gates = dgate()
    chosen = gates * (grad_gates - jnp.sum(gates * grad_gates, axis=1, keepdims=True))
    grad_logits = chosen.astype(BF)
    grad_normed = dx_ref[...] + dot_nt(grad_logits, columns(QKV, LANE))
    scaled = grad_normed * gain_two
    grad_after = dout_ref[...].astype(F32) + (
        factor_two * scaled - after * factor_two**3 * jnp.mean(scaled * after, axis=1, keepdims=True)
    )
    grad_gain_two = jnp.sum(grad_normed * after * factor_two, axis=0, keepdims=True)
    gin_ref[...] = grad_after
    grad_branch = (residual_scale * grad_after).astype(BF)
    for at in range(0, D, FF):
        put(go_ref, slice(at, at + FF), dot_tn(o_ref[...], grad_branch[:, at : at + FF]))
    do_ref[...] = dot_nt(grad_branch, columns(W_O, D)).astype(BF)
    grad_router = dot_tn(n2_ref[...], grad_logits)
    yield

    cosines, sines = cos_ref[...], sin_ref[...]
    key_back, value_back = [], []
    for g in range(KVH):
        at = slice(g * LANE, (g + 1) * LANE)
        queries = halves(q_ref[:, at].astype(F32), low).astype(BF)
        outs = halves(do_ref[:, at].astype(F32), low).astype(BF)
        if g + 1 < KVH:
            p_copy(g + 1).start()
        p_copy(g).wait()
        weights = p_ref[g % 2]
        grad_weights = dot_nt(outs, vd_ref[:, at])
        total = jnp.sum(weights * grad_weights, axis=1, keepdims=True)
        grad_scores = (weights * (grad_weights - total)).astype(BF)
        block = dot(grad_scores, kd_ref[:, at])
        block = jnp.where(low, block[:tokens], block[tokens:]) * score_scale
        dqkv_ref[:, at] = (block * cosines - turned(block, lane) * sines).astype(BF)
        block = dot_tn(grad_scores, queries) * score_scale
        key_back.append(block + pltpu.roll(block, HD, 1))
        block = dot_tn(weights.astype(BF), outs)
        value_back.append(block + pltpu.roll(block, HD, 1))
        if g == KVH // 2 - 1:
            yield
    for m in range(KVH // 2):
        block = jnp.where(low, key_back[2 * m], key_back[2 * m + 1])
        at = slice(H * HD + m * LANE, H * HD + (m + 1) * LANE)
        dqkv_ref[:, at] = (block * cosines - turned(block, lane) * sines).astype(BF)
        at = slice(H * HD + KVH * HD + m * LANE, H * HD + KVH * HD + (m + 1) * LANE)
        dqkv_ref[:, at] = jnp.where(low, value_back[2 * m], value_back[2 * m + 1]).astype(BF)
    yield

    source = x_ref[...].astype(F32)
    factor_one = lax.rsqrt(jnp.mean(source * source, axis=1, keepdims=True) + norm_eps)
    normed = (source * factor_one * gain_one).astype(BF)
    for at in range(0, H * HD, FF):
        put(gq_ref, slice(at, at + FF), dot_tn(normed, dqkv_ref[:, at : at + FF]))
    yield
    grad_normed = dot_nt(dqkv_ref[...], columns(0, QKV))
    scaled = grad_normed * gain_one
    grad_vector = factor_one * scaled - source * factor_one**3 * jnp.mean(scaled * source, axis=1, keepdims=True)
    gin_ref[...] += grad_vector
    grad_gain_one = jnp.sum(grad_normed * source * factor_one, axis=0, keepdims=True)
    gains = jnp.concatenate([grad_gain_one, grad_gain_two, jnp.zeros((6, D), F32)], axis=0).T
    at = lanes_of(D)
    extra = jnp.where(at == E, gains[:, 0:1], jnp.where(at == E + 1, gains[:, 1:2], grad_router))
    put(gkv_ref, slice(D, D + LANE), extra)
    for at in range(0, QKV - H * HD, FF):
        put(gkv_ref, slice(at, at + FF), dot_tn(normed, dqkv_ref[:, H * HD + at : H * HD + at + FF]))


def add_rows(target, first, second, rows, step):
    def some(i, carry):
        at = pl.ds(pl.multiple_of(i * step, step), step)
        target[at] = (first[at].astype(F32) + second[at].astype(F32)).astype(target.dtype)
        return carry

    lax.fori_loop(0, rows // step, some, 0)


def layer(
    replicas, chips,
    x_ref, len_ref, routes_ref, table_ref, wq_ref, wk_ref, wv_ref, wo_ref, wr_ref, g1_ref, g2_ref, dout_ref, we_hbm,
    gin_ref, out_ref, results_ref, total_ref, ge_hbm, p_hbm, heads_hbm, do_all, y_via, y_from, kv_via, kv_from, q_via, q_from,
    o_via, o_from, *rest,
):
    bits = replicas.bit_length() - 1
    roomy = chips <= 4
    arrived, y_core, rest = rest[:bits], rest[bits], rest[bits + 1 :]
    if not roomy:
        (core_ref, from_ref), rest = rest[:2], rest[2:]
    (w_all, h1_ref, gd_ref, cos_ref, sin_ref), rest = rest[:5], rest[5:]
    (heads_sem, own_sem, z_up, z_down, z_recv, xy_send, xy_recv, mate_send, mate_recv, do_send, do_recv), rest = rest[:11], rest[11:]
    (ge_ref, n2_all, gt_all, via_ref, pair_ref, dgt_ref, dgt_all, y_ref, kv_core, q_core, o_core, parts_ref, smalls_ref), rest = (
        rest[:13], rest[13:]
    )
    dx_ref = gin_ref
    if roomy:
        (core_ref, from_ref), rest = rest[:2], rest[2:]
    (n2_up, n2_down, n2_mate, n2_recv, gt_up, gt_down, gt_mate, gt_recv,
     core_send, core_recv, far_send, far_recv, pair_send, via_recv, dgt_send, dgt_recv, yc_send, yc_recv,
     do_sem, we_sem, stage_sem, ge_sem, p_sem, ar_send, ar_recv, ar_free,
     *sum_sems, part_send, part_recv, small_send, small_recv, result_send, result_recv) = rest
    y_sems, kv_sems, q_sems, o_sems = sum_sems[:3], sum_sems[3:7], sum_sems[7:11], sum_sems[11:]
    local, tokens, rows = ge_ref.shape[0], x_ref.shape[0], q_core.shape[1]
    r, f = lax.axis_index("replica"), lax.axis_index("fsdp")
    z, c = f // 2, f % 2
    mate, above, below = (r, z * 2 + 1 - c), (r, f + 2), (r, f - 2)
    make = Copies().make

    peers = [mate]
    for k in range(1, chips):
        to = (z + k) % chips
        peers += [(r, to * 2 + c), (r, to * 2 + 1 - c)]
    greet(peers + [((r + d) % replicas, f) for d in range(1, replicas)])
    load_experts = pltpu.make_async_copy(we_hbm, ge_ref, we_sem.at[0])
    load_experts.start()
    own_dout = pltpu.make_async_copy(dout_ref, do_all.at[z, c], own_sem.at[0])
    own_dout.start()
    packed = [wr_ref[...].astype(F32), g1_ref[...].astype(F32), g2_ref[...].astype(F32)]
    packed = jnp.concatenate(packed + [jnp.zeros((LANE - E - 2, rows), F32)], axis=0)
    own = w_all.at[z, c]
    own[:, : H * HD] = wq_ref[...]
    own[:, H * HD : H * HD + KVH * HD] = wk_ref[...]
    own[:, H * HD + KVH * HD : QKV] = wv_ref[...]
    own[:, QKV:W_O] = packed.T.astype(BF)
    own[:, W_O:] = wo_ref[...]
    pl.semaphore_wait(pltpu.get_barrier_semaphore(), len(peers) + replicas - 1)

    def part(kind):
        if kind == 0:
            return pl.ds(pl.multiple_of(r * (QKV // replicas), LANE), QKV // replicas)
        if kind == 1:
            return pl.ds(QKV, LANE)
        return pl.ds(pl.multiple_of(W_O + r * (D // replicas), LANE), D // replicas)

    def along(zb, kind, up):
        ref = w_all.at[zb, c, :, part(kind)]
        return make(ref, ref, (z_up if up else z_down).at[kind, zb], z_recv.at[kind, zb], above if up else below)

    def across(zb, kind, d):
        ref = w_all.at[zb, c, :, part(kind)]
        return make(ref, ref, xy_send.at[kind, zb, d], xy_recv.at[kind, zb, r], ((r + d) % replicas, f))

    def wait_across(zb, kind):
        for d in range(1, replicas):
            peer = (r + d) % replicas
            ref = w_all.at[zb, c, :, part(kind)]
            make(ref, ref, xy_send.at[kind, zb, d], xy_recv.at[kind, zb, peer], (peer, f)).wait_recv()

    def to_mate(zb, core, late):
        ref = w_all.at[zb, core, :, pl.ds(W_O, D) if late else pl.ds(0, W_O)]
        return make(ref, ref, mate_send.at[late, zb], mate_recv.at[late, zb], mate)

    def dout_copy(zb, core, way):
        source = do_all.at[zb, core]
        return make(source, do_all.at[zb, core], do_send.at[way, zb], do_recv.at[zb, core], (above, below, mate)[way])

    def both_sides(k, act):
        @pl.when(z >= k)
        def _():
            act(z - k, True)

        @pl.when(z < chips - k)
        def _():
            act(z + k, False)

    def onward(up):
        return z < chips - 1 if up else z > 0

    def dout_arrive(zb, low):
        dout_copy(zb, c, 0 if low else 1).wait_recv()

        @pl.when(onward(low))
        def _():
            dout_copy(zb, c, 0 if low else 1).start()

        dout_copy(zb, c, 2).start()

    def columns(start, size):
        return w_all.reshape(D, W_O + D)[:, start : start + size]

    def forward(p_ref, q_ref, kd_ref, vd_ref, o_ref):
        for kind in range(3):
            both_sides(1, lambda zb, low: along(z, kind, not low).start())
        for late in range(2):
            to_mate(z, c, late).start()

        source = x_ref[...].astype(F32)
        factor = lax.rsqrt(jnp.mean(source * source, axis=1, keepdims=True) + norm_eps)
        lane = lanes_of(tokens)
        low_lane = lane < HD
        row = lax.broadcasted_iota(jnp.int32, (tokens, tokens), 0)
        column = lax.broadcasted_iota(jnp.int32, (tokens, tokens), 1)
        row_at = lax.broadcasted_iota(jnp.int32, (tokens, 1), 0)
        column_at = lax.broadcasted_iota(jnp.int32, (1, tokens), 1)
        row_segment = jnp.zeros((tokens, 1), jnp.int32)
        row_start = jnp.zeros((tokens, 1), jnp.int32)
        column_segment = jnp.zeros((1, tokens), jnp.int32)
        end = jnp.int32(0)
        for j in range(len_ref.shape[1]):
            end = end + len_ref[0, j]
            row_segment += (row_at >= end).astype(jnp.int32)
            row_start = jnp.maximum(row_start, jnp.where(row_at >= end, end, 0))
            column_segment += (column_at >= end).astype(jnp.int32)
        place = (column == row - row_start).astype(F32).astype(BF)
        found = dot(place, table_ref[...])
        found = [found[:, i * LANE : (i + 1) * LANE] for i in range(6)]
        cosines, sines = found[0] + found[1] + found[2], found[3] + found[4] + found[5]
        cos_ref[...] = cosines
        sin_ref[...] = sines

        own_dout.wait()
        for k in range(1, chips):
            for kind in range(3):

                def arrive(zb, low, kind=kind):
                    along(zb, kind, low).wait_recv()

                    @pl.when(onward(low))
                    def _():
                        along(zb, kind, low).start()

                    if kind != 1:
                        for d in range(1, replicas):
                            across(zb, kind, d).start()

                both_sides(k, arrive)
            if k == min(2, chips - 1):
                both_sides(1, lambda zb, low: dout_copy(z, c, 1 if low else 0).start())
                dout_copy(z, c, 2).start()

        def share(k, late):
            def act(zb, low):
                wait_across(zb, 2 if late else 0)
                to_mate(zb, c, late).start()

            both_sides(k, act)

        for k in range(1, chips):
            share(k, 0)
        if chips > 1:
            both_sides(1, dout_arrive)
        for k in range(chips):
            to_mate(k, 1 - c, 0).wait_recv()

        small = columns(QKV, LANE)
        gains = small.astype(F32).T
        gain_one, gain_two = gains[E : E + 1], gains[E + 1 : E + 2]
        normed = (source * factor * gain_one).astype(BF)
        q_all = dot(normed, columns(0, H * HD))
        for g in range(H // 2):
            at = slice(g * LANE, (g + 1) * LANE)
            block = q_all[:, at]
            q_ref[:, at] = (block * cosines + turned(block, lane) * sines).astype(BF)
        kv = dot(normed, columns(H * HD, 2 * KVH * HD))
        for m in range(KVH // 2):
            block = kv[:, m * LANE : (m + 1) * LANE]
            block = block * cosines + turned(block, lane) * sines
            other = pltpu.roll(block, HD, 1)
            kd_ref[:, 2 * m * LANE : (2 * m + 1) * LANE] = jnp.where(low_lane, block, other).astype(BF)
            kd_ref[:, (2 * m + 1) * LANE : (2 * m + 2) * LANE] = jnp.where(low_lane, other, block).astype(BF)
            block = kv[:, KVH * HD + m * LANE : KVH * HD + (m + 1) * LANE]
            other = pltpu.roll(block, HD, 1)
            vd_ref[:, 2 * m * LANE : (2 * m + 1) * LANE] = jnp.where(low_lane, block, other).astype(BF)
            vd_ref[:, (2 * m + 1) * LANE : (2 * m + 2) * LANE] = jnp.where(low_lane, other, block).astype(BF)
        saves = [
            pltpu.make_async_copy(ref, heads_hbm.at[i], heads_sem.at[i]) for i, ref in enumerate((q_ref, kd_ref, vd_ref, o_ref))
        ]
        for save in saves[:3]:
            save.start()
        bias = jnp.where((row_segment == column_segment) & (column <= row), 0.0, masked_score)
        bias = jnp.concatenate([bias, bias], axis=0)

        def p_copy(g):
            return pltpu.make_async_copy(p_ref.at[g % 2], p_hbm.at[g], p_sem.at[g % 2])

        for g in range(KVH):
            at = slice(g * LANE, (g + 1) * LANE)
            queries = halves(q_ref[:, at].astype(F32), low_lane).astype(BF)
            scores = dot_nt(queries, kd_ref[:, at]) * score_scale + bias
            shifted = jnp.exp(scores - jnp.max(scores, axis=1, keepdims=True))
            weights = shifted * (1.0 / jnp.sum(shifted, axis=1, keepdims=True))
            if g >= 2:
                p_copy(g - 2).wait()
            p_ref[g % 2] = weights
            p_copy(g).start()
            mixed = dot(weights.astype(BF), vd_ref[:, at])
            o_ref[:, at] = jnp.where(low_lane, mixed[:tokens], mixed[tokens:]).astype(BF)

        saves[3].start()
        if chips > 2:
            both_sides(2, dout_arrive)
        for k in range(1, chips):
            share(k, 1)

        for k in range(chips):
            to_mate(k, 1 - c, 1).wait_recv()
        after = source + residual_scale * dot(o_ref[...], columns(W_O, D))
        h1_ref[...] = after
        factor = lax.rsqrt(jnp.mean(after * after, axis=1, keepdims=True) + norm_eps)
        normed = (after * factor * gain_two).astype(BF)
        n2_all[z, c] = normed
        logits = dot(normed, small).T[:E]
        expert = lax.broadcasted_iota(jnp.int32, (E, tokens), 0)
        routed = routes_ref[0:1] == expert
        for j in range(1, TOPK):
            routed |= routes_ref[j : j + 1] == expert
        top = jnp.max(jnp.where(routed, logits, masked_score), axis=0, keepdims=True)
        powers = jnp.where(routed, jnp.exp(logits - top), 0.0)
        gates = powers / jnp.sum(powers, axis=0, keepdims=True)
        gates = jnp.where(routed, gates, -1.0)
        gt_all[z, c] = gates
        gd_ref[...] = jnp.concatenate([gates, jnp.full((LANE - E, tokens), -1.0, F32)], axis=0).T
        for g in (KVH - 2, KVH - 1):
            p_copy(g).wait()
        for save in saves:
            save.wait()

    pl.run_scoped(forward, pltpu.VMEM((2, 2 * tokens, tokens), F32), *[pltpu.VMEM((tokens, D), BF)] * 4)

    def bit_of(b):
        return (r // (1 << b)) % 2

    def partner(b):
        return (r + (1 - 2 * bit_of(b)) * (1 << b), f)

    stages = {}

    def landed(ref, name):
        stage, sem = stages[name]
        if ref.shape != stage.shape:
            stage = stage.at[pl.ds(0, ref.shape[0])]
        copy = pltpu.make_async_copy(ref, stage, sem)
        copy.start()
        copy.wait()
        return stage

    def halving(e):
        size = ge_ref.shape[1] // bits
        orders = [[(g + k) % bits for k in range(bits)] for g in range(bits)]
        starts = [[] for _ in range(bits)]
        for g in range(bits):
            at = g * size
            for k in range(bits):
                starts[g].append(at)
                at = at + bit_of(orders[g][k]) * (size >> (k + 1))
            starts[g].append(at)

        def region(g, k):
            half = size >> (k + 1)
            return ge_ref.at[e, pl.ds(pl.multiple_of(starts[g][k + 1], half), half)]

        def exchange(g, k):
            half, job = size >> (k + 1), e * bits + g
            give = pl.multiple_of(starts[g][k] + (1 - bit_of(orders[g][k])) * half, half)
            return make(
                ge_ref.at[e, pl.ds(give, half)], arrived[k].at[job], ar_send.at[job, k], ar_recv.at[job, k],
                partner(orders[g][k]),
            )

        def spread(g, k):
            job, ref = e * bits + g, region(g, k)
            return make(ref, ref, ar_send.at[job, bits + k], ar_recv.at[job, bits + k], partner(orders[g][k]))

        def spread_once_free(g, k):
            pl.semaphore_wait(ar_free.at[e * bits + g, k], 1)
            spread(g, k).start()

        yield
        for g in range(bits):
            exchange(g, 0).start()
        yield
        for k in range(bits):
            half = size >> (k + 1)
            for g in range(bits):
                job = e * bits + g
                exchange(g, k).wait_recv()
                own = region(g, k)
                add_rows(own, own, landed(arrived[k].at[job], "halves"), half, min(half, 64))
                if k < bits - 1:
                    exchange(g, k + 1).start()
                exchange(g, k).wait_send()
                pl.semaphore_signal(
                    ar_free.at[job, k], inc=1, device_id=partner(orders[g][k]), device_id_type=pl.DeviceIdType.MESH
                )
                if k == bits - 1:
                    spread_once_free(g, k)
            yield
        for k in range(bits - 1, -1, -1):
            for g in range(bits):
                spread(g, k).wait_recv()
                if k > 0:
                    spread_once_free(g, k - 1)
            yield
        for g in range(bits):
            for k in range(bits):
                spread(g, k).wait_send()
        pltpu.make_async_copy(ge_ref.at[e], ge_hbm.at[e], ge_sem.at[e]).start()

    sums = [halving(e) for e in range(local)] if bits else []
    first, last = sums[:1], sums[1:]
    for process in sums:
        next(process)

    def pass_on(zb, how):
        to = {"up": above, "down": below, "mate": mate}[how]
        sems = {"up": (n2_up, gt_up), "down": (n2_down, gt_down), "mate": (n2_mate, gt_mate)}[how]
        return [
            make(ref.at[zb, c], ref.at[zb, c], sem.at[zb], recv.at[zb, c], to)
            for ref, sem, recv in ((gt_all, sems[1], gt_recv), (n2_all, sems[0], n2_recv))
        ]

    def got(zb, core):
        for ref, sem, recv in ((gt_all, gt_mate, gt_recv), (n2_all, n2_mate, n2_recv)):
            make(ref.at[zb, core], ref.at[zb, core], sem.at[zb], recv.at[zb, core], mate).wait_recv()

    def start(copies):
        for copy in copies:
            copy.start()

    @pl.when(z < chips - 1)
    def _():
        start(pass_on(z, "up"))

    @pl.when(z > 0)
    def _():
        start(pass_on(z, "down"))

    start(pass_on(z, "mate"))
    inner = jnp.minimum(z, chips - 1 - z)

    def place(t):
        k = (t + 1) // 2
        near = jnp.where(t % 2 == 1, z - k, z + k)
        return jnp.where(t <= 2 * inner, near, jnp.where(2 * z < chips - 1, t, chips - 1 - t))

    def far(zc):
        return jnp.where(zc > z, zc - z, z - zc)

    def side_of(zc):
        return jnp.where(zc > z, 1, 0)

    def relay(k, low, high):
        @pl.when(low)
        def _():
            pl.when(k > 2)(lambda: dout_arrive(z - k, True))
            got(z - k, c)

            @pl.when(z < chips - 1)
            def _():
                start(pass_on(z - k, "up"))

            start(pass_on(z - k, "mate"))

        @pl.when(high)
        def _():
            pl.when(k > 2)(lambda: dout_arrive(z + k, False))
            got(z + k, c)

            @pl.when(z > 0)
            def _():
                start(pass_on(z + k, "down"))

            start(pass_on(z + k, "mate"))

    def early(t):
        return (t >= 2) & (t % 2 == 0) & (t <= 2 * inner) & (t < chips - 1)

    def pair_copy(side):
        owner = z + 2 * side - 1
        return make(pair_ref.at[side], from_ref.at[z], pair_send.at[side], far_recv.at[z], (r, owner * 2 + c))

    def experts_and_sums(do_buf, xs_ref, dye_ref, dgu_ref, hx_ref, dxp_ref, yps_ref, core_stage):
        stages["core"] = (core_stage, stage_sem.at[0])
        before = lax.broadcasted_iota(jnp.int32, (tokens, tokens), 0) < lax.broadcasted_iota(jnp.int32, (tokens, tokens), 1)
        before = before.astype(F32).astype(BF)
        slot_index = lax.broadcasted_iota(jnp.int32, (CAP, tokens), 0).astype(F32)
        pair = 2 * CAP

        def do_copy(zc):
            return pltpu.make_async_copy(do_all.at[zc], do_buf, do_sem.at[0])

        def core_copy(zc, slot, t):
            return make(dxp_ref.at[slot, 1 - c], core_ref.at[zc], core_send.at[t], core_recv.at[zc], mate)

        def y_copy(zc, slot, t):
            return make(yps_ref.at[slot], y_core.at[zc], yc_send.at[t], yc_recv.at[zc], mate)

        def via_copy(zc, slot, t):
            side = side_of(zc)
            return make(
                dxp_ref.at[slot, c], via_ref.at[side], far_send.at[t], via_recv.at[side], (r, (z + 2 * side - 1) * 2 + c)
            )

        def far_copy(zc, slot, t):
            return make(dxp_ref.at[slot, c], from_ref.at[z], far_send.at[t], far_recv.at[z], (r, zc * 2 + c))

        def dgt_copy(zc, core, t):
            return make(dgt_ref.at[t, core], dgt_all.at[f], dgt_send.at[t, core], dgt_recv.at[f], (r, zc * 2 + core))

        def free_slot(t, slot):
            core_copy(z, slot, t).wait_send()
            y_copy(z, slot, t).wait_send()

            @pl.when(far(place(t)) >= 2)
            def _():
                far_copy(z, slot, t).wait_send()

        def add_ye(zc):
            make(y_core.at[zc], y_core.at[zc], yc_send.at[0], yc_recv.at[zc], mate).wait_recv()
            add_rows(y_ref.at[zc], y_ref.at[zc], landed(y_core.at[zc], "core"), tokens, 64)
            send_sem, _, from_recv = y_sems


        def chunk(t, carry):
            zc = place(t)
            slot = t % 2

            @pl.when(t > 0)
            def _():
                add_ye(place(t - 1))

            k = far(zc)
            both = (t % 2 == 1) & (t <= 2 * inner)
            single = (t > 2 * inner) & jnp.logical_not(early(t - 1))
            relay(k, both | (single & (zc < z)), both | (single & (zc > z)))
            dout_copy(zc, 1 - c, 2).wait_recv()
            do_copy(zc).start()
            got(zc, 1 - c)
            do_copy(zc).wait()

            @pl.when(t == 0)
            def _():
                load_experts.wait()

            @pl.when(t >= 2)
            def _():
                free_slot(t - 2, slot)

            picks, gates, dms = [], [], []
            at_chip = pl.multiple_of(zc * pair, 16)
            for core in range(2):
                mine = [gt_all[zc, core, pl.ds(f * local + i, 1), :] for i in range(local)]
                mine = jnp.concatenate(mine, axis=0) if local > 1 else mine[0]
                rank = jnp.where(mine >= 0.0, dot((mine >= 0.0).astype(F32).astype(BF), before), -1.0)
                chosen = [slot_index == rank[i : i + 1] for i in range(local)]
                gates.append([jnp.sum(jnp.where(chosen[i], mine[i : i + 1], 0.0), axis=1, keepdims=True) for i in range(local)])
                picks.append([one.astype(F32) for one in chosen])
                pick = jnp.concatenate([one.astype(BF) for one in picks[core]], axis=0)
                taken = dot(pick, n2_all[zc, core]).astype(BF)
                grads = dot(pick, do_buf[core])
                dms.append(grads.astype(BF))
                grads = grads * residual_scale
                at = pl.ds(pl.multiple_of(at_chip + core * CAP, 16), CAP)
                for i in range(local):
                    part = slice(i * CAP, (i + 1) * CAP)
                    xs_ref[i, at] = taken[part]
                    dye_ref[i, at] = (gates[core][i] * grads[part]).astype(BF)
            at = pl.ds(at_chip, pair)
            mades, backs = [], []
            for i in range(local):
                slots = xs_ref[i, at]
                gate_pre = dot_nt(slots, ge_ref[i, :FF])
                up_pre = dot_nt(slots, ge_ref[i, FF : 2 * FF])
                grad_act = dot_nt(dye_ref[i, at], ge_ref[i, 2 * FF :])
                sigmoid = 1.0 / (1.0 + jnp.exp(-gate_pre))
                silu = gate_pre * sigmoid
                act = (silu * up_pre).astype(BF)
                hx_ref[i, at] = act
                grad_gate = (grad_act * up_pre * (sigmoid * (1.0 + gate_pre * (1.0 - sigmoid)))).astype(BF)
                grad_up = (grad_act * silu).astype(BF)
                dgu_ref[i, at, :FF] = grad_gate
                dgu_ref[i, at, FF:] = grad_up
                backs.append((dot(grad_gate, ge_ref[i, :FF]) + dot(grad_up, ge_ref[i, FF : 2 * FF])).astype(BF))
            for core in range(2):
                pick = jnp.concatenate([one.astype(BF) for one in picks[core]], axis=0)
                part = slice(core * CAP, (core + 1) * CAP)
                sent = jnp.concatenate([backs[i][part] for i in range(local)], axis=0)
                dxp_ref[slot, core] = dot_tn(pick, sent).astype(BF)
            core_copy(zc, slot, t).start()
            for i in range(local):
                made = dot(hx_ref[i, at], ge_ref[i, 2 * FF :]).astype(BF)
                mades.append(made)
                for core in range(2):
                    part = slice(core * CAP, (core + 1) * CAP)
                    grads = dms[core][i * CAP : (i + 1) * CAP].astype(F32) * residual_scale
                    value = jnp.sum(grads * made[part].astype(F32), axis=1, keepdims=True)
                    dgt_ref[t, core, i : i + 1] = jnp.sum(picks[core][i] * value, axis=0, keepdims=True)
            for core in range(2):

                @pl.when((t > 0) | (c != core))
                def _():
                    dgt_copy(zc, core, t).start()

            @pl.when(early(t))
            def _():
                k_next = t // 2 + 1
                relay(k_next, z >= k_next, z + k_next < chips)

            for core in range(2):
                pick = jnp.concatenate([one.astype(BF) for one in picks[core]], axis=0)
                part = slice(core * CAP, (core + 1) * CAP)
                sent = jnp.concatenate([(gates[core][i] * mades[i][part].astype(F32)).astype(BF) for i in range(local)], axis=0)
                mixed = dot_tn(pick, sent).astype(BF)

                @pl.when(c == core)
                def _():
                    y_ref[zc] = mixed

                @pl.when(c != core)
                def _():
                    yps_ref[slot] = mixed

            y_copy(zc, slot, t).start()
            core_copy(zc, slot, t).wait_recv()
            there = core_ref.at[zc] if roomy else landed(core_ref.at[zc], "core")
            own = dxp_ref.at[slot, c]

            @pl.when(k == 0)
            def _():
                dx_ref[...] = own[...].astype(F32) + there[...].astype(F32)

            @pl.when(k == 1)
            def _():
                side = side_of(zc)
                add_rows(pair_ref.at[side], own, there, tokens, 64)

                @pl.when((z == 0) | (z == chips - 1))
                def _():
                    pair_copy(side).start()

            @pl.when(k >= 2)
            def _():
                add_rows(own, own, there, tokens, 64)

                @pl.when(k == 2)
                def _():
                    via_copy(zc, slot, t).start()

                @pl.when(k > 2)
                def _():
                    far_copy(zc, slot, t).start()

            return carry

        lax.fori_loop(0, chips, chunk, 0)

        for i in range(local):
            ge_ref[i, :FF] = dot_tn(dgu_ref[i, :, :FF], xs_ref[i]).astype(BF)
            ge_ref[i, FF : 2 * FF] = dot_tn(dgu_ref[i, :, FF:], xs_ref[i]).astype(BF)
            ge_ref[i, 2 * FF :] = dot_tn(hx_ref[i], dye_ref[i]).astype(BF)
            if bits:
                next(sums[i])
            if i > 0:
                continue

            @pl.when((z > 0) & (z < chips - 1))
            def _():
                for side in range(2):
                    make(via_ref.at[side], via_ref.at[side], far_send.at[0], via_recv.at[side], mate).wait_recv()
                    add_rows(pair_ref.at[side], pair_ref.at[side], via_ref.at[side], tokens, 64)
                    pair_copy(side).start()

        add_ye(place(chips - 1))
        for t in range(max(chips - 2, 0), chips):
            free_slot(t, t % 2)
        for t in range(chips):
            for core in range(2):

                @pl.when((t > 0) | (c != core))
                def _():
                    dgt_copy(z, core, t).wait_send()

    slots = chips * 2 * CAP
    pl.run_scoped(
        experts_and_sums,
        pltpu.VMEM((2, tokens, D), BF), pltpu.VMEM((local, slots, D), BF), pltpu.VMEM((local, slots, D), BF),
        pltpu.VMEM((local, slots, 2 * FF), BF), pltpu.VMEM((local, slots, FF), BF), pltpu.VMEM((2, 2, tokens, D), BF),
        pltpu.VMEM((2, tokens, D), BF), pltpu.VMEM((tokens, D), BF),
    )

    def line(own, size, step, core_add, name, reach, via, arrive, send_sem, via_recv, from_recv):
        def direct(k):
            return make(own(k), arrive.at[z], send_sem.at[k], from_recv.at[z], (r, k * 2 + c))

        def passing(k, side):
            return make(own(k), via.at[side], send_sem.at[k], via_recv.at[side], (r, (z + 2 * side - 1) * 2 + c))

        def within(k):
            return (k >= 0) & (k < chips)

        for d in range(chips - 1, 0, -1):
            for side in range(2):
                way = 1 if side else -1
                owner = z + d * way

                @pl.when(within(owner))
                def _():
                    core_add(owner)
                    if d > reach + 1:
                        direct(owner).start()
                    elif d == reach + 1:
                        passing(owner, side).start()
                    elif d == reach:
                        pl.when(jnp.logical_not(within(z - way)))(lambda: direct(owner).start())

        core_add(z)
        yield
        for side in range(2):
            way = 1 if side else -1
            owner = z + reach * way

            @pl.when(within(owner) & within(z - way))
            def _():
                make(via.at[side], via.at[side], send_sem.at[0], via_recv.at[side], mate).wait_recv()
                add_rows(own(owner), own(owner), landed(via.at[side], name), size, step)
                direct(owner).start()

        yield
        for k in range(chips):

            @pl.when((z != k) & (far(k) != reach + 1))
            def _():
                make(arrive.at[k], arrive.at[k], send_sem.at[0], from_recv.at[k], mate).wait_recv()
                add_rows(own(z), own(z), landed(arrive.at[k], name), size, step)

        for k in range(chips):

            @pl.when(z != k)
            def _():
                direct(k).wait_send()

    def mixture():
        yield from line(lambda k: y_ref.at[k], tokens, 64, lambda k: None, "tokens", 1, y_via, y_from, *y_sems)
        out_ref[...] = (h1_ref[...] + residual_scale * y_ref[z].astype(F32)).astype(BF)

    def attention(q_ref, kd_ref, vd_ref, o_ref, p_ref, do_ref, dqkv_ref, gkv_ref, gq_ref, go_ref, halves_stage, tokens_stage, kv_stage, o_stage):
        loads = [
            pltpu.make_async_copy(heads_hbm.at[i], ref, heads_sem.at[i]) for i, ref in enumerate((q_ref, kd_ref, vd_ref, o_ref))
        ]
        start(loads)
        stages["halves"] = (halves_stage, stage_sem.at[1])
        stages["tokens"] = (tokens_stage, stage_sem.at[2])
        stages["kv"] = (kv_stage, stage_sem.at[3])
        stages["o"] = (o_stage, stage_sem.at[4])
        def projection(index, name, grad_ref, core, via, arrive, sems):
            core_sem, *sems = sems
            parts, results, wide = parts_ref.at[index], results_ref.at[index], D // replicas
            crossing = make(grad_ref.at[:, 1 - c], core, core_sem.at[0], core_sem.at[1], mate)
            crossing.start()
            yield
            crossing.wait_recv()

            def own(k):
                return grad_ref.at[k, c]

            yield from line(
                own, rows, 16, lambda k: add_rows(own(k), own(k), core.at[k], rows, 16), name, 1, via, arrive, *sems
            )
            crossing.wait_send()
            mine = grad_ref.at[z, c]

            def columns(part):
                return pl.ds(pl.multiple_of(part * wide, LANE), wide)

            def part_copy(d):
                to = (r + d) % replicas
                return make(
                    mine.at[:, columns(to)], parts.at[r], part_send.at[index, d], part_recv.at[index, r], (to, f)
                )

            def small_copy(d):
                to = (r + d) % replicas
                return make(mine.at[:, pl.ds(D, LANE)], smalls_ref.at[r], small_send.at[d], small_recv.at[r], (to, f))

            for d in range(1, replicas):
                part_copy(d).start()
                if index == 0:
                    small_copy(d).start()
            parts[r] = mine[:, columns(r)]
            if index == 0:
                smalls_ref[r] = mine[:, pl.ds(D, LANE)]
            yield
            for d in range(1, replicas):
                peer = (r + d) % replicas
                make(
                    parts.at[peer], parts.at[peer], part_send.at[index, d], part_recv.at[index, peer], (peer, f)
                ).wait_recv()
                if index == 0:
                    make(
                        smalls_ref.at[peer], smalls_ref.at[peer], small_send.at[d], small_recv.at[peer], (peer, f)
                    ).wait_recv()
            total = parts[0].astype(F32)
            for k in range(1, replicas):
                total = total + parts[k].astype(F32)
            results[r] = total.astype(BF)

            def result_copy(d):
                to = (r + d) % replicas
                return make(
                    results.at[r], results.at[r], result_send.at[index, d], result_recv.at[index, r], (to, f)
                )

            for d in range(1, replicas):
                result_copy(d).start()
            if index == 0:
                small = smalls_ref[0].astype(F32)
                for k in range(1, replicas):
                    small = small + smalls_ref[k].astype(F32)
                total_ref[...] = small
            yield
            for d in range(1, replicas):
                peer = (r + d) % replicas
                make(
                    results.at[peer], results.at[peer], result_send.at[index, d], result_recv.at[index, peer], (peer, f)
                ).wait_recv()
            for d in range(1, replicas):
                part_copy(d).wait_send()
                if index == 0:
                    small_copy(d).wait_send()
                result_copy(d).wait_send()

        moe = [mixture()]
        kvs = [projection(0, "kv", gkv_ref, kv_core, kv_via, kv_from, kv_sems)]
        outs = [projection(1, "o", go_ref, o_core, o_via, o_from, o_sems)]
        qs = [projection(2, "o", gq_ref, q_core, q_via, q_from, q_sems)]

        def go(*turns):
            for turn in turns:
                for process in turn:
                    next(process, None)

        def dgate():
            found = [dgt_all[k, :local] for k in range(2 * chips)]
            return jnp.concatenate(found + [jnp.zeros((LANE - E, tokens), F32)], axis=0).T

        for k in range(chips):

            @pl.when((z == k + 1) | (z + 1 == k) | (z > k + 2) | (z + 2 < k))
            def _():
                make(from_ref.at[k], from_ref.at[k], far_send.at[0], far_recv.at[k], mate).wait_recv()
                there = from_ref.at[k] if roomy else landed(from_ref.at[k], "tokens")
                add_rows(dx_ref, dx_ref, there, tokens, 64)

        for k in range(2 * chips):

            @pl.when(f == k)
            def _():
                for core in range(2):

                    @pl.when(c == core)
                    def _():
                        dgt_all[k] = dgt_ref[0, core]

            @pl.when(f != k)
            def _():
                make(dgt_all.at[k], dgt_all.at[k], dgt_send.at[0, 0], dgt_recv.at[k], mate).wait_recv()

        for load in loads:
            load.wait()
        backward = attention_backward(
            x_ref, dout_ref, cos_ref, sin_ref, columns, q_ref, kd_ref, vd_ref, p_hbm, o_ref, h1_ref, n2_all.at[z, c], gd_ref,
            dx_ref, dgate, gin_ref, gq_ref, gkv_ref, go_ref, do_ref, dqkv_ref, p_ref, p_sem,
        )
        next(backward)
        go(outs)
        next(backward)
        go(first)
        next(backward)
        go(outs)
        next(backward)
        go(qs)
        next(backward, None)
        go(kvs, last, qs, first, kvs, last, outs, first, moe, last, qs, outs, kvs, outs, first, qs, outs, moe, qs, kvs, moe, last)
        go(qs, kvs, kvs)
        go(*[moe + outs + qs + kvs + sums] * (2 * bits + 8))

    size = ge_ref.shape[1] // max(bits, 1)
    pl.run_scoped(
        attention, *[pltpu.VMEM((tokens, D), BF)] * 4,
        pltpu.VMEM((2, 2 * tokens, tokens), F32), pltpu.VMEM((tokens, D), BF),
        pltpu.VMEM((tokens, QKV), BF), pltpu.VMEM((chips, 2, rows, D + LANE), BF), pltpu.VMEM((chips, 2, rows, D), BF),
        pltpu.VMEM((chips, 2, rows, D), BF), pltpu.VMEM((size // 2, D), BF), pltpu.VMEM((tokens, D), BF),
        pltpu.VMEM((rows, D + LANE), BF), pltpu.VMEM((rows, D), BF),
    )

    for e in range(local):
        copy = pltpu.make_async_copy(ge_ref.at[e], ge_hbm.at[e], ge_sem.at[e])
        if not bits:
            copy.start()
        copy.wait()
    for side in range(2):

        @pl.when(z > 0 if side == 0 else z < chips - 1)
        def _():
            pair_copy(side).wait_send()

    for k in range(chips):

        @pl.when((z >= k) & (z < chips - 1))
        def _():
            for copy in pass_on(k, "up"):
                copy.wait_send()

        @pl.when((z <= k) & (z > 0))
        def _():
            for copy in pass_on(k, "down"):
                copy.wait_send()

        for copy in pass_on(k, "mate"):
            copy.wait_send()

    for k in range(chips):
        for late in range(2):
            to_mate(k, c, late).wait_send()
        dout_copy(k, c, 2).wait_send()

        @pl.when((z >= k) & (z < chips - 1))
        def _():
            dout_copy(k, c, 0).wait_send()
            for kind in range(3):
                along(k, kind, True).wait_send()

        @pl.when((z <= k) & (z > 0))
        def _():
            dout_copy(k, c, 1).wait_send()
            for kind in range(3):
                along(k, kind, False).wait_send()

        @pl.when(z != k)
        def _():
            for d in range(1, replicas):
                for kind in (0, 2):
                    across(k, kind, d).wait_send()


def finish(gexp_ref, results_ref, total_ref, gin_ref, out_ref, *outs):
    layer_out, grad_in, gains_one, query, key, value, output, gains_two, router, expert = outs
    expert[...] = gexp_ref[...].astype(F32)
    layer_out[...] = out_ref[...]
    grad_in[...] = gin_ref[...]
    for index, targets in ((0, (key, value)), (1, (output,)), (2, (query,))):
        start, wide = 0, results_ref.shape[3]
        for ref in targets:
            for at in range(0, ref.shape[1], LANE):
                part, column = divmod(start + at, wide)
                ref[:, at : at + LANE] = results_ref[index, part, :, column : column + LANE].astype(F32)
            start += ref.shape[1]

    @pl.when(pl.program_id(0) == 0)
    def _():
        small = total_ref[...].T
        router[...] = small[:E]
        gains_one[...] = small[E : E + 1]
        gains_two[...] = small[E + 1 : E + 2]


def call(kernel, out_shape, args, scratch=(), outside=0, out_outside=0, **params):
    spaces = [pltpu.SMEM if a.dtype == jnp.int32 and a.size <= 16 else pltpu.VMEM for a in args]
    spaces[len(args) - outside :] = [pl.ANY] * outside
    return pl.pallas_call(
        kernel,
        out_shape=out_shape,
        in_specs=[pl.BlockSpec(memory_space=space) for space in spaces],
        out_specs=[
            pl.BlockSpec(memory_space=pltpu.VMEM if i < len(out_shape) - out_outside else pl.ANY)
            for i in range(len(out_shape))
        ],
        scratch_shapes=list(scratch),
        compiler_params=pltpu.CompilerParams(
            vmem_limit_bytes=VMEM_LIMIT, has_side_effects="collective_id" in params, **params
        ),
    )(*args)


def shape(dims, dtype):
    return jax.ShapeDtypeStruct(dims, dtype)


def make_body(mesh):
    group, replicas = mesh.shape["fsdp"], mesh.shape["replica"]
    local = E // group

    def body(
        hidden_in, seq_lengths, routes, norm1_gain, w_query, w_key, w_value, w_output, norm2_gain, w_router,
        expert_weights, out_cotangent,
    ):
        tokens = hidden_in.shape[0]
        rows = w_query.shape[0]
        chips = group // 2
        dma = pltpu.SemaphoreType.DMA
        bits = replicas.bit_length() - 1
        size = 3 * FF // bits if bits else 0
        roomy = chips <= 4
        landing = [shape((local * bits, size >> (k + 1), D), BF) for k in range(bits)]
        blocks = [shape((chips, tokens, D), BF)] * 2
        landing += [shape((chips, tokens, D), BF)]
        if not roomy:
            landing += blocks
        outs = call(
            functools.partial(layer, replicas, chips),
            [
                shape((tokens, D), F32), shape((tokens, D), BF), shape((3, replicas, rows, D // replicas), BF),
                shape((rows, LANE), F32), shape((local, 3 * FF, D), BF),
                shape((KVH, 2 * tokens, tokens), F32), shape((4, tokens, D), BF), shape((chips, 2, tokens, D), BF),
                shape((2, tokens, D), BF), shape((chips, tokens, D), BF), shape((2, rows, D + LANE), BF),
                shape((chips, rows, D + LANE), BF), shape((2, rows, D), BF), shape((chips, rows, D), BF),
                shape((2, rows, D), BF), shape((chips, rows, D), BF),
            ]
            + landing,
            (
                hidden_in, seq_lengths, routes.T, rope_table(tokens), w_query, w_key, w_value, w_output, w_router.T,
                norm1_gain[None], norm2_gain[None], out_cotangent, expert_weights,
            ),
            [
                pltpu.VMEM((chips, 2, rows, W_O + D), BF), pltpu.VMEM((tokens, D), F32),
                pltpu.VMEM((tokens, LANE), F32), pltpu.VMEM((tokens, LANE), F32), pltpu.VMEM((tokens, LANE), F32),
                dma((4,)), dma((1,)), dma((3, chips)), dma((3, chips)), dma((3, chips)), dma((3, chips, replicas)),
                dma((3, chips, replicas)), dma((2, chips)), dma((2, chips)), dma((3, chips)), dma((chips, 2)),
                pltpu.VMEM((local, 3 * FF, D), BF), pltpu.VMEM((chips, 2, tokens, D), BF),
                pltpu.VMEM((chips, 2, E, tokens), F32), pltpu.VMEM((2, tokens, D), BF), pltpu.VMEM((2, tokens, D), BF),
                pltpu.VMEM((chips, 2, 8, tokens), F32), pltpu.VMEM((group, 8, tokens), F32),
                pltpu.VMEM((chips, tokens, D), BF), pltpu.VMEM((chips, rows, D + LANE), BF), pltpu.VMEM((chips, rows, D), BF),
                pltpu.VMEM((chips, rows, D), BF), pltpu.VMEM((3, replicas, rows, D // replicas), BF),
                pltpu.VMEM((replicas, rows, LANE), BF),
            ]
            + ([pltpu.VMEM(b.shape, b.dtype) for b in blocks] if roomy else [])
            + ([dma((chips,))] * 3 + [dma((chips, 2))]) * 2 + [dma((chips,))] * 4 + [dma((2,))] * 2
            + [dma((chips, 2)), dma((group,)), dma((chips,)), dma((chips,))]
            + [dma((1,)), dma((1,)), dma((5,)), dma((local,)), dma((2,))]
            + [dma((max(local * bits, 1), max(2 * bits, 1)))] * 2
            + [pltpu.SemaphoreType.REGULAR((max(local * bits, 1), max(bits, 1)))]
            + [dma((chips,)), dma((2,)), dma((chips,))] + [dma((2,)), dma((chips,)), dma((2,)), dma((chips,))] * 3
            + [dma((3, replicas))] * 2 + [dma((replicas,))] * 2 + [dma((3, replicas))] * 2,
            outside=1,
            out_outside=12 + len(landing),
            collective_id=0,
        )
        grad_in, layer_out, results, total, grad_experts = outs[:5]
        steps = 4

        def moving(a, dim=0):
            block = tuple(n // steps if i == dim else n for i, n in enumerate(a.shape))
            return pl.BlockSpec(block, lambda i: tuple(i if at == dim else 0 for at in range(len(block))))

        def still(a):
            return pl.BlockSpec(a.shape, lambda i: (0,) * len(a.shape))

        grad_experts = grad_experts.reshape(local * 3 * FF, D)
        gain, router = shape((1, rows), F32), shape((E, rows), F32)
        wide, narrow = shape((rows, D), F32), shape((rows, KVH * HD), F32)
        out_shapes = [
            shape((tokens, D), BF), shape((tokens, D), F32), gain, wide, narrow, narrow, wide, gain, router,
            shape((local * 3 * FF, D), F32),
        ]
        outs = pl.pallas_call(
            finish,
            grid=(steps,),
            in_specs=[moving(grad_experts), moving(results, 2), still(total), moving(grad_in), moving(layer_out)],
            out_specs=[still(a) if a in (gain, router) else moving(a) for a in out_shapes],
            out_shape=out_shapes,
            compiler_params=pltpu.CompilerParams(vmem_limit_bytes=VMEM_LIMIT),
        )(grad_experts, results, total, grad_in, layer_out)
        return (
            outs[0], outs[1], outs[2][0], outs[3], outs[4], outs[5], outs[6], outs[7][0], outs[8].T,
            outs[9].reshape(local, 3 * FF, D),
        )

    return body


def solution(mesh):
    tokens, weights = P(("replica", "fsdp"), None), P("fsdp", None)
    return jax.shard_map(
        make_body(mesh),
        mesh=mesh,
        in_specs=(
            tokens, tokens, tokens, P("fsdp"), weights, weights, weights, weights, P("fsdp"), weights,
            P("fsdp", None, None), tokens,
        ),
        out_specs=(
            tokens, tokens, P("fsdp"), weights, weights, weights, weights, P("fsdp"), weights, P("fsdp", None, None),
        ),
        check_vma=False,
    )
```
